32 devices in a mesh: seq: 4 (over z), exp: 8 (over y, x, core).
Axes of the slice: x: 2, y: 2, z: 4, core: 2. Of those that a mesh axis runs over, the one named last changes fastest.
Arguments:
- layer_in: bfloat16 [2, 4096, 768], P(None, ('seq', 'exp')), may hold values from -6 to 6
- mixer_gain: float32 [768], replicated, may hold values from 0.5 to 1.5
- in_proj: bfloat16 [768, 3072], replicated, may hold values from -0.21875 to 0.21875
- conv_weight: float32 [4, 1536], replicated, may hold values from -3 to 3
- conv_bias: float32 [1536], replicated, may hold values from -3 to 3
- state_proj: bfloat16 [1536, 80], replicated, may hold values from -0.15625 to 0.15625
- delta_proj: bfloat16 [48, 1536], replicated, may hold values from -0.875 to 0.875
- delta_bias: float32 [1536], replicated, may hold values from -7 to -3
- decay_log: float32 [16, 1536], replicated, may hold values from -4 to 1.5
- skip_gain: float32 [1536], replicated, may hold values from 0.5 to 1.5
- out_proj: bfloat16 [1536, 768], replicated, may hold values from -0.3125 to 0.3125
- expert_norm: float32 [768], replicated, may hold values from 0.5 to 1.5
- router_weight: float32 [768, 8], replicated, may hold values from -0.15 to 0.15
- expert_up: bfloat16 [8, 768, 3072], P('exp', None, 'seq'), may hold values from -0.21875 to 0.21875
- expert_down: bfloat16 [8, 3072, 768], P('exp', 'seq'), may hold values from -6 to 6
- expert_ids: int32 [2, 4096], P(None, ('seq', 'exp')), may hold values from 0 to 7
- capacity_slot: int32 [2, 4096], P(None, ('seq', 'exp')), may hold values from 0 to 40, as said below
- out_grad: bfloat16 [2, 4096, 768], P(None, ('seq', 'exp')), may hold values from -6 to 6
Outputs:
- layer_out: bfloat16 [2, 4096, 768], P(None, ('seq', 'exp'))
- in_grad: float32 [2, 4096, 768], P(None, ('seq', 'exp'))
- grad_mixer_gain: float32 [768], replicated
- grad_in_proj: float32 [768, 3072], replicated
- grad_conv_weight: float32 [4, 1536], replicated
- grad_conv_bias: float32 [1536], replicated
- grad_state_proj: float32 [1536, 80], replicated
- grad_delta_proj: float32 [48, 1536], replicated
- grad_delta_bias: float32 [1536], replicated
- grad_decay_log: float32 [16, 1536], replicated
- grad_skip_gain: float32 [1536], replicated
- grad_out_proj: float32 [1536, 768], replicated
- grad_expert_norm: float32 [768], replicated
- grad_router: float32 [768, 8], replicated
- grad_expert_up: float32 [8, 768, 3072], P('exp', None, 'seq')
- grad_expert_down: float32 [8, 3072, 768], P('exp', 'seq')
The draws below stay inside these ranges and needn't reach their ends.
Inputs may be any that keep to these rules, and one draw needn't show every extreme that they name: Each device holds the same 128 positions of every sequence; its 256 tokens are ordered by sequence, then position. capacity_slot is the number of earlier tokens of the same device with the same expert, or 40 where that number is 40 or more (such tokens are dropped).
All inputs are finite; a program needn't handle non-finite values.
Results may differ from the reference program's by a relative error of at most 0.011.
Values may be sent and summed in bfloat16 or wider, within the bound.
A program may use at most 256 MiB of HBM per device.

```python
import jax
import jax.numpy as jnp
from jax import lax

D = 768
DI = 1536
NS = 16
R = 48
KW = 4
FF = 3072
SEQS = 2
PIECE = 128
EXPERTS = 8
LENGTH = 4096
CAP = 40


def route_tables(key):
    devices = LENGTH // PIECE
    per_device = SEQS * PIECE
    capacity = (5 * per_device + 4 * EXPERTS - 1) // (4 * EXPERTS)
    base_key = jax.random.fold_in(key, 7)
    key_choice, key_favored, key_order = jax.random.split(base_key, 3)
    chosen = jax.random.randint(key_choice, (devices, per_device), 0, EXPERTS)
    favored = jax.random.randint(key_favored, (devices, 1), 0, EXPERTS)
    orders = jax.vmap(lambda order_key: jax.random.permutation(order_key, per_device))(jax.random.split(key_order, devices))
    forced = orders < min(capacity + 8, per_device)
    chosen = jnp.where(forced, favored, chosen).astype(jnp.int32)
    marks = (chosen[:, :, None] == jnp.arange(EXPERTS, dtype=jnp.int32)[None, None, :]).astype(jnp.int32)
    before = jnp.cumsum(marks, axis=1) - marks
    ranking = jnp.sum(before * marks, axis=2)
    slots = jnp.minimum(ranking, capacity).astype(jnp.int32)

    def arrange(values):
        return values.reshape(devices, SEQS, PIECE).transpose(1, 0, 2).reshape(SEQS, devices * PIECE)
    return (arrange(chosen).astype(jnp.int32), arrange(slots).astype(jnp.int32))


def draw_expert_ids(key, part):
    return route_tables(key)[0]


def draw_capacity_slot(key, part):
    return route_tables(key)[1]


def levels(stream_key, shape, cuts, smallest, largest):
    level, own = 1.0, jax.random.fold_in(stream_key, 6)
    for position, blocks in cuts:
        heights = jnp.exp(jax.random.uniform(jax.random.fold_in(own, position), (blocks,), jnp.float32, smallest / len(cuts), largest / len(cuts)))
        level = level * jnp.repeat(heights, shape[position] // blocks).reshape([-1 if axis == position else 1 for axis in range(len(shape))])
    return level


def normal_values(rng, extent, scale, limit, cuts=(), kind=jnp.bfloat16):
    factor_of = levels(rng, extent, cuts, -0.22, 0.18) if cuts else 1.0
    entries = jax.random.normal(rng, extent, jnp.float32) * scale * factor_of
    return jnp.minimum(jnp.maximum(entries, -limit), limit).astype(kind)


def setup_inputs(seed: int = 0) -> dict:
    arg_keys = jax.random.split(jax.random.key(seed), 19)
    return {
        "layer_in": normal_values(arg_keys[0], (SEQS, LENGTH, D), 1.0, 6.0, ((1, 32),)),
        "mixer_gain": jnp.clip(1.0 + 0.1 * jax.random.normal(arg_keys[1], (D,), jnp.float32), 0.5, 1.5),
        "in_proj": normal_values(arg_keys[2], (D, 2 * DI), D ** -0.5, 0.21875),
        "conv_weight": normal_values(arg_keys[3], (KW, DI), KW ** -0.5, 3.0, (), jnp.float32),
        "conv_bias": normal_values(arg_keys[4], (DI,), 0.5, 3.0, (), jnp.float32),
        "state_proj": normal_values(arg_keys[5], (DI, R + 2 * NS), DI ** -0.5, 0.15625),
        "delta_proj": normal_values(arg_keys[6], (R, DI), R ** -0.5, 0.875),
        "delta_bias": jnp.clip(jax.random.uniform(arg_keys[7], (DI,), jnp.float32, -7.0, -3.0), -7.0, -3.0),
        "decay_log": jnp.clip(jax.random.uniform(arg_keys[8], (NS, DI), jnp.float32, -4.0, 1.5), -4.0, 1.5),
        "skip_gain": jnp.clip(jax.random.uniform(arg_keys[9], (DI,), jnp.float32, 0.5, 1.5), 0.5, 1.5),
        "out_proj": normal_values(arg_keys[10], (DI, D), (DI // 4) ** -0.5, 0.3125),
        "expert_norm": jnp.clip(1.0 + 0.1 * jax.random.normal(arg_keys[11], (D,), jnp.float32), 0.5, 1.5),
        "router_weight": normal_values(arg_keys[12], (D, EXPERTS), 0.025, 0.15, (), jnp.float32),
        "expert_up": normal_values(arg_keys[13], (EXPERTS, D, FF), D ** -0.5, 0.21875, ((0, 8), (2, 4))),
        "expert_down": normal_values(arg_keys[14], (EXPERTS, FF, D), 1 ** -0.5, 6.0, ((0, 8), (1, 4))),
        "expert_ids": draw_expert_ids(jax.random.fold_in(arg_keys[18], 71), 0),
        "capacity_slot": draw_capacity_slot(jax.random.fold_in(arg_keys[18], 71), 0),
        "out_grad": normal_values(arg_keys[17], (SEQS, LENGTH, D), 1.0, 6.0, ((1, 32),)),
    }


@jax.custom_vjp
def low(v):
    return lax.optimization_barrier(v.astype(jnp.bfloat16)).astype(jnp.float32)

@jax.custom_vjp
def low_back(v):
    return v

def low_keep(v):
    return (low(v), None)

def low_pass(kept, grad):
    return (grad,)

def back_keep(v):
    return (v, None)

def back_low(kept, grad):
    return (low(grad),)
low.defvjp(low_keep, low_pass)
low_back.defvjp(back_keep, back_low)

def matmul(left, right):
    return jnp.dot(left, right, precision=lax.Precision.HIGHEST, preferred_element_type=jnp.float32)

def rms_norm(values, gain_vec):
    return values * lax.rsqrt(lax.optimization_barrier(jnp.mean(values * values, axis=-1, keepdims=True)) + 1e-05) * gain_vec

def scan_block(state, pieces, decay_rates):

    def one_step(carried, inputs):
        delta_now, drive_now, in_now, out_now = inputs
        carried = jnp.exp(delta_now[None, :] * decay_rates) * carried + in_now[:, None] * drive_now[None, :]
        return (carried, lax.optimization_barrier(jnp.sum(out_now[:, None] * carried, axis=0)))
    return lax.scan(one_step, state, pieces)

def selective_scan(delta, drive, in_coef, out_coef, decay_rates):
    blocks = LENGTH // PIECE
    shaped = tuple((values.reshape(blocks, PIECE, values.shape[-1]) for values in (delta, drive, in_coef, out_coef)))

    def block_step(state, pieces):
        return scan_block(state, pieces, decay_rates)
    initial = jnp.zeros((NS, DI), jnp.float32)
    final_state, outputs = lax.scan(jax.checkpoint(block_step), initial, shaped)
    return outputs.reshape(LENGTH, DI)

def mixer_sequence(seq_in, params):
    mixer_gain, in_proj, conv_weight, conv_bias, state_proj, delta_proj, delta_bias, decay_log, skip_gain, out_proj, expert_norm = params
    normed = low(rms_norm(seq_in, mixer_gain))
    projected = low_back(matmul(normed, in_proj))
    inner = projected[:, :DI]
    gate_half = projected[:, DI:]
    padded = jnp.concatenate([jnp.zeros((KW - 1, DI), jnp.float32), inner], axis=0)
    conv_pre = conv_bias[None, :]
    for tap in range(KW):
        conv_pre = conv_pre + conv_weight[tap][None, :] * padded[tap:tap + LENGTH]
    conv_act = jax.nn.silu(conv_pre)
    projections = matmul(conv_act, state_proj)
    delta_low = projections[:, :R]
    in_coef = projections[:, R:R + NS]
    out_coef = projections[:, R + NS:]
    delta = jax.nn.softplus(matmul(delta_low, delta_proj) + delta_bias)
    decay_rates = -jnp.exp(decay_log)
    scanned = selective_scan(delta, delta * conv_act, in_coef, out_coef, decay_rates)
    mixed = low((scanned + skip_gain * conv_act) * jax.nn.silu(gate_half))
    mixer_out = low_back(matmul(mixed, out_proj))
    resid = seq_in + mixer_out
    return (resid, low(rms_norm(resid, expert_norm)))

def layer_forward(layer_in, mixer_gain, in_proj, conv_weight, conv_bias, state_proj, delta_proj, delta_bias, decay_log, skip_gain, out_proj, expert_norm, router_weight, expert_up, expert_down, expert_ids, capacity_slot):
    params = (mixer_gain, in_proj, conv_weight, conv_bias, state_proj, delta_proj, delta_bias, decay_log, skip_gain, out_proj, expert_norm)

    def per_sequence(carried, seq_in):
        return (carried, mixer_sequence(seq_in, params))
    unused, outputs = lax.scan(jax.checkpoint(per_sequence), jnp.zeros((), jnp.float32), layer_in)
    resid, normed = outputs
    count = SEQS * LENGTH
    flat_resid = resid.reshape(count, D)
    flat_normed = normed.reshape(count, D)
    shares = jax.nn.softmax(matmul(flat_normed, router_weight), axis=-1)
    flat_ids = expert_ids.reshape(count).astype(jnp.int32)
    flat_slot = capacity_slot.reshape(count).astype(jnp.int32)
    onehot = (flat_ids[:, None] == jnp.arange(EXPERTS, dtype=jnp.int32)[None, :]).astype(jnp.float32)
    gate_vals = lax.optimization_barrier(jnp.sum(shares * onehot, axis=-1))
    kept = (flat_slot < CAP).astype(jnp.float32)
    per_expert = LENGTH // PIECE * CAP
    positions = jnp.tile(jnp.arange(LENGTH, dtype=jnp.int32), SEQS)
    owner = (positions // PIECE).astype(jnp.int32)
    target = jnp.where(flat_slot < CAP, flat_ids * per_expert + owner * CAP + flat_slot, EXPERTS * per_expert).astype(jnp.int32)
    table = jnp.full((EXPERTS * per_expert + 1,), count, jnp.int32).at[target].set(jnp.arange(count, dtype=jnp.int32))
    table = table[:-1].reshape(EXPERTS, per_expert).astype(jnp.int32)
    sent_rows = jnp.concatenate([low_back(flat_normed), jnp.zeros((1, D), jnp.float32)], axis=0)

    def expert_apply(pieces):
        row_index, up_weight, down_weight = pieces
        rows = sent_rows[row_index]
        pre_act = low_back(matmul(rows, up_weight))
        hidden = low(jax.nn.gelu(pre_act, approximate=False))
        return low(low_back(matmul(hidden, down_weight)))
    results = lax.map(jax.checkpoint(expert_apply), (table, expert_up, expert_down))
    padded_out = jnp.concatenate([results.reshape(EXPERTS * per_expert, D), jnp.zeros((1, D), jnp.float32)], axis=0)
    token_out = padded_out[target]
    layer_out = flat_resid + (kept * gate_vals)[:, None] * token_out
    return layer_out.reshape(SEQS, LENGTH, D)

def reference(layer_in, mixer_gain, in_proj, conv_weight, conv_bias, state_proj, delta_proj, delta_bias, decay_log, skip_gain, out_proj, expert_norm, router_weight, expert_up, expert_down, expert_ids, capacity_slot, out_grad):
    floats = tuple((value.astype(jnp.float32) for value in (layer_in, mixer_gain, in_proj, conv_weight, conv_bias, state_proj, delta_proj, delta_bias, decay_log, skip_gain, out_proj, expert_norm, router_weight, expert_up, expert_down)))

    def forward(*values):
        return layer_forward(*values, expert_ids, capacity_slot)
    result, pullback = jax.vjp(forward, *floats)
    grads = pullback(out_grad.astype(jnp.float32))
    return (result.astype(jnp.bfloat16), grads[0], grads[1], grads[2], grads[3], grads[4], grads[5], grads[6], grads[7], grads[8], grads[9], grads[10], grads[11], grads[12], grads[13], grads[14])
```

```python
import functools

import jax
import jax.numpy as jnp
from jax import lax
from jax.experimental import pallas as pl
from jax.experimental.pallas import tpu as pltpu
from jax.sharding import PartitionSpec as P

BLK = 16
LANES = 128
GROUP = 512
LOG2E = 1.4426950408889634
LN2 = 0.6931471805599453
VMEM_BYTES = 50 * 1024 * 1024


EPSILON = 1e-05


def shifted(shard, axis, by):
    devices = lax.axis_size(axis)
    pairs = [(i, i + by) for i in range(devices) if 0 <= i + by < devices]
    return lax.ppermute(shard, axis, pairs)


def half_dot(left, right):
    return jnp.dot(left, right, preferred_element_type=jnp.float32)


def exact_dot(left, right):
    return jnp.dot(left, right, precision=lax.Precision.HIGHEST, preferred_element_type=jnp.float32)


def rows_dot(left, right, precision=None):
    return lax.dot_general(
        left,
        right,
        (((0,), (0,)), ((), ())),
        precision=precision,
        preferred_element_type=jnp.float32,
    )


def cols_dot(left, right, precision=None):
    return lax.dot_general(
        left,
        right,
        (((1,), (1,)), ((), ())),
        precision=precision,
        preferred_element_type=jnp.float32,
    )


def norm_forward(values, gain_vec):
    scaling = lax.rsqrt(jnp.mean(values * values, axis=-1, keepdims=True) + EPSILON)
    return (values * scaling * gain_vec, scaling)


def norm_backward(values, scaling, gain_vec, incoming):
    normal = values * scaling
    weighted = incoming * gain_vec
    grad_gain = jnp.sum(incoming * normal, axis=0)
    grad_values = scaling * (
        weighted - normal * jnp.mean(weighted * normal, axis=-1, keepdims=True)
    )
    return (grad_values, grad_gain)


def silu_slope(values):
    sigma = jax.nn.sigmoid(values)
    return sigma * (1.0 + values * (1.0 - sigma))


def exact_gelu(values):
    return jax.nn.gelu(values, approximate=False)


def spread(coef, lanes):
    return jnp.broadcast_to(coef[:, :, None], coef.shape + (lanes,))


def diagonal(coef, block):
    tokens, states = coef.shape
    column = jnp.arange(block * states, dtype=jnp.int32)[None, :] // states
    row = jnp.arange(tokens, dtype=jnp.int32)[:, None] % block
    return jnp.where(column == row, jnp.tile(coef, (1, block)), 0.0).astype(jnp.bfloat16)


def undiagonal(product, block, states):
    tokens = product.shape[0]
    column = jnp.arange(block * states, dtype=jnp.int32)[None, :] // states
    row = jnp.arange(tokens, dtype=jnp.int32)[:, None] % block
    masked = jnp.where(column == row, product, 0.0)
    return jnp.sum(masked.reshape(tokens, block, states), axis=1)


def lane_parts(ref, k, states):
    width = ref.shape[-1]
    return [
        jnp.broadcast_to(ref[k : k + 1, at : at + LANES], (states, LANES))
        for at in range(0, width, LANES)
    ]


def block_of(ref, i):
    return ref.at[pl.ds(pl.multiple_of(i * BLK, BLK), BLK), :]


def rates_of(log_ref):
    rates = -jnp.exp(log_ref[...]) * LOG2E
    return [rates[:, at : at + LANES] for at in range(0, rates.shape[1], LANES)]


def first_pass_kernel(delta_ref, conv_ref, in_ref, log_ref, end_ref, drive):
    steps, width = delta_ref.shape
    states = log_ref.shape[0]
    rates = rates_of(log_ref)
    drive[...] = delta_ref[...] * conv_ref[...]

    def block(i, state):
        state = list(state)
        for k in range(BLK):
            t = i * BLK + k
            inward = in_ref[t]
            deltas = lane_parts(block_of(delta_ref, i), k, states)
            drives = lane_parts(block_of(drive, i), k, states)
            for j in range(width // LANES):
                state[j] = jnp.exp2(deltas[j] * rates[j]) * state[j] + inward * drives[j]
        return tuple(state)

    zero = tuple(jnp.zeros((states, LANES), jnp.float32) for _ in range(width // LANES))
    last = lax.fori_loop(0, steps // BLK, block, zero)
    for j in range(width // LANES):
        end_ref[0, :, j * LANES : (j + 1) * LANES] = last[j]


def second_pass_kernel(
    delta_ref, conv_ref, in_ref, log_ref, start_ref, out_ref, rest_ref, scanned_ref, drive, stack
):
    steps, width = delta_ref.shape
    states = log_ref.shape[0]
    rates = rates_of(log_ref)
    drive[...] = delta_ref[...] * conv_ref[...]

    def block(i, state):
        state = list(state)
        for k in range(BLK):
            t = i * BLK + k
            inward = in_ref[t]
            deltas = lane_parts(block_of(delta_ref, i), k, states)
            drives = lane_parts(block_of(drive, i), k, states)
            for j in range(width // LANES):
                state[j] = jnp.exp2(deltas[j] * rates[j]) * state[j] + inward * drives[j]
                stack[k * states : (k + 1) * states, j * LANES : (j + 1) * LANES] = state[j].astype(
                    jnp.bfloat16
                )
        rows = pl.ds(pl.multiple_of(i * BLK, BLK), BLK)
        both = jnp.concatenate([out_ref[rows, :], rest_ref[rows, :]], axis=0)
        product = jnp.dot(both, stack[...], preferred_element_type=jnp.float32)
        scanned_ref[rows, :] = product[:BLK] + product[BLK:]
        return tuple(state)

    begin = tuple(start_ref[0, :, j * LANES : (j + 1) * LANES] for j in range(width // LANES))
    lax.fori_loop(0, steps // BLK, block, begin)


def back_summary_kernel(delta_ref, grad_ref, out_ref, log_ref, end_ref):
    steps, width = delta_ref.shape
    states = log_ref.shape[0]
    rates = rates_of(log_ref)
    blocks = steps // BLK

    def block(i, state):
        state = list(state)
        for k in reversed(range(BLK)):
            t = (blocks - 1 - i) * BLK + k
            outward = out_ref[t]
            deltas = lane_parts(block_of(delta_ref, blocks - 1 - i), k, states)
            grads = lane_parts(block_of(grad_ref, blocks - 1 - i), k, states)
            for j in range(width // LANES):
                state[j] = jnp.exp2(deltas[j] * rates[j]) * (state[j] + outward * grads[j])
        return tuple(state)

    zero = tuple(jnp.zeros((states, LANES), jnp.float32) for _ in range(width // LANES))
    last = lax.fori_loop(0, blocks, block, zero)
    for j in range(width // LANES):
        end_ref[0, :, j * LANES : (j + 1) * LANES] = last[j]


def backward_kernel(
    delta_ref,
    conv_ref,
    grad_ref,
    in_ref,
    out_ref,
    in_diag_ref,
    log_ref,
    start_ref,
    finish_ref,
    grad_delta_ref,
    grad_conv_ref,
    grad_in_ref,
    grad_out_ref,
    grad_log_ref,
    drive,
    decays,
    carried,
    stack,
    slope,
):
    steps, width = delta_ref.shape
    states = log_ref.shape[0]
    parts = width // LANES
    rates = rates_of(log_ref)
    blocks = steps // BLK
    drive[...] = delta_ref[...] * conv_ref[...]
    first = pl.program_id(1) == 0

    def forward(i, state):
        state = list(state)
        for k in range(BLK):
            t = i * BLK + k
            inward = in_ref[t]
            deltas = lane_parts(block_of(delta_ref, i), k, states)
            drives = lane_parts(block_of(drive, i), k, states)
            for j in range(parts):
                at = slice(j * LANES, (j + 1) * LANES)
                decay = jnp.exp2(deltas[j] * rates[j])
                kept = decay * state[j]
                decays[t, :, at] = decay
                carried[t, :, at] = kept
                state[j] = kept + inward * drives[j]
                stack[k * states : (k + 1) * states, at] = state[j].astype(jnp.bfloat16)
        rows = pl.ds(pl.multiple_of(i * BLK, BLK), BLK)
        partial = cols_dot(grad_ref[rows, :].astype(jnp.bfloat16), stack[...])

        @pl.when(first)
        def _():
            grad_out_ref[rows, :] = partial

        @pl.when(jnp.logical_not(first))
        def _():
            grad_out_ref[rows, :] += partial

        return tuple(state)

    begin = tuple(start_ref[0, :, j * LANES : (j + 1) * LANES] for j in range(parts))
    lax.fori_loop(0, blocks, forward, begin)
    column = lax.broadcasted_iota(jnp.int32, (BLK, BLK * states), 1) // states
    row = lax.broadcasted_iota(jnp.int32, (BLK, BLK * states), 0)
    ones = jnp.where(column == row, 1.0, 0.0).astype(jnp.bfloat16)

    def backward(i, state):
        adjoint, gathered = list(state[:parts]), list(state[parts:])
        for k in reversed(range(BLK)):
            t = (blocks - 1 - i) * BLK + k
            outward = out_ref[t]
            deltas = lane_parts(block_of(delta_ref, blocks - 1 - i), k, states)
            grads = lane_parts(block_of(grad_ref, blocks - 1 - i), k, states)
            for j in range(parts):
                at = slice(j * LANES, (j + 1) * LANES)
                whole = adjoint[j] + outward * grads[j]
                exponent = whole * carried[t, :, at]
                gathered[j] = gathered[j] + exponent * deltas[j]
                slope[k * states : (k + 1) * states, at] = (exponent * rates[j]).astype(
                    jnp.bfloat16
                )
                stack[k * states : (k + 1) * states, at] = whole.astype(jnp.bfloat16)
                adjoint[j] = decays[t, :, at] * whole
        rows = pl.ds(pl.multiple_of((blocks - 1 - i) * BLK, BLK), BLK)
        driven = jnp.dot(in_diag_ref[rows, :], stack[...], preferred_element_type=jnp.float32)
        summed = jnp.dot(ones, slope[...], preferred_element_type=jnp.float32) * LN2
        grad_delta_ref[rows, :] = summed + driven * conv_ref[rows, :]
        grad_conv_ref[rows, :] = driven * delta_ref[rows, :]
        partial = cols_dot(drive[rows, :].astype(jnp.bfloat16), stack[...])

        @pl.when(first)
        def _():
            grad_in_ref[rows, :] = partial

        @pl.when(jnp.logical_not(first))
        def _():
            grad_in_ref[rows, :] += partial

        return tuple(adjoint + gathered)

    ends = tuple(finish_ref[0, :, j * LANES : (j + 1) * LANES] for j in range(parts))
    zero = tuple(jnp.zeros((states, LANES), jnp.float32) for _ in range(parts))
    last = lax.fori_loop(0, blocks, backward, ends + zero)
    for j in range(parts):
        grad_log_ref[0, :, j * LANES : (j + 1) * LANES] = last[parts + j] * rates[j] * LN2


def scan_call(kernel, name, sequences, states, operands, results, scratch):
    tokens, width = next(value.shape for kind, value in operands if kind == "wide")
    steps = tokens // sequences
    specs = {
        "wide": pl.BlockSpec((steps, GROUP), lambda q, j: (q, j)),
        "spread": pl.BlockSpec((steps, states, LANES), lambda q, j: (q, 0, 0)),
        "narrow": pl.BlockSpec((steps, BLK * states), lambda q, j: (q, 0)),
        "rates": pl.BlockSpec((states, GROUP), lambda q, j: (0, j)),
        "state": pl.BlockSpec((1, states, GROUP), lambda q, j: (q, 0, j)),
    }
    shapes = {
        "wide": (tokens, width),
        "narrow": (tokens, BLK * states),
        "state": (sequences, states, width),
    }
    return pl.pallas_call(
        kernel,
        name=name,
        grid=(sequences, width // GROUP),
        in_specs=[specs[kind] for kind, _ in operands],
        out_specs=[specs[kind] for kind in results],
        out_shape=[jax.ShapeDtypeStruct(shapes[kind], jnp.float32) for kind in results],
        scratch_shapes=scratch,
        compiler_params=pltpu.CompilerParams(
            dimension_semantics=("arbitrary", "arbitrary"), vmem_limit_bytes=VMEM_BYTES
        ),
        cost_estimate=pl.CostEstimate(
            flops=20 * tokens * states * width,
            transcendentals=tokens * states * width,
            bytes_accessed=16 * tokens * width,
        ),
    )(*(value for _, value in operands))


MESH = pl.DeviceIdType.MESH


def remote(src, dst, send, arrive, axis, peer):
    return pltpu.make_async_remote_copy(
        src_ref=src,
        dst_ref=dst,
        send_sem=send,
        recv_sem=arrive,
        device_id={axis: peer},
        device_id_type=MESH,
    )


def greet(axes):
    barrier = pltpu.get_barrier_semaphore()
    total = 0
    for axis, size in axes:
        mine = lax.axis_index(axis)
        for k in range(1, size):
            pl.semaphore_signal(
                barrier, inc=1, device_id={axis: lax.rem(mine + k, size)}, device_id_type=MESH
            )
        total += size - 1
    pl.semaphore_wait(barrier, total)


def exchange_kernel(
    reverse,
    planes,
    members,
    end_ref,
    sum_ref,
    rates_ref,
    carry_ref,
    packed,
    landed,
    summary,
    totals,
    starts,
    carries,
    send_one,
    recv_one,
    send_two,
    recv_two,
    send_three,
    recv_three,
):
    sequences, states, width = end_ref.shape
    rows = sequences * states // members
    plane, member = lax.axis_index("seq"), lax.axis_index("exp")
    rates = -jnp.exp(rates_ref[...])
    for i in range(members):
        q, n = (i * rows) // states, (i * rows) % states
        packed[i, :rows] = end_ref[q, n : n + rows]
        packed[i, rows:] = sum_ref[q : q + 1]
    greet((("seq", planes), ("exp", members)))
    for k in range(1, members):
        other = lax.rem(member + k, members)
        remote(
            packed.at[other],
            landed.at[member],
            send_one.at[k],
            recv_one.at[member],
            "exp",
            other,
        ).start()
    landed[member] = packed[member]
    for k in range(1, members):
        other = lax.rem(member + k, members)
        remote(
            packed.at[other], landed.at[other], send_one.at[k], recv_one.at[other], "exp", other
        ).wait()
    order = range(members)[::-1] if reverse else range(members)
    plane_order = range(planes)[::-1] if reverse else range(planes)

    def through(piece, before):
        return jnp.exp(piece[rows:] * rates) * before + piece[:rows]

    state = jnp.zeros((rows, width), jnp.float32)
    total = jnp.zeros((1, width), jnp.float32)
    for i in order:
        piece = landed[i]
        state = through(piece, state)
        total = total + piece[rows:]
    summary[:rows] = state
    summary[rows:] = total
    for k in range(1, planes):
        other = lax.rem(plane + k, planes)
        remote(
            summary, totals.at[plane], send_two.at[k], recv_two.at[plane], "seq", other
        ).start()
    totals[plane] = summary[...]
    for k in range(1, planes):
        other = lax.rem(plane + k, planes)
        remote(summary, totals.at[other], send_two.at[k], recv_two.at[other], "seq", other).wait()
    state = jnp.zeros((rows, width), jnp.float32)
    for s in plane_order:
        reached = plane < s if reverse else plane > s
        state = jnp.where(reached, through(totals[s], state), state)
    for i in order:
        starts[i] = state
        state = through(landed[i], state)
    for k in range(1, members):
        other = lax.rem(member + k, members)
        remote(
            starts.at[other],
            carries.at[member],
            send_three.at[k],
            recv_three.at[member],
            "exp",
            other,
        ).start()
    carries[member] = starts[member]
    for k in range(1, members):
        other = lax.rem(member + k, members)
        remote(
            starts.at[other],
            carries.at[other],
            send_three.at[k],
            recv_three.at[other],
            "exp",
            other,
        ).wait()
    for i in range(members):
        q, n = (i * rows) // states, (i * rows) % states
        carry_ref[q, n : n + rows] = carries[i]


def exchange(local_end, delta_sum, decay_log, reverse):
    sequences, states, width = local_end.shape
    planes, members = lax.axis_size("seq"), lax.axis_size("exp")
    rows = sequences * states // members
    first_row = lax.rem(lax.axis_index("exp") * rows, states)
    own_rates = lax.dynamic_slice(decay_log, (first_row, 0), (rows, width))
    vmem = pl.BlockSpec(memory_space=pltpu.VMEM)
    piece = (rows + 1, width)
    return pl.pallas_call(
        functools.partial(exchange_kernel, reverse, planes, members),
        name="state_exchange_back" if reverse else "state_exchange",
        in_specs=[vmem] * 3,
        out_specs=vmem,
        out_shape=jax.ShapeDtypeStruct(local_end.shape, jnp.float32),
        scratch_shapes=[
            pltpu.VMEM((members,) + piece, jnp.float32),
            pltpu.VMEM((members,) + piece, jnp.float32),
            pltpu.VMEM(piece, jnp.float32),
            pltpu.VMEM((planes,) + piece, jnp.float32),
            pltpu.VMEM((members, rows, width), jnp.float32),
            pltpu.VMEM((members, rows, width), jnp.float32),
            pltpu.SemaphoreType.DMA((members,)),
            pltpu.SemaphoreType.DMA((members,)),
            pltpu.SemaphoreType.DMA((planes,)),
            pltpu.SemaphoreType.DMA((planes,)),
            pltpu.SemaphoreType.DMA((members,)),
            pltpu.SemaphoreType.DMA((members,)),
        ],
        compiler_params=pltpu.CompilerParams(
            collective_id=2 if reverse else 1,
            has_side_effects=True,
            vmem_limit_bytes=VMEM_BYTES,
        ),
        cost_estimate=pl.CostEstimate(flops=10**6, transcendentals=10**5, bytes_accessed=2 * 10**7),
    )(local_end, delta_sum, own_rates)


def total_kernel(planes, chips, count, *refs):
    given, results = refs[:count], refs[count : 2 * count]
    halves, slots, sums, finals = (refs[(2 + i) * count : (3 + i) * count] for i in range(4))
    sends, arrivals = refs[6 * count : 6 * count + 6], refs[6 * count + 6 :]
    plane, member = lax.axis_index("seq"), lax.axis_index("exp")
    chip, core = member // 2, lax.rem(member, 2)
    partner = member + 1 - 2 * core
    barrier = pltpu.get_barrier_semaphore()
    pl.semaphore_signal(barrier, inc=1, device_id={"exp": partner}, device_id_type=MESH)

    def chip_peer(k):
        other = lax.rem(chip + k, chips)
        return other, other * 2 + core

    def plane_peer(k):
        return lax.rem(plane + k, planes)

    for k in range(1, chips):
        pl.semaphore_signal(
            barrier, inc=1, device_id={"exp": chip_peer(k)[1]}, device_id_type=MESH
        )
    for k in range(1, planes):
        pl.semaphore_signal(
            barrier, inc=1, device_id={"seq": plane_peer(k)}, device_id_type=MESH
        )
    pl.semaphore_wait(barrier, chips + planes - 1)

    def pair_half(i):
        return remote(
            given[i].at[1 - core], halves[i], sends[0].at[i], arrivals[0].at[i], "exp", partner
        )

    def scatter_chip(i, k, arriving):
        other, device = chip_peer(k)
        slot = other if arriving else chip
        return remote(
            halves[i].at[other],
            slots[i].at[slot],
            sends[1].at[i, k],
            arrivals[1].at[i, slot],
            "exp",
            device,
        )

    def scatter_plane(i, k, arriving):
        other = plane_peer(k)
        slot = other if arriving else plane
        return remote(
            sums[i].at[other],
            finals[i].at[slot],
            sends[2].at[i, k],
            arrivals[2].at[i, slot],
            "seq",
            other,
        )

    def gather_plane(i, k, arriving):
        other = plane_peer(k)
        slot = other if arriving else plane
        return remote(
            results[i].at[core, chip, plane],
            results[i].at[core, chip, slot],
            sends[3].at[i, k],
            arrivals[3].at[i, slot],
            "seq",
            other,
        )

    def gather_chip(i, k, arriving):
        other, device = chip_peer(k)
        slot = other if arriving else chip
        return remote(
            results[i].at[core, chip],
            results[i].at[core, slot],
            sends[4].at[i, k],
            arrivals[4].at[i, slot],
            "exp",
            device,
        )

    def pair_gather(i, k, arriving):
        other = lax.rem(chip + k, chips)
        half = 1 - core if arriving else core
        return remote(
            results[i].at[core, other],
            results[i].at[half, other],
            sends[5].at[i, k],
            arrivals[5].at[i, other],
            "exp",
            partner,
        )

    wide, half = jnp.float32, jnp.bfloat16
    for i in range(count):
        pair_half(i).start()
    for i in range(count):
        pair_half(i).wait()
        halves[i][...] = (given[i][core].astype(wide) + halves[i][...].astype(wide)).astype(half)
        for k in range(1, chips):
            scatter_chip(i, k, False).start()
        slots[i][chip] = halves[i][chip]
    for i in range(count):
        for k in range(1, chips):
            scatter_chip(i, k, True).wait_recv()
        added = slots[i][0].astype(wide)
        for k in range(1, chips):
            added = added + slots[i][k].astype(wide)
        sums[i][...] = added.astype(half)
        for k in range(1, planes):
            scatter_plane(i, k, False).start()
        finals[i][plane] = sums[i][plane]
    for i in range(count):
        for k in range(1, planes):
            scatter_plane(i, k, True).wait_recv()
        added = finals[i][0].astype(wide)
        for k in range(1, planes):
            added = added + finals[i][k].astype(wide)
        results[i][core, chip, plane] = added.astype(half)
        for k in range(1, planes):
            gather_plane(i, k, False).start()
    for i in range(count):
        for k in range(1, planes):
            gather_plane(i, k, True).wait_recv()
        for k in range(1, chips):
            gather_chip(i, k, False).start()
        pair_gather(i, 0, False).start()
    for i in range(count):
        for k in range(1, chips):
            gather_chip(i, k, True).wait_recv()
            pair_gather(i, k, False).start()
    for i in range(count):
        for k in range(chips):
            pair_gather(i, k, True).wait_recv()
            pair_gather(i, k, False).wait_send()
        for k in range(1, chips):
            scatter_chip(i, k, False).wait_send()
            gather_chip(i, k, False).wait_send()
        for k in range(1, planes):
            scatter_plane(i, k, False).wait_send()
            gather_plane(i, k, False).wait_send()


def total(arrays, collective_id, name):
    planes, members = lax.axis_size("seq"), lax.axis_size("exp")
    chips, count = members // 2, len(arrays)
    shaped = [
        value.reshape((2, chips, planes, value.shape[0] // (members * planes), value.shape[1]))
        for value in arrays
    ]
    tails = [value.shape[3:] for value in shaped]
    vmem = pl.BlockSpec(memory_space=pltpu.VMEM)

    def scratch(*lead):
        return [pltpu.VMEM(lead + tail, jnp.bfloat16) for tail in tails]

    semaphores = [
        pltpu.SemaphoreType.DMA((count,)),
        pltpu.SemaphoreType.DMA((count, chips)),
        pltpu.SemaphoreType.DMA((count, planes)),
        pltpu.SemaphoreType.DMA((count, planes)),
        pltpu.SemaphoreType.DMA((count, chips)),
        pltpu.SemaphoreType.DMA((count, chips)),
    ]
    results = pl.pallas_call(
        functools.partial(total_kernel, planes, chips, count),
        name=name,
        in_specs=[vmem] * count,
        out_specs=[vmem] * count,
        out_shape=[jax.ShapeDtypeStruct(value.shape, jnp.bfloat16) for value in shaped],
        scratch_shapes=scratch(chips, planes)
        + scratch(chips, planes)
        + scratch(planes)
        + scratch(planes)
        + semaphores
        + semaphores,
        compiler_params=pltpu.CompilerParams(
            collective_id=collective_id, has_side_effects=True, vmem_limit_bytes=VMEM_BYTES
        ),
        cost_estimate=pl.CostEstimate(flops=10**7, transcendentals=0, bytes_accessed=10**8),
    )(*shaped)
    return [result.reshape(value.shape) for result, value in zip(results, arrays)]


def on_device(
    layer_in,
    mixer_gain,
    in_proj,
    conv_weight,
    conv_bias,
    state_proj,
    delta_proj,
    delta_bias,
    decay_log,
    skip_gain,
    out_proj,
    expert_norm,
    router_weight,
    expert_up,
    expert_down,
    expert_ids,
    capacity_slot,
    out_grad,
):
    sequences, piece_len, width = layer_in.shape
    tokens = sequences * piece_len
    taps, inner_width = conv_weight.shape
    low_rank = delta_proj.shape[0]
    states = decay_log.shape[0]
    experts = router_weight.shape[1]
    senders = lax.axis_size("exp")
    capacity = (5 * tokens + 4 * experts - 1) // (4 * experts)
    flat_in = layer_in.reshape(tokens, width).astype(jnp.float32)
    normed_one, scaling_one = norm_forward(flat_in, mixer_gain)
    normed_half = normed_one.astype(jnp.bfloat16)
    projected = half_dot(normed_half, in_proj)
    inner = projected[:, :inner_width]
    gate_half = projected[:, inner_width:]
    inner_seq = inner.reshape(sequences, piece_len, inner_width)
    left_rim = shifted(inner_seq[:, piece_len - (taps - 1) :, :], ("seq", "exp"), 1)
    extended = jnp.concatenate([left_rim, inner_seq], axis=1)
    conv_pre = conv_bias + conv_weight[0] * extended[:, 0:piece_len, :]
    for tap in range(1, taps):
        conv_pre = conv_pre + conv_weight[tap] * extended[:, tap : tap + piece_len, :]
    conv_flat = jax.nn.silu(conv_pre).reshape(tokens, inner_width)
    projections = exact_dot(conv_flat, state_proj.astype(jnp.float32))
    delta_low = projections[:, :low_rank]
    in_coef = projections[:, low_rank : low_rank + states]
    out_coef = projections[:, low_rank + states :]
    delta_pre = exact_dot(delta_low, delta_proj.astype(jnp.float32)) + delta_bias
    delta = jax.nn.softplus(delta_pre)
    steps_by = (piece_len, GROUP)
    in_spread, out_spread = spread(in_coef, LANES), spread(out_coef, LANES)
    in_diag, out_diag = diagonal(in_coef, BLK), diagonal(out_coef, BLK)
    out_rest = diagonal(out_coef - lax.reduce_precision(out_coef, 8, 7), BLK)
    float_steps = pltpu.VMEM(steps_by, jnp.float32)
    stack_of = pltpu.VMEM((BLK * states, GROUP), jnp.bfloat16)
    (local_end,) = scan_call(
        first_pass_kernel,
        "first_pass",
        sequences,
        states,
        [("wide", delta), ("wide", conv_flat), ("spread", in_spread), ("rates", decay_log)],
        ["state"],
        [float_steps],
    )
    delta_sum = jnp.sum(delta.reshape(sequences, piece_len, inner_width), axis=1)
    carried = exchange(local_end, delta_sum, decay_log, False)
    (scanned,) = scan_call(
        second_pass_kernel,
        "second_pass",
        sequences,
        states,
        [
            ("wide", delta),
            ("wide", conv_flat),
            ("spread", in_spread),
            ("rates", decay_log),
            ("state", carried),
            ("narrow", out_diag),
            ("narrow", out_rest),
        ],
        ["wide"],
        [float_steps, stack_of],
    )
    mixer_pre = scanned + skip_gain * conv_flat
    gate_act = jax.nn.silu(gate_half)
    mixed = (mixer_pre * gate_act).astype(jnp.bfloat16)
    resid = flat_in + half_dot(mixed, out_proj)
    normed_two, scaling_two = norm_forward(resid, expert_norm)
    routed = normed_two.astype(jnp.bfloat16)
    flat_ids = expert_ids.reshape(tokens)
    flat_slot = capacity_slot.reshape(tokens)
    target = jnp.where(flat_slot < capacity, flat_ids * capacity + flat_slot, experts * capacity)
    slot_rows = jnp.arange(experts * capacity, dtype=jnp.int32)
    picks = (slot_rows[:, None] == target[None, :]).astype(jnp.bfloat16)
    group = lax.axis_size("seq")
    expert = lax.axis_index("exp")

    def to_experts(values):
        buffer = half_dot(picks, values).astype(jnp.bfloat16)
        arrived = lax.all_to_all(
            buffer.reshape(experts, capacity, width), "exp", split_axis=0, concat_axis=0, tiled=True
        )
        return lax.all_gather(arrived.reshape(senders * capacity, width), "seq", axis=0, tiled=True)

    def to_tokens(partial):
        mine = lax.psum_scatter(partial, "seq", scatter_dimension=0, tiled=True)
        back = lax.all_to_all(
            mine.reshape(senders, capacity, width), "exp", split_axis=0, concat_axis=0, tiled=True
        )
        return rows_dot(picks, back.reshape(experts * capacity, width))

    grad_rows = to_experts(out_grad.reshape(tokens, width)).astype(jnp.float32)
    rows = to_experts(routed)
    rows_wide = rows.astype(jnp.float32)
    shares = jax.nn.softmax(exact_dot(rows_wide, router_weight), axis=-1)
    chosen = (jnp.arange(experts, dtype=jnp.int32) == expert).astype(jnp.float32)[None, :]
    gate = jnp.sum(shares * chosen, axis=-1, keepdims=True)
    up, down = expert_up[0], expert_down[0]
    pre_act = half_dot(rows, up)
    hidden_act, gelu_back = jax.vjp(exact_gelu, pre_act)
    hidden_half = hidden_act.astype(jnp.bfloat16)
    expert_out = half_dot(hidden_half, down)
    grad_sent = (gate * grad_rows).astype(jnp.bfloat16)
    grad_gate = jnp.sum(grad_rows * expert_out, axis=-1, keepdims=True)
    grad_logits = grad_gate * gate * (chosen - shares)
    grad_router = rows_dot(rows_wide, grad_logits, lax.Precision.HIGHEST)
    grad_down = rows_dot(hidden_half, grad_sent)
    grad_pre = gelu_back(cols_dot(grad_sent, down))[0].astype(jnp.bfloat16)
    grad_up = rows_dot(rows, grad_pre)
    grad_row_in = cols_dot(grad_pre, up) + cols_dot(
        grad_logits, router_weight, lax.Precision.HIGHEST
    )
    grad_routed = to_tokens(grad_row_in.astype(jnp.bfloat16))
    layer_out = (
        (resid + to_tokens((gate * expert_out).astype(jnp.bfloat16)))
        .astype(jnp.bfloat16)
        .reshape(sequences, piece_len, width)
    )
    grad_top = out_grad.reshape(tokens, width).astype(jnp.float32)
    grad_up_own, grad_down_own = grad_up[None], grad_down[None]
    grad_resid_norm, grad_expert_norm = norm_backward(resid, scaling_two, expert_norm, grad_routed)
    grad_resid = grad_top + grad_resid_norm
    grad_mixer = grad_resid.astype(jnp.bfloat16)
    grad_out_proj = rows_dot(mixed, grad_mixer)
    grad_mixed = cols_dot(grad_mixer, out_proj)
    grad_scan = grad_mixed * gate_act
    grad_gate_half = grad_mixed * mixer_pre * silu_slope(gate_half)
    grad_gate_half = grad_gate_half.astype(jnp.bfloat16)
    grad_in_gate = rows_dot(normed_half, grad_gate_half)
    grad_normed_gate = cols_dot(grad_gate_half, in_proj[:, inner_width:])
    grad_skip_gain = jnp.sum(grad_scan * conv_flat, axis=0)
    (gradient_first,) = scan_call(
        back_summary_kernel,
        "back_summary",
        sequences,
        states,
        [("wide", delta), ("wide", grad_scan), ("spread", out_spread), ("rates", decay_log)],
        ["state"],
        [],
    )
    carried_back = exchange(gradient_first, delta_sum, decay_log, True)
    full_steps = pltpu.VMEM((piece_len, states, GROUP), jnp.float32)
    grad_delta, grad_conv_scan, grad_in_wide, grad_out_wide, grad_log_parts = scan_call(
        backward_kernel,
        "backward_scan",
        sequences,
        states,
        [
            ("wide", delta),
            ("wide", conv_flat),
            ("wide", grad_scan),
            ("spread", in_spread),
            ("spread", out_spread),
            ("narrow", in_diag),
            ("rates", decay_log),
            ("state", carried),
            ("state", carried_back),
        ],
        ["wide", "wide", "narrow", "narrow", "state"],
        [float_steps, full_steps, full_steps, stack_of, stack_of],
    )
    grad_decay_log = jnp.sum(grad_log_parts, axis=0)
    grad_in_coef = undiagonal(grad_in_wide, BLK, states)
    grad_out_coef = undiagonal(grad_out_wide, BLK, states)
    grad_conv_act = grad_scan * skip_gain + grad_conv_scan
    grad_delta_pre = grad_delta * jax.nn.sigmoid(delta_pre)
    grad_delta_bias = jnp.sum(grad_delta_pre, axis=0)
    grad_delta_proj = rows_dot(delta_low, grad_delta_pre, lax.Precision.HIGHEST)
    grad_delta_low = cols_dot(grad_delta_pre, delta_proj.astype(jnp.float32), lax.Precision.HIGHEST)
    grad_projections = jnp.concatenate([grad_delta_low, grad_in_coef, grad_out_coef], axis=-1)
    grad_state_proj = rows_dot(conv_flat, grad_projections, lax.Precision.HIGHEST)
    grad_conv_act = grad_conv_act + cols_dot(
        grad_projections, state_proj.astype(jnp.float32), lax.Precision.HIGHEST
    )
    grad_conv_pre = grad_conv_act.reshape(sequences, piece_len, inner_width) * silu_slope(conv_pre)
    grad_conv_bias = jnp.sum(grad_conv_pre, axis=(0, 1))
    grad_conv_weight = jnp.stack(
        [
            jnp.sum(grad_conv_pre * extended[:, tap : tap + piece_len, :], axis=(0, 1))
            for tap in range(taps)
        ]
    )
    grad_extended = jnp.zeros_like(extended)
    for tap in range(taps):
        grad_extended = grad_extended.at[:, tap : tap + piece_len, :].add(
            conv_weight[tap] * grad_conv_pre
        )
    rim_back = shifted(
        grad_extended[:, : taps - 1, :].astype(jnp.bfloat16), ("seq", "exp"), -1
    ).astype(jnp.float32)
    grad_inner = grad_extended[:, taps - 1 :, :].at[:, piece_len - (taps - 1) :, :].add(rim_back)
    grad_inner = grad_inner.reshape(tokens, inner_width).astype(jnp.bfloat16)
    grad_in_inner = rows_dot(normed_half, grad_inner)
    grad_normed_one = grad_normed_gate + cols_dot(grad_inner, in_proj[:, :inner_width])
    grad_flat_in, grad_mixer_gain = norm_backward(flat_in, scaling_one, mixer_gain, grad_normed_one)
    in_grad = (grad_resid + grad_flat_in).reshape(sequences, piece_len, width)
    def as_rows(values):
        blocks = values.shape[1] // width
        return jnp.concatenate(
            [values[:, at * width : (at + 1) * width] for at in range(blocks)], axis=0
        ).astype(jnp.bfloat16)

    def as_columns(values):
        return jnp.concatenate(
            [values[at : at + width] for at in range(0, values.shape[0], width)], axis=1
        ).astype(jnp.float32)

    small = [
        grad_state_proj.T,
        grad_delta_proj,
        grad_decay_log,
        grad_conv_weight,
        grad_conv_bias[None],
        grad_delta_bias[None],
        grad_skip_gain[None],
        jnp.concatenate([grad_mixer_gain, grad_expert_norm])[None],
        grad_router.T.reshape(experts * width // inner_width, inner_width),
    ]
    heights = [value.shape[0] for value in small]
    devices = lax.axis_size("seq") * senders
    spare = -sum(heights) % (devices // 2)
    packed = as_rows(
        jnp.concatenate(small + [jnp.zeros((spare, inner_width), jnp.float32)], axis=0)
    )
    sum_out, sum_gate, sum_inner, sum_small = total(
        [grad_out_proj.astype(jnp.bfloat16), as_rows(grad_in_gate), as_rows(grad_in_inner), packed],
        3,
        "grad_total",
    )
    grad_in_proj = jnp.concatenate([as_columns(sum_inner), as_columns(sum_gate)], axis=1)
    half_height = sum_small.shape[0] // 2
    small_wide = jnp.concatenate([sum_small[:half_height], sum_small[half_height:]], axis=1).astype(
        jnp.float32
    )
    offsets = [sum(heights[:at]) for at in range(len(heights) + 1)]
    pieces = [small_wide[offsets[at] : offsets[at + 1]] for at in range(len(heights))]
    summed = (
        pieces[7][0, :width],
        grad_in_proj,
        pieces[3],
        pieces[4][0],
        pieces[0].T,
        pieces[1],
        pieces[5][0],
        pieces[2],
        pieces[6][0],
        sum_out.astype(jnp.float32),
        pieces[7][0, width:],
        pieces[8].reshape(experts, width).T,
    )
    return (
        layer_out,
        in_grad,
        summed[0],
        summed[1],
        summed[2],
        summed[3],
        summed[4],
        summed[5],
        summed[6],
        summed[7],
        summed[8],
        summed[9],
        summed[10],
        summed[11],
        grad_up_own,
        grad_down_own,
    )


def solution(mesh):
    placed = (
        P(None, ("seq", "exp"), None),
        P(),
        P(),
        P(),
        P(),
        P(),
        P(),
        P(),
        P(),
        P(),
        P(),
        P(),
        P(),
        P("exp", None, "seq"),
        P("exp", "seq", None),
        P(None, ("seq", "exp")),
        P(None, ("seq", "exp")),
        P(None, ("seq", "exp"), None),
    )
    return jax.shard_map(
        on_device,
        mesh=mesh,
        in_specs=placed,
        out_specs=(
            P(None, ("seq", "exp"), None),
            P(None, ("seq", "exp"), None),
            P(),
            P(),
            P(),
            P(),
            P(),
            P(),
            P(),
            P(),
            P(),
            P(),
            P(),
            P(),
            P("exp", None, "seq"),
            P("exp", "seq", None),
        ),
        check_vma=False,
    )
```

```python
import functools
import math

import jax
import jax.numpy as jnp
from jax import lax
from jax.experimental import pallas as pl
from jax.experimental.pallas import tpu as pltpu
from jax.sharding import PartitionSpec as P

BLK = 16
LANES = 128
GROUP = 512
LOG2E = 1.4426950408889634
LN2 = 0.6931471805599453
VMEM_BYTES = 50 * 1024 * 1024


EPSILON = 1e-05


def shifted(shard, axis, by):
    devices = lax.axis_size(axis)
    pairs = [(i, i + by) for i in range(devices) if 0 <= i + by < devices]
    return lax.ppermute(shard, axis, pairs)


def half_dot(left, right):
    return jnp.dot(left, right, preferred_element_type=jnp.float32)


def exact_dot(left, right):
    return jnp.dot(left, right, precision=lax.Precision.HIGHEST, preferred_element_type=jnp.float32)


def rows_dot(left, right, precision=None):
    return lax.dot_general(
        left,
        right,
        (((0,), (0,)), ((), ())),
        precision=precision,
        preferred_element_type=jnp.float32,
    )


def cols_dot(left, right, precision=None):
    return lax.dot_general(
        left,
        right,
        (((1,), (1,)), ((), ())),
        precision=precision,
        preferred_element_type=jnp.float32,
    )


def norm_forward(values, gain_vec):
    scaling = lax.rsqrt(jnp.mean(values * values, axis=-1, keepdims=True) + EPSILON)
    return (values * scaling * gain_vec, scaling)


def norm_backward(values, scaling, gain_vec, incoming):
    normal = values * scaling
    weighted = incoming * gain_vec
    grad_gain = jnp.sum(incoming * normal, axis=0)
    grad_values = scaling * (
        weighted - normal * jnp.mean(weighted * normal, axis=-1, keepdims=True)
    )
    return (grad_values, grad_gain)


def silu_slope(values):
    sigma = jax.nn.sigmoid(values)
    return sigma * (1.0 + values * (1.0 - sigma))


def exact_gelu(values):
    return jax.nn.gelu(values, approximate=False)


def spread(coef, lanes):
    return jnp.broadcast_to(coef[:, :, None], coef.shape + (lanes,))


def diagonal(coef, block):
    tokens, states = coef.shape
    column = jnp.arange(block * states, dtype=jnp.int32)[None, :] // states
    row = jnp.arange(tokens, dtype=jnp.int32)[:, None] % block
    return jnp.where(column == row, jnp.tile(coef, (1, block)), 0.0).astype(jnp.bfloat16)


def undiagonal(product, block, states):
    tokens = product.shape[0]
    column = jnp.arange(block * states, dtype=jnp.int32)[None, :] // states
    row = jnp.arange(tokens, dtype=jnp.int32)[:, None] % block
    masked = jnp.where(column == row, product, 0.0)
    return jnp.sum(masked.reshape(tokens, block, states), axis=1)


def lane_parts(ref, k, states):
    width = ref.shape[-1]
    return [
        jnp.broadcast_to(ref[k : k + 1, at : at + LANES], (states, LANES))
        for at in range(0, width, LANES)
    ]


def block_of(ref, i):
    return ref.at[pl.ds(pl.multiple_of(i * BLK, BLK), BLK), :]


def rates_of(log_ref):
    rates = -jnp.exp(log_ref[...]) * LOG2E
    return [rates[:, at : at + LANES] for at in range(0, rates.shape[1], LANES)]


def first_pass_kernel(delta_ref, conv_ref, in_ref, log_ref, end_ref, drive):
    steps, width = delta_ref.shape
    states = log_ref.shape[0]
    rates = rates_of(log_ref)
    drive[...] = delta_ref[...] * conv_ref[...]

    def block(i, state):
        state = list(state)
        for k in range(BLK):
            t = i * BLK + k
            inward = in_ref[t]
            deltas = lane_parts(block_of(delta_ref, i), k, states)
            drives = lane_parts(block_of(drive, i), k, states)
            for j in range(width // LANES):
                state[j] = jnp.exp2(deltas[j] * rates[j]) * state[j] + inward * drives[j]
        return tuple(state)

    zero = tuple(jnp.zeros((states, LANES), jnp.float32) for _ in range(width // LANES))
    last = lax.fori_loop(0, steps // BLK, block, zero)
    for j in range(width // LANES):
        end_ref[0, :, j * LANES : (j + 1) * LANES] = last[j]


def second_pass_kernel(
    delta_ref, conv_ref, in_ref, log_ref, start_ref, out_ref, rest_ref, scanned_ref, drive, stack
):
    steps, width = delta_ref.shape
    states = log_ref.shape[0]
    rates = rates_of(log_ref)
    drive[...] = delta_ref[...] * conv_ref[...]

    def block(i, state):
        state = list(state)
        for k in range(BLK):
            t = i * BLK + k
            inward = in_ref[t]
            deltas = lane_parts(block_of(delta_ref, i), k, states)
            drives = lane_parts(block_of(drive, i), k, states)
            for j in range(width // LANES):
                state[j] = jnp.exp2(deltas[j] * rates[j]) * state[j] + inward * drives[j]
                stack[k * states : (k + 1) * states, j * LANES : (j + 1) * LANES] = state[j].astype(
                    jnp.bfloat16
                )
        rows = pl.ds(pl.multiple_of(i * BLK, BLK), BLK)
        both = jnp.concatenate([out_ref[rows, :], rest_ref[rows, :]], axis=0)
        product = jnp.dot(both, stack[...], preferred_element_type=jnp.float32)
        scanned_ref[rows, :] = product[:BLK] + product[BLK:]
        return tuple(state)

    begin = tuple(start_ref[0, :, j * LANES : (j + 1) * LANES] for j in range(width // LANES))
    lax.fori_loop(0, steps // BLK, block, begin)


def back_summary_kernel(delta_ref, grad_ref, out_ref, log_ref, end_ref):
    steps, width = delta_ref.shape
    states = log_ref.shape[0]
    rates = rates_of(log_ref)
    blocks = steps // BLK

    def block(i, state):
        state = list(state)
        for k in reversed(range(BLK)):
            t = (blocks - 1 - i) * BLK + k
            outward = out_ref[t]
            deltas = lane_parts(block_of(delta_ref, blocks - 1 - i), k, states)
            grads = lane_parts(block_of(grad_ref, blocks - 1 - i), k, states)
            for j in range(width // LANES):
                state[j] = jnp.exp2(deltas[j] * rates[j]) * (state[j] + outward * grads[j])
        return tuple(state)

    zero = tuple(jnp.zeros((states, LANES), jnp.float32) for _ in range(width // LANES))
    last = lax.fori_loop(0, blocks, block, zero)
    for j in range(width // LANES):
        end_ref[0, :, j * LANES : (j + 1) * LANES] = last[j]


def backward_kernel(
    middle,
    delta_ref,
    conv_ref,
    grad_ref,
    in_ref,
    out_ref,
    in_diag_ref,
    log_ref,
    start_ref,
    finish_ref,
    grad_delta_ref,
    grad_conv_ref,
    grad_in_ref,
    grad_out_ref,
    grad_log_ref,
    drive,
    decays,
    carried,
    stack,
    slope,
):
    steps, width = delta_ref.shape
    states = log_ref.shape[0]
    parts = width // LANES
    rates = rates_of(log_ref)
    blocks = steps // BLK
    drive[...] = delta_ref[...] * conv_ref[...]
    first = pl.program_id(1) == 0

    def forward(i, state):
        state = list(state)
        for k in range(BLK):
            t = i * BLK + k
            inward = in_ref[t]
            deltas = lane_parts(block_of(delta_ref, i), k, states)
            drives = lane_parts(block_of(drive, i), k, states)
            for j in range(parts):
                at = slice(j * LANES, (j + 1) * LANES)
                decay = jnp.exp2(deltas[j] * rates[j])
                kept = decay * state[j]
                decays[t, :, at] = decay
                carried[t, :, at] = kept
                state[j] = kept + inward * drives[j]
                stack[k * states : (k + 1) * states, at] = state[j].astype(jnp.bfloat16)
        rows = pl.ds(pl.multiple_of(i * BLK, BLK), BLK)
        partial = cols_dot(grad_ref[rows, :].astype(jnp.bfloat16), stack[...])

        @pl.when(first)
        def _():
            grad_out_ref[rows, :] = partial

        @pl.when(jnp.logical_not(first))
        def _():
            grad_out_ref[rows, :] += partial

        return tuple(state)

    begin = tuple(start_ref[0, :, j * LANES : (j + 1) * LANES] for j in range(parts))
    lax.fori_loop(0, blocks, forward, begin)
    middle()
    column = lax.broadcasted_iota(jnp.int32, (BLK, BLK * states), 1) // states
    row = lax.broadcasted_iota(jnp.int32, (BLK, BLK * states), 0)
    ones = jnp.where(column == row, 1.0, 0.0).astype(jnp.bfloat16)

    def backward(i, state):
        adjoint, gathered = list(state[:parts]), list(state[parts:])
        for k in reversed(range(BLK)):
            t = (blocks - 1 - i) * BLK + k
            outward = out_ref[t]
            deltas = lane_parts(block_of(delta_ref, blocks - 1 - i), k, states)
            grads = lane_parts(block_of(grad_ref, blocks - 1 - i), k, states)
            for j in range(parts):
                at = slice(j * LANES, (j + 1) * LANES)
                whole = adjoint[j] + outward * grads[j]
                exponent = whole * carried[t, :, at]
                gathered[j] = gathered[j] + exponent * deltas[j]
                slope[k * states : (k + 1) * states, at] = (exponent * rates[j]).astype(
                    jnp.bfloat16
                )
                stack[k * states : (k + 1) * states, at] = whole.astype(jnp.bfloat16)
                adjoint[j] = decays[t, :, at] * whole
        rows = pl.ds(pl.multiple_of((blocks - 1 - i) * BLK, BLK), BLK)
        driven = jnp.dot(in_diag_ref[rows, :], stack[...], preferred_element_type=jnp.float32)
        summed = jnp.dot(ones, slope[...], preferred_element_type=jnp.float32) * LN2
        grad_delta_ref[rows, :] = summed + driven * conv_ref[rows, :]
        grad_conv_ref[rows, :] = driven * delta_ref[rows, :]
        partial = cols_dot(drive[rows, :].astype(jnp.bfloat16), stack[...])

        @pl.when(first)
        def _():
            grad_in_ref[rows, :] = partial

        @pl.when(jnp.logical_not(first))
        def _():
            grad_in_ref[rows, :] += partial

        return tuple(adjoint + gathered)

    ends = tuple(finish_ref[0, :, j * LANES : (j + 1) * LANES] for j in range(parts))
    zero = tuple(jnp.zeros((states, LANES), jnp.float32) for _ in range(parts))
    last = lax.fori_loop(0, blocks, backward, ends + zero)
    for j in range(parts):
        grad_log_ref[0, :, j * LANES : (j + 1) * LANES] = last[parts + j] * rates[j] * LN2


def scan_call(kernel, name, sequences, states, operands, results, scratch, early=None):
    tokens, width = next(value.shape for kind, value in operands if kind == "wide")
    steps = tokens // sequences
    specs = {
        "wide": pl.BlockSpec((steps, GROUP), lambda q, j: (q, j)),
        "spread": pl.BlockSpec((steps, states, LANES), lambda q, j: (q, 0, 0)),
        "narrow": pl.BlockSpec((steps, BLK * states), lambda q, j: (q, 0)),
        "rates": pl.BlockSpec((states, GROUP), lambda q, j: (0, j)),
        "state": pl.BlockSpec((1, states, GROUP), lambda q, j: (q, 0, j)),
    }
    shapes = {
        "wide": (tokens, width),
        "narrow": (tokens, BLK * states),
        "state": (sequences, states, width),
    }
    in_specs = [specs[kind] for kind, _ in operands]
    out_specs = [specs[kind] for kind in results]
    out_shape = [jax.ShapeDtypeStruct(shapes[kind], jnp.float32) for kind in results]
    sending = {}
    if early:
        planes, side, *moving = early
        tails = [value.shape[4:] for value in moving[:2]]
        kernel = functools.partial(kernel, planes, side)
        whole, anywhere = (pl.BlockSpec(memory_space=space) for space in (pltpu.VMEM, pl.ANY))
        in_specs += [whole, whole, anywhere]
        out_specs += [whole, whole, anywhere]
        out_shape += [jax.ShapeDtypeStruct((planes,) + tail, jnp.bfloat16) for tail in tails]
        out_shape.append(jax.ShapeDtypeStruct(moving[2].shape, jnp.bfloat16))
        operands = operands + [("early", value) for value in moving]
        semaphores = stage_semaphores(2, planes, side)[:5]
        scratch = scratch + scatter_buffers(tails, planes, side)
        scratch = scratch + [pltpu.VMEM((planes,) + tail, jnp.bfloat16) for tail in tails]
        scratch = scratch + semaphores + semaphores
        scratch = scratch + [pltpu.SemaphoreType.DMA, pltpu.SemaphoreType.DMA]
        sending = dict(collective_id=6, has_side_effects=True)
    return pl.pallas_call(
        kernel,
        name=name,
        grid=(sequences, width // GROUP),
        in_specs=in_specs,
        out_specs=out_specs,
        out_shape=out_shape,
        scratch_shapes=scratch,
        compiler_params=pltpu.CompilerParams(
            dimension_semantics=("arbitrary", "arbitrary"),
            vmem_limit_bytes=VMEM_BYTES,
            **sending,
        ),
        cost_estimate=pl.CostEstimate(
            flops=20 * tokens * states * width,
            transcendentals=tokens * states * width,
            bytes_accessed=16 * tokens * width,
        ),
    )(*(value for _, value in operands))


MESH = pl.DeviceIdType.MESH


def remote(src, dst, send, arrive, axis, peer):
    return pltpu.make_async_remote_copy(
        src_ref=src,
        dst_ref=dst,
        send_sem=send,
        recv_sem=arrive,
        device_id={axis: peer},
        device_id_type=MESH,
    )


def greet(axes):
    barrier = pltpu.get_barrier_semaphore()
    total = 0
    for axis, size in axes:
        mine = lax.axis_index(axis)
        for k in range(1, size):
            pl.semaphore_signal(
                barrier, inc=1, device_id={axis: lax.rem(mine + k, size)}, device_id_type=MESH
            )
        total += size - 1
    pl.semaphore_wait(barrier, total)


def exchange_kernel(
    reverse,
    planes,
    members,
    end_ref,
    sum_ref,
    rates_ref,
    carry_ref,
    packed,
    landed,
    summary,
    totals,
    starts,
    carries,
    send_one,
    recv_one,
    send_two,
    recv_two,
    send_three,
    recv_three,
):
    sequences, states, width = end_ref.shape
    rows = sequences * states // members
    plane, member = lax.axis_index("seq"), lax.axis_index("exp")
    rates = -jnp.exp(rates_ref[...])
    for i in range(members):
        q, n = (i * rows) // states, (i * rows) % states
        packed[i, :rows] = end_ref[q, n : n + rows]
        packed[i, rows:] = sum_ref[q : q + 1]
    greet((("seq", planes), ("exp", members)))
    for k in range(1, members):
        other = lax.rem(member + k, members)
        remote(
            packed.at[other],
            landed.at[member],
            send_one.at[k],
            recv_one.at[member],
            "exp",
            other,
        ).start()
    landed[member] = packed[member]
    for k in range(1, members):
        other = lax.rem(member + k, members)
        remote(
            packed.at[other], landed.at[other], send_one.at[k], recv_one.at[other], "exp", other
        ).wait()
    order = range(members)[::-1] if reverse else range(members)
    plane_order = range(planes)[::-1] if reverse else range(planes)

    def through(piece, before):
        return jnp.exp(piece[rows:] * rates) * before + piece[:rows]

    state = jnp.zeros((rows, width), jnp.float32)
    total = jnp.zeros((1, width), jnp.float32)
    for i in order:
        piece = landed[i]
        state = through(piece, state)
        total = total + piece[rows:]
    summary[:rows] = state
    summary[rows:] = total
    for k in range(1, planes):
        other = lax.rem(plane + k, planes)
        remote(
            summary, totals.at[plane], send_two.at[k], recv_two.at[plane], "seq", other
        ).start()
    totals[plane] = summary[...]
    for k in range(1, planes):
        other = lax.rem(plane + k, planes)
        remote(summary, totals.at[other], send_two.at[k], recv_two.at[other], "seq", other).wait()
    state = jnp.zeros((rows, width), jnp.float32)
    for s in plane_order:
        reached = plane < s if reverse else plane > s
        state = jnp.where(reached, through(totals[s], state), state)
    for i in order:
        starts[i] = state
        state = through(landed[i], state)
    for k in range(1, members):
        other = lax.rem(member + k, members)
        remote(
            starts.at[other],
            carries.at[member],
            send_three.at[k],
            recv_three.at[member],
            "exp",
            other,
        ).start()
    carries[member] = starts[member]
    for k in range(1, members):
        other = lax.rem(member + k, members)
        remote(
            starts.at[other],
            carries.at[other],
            send_three.at[k],
            recv_three.at[other],
            "exp",
            other,
        ).wait()
    for i in range(members):
        q, n = (i * rows) // states, (i * rows) % states
        carry_ref[q, n : n + rows] = carries[i]


def exchange(local_end, delta_sum, decay_log, reverse):
    sequences, states, width = local_end.shape
    planes, members = lax.axis_size("seq"), lax.axis_size("exp")
    rows = sequences * states // members
    first_row = lax.rem(lax.axis_index("exp") * rows, states)
    own_rates = lax.dynamic_slice(decay_log, (first_row, 0), (rows, width))
    vmem = pl.BlockSpec(memory_space=pltpu.VMEM)
    piece = (rows + 1, width)
    return pl.pallas_call(
        functools.partial(exchange_kernel, reverse, planes, members),
        name="state_exchange_back" if reverse else "state_exchange",
        in_specs=[vmem] * 3,
        out_specs=vmem,
        out_shape=jax.ShapeDtypeStruct(local_end.shape, jnp.float32),
        scratch_shapes=[
            pltpu.VMEM((members,) + piece, jnp.float32),
            pltpu.VMEM((members,) + piece, jnp.float32),
            pltpu.VMEM(piece, jnp.float32),
            pltpu.VMEM((planes,) + piece, jnp.float32),
            pltpu.VMEM((members, rows, width), jnp.float32),
            pltpu.VMEM((members, rows, width), jnp.float32),
            pltpu.SemaphoreType.DMA((members,)),
            pltpu.SemaphoreType.DMA((members,)),
            pltpu.SemaphoreType.DMA((planes,)),
            pltpu.SemaphoreType.DMA((planes,)),
            pltpu.SemaphoreType.DMA((members,)),
            pltpu.SemaphoreType.DMA((members,)),
        ],
        compiler_params=pltpu.CompilerParams(
            collective_id=2 if reverse else 1,
            has_side_effects=True,
            vmem_limit_bytes=VMEM_BYTES,
        ),
        cost_estimate=pl.CostEstimate(flops=10**6, transcendentals=10**5, bytes_accessed=2 * 10**7),
    )(local_end, delta_sum, own_rates)


class Sums:
    def __init__(self, planes, side, sends, arrivals):
        self.planes, self.side = planes, side
        self.plane, self.member = lax.axis_index("seq"), lax.axis_index("exp")
        chip, self.core = self.member // 2, lax.rem(self.member, 2)
        high, low = chip // side, lax.rem(chip, side)
        self.first = low + (high - low) * self.core
        self.second = high + (low - high) * self.core
        self.partner = self.member + 1 - 2 * self.core
        self.sends, self.arrivals = sends, arrivals

    def chip_at(self, first, second):
        low = first + (second - first) * self.core
        high = second + (first - second) * self.core
        return (high * self.side + low) * 2 + self.core

    def first_peer(self, k):
        other = lax.rem(self.first + k, self.side)
        return other, self.chip_at(other, self.second)

    def second_peer(self, k):
        other = lax.rem(self.second + k, self.side)
        return other, self.chip_at(self.first, other)

    def plane_peer(self, k):
        return lax.rem(self.plane + k, self.planes)

    def signal_peers(self, barrier):
        peers = [{"exp": self.partner}]
        peers += [{"exp": self.first_peer(k)[1]} for k in range(1, self.side)]
        peers += [{"exp": self.second_peer(k)[1]} for k in range(1, self.side)]
        peers += [{"seq": self.plane_peer(k)} for k in range(1, self.planes)]
        for peer in peers:
            pl.semaphore_signal(barrier, inc=1, device_id=peer, device_id_type=MESH)
        return len(peers)

    def move(self, stage, at, slot, src, dst, axis, peer):
        return remote(
            src, dst, self.sends[stage].at[at], self.arrivals[stage].at[slot], axis, peer
        )

    def pair_half(self, i, given, half):
        return self.move(0, i, i, given.at[1 - self.core], half, "exp", self.partner)

    def scatter_first(self, i, k, half, slots, arriving):
        other, device = self.first_peer(k)
        slot = other if arriving else self.first
        return self.move(1, (i, k), (i, slot), half.at[other], slots.at[slot], "exp", device)

    def scatter_second(self, i, k, quarter, slots, arriving):
        other, device = self.second_peer(k)
        slot = other if arriving else self.second
        return self.move(2, (i, k), (i, slot), quarter.at[other], slots.at[slot], "exp", device)

    def scatter_plane(self, i, k, eighth, slots, arriving):
        other = self.plane_peer(k)
        slot = other if arriving else self.plane
        return self.move(3, (i, k), (i, slot), eighth.at[other], slots.at[slot], "seq", other)

    def gather_plane(self, i, k, block, arriving):
        other = self.plane_peer(k)
        slot = other if arriving else self.plane
        return self.move(
            4, (i, k), (i, slot), block.at[self.plane], block.at[slot], "seq", other
        )

    def gather_second(self, i, k, result, arriving):
        other, device = self.second_peer(k)
        slot = other if arriving else self.second
        row = result.at[self.core, self.first]
        return self.move(5, (i, k), (i, slot), row.at[self.second], row.at[slot], "exp", device)

    def gather_first(self, i, k, result, arriving):
        other, device = self.first_peer(k)
        slot = other if arriving else self.first
        own = result.at[self.core]
        return self.move(6, (i, k), (i, slot), own.at[self.first], own.at[slot], "exp", device)

    def pair_gather(self, i, k, result, arriving):
        other = lax.rem(self.first + k, self.side)
        low = lax.rem(self.partner // 2, self.side)
        theirs = low + (self.partner // (2 * self.side) - low) * (1 - self.core)
        other = lax.rem(theirs + k, self.side) if arriving else other
        half = 1 - self.core if arriving else self.core
        mine = result.at[self.core, lax.rem(self.first + k, self.side)]
        return self.move(7, (i, k), (i, k), mine, result.at[half, other], "exp", self.partner)

    def after_pair(self, i, given, half, slots):
        self.pair_half(i, given, half).wait()
        own = self.core
        for at in range(self.side):
            for to in range(self.side):
                both = given[own, at, to].astype(jnp.float32) + half[at, to].astype(jnp.float32)
                half[at, to] = both.astype(jnp.bfloat16)
        for k in range(1, self.side):
            self.scatter_first(i, k, half, slots, False).start()
        slots[self.first] = half[self.first]

    def after_first(self, i, half, slots, quarter, slots_two):
        for k in range(1, self.side):
            self.scatter_first(i, k, half, slots, True).wait_recv()
        for at in range(self.side):
            added = slots[0, at].astype(jnp.float32)
            for k in range(1, self.side):
                added = added + slots[k, at].astype(jnp.float32)
            quarter[at] = added.astype(jnp.bfloat16)
        for k in range(1, self.side):
            self.scatter_second(i, k, quarter, slots_two, False).start()
        slots_two[self.second] = quarter[self.second]

    def after_second(self, i, quarter, slots_two, eighth, slots_three):
        for k in range(1, self.side):
            self.scatter_second(i, k, quarter, slots_two, True).wait_recv()
        added = slots_two[0].astype(jnp.float32)
        for k in range(1, self.side):
            added = added + slots_two[k].astype(jnp.float32)
        eighth[...] = added.astype(jnp.bfloat16)
        for k in range(1, self.planes):
            self.scatter_plane(i, k, eighth, slots_three, False).start()
        slots_three[self.plane] = eighth[self.plane]

    def after_planes(self, i, eighth, slots_three, block):
        for k in range(1, self.planes):
            self.scatter_plane(i, k, eighth, slots_three, True).wait_recv()
        added = slots_three[0].astype(jnp.float32)
        for k in range(1, self.planes):
            added = added + slots_three[k].astype(jnp.float32)
        block[self.plane] = added.astype(jnp.bfloat16)
        for k in range(1, self.planes):
            self.gather_plane(i, k, block, False).start()

    def planes_gathered(self, i, block):
        for k in range(1, self.planes):
            self.gather_plane(i, k, block, True).wait_recv()

    def scatter_sent(self, i, half, slots, quarter, slots_two, eighth, slots_three, block):
        for k in range(1, self.side):
            self.scatter_first(i, k, half, slots, False).wait_send()
            self.scatter_second(i, k, quarter, slots_two, False).wait_send()
        for k in range(1, self.planes):
            self.scatter_plane(i, k, eighth, slots_three, False).wait_send()
            self.gather_plane(i, k, block, False).wait_send()

    def gather_start(self, i, block, result):
        result[self.core, self.first, self.second] = block[...]
        for k in range(1, self.side):
            self.gather_second(i, k, result, False).start()

    def gather_across(self, i, result):
        for k in range(1, self.side):
            self.gather_second(i, k, result, True).wait_recv()
        for k in range(1, self.side):
            self.gather_first(i, k, result, False).start()
        self.pair_gather(i, 0, result, False).start()

    def gather_pass(self, i, result):
        for k in range(1, self.side):
            self.gather_first(i, k, result, True).wait_recv()
            self.pair_gather(i, k, result, False).start()

    def gather_end(self, i, result):
        for k in range(self.side):
            self.pair_gather(i, k, result, True).wait_recv()
            self.pair_gather(i, k, result, False).wait_send()
        for k in range(1, self.side):
            self.gather_first(i, k, result, False).wait_send()
            self.gather_second(i, k, result, False).wait_send()


def stage_semaphores(count, planes, side):
    each = [(count,)] + [(count, size) for size in (side, side, planes, planes, side, side, side)]
    return [pltpu.SemaphoreType.DMA(shape) for shape in each]


def scatter_buffers(tails, planes, side):
    leads = [(side, side, planes), (side, side, planes), (side, planes), (side, planes)]
    leads += [(planes,), (planes,)]
    return [pltpu.VMEM(lead + tail, jnp.bfloat16) for lead in leads for tail in tails]


def neighbour_plane():
    plane = lax.axis_index("seq")
    return {"seq": plane + 1 - 2 * lax.rem(plane, 2)}


def swapped(src, dst, send, arrive):
    return pltpu.make_async_remote_copy(
        src_ref=src,
        dst_ref=dst,
        send_sem=send,
        recv_sem=arrive,
        device_id=neighbour_plane(),
        device_id_type=MESH,
    )


class Routes:
    def __init__(self, planes, members, sends, arrivals, local):
        self.planes, self.members = planes, members
        self.plane, self.member = lax.axis_index("seq"), lax.axis_index("exp")
        self.hops = planes // 2
        self.sends, self.arrivals, self.local = sends, arrivals, local
        self.pairs = [
            (hop, k) for hop in reversed(range(self.hops)) for k in range(members) if hop or k
        ]

    def device(self, hop, k):
        return {
            "seq": lax.rem(self.plane + 2 * hop, self.planes),
            "exp": lax.rem(self.member + k, self.members),
        }

    def signal_peers(self, barrier):
        for hop, k in self.pairs:
            pl.semaphore_signal(
                barrier, inc=1, device_id=self.device(hop, k), device_id_type=MESH
            )
        return len(self.pairs)

    def moved(self, given, landed, returning, hop, k, arriving):
        device = self.device(hop, k)
        other = device["exp"]
        slot = hop if arriving else (-hop) % self.hops
        sender = other if arriving else self.member
        return pltpu.make_async_remote_copy(
            src_ref=given.at[hop, other] if returning else given.at[other],
            dst_ref=landed.at[slot, sender],
            send_sem=self.sends.at[hop, k],
            recv_sem=self.arrivals.at[slot, sender],
            device_id=device,
            device_id_type=MESH,
        )

    def own(self, given, landed, returning):
        src = given.at[0, self.member] if returning else given.at[self.member]
        return pltpu.make_async_copy(src, landed.at[0, self.member], self.local)

    def start(self, given, landed, returning):
        for hop, k in self.pairs:
            self.moved(given, landed, returning, hop, k, False).start()
        self.own(given, landed, returning).start()

    def wait(self, given, landed, returning):
        for hop, k in self.pairs:
            self.moved(given, landed, returning, hop, k, True).wait_recv()
        self.own(given, landed, returning).wait()
        for hop, k in self.pairs:
            self.moved(given, landed, returning, hop, k, False).wait_send()


def route_semaphores(planes, members):
    shape = (planes // 2, members)
    return [
        pltpu.SemaphoreType.DMA(shape),
        pltpu.SemaphoreType.DMA(shape),
        pltpu.SemaphoreType.DMA,
    ]


def two_part(left, right, dims):
    high = left.astype(jnp.bfloat16)
    rest = (left - high.astype(jnp.float32)).astype(jnp.bfloat16)
    numbers = (dims, ((), ()))
    wide = jnp.float32
    return lax.dot_general(high, right, numbers, preferred_element_type=wide) + lax.dot_general(
        rest, right, numbers, preferred_element_type=wide
    )


def finish_kernel(
    planes,
    side,
    grad_delta_ref,
    grad_conv_ref,
    grad_in_ref,
    grad_out_ref,
    grad_log_ref,
    grad_scan_ref,
    delta_pre_ref,
    delta_low_ref,
    conv_ref,
    conv_pre_ref,
    extended_ref,
    normed_ref,
    normed_gate_ref,
    layer_ref,
    grad_resid_ref,
    delta_proj_ref,
    state_proj_ref,
    in_proj_ref,
    conv_weight_ref,
    skip_ref,
    mixer_gain_ref,
    skip_grad_ref,
    norm_grad_ref,
    router_grad_ref,
    early_out_ref,
    early_gate_ref,
    returned_ref,
    far_ref,
    in_grad_ref,
    total_out_ref,
    total_gate_ref,
    total_left_ref,
    total_right_ref,
    total_small_ref,
    landed_ref,
    near_ref,
    slopes,
    low_grads,
    padded,
    grad_inner,
    small,
    rim_out,
    rim_in,
    *rest,
):
    givens, buffers, (rim_sent, rim_landed) = rest[:3], rest[3:21], rest[21:23]
    semaphores = rest[23:]
    routes = Routes(planes, 2 * side * side, *semaphores[16:19])
    cut_rows = far_ref.shape[1] // 2
    swaps = [
        swapped(far_ref.at[:, at], near_ref.at[:, at], semaphores[19].at[i], semaphores[20].at[i])
        for i, at in enumerate((pl.ds(0, cut_rows), pl.ds(cut_rows, cut_rows)))
    ]
    totals = (total_left_ref, total_right_ref, total_small_ref)
    tail = [tuple(buffers[3 * stage + i] for stage in range(6)) for i in range(3)]
    chips = side * side
    tokens, inner_width = grad_delta_ref.shape
    width = layer_ref.shape[1]
    low_rank = delta_low_ref.shape[1]
    taps = conv_weight_ref.shape[0]
    sequences = extended_ref.shape[0]
    piece = tokens // sequences
    states = grad_log_ref.shape[1]
    wide, half = jnp.float32, jnp.bfloat16
    sums = Sums(planes, side, semaphores[:8], semaphores[8:16])
    place = sums.plane * (2 * chips) + sums.member
    devices = 2 * chips * planes
    before, after = lax.rem(place + devices - 1, devices), lax.rem(place + 1, devices)

    def device(at):
        return {"seq": at // (2 * chips), "exp": lax.rem(at, 2 * chips)}

    barrier = pltpu.get_barrier_semaphore()
    for peer in (before, after):
        pl.semaphore_signal(barrier, inc=1, device_id=device(peer), device_id_type=MESH)
    pl.semaphore_signal(barrier, inc=1, device_id=neighbour_plane(), device_id_type=MESH)
    greeted = 3 + sums.signal_peers(barrier) + routes.signal_peers(barrier)
    pl.semaphore_wait(barrier, greeted)
    early = [(total_out_ref, early_out_ref), (total_gate_ref, early_gate_ref)]
    for i, (result, own) in enumerate(early):
        sums.gather_start(i, own, result)
    swaps[0].start()

    unit = 256
    count = inner_width // unit
    low_grads[...] = jnp.zeros(low_grads.shape, wide)
    small[...] = jnp.zeros(small.shape, wide)

    def lanes(j):
        return pl.ds(pl.multiple_of(j * unit, unit), unit)

    at_delta = low_rank + 2 * states
    at_log = at_delta + low_rank
    at_conv = at_log + states

    def first(j, carry):
        at = lanes(j)
        slope = grad_delta_ref[:, at] * jax.nn.sigmoid(delta_pre_ref[:, at])
        small[at_conv + taps + 1 : at_conv + taps + 2, at] = jnp.sum(slope, axis=0, keepdims=True)
        small[at_delta:at_log, at] = rows_dot(delta_low_ref[...], slope, lax.Precision.HIGHEST)
        low_grads[...] += two_part(slope, delta_proj_ref[:, at], ((1,), (1,)))
        return carry

    lax.fori_loop(0, count, first, 0)
    for i, (result, _) in enumerate(early):
        sums.gather_across(i, result)
    block = grad_in_ref.shape[1] // states
    column = lax.broadcasted_iota(jnp.int32, grad_in_ref.shape, 1) // states
    row = lax.rem(lax.broadcasted_iota(jnp.int32, grad_in_ref.shape, 0), block)
    fold = jnp.where(
        lax.rem(lax.broadcasted_iota(jnp.int32, (grad_in_ref.shape[1], states), 0), states)
        == lax.broadcasted_iota(jnp.int32, (grad_in_ref.shape[1], states), 1),
        1.0,
        0.0,
    ).astype(half)

    def folded(ref):
        return two_part(jnp.where(column == row, ref[...], 0.0), fold, ((1,), (0,)))

    coefs = jnp.concatenate([low_grads[...], folded(grad_in_ref), folded(grad_out_ref)], axis=1)
    rim_out[...] = jnp.zeros(rim_out.shape, half)

    def second(j, carry):
        at = lanes(j)
        small[:at_delta, at] = rows_dot(coefs, conv_ref[:, at], lax.Precision.HIGHEST)
        through = two_part(coefs, state_proj_ref[:, at], ((1,), (0,)))
        through = through + grad_scan_ref[:, at] * skip_ref[:, at] + grad_conv_ref[:, at]
        pre = conv_pre_ref[:, at]
        sigma = jax.nn.sigmoid(pre)
        through = through * (sigma * (1.0 + pre * (1.0 - sigma)))
        small[at_conv + taps : at_conv + taps + 1, at] = jnp.sum(through, axis=0, keepdims=True)
        for q in range(sequences):
            padded[q, :8] = jnp.zeros((8, unit), wide)
            padded[q, 8 + piece :] = jnp.zeros((8, unit), wide)
            padded[q, 8 : 8 + piece] = through[q * piece : (q + 1) * piece]
            result = jnp.zeros((piece, unit), wide)
            rim = jnp.zeros((8, unit), wide)
            for tap in range(taps):
                weight = conv_weight_ref[tap : tap + 1, at]
                shift = taps - 1 - tap
                result = result + weight * padded[q, 8 + shift : 8 + shift + piece]
                rim = rim + weight * padded[q, 8 - tap : 16 - tap]
            grad_inner[q * piece : (q + 1) * piece, at] = result
            rim_out[q, 8 - (taps - 1) :, at] = rim[: taps - 1].astype(half)
        for tap in range(taps):
            start = 8 - (taps - 1) + tap
            product = jnp.zeros((1, unit), wide)
            for q in range(sequences):
                product = product + jnp.sum(
                    padded[q, 8 : 8 + piece] * extended_ref[q, start : start + piece, at],
                    axis=0,
                    keepdims=True,
                )
            small[at_conv + tap : at_conv + tap + 1, at] = product
        return carry

    lax.fori_loop(0, count, second, 0)
    rim_copy = pltpu.make_async_remote_copy(
        src_ref=rim_out,
        dst_ref=rim_in,
        send_sem=rim_sent,
        recv_sem=rim_landed,
        device_id=device(before),
        device_id_type=MESH,
    )
    rim_copy.start()
    routes.start(returned_ref, landed_ref, True)
    swaps[1].start()
    for i, (result, _) in enumerate(early):
        sums.gather_pass(i, result)
    at_end = at_conv + taps + 2
    log_total = grad_log_ref[0]
    for q in range(1, sequences):
        log_total = log_total + grad_log_ref[q]
    small[at_log:at_conv] = log_total
    small[at_end : at_end + 1] = skip_grad_ref[...]
    small[at_end + 1 : at_end + 2, width:] = norm_grad_ref[...]
    for k in range(router_grad_ref.shape[0]):
        line = at_end + 2 + k // 2
        small[line : line + 1, (k % 2) * width : (k % 2 + 1) * width] = router_grad_ref[k : k + 1]
    rim_copy.wait()
    keep = jnp.where(place < devices - 1, 1.0, 0.0)
    for q in range(sequences):
        rows = slice((q + 1) * piece - 8, (q + 1) * piece)
        grad_inner[rows, :] += keep * rim_in[q].astype(wide)
    slopes[...] = grad_inner[...].astype(half)
    tall = width // chips
    size = tall // planes
    cut = size // 2
    for c in range(2):
        for m in range(chips):
            product = rows_dot(
                normed_ref[:, m * tall : (m + 1) * tall], slopes[:, c * width : (c + 1) * width]
            ).astype(half)
            for z in range(planes):
                givens[0][c, m // side, m % side, z] = product[z * size : z * size + cut]
                givens[1][c, m // side, m % side, z] = product[z * size + cut : (z + 1) * size]
    for i in range(2):
        sums.pair_half(i, givens[i], tail[i][0]).start()
    normed_grad = normed_gate_ref[...] + cols_dot(slopes[...], in_proj_ref[...])
    layer = layer_ref[...].astype(wide)
    scaling = lax.rsqrt(jnp.mean(layer * layer, axis=-1, keepdims=True) + EPSILON)
    normal = layer * scaling
    small[at_end + 1 : at_end + 2, :width] = jnp.sum(normed_grad * normal, axis=0, keepdims=True)
    low = givens[2].shape[4]
    for c in range(2):
        for m in range(chips):
            for z in range(planes):
                line = (m * planes + z) * low
                givens[2][c, m // side, m % side, z] = small[
                    line : line + low, c * width : (c + 1) * width
                ].astype(half)
    sums.pair_half(2, givens[2], tail[2][0]).start()
    every = range(3)
    for i in every:
        sums.after_pair(i, givens[i], *tail[i][:2])
    weighted = normed_grad * mixer_gain_ref[...]
    in_grad_ref[...] = grad_resid_ref[...] + scaling * (
        weighted - normal * jnp.mean(weighted * normal, axis=-1, keepdims=True)
    )
    for i in every:
        sums.after_first(i, *tail[i][:4])
    for i in every:
        sums.after_second(i, *tail[i][2:6])
    blocks = [total.at[sums.core, sums.first, sums.second] for total in totals]
    for i in every:
        sums.after_planes(i, *tail[i][4:6], blocks[i])
    for i in every:
        sums.planes_gathered(i, blocks[i])
        for k in range(1, side):
            sums.gather_second(2 + i, k, totals[i], False).start()
    for i in every:
        sums.gather_across(2 + i, totals[i])
    for i in every:
        sums.gather_pass(2 + i, totals[i])
    for i, (result, _) in enumerate(early):
        sums.gather_end(i, result)
    routes.wait(returned_ref, landed_ref, True)
    for swap in swaps:
        swap.wait()
    for i in every:
        sums.scatter_sent(i, *tail[i], blocks[i])
        sums.gather_end(2 + i, totals[i])


def finish(operands, small_height, side):
    planes = lax.axis_size("seq")
    tokens, inner_width = operands[0].shape
    layer = operands[13]
    width = layer.shape[1]
    sequences = operands[4].shape[0]
    low = -(-small_height // (side * side * planes))
    lead = (2, side, side, planes)
    big = lead + operands[24].shape[1:]
    split = lead + (big[4] // 2, width)
    little = lead + (low, width)
    tails = [split[4:], split[4:], little[4:]]
    vmem, anywhere = (pl.BlockSpec(memory_space=space) for space in (pltpu.VMEM, pl.ANY))
    half, wide = jnp.bfloat16, jnp.float32
    moved = [jax.ShapeDtypeStruct(value.shape, half) for value in operands[-2:]]
    return pl.pallas_call(
        functools.partial(finish_kernel, planes, side),
        name="finish_gradients",
        in_specs=[vmem] * (len(operands) - 2) + [anywhere] * 2,
        out_specs=[vmem] * 6 + [anywhere] * 2,
        out_shape=[jax.ShapeDtypeStruct((tokens, width), wide)]
        + [jax.ShapeDtypeStruct(shape, half) for shape in (big, big, split, split, little)]
        + moved,
        scratch_shapes=[
            pltpu.VMEM((tokens, inner_width), half),
            pltpu.VMEM((tokens, operands[7].shape[1]), wide),
            pltpu.VMEM((sequences, tokens // sequences + 16, 256), wide),
            pltpu.VMEM((tokens, inner_width), wide),
            pltpu.VMEM((low * side * side * planes, inner_width), wide),
            pltpu.VMEM((sequences, 8, inner_width), half),
            pltpu.VMEM((sequences, 8, inner_width), half),
            pltpu.VMEM(split, half),
            pltpu.VMEM(split, half),
            pltpu.VMEM(little, half),
        ]
        + scatter_buffers(tails, planes, side)
        + [pltpu.SemaphoreType.DMA, pltpu.SemaphoreType.DMA]
        + stage_semaphores(5, planes, side)
        + stage_semaphores(5, planes, side)
        + route_semaphores(planes, 2 * side * side)
        + [pltpu.SemaphoreType.DMA((2,)), pltpu.SemaphoreType.DMA((2,))],
        compiler_params=pltpu.CompilerParams(
            collective_id=3, has_side_effects=True, vmem_limit_bytes=60 * 1024 * 1024
        ),
        cost_estimate=pl.CostEstimate(flops=10**8, transcendentals=0, bytes_accessed=2 * 10**8),
    )(*operands)


def backward_sum_kernel(planes, side, *refs):
    inputs, given, far_ref, results, owns = refs[:9], refs[9:11], refs[11], refs[12:17], refs[17:19]
    near_ref, scratch, buffers, semaphores = refs[19], refs[20:25], refs[25:37], refs[39:]
    blocks = refs[37:39]
    halves, slots, quarters, slots_two, eighths, slots_three = (
        buffers[2 * i : 2 * i + 2] for i in range(6)
    )
    sums = Sums(planes, side, semaphores[:5], semaphores[5:10])
    swap = swapped(far_ref, near_ref, *semaphores[10:])
    step = pl.program_id(0) * pl.num_programs(1) + pl.program_id(1)
    last = pl.num_programs(0) * pl.num_programs(1) - 1

    def begin(_):
        barrier = pltpu.get_barrier_semaphore()
        pl.semaphore_signal(barrier, inc=1, device_id=neighbour_plane(), device_id_type=MESH)
        pl.semaphore_wait(barrier, sums.signal_peers(barrier) + 1)
        for i in range(2):
            sums.pair_half(i, given[i], halves[i]).start()
        swap.start()

    def pairs(i):
        sums.after_pair(i, given[i], halves[i], slots[i])

    def firsts(i):
        sums.after_first(i, halves[i], slots[i], quarters[i], slots_two[i])

    def seconds(i):
        sums.after_second(i, quarters[i], slots_two[i], eighths[i], slots_three[i])

    def across(i):
        sums.after_planes(i, eighths[i], slots_three[i], blocks[i])

    def at(point, stage, which):
        @pl.when(step == point)
        def _():
            for i in which:
                stage(i)

    at(0, begin, [0])
    at(1, pairs, [0, 1])
    at(3, firsts, [0])
    at(4, seconds, [0])
    at(last, across, [0])

    def middle():
        at(3, firsts, [1])
        at(4, seconds, [1])
        at(last, across, [1])

    backward_kernel(middle, *inputs, *results, *scratch)

    @pl.when(step == last)
    def _():
        for i in range(2):
            sums.planes_gathered(i, blocks[i])
            owns[i][...] = blocks[i][...]
            parts = (halves, slots, quarters, slots_two, eighths, slots_three, blocks)
            sums.scatter_sent(i, *(part[i] for part in parts))
        swap.wait()


def dispatch_kernel(planes, members, returning, given, landed, *semaphores):
    routes = Routes(planes, members, *semaphores)
    barrier = pltpu.get_barrier_semaphore()
    pl.semaphore_wait(barrier, routes.signal_peers(barrier))
    routes.start(given, landed, returning)
    routes.wait(given, landed, returning)


def dispatch(values, returning, collective_id, name):
    planes, members = lax.axis_size("seq"), lax.axis_size("exp")
    anywhere = pl.BlockSpec(memory_space=pl.ANY)
    shape = (planes // 2, members) + values.shape[-2:]
    return pl.pallas_call(
        functools.partial(dispatch_kernel, planes, members, returning),
        name=name,
        in_specs=[anywhere],
        out_specs=anywhere,
        out_shape=jax.ShapeDtypeStruct(shape, jnp.bfloat16),
        scratch_shapes=route_semaphores(planes, members),
        compiler_params=pltpu.CompilerParams(collective_id=collective_id, has_side_effects=True),
        cost_estimate=pl.CostEstimate(flops=10**6, transcendentals=0, bytes_accessed=5 * 10**7),
    )(values)


def expert_kernel(
    rows_ref,
    grads_ref,
    up_ref,
    down_ref,
    near_up_ref,
    near_down_ref,
    router_ref,
    chosen_ref,
    out_ref,
    grad_row_ref,
    grad_up_ref,
    grad_down_ref,
    far_up_ref,
    far_down_ref,
    grad_router_ref,
    sent,
    out_sum,
    row_sum,
    hidden,
    grad_pre,
    shares_kept,
):
    count = rows_ref.shape[0]
    step = pl.program_id(0)
    chunk = count // 4
    wide, half = jnp.float32, jnp.bfloat16

    def chunks(body):
        def run(i, carry):
            body(pl.ds(pl.multiple_of(i * chunk, chunk), chunk))
            return carry

        lax.fori_loop(0, count // chunk, run, 0)

    @pl.when(step == 0)
    def _():
        def prepare(at):
            logits = lax.dot_general(
                rows_ref[at, :].astype(wide),
                router_ref[...],
                (((1,), (1,)), ((), ())),
                precision=lax.Precision.HIGHEST,
                preferred_element_type=wide,
            )
            raised = jnp.exp(logits - jnp.max(logits, axis=-1, keepdims=True))
            shares = raised / jnp.sum(raised, axis=-1, keepdims=True)
            gate = jnp.sum(shares * chosen_ref[...], axis=-1, keepdims=True)
            shares_kept[at, :] = shares
            sent[at, :] = (gate * grads_ref[at, :].astype(wide)).astype(half)
            out_sum[at, :] = jnp.zeros((chunk, out_sum.shape[1]), wide)
            row_sum[at, :] = jnp.zeros((chunk, row_sum.shape[1]), wide)

        chunks(prepare)

    def apply(up, down, at):
        pre = half_dot(rows_ref[at, :], up)
        phi = 0.5 * (1.0 + lax.erf(pre * 0.7071067811865476))
        slope = phi + pre * (jnp.exp(-0.5 * pre * pre) * 0.3989422804014327)
        active = (pre * phi).astype(half)
        hidden[at, :] = active
        out_sum[at, :] += half_dot(active, down)
        back = (slope * cols_dot(sent[at, :], down)).astype(half)
        grad_pre[at, :] = back
        row_sum[at, :] += cols_dot(back, up)

    chunks(functools.partial(apply, up_ref[0], down_ref[0]))
    grad_up_ref[0] = rows_dot(rows_ref[...], grad_pre[...])
    grad_down_ref[0] = rows_dot(hidden[...], sent[...])
    chunks(functools.partial(apply, near_up_ref[0], near_down_ref[0]))
    far_up_ref[0] = rows_dot(rows_ref[...], grad_pre[...]).astype(half)
    far_down_ref[0] = rows_dot(hidden[...], sent[...]).astype(half)

    @pl.when(step == pl.num_programs(0) - 1)
    def _():
        grad_router_ref[...] = jnp.zeros(grad_router_ref.shape, wide)

        def finish(at):
            shares = shares_kept[at, :]
            chosen = chosen_ref[...]
            gate = jnp.sum(shares * chosen, axis=-1, keepdims=True)
            grad_gate = jnp.sum(
                grads_ref[at, :].astype(wide) * out_sum[at, :], axis=-1, keepdims=True
            )
            grad_logits = grad_gate * gate * (chosen - shares)
            out_ref[at, :] = (gate * out_sum[at, :]).astype(half)
            grad_row_ref[at, :] = (
                row_sum[at, :]
                + jnp.dot(
                    grad_logits,
                    router_ref[...],
                    precision=lax.Precision.HIGHEST,
                    preferred_element_type=wide,
                )
            ).astype(half)
            grad_router_ref[...] += rows_dot(
                grad_logits, rows_ref[at, :].astype(wide), lax.Precision.HIGHEST
            )

        chunks(finish)


def expert_apply(rows, grads, weights, router, chosen):
    count, width = rows.shape
    experts = router.shape[0]
    up, down = weights[:2]
    unit = 256
    whole = pl.BlockSpec((count, width), lambda h: (0, 0))
    up_block = pl.BlockSpec((1, width, unit), lambda h: (0, 0, h))
    down_block = pl.BlockSpec((1, unit, width), lambda h: (0, h, 0))
    router_block = pl.BlockSpec((experts, width), lambda h: (0, 0))
    chosen_block = pl.BlockSpec((1, experts), lambda h: (0, 0))
    both = [up_block, down_block]
    half, wide = jnp.bfloat16, jnp.float32
    return pl.pallas_call(
        expert_kernel,
        name="expert_apply",
        grid=(up.shape[2] // unit,),
        in_specs=[whole, whole] + both + both + [router_block, chosen_block],
        out_specs=[whole, whole] + both + both + [router_block],
        out_shape=[
            jax.ShapeDtypeStruct((count, width), half),
            jax.ShapeDtypeStruct((count, width), half),
            jax.ShapeDtypeStruct(up.shape, wide),
            jax.ShapeDtypeStruct(down.shape, wide),
            jax.ShapeDtypeStruct(up.shape, half),
            jax.ShapeDtypeStruct(down.shape, half),
            jax.ShapeDtypeStruct(router.shape, wide),
        ],
        scratch_shapes=[
            pltpu.VMEM((count, width), half),
            pltpu.VMEM((count, width), wide),
            pltpu.VMEM((count, width), wide),
            pltpu.VMEM((count, unit), half),
            pltpu.VMEM((count, unit), half),
            pltpu.VMEM((count, experts), wide),
        ],
        compiler_params=pltpu.CompilerParams(
            dimension_semantics=("arbitrary",), vmem_limit_bytes=VMEM_BYTES
        ),
        cost_estimate=pl.CostEstimate(
            flops=24 * count * width * up.shape[2],
            transcendentals=4 * count * up.shape[2],
            bytes_accessed=3 * 10**7,
        ),
    )(rows, grads, *weights, router, chosen)


def on_device(
    layer_in,
    mixer_gain,
    in_proj,
    conv_weight,
    conv_bias,
    state_proj,
    delta_proj,
    delta_bias,
    decay_log,
    skip_gain,
    out_proj,
    expert_norm,
    router_weight,
    expert_up,
    expert_down,
    expert_ids,
    capacity_slot,
    out_grad,
):
    sequences, piece_len, width = layer_in.shape
    tokens = sequences * piece_len
    taps, inner_width = conv_weight.shape
    low_rank = delta_proj.shape[0]
    states = decay_log.shape[0]
    experts = router_weight.shape[1]
    senders = lax.axis_size("exp")
    capacity = (5 * tokens + 4 * experts - 1) // (4 * experts)
    flat_in = layer_in.reshape(tokens, width).astype(jnp.float32)
    normed_one, scaling_one = norm_forward(flat_in, mixer_gain)
    normed_half = normed_one.astype(jnp.bfloat16)
    projected = half_dot(normed_half, in_proj)
    inner = projected[:, :inner_width]
    gate_half = projected[:, inner_width:]
    inner_seq = inner.reshape(sequences, piece_len, inner_width)
    left_rim = shifted(inner_seq[:, piece_len - (taps - 1) :, :], ("seq", "exp"), 1)
    lead = 8 - (taps - 1)
    blank = jnp.zeros((sequences, lead, inner_width), jnp.float32)
    extended = jnp.concatenate([blank, left_rim, inner_seq], axis=1)
    conv_pre = conv_bias + conv_weight[0] * extended[:, lead : lead + piece_len, :]
    for tap in range(1, taps):
        conv_pre = conv_pre + conv_weight[tap] * extended[:, lead + tap : lead + tap + piece_len, :]
    conv_flat = jax.nn.silu(conv_pre).reshape(tokens, inner_width)
    projections = exact_dot(conv_flat, state_proj.astype(jnp.float32))
    delta_low = projections[:, :low_rank]
    in_coef = projections[:, low_rank : low_rank + states]
    out_coef = projections[:, low_rank + states :]
    delta_pre = exact_dot(delta_low, delta_proj.astype(jnp.float32)) + delta_bias
    delta = jax.nn.softplus(delta_pre)
    steps_by = (piece_len, GROUP)
    in_spread, out_spread = spread(in_coef, LANES), spread(out_coef, LANES)
    in_diag, out_diag = diagonal(in_coef, BLK), diagonal(out_coef, BLK)
    out_rest = diagonal(out_coef - lax.reduce_precision(out_coef, 8, 7), BLK)
    float_steps = pltpu.VMEM(steps_by, jnp.float32)
    stack_of = pltpu.VMEM((BLK * states, GROUP), jnp.bfloat16)
    (local_end,) = scan_call(
        first_pass_kernel,
        "first_pass",
        sequences,
        states,
        [("wide", delta), ("wide", conv_flat), ("spread", in_spread), ("rates", decay_log)],
        ["state"],
        [float_steps],
    )
    delta_sum = jnp.sum(delta.reshape(sequences, piece_len, inner_width), axis=1)
    carried = exchange(local_end, delta_sum, decay_log, False)
    (scanned,) = scan_call(
        second_pass_kernel,
        "second_pass",
        sequences,
        states,
        [
            ("wide", delta),
            ("wide", conv_flat),
            ("spread", in_spread),
            ("rates", decay_log),
            ("state", carried),
            ("narrow", out_diag),
            ("narrow", out_rest),
        ],
        ["wide"],
        [float_steps, stack_of],
    )
    mixer_pre = scanned + skip_gain * conv_flat
    gate_act = jax.nn.silu(gate_half)
    mixed = (mixer_pre * gate_act).astype(jnp.bfloat16)
    resid = flat_in + half_dot(mixed, out_proj)
    normed_two, scaling_two = norm_forward(resid, expert_norm)
    routed = normed_two.astype(jnp.bfloat16)
    flat_ids = expert_ids.reshape(tokens)
    flat_slot = capacity_slot.reshape(tokens)
    target = jnp.where(flat_slot < capacity, flat_ids * capacity + flat_slot, experts * capacity)
    slot_rows = jnp.arange(experts * capacity, dtype=jnp.int32)
    picks = (slot_rows[:, None] == target[None, :]).astype(jnp.bfloat16)
    planes = lax.axis_size("seq")
    hops = planes // 2

    def along_planes(values, by):
        pairs = [(at, (at + by) % planes) for at in range(planes)]
        return lax.ppermute(values, "seq", pairs)

    def with_neighbour(values):
        pairs = [(at, at ^ 1) for at in range(planes)]
        return lax.ppermute(values, "seq", pairs)

    def swapped(values):
        return lax.all_to_all(values, "exp", split_axis=0, concat_axis=0, tiled=True)

    def to_slots(values):
        buffer = half_dot(picks, values).astype(jnp.bfloat16)
        return buffer.reshape(experts, capacity, width)

    weights = [expert_up, expert_down, with_neighbour(expert_up), with_neighbour(expert_down)]
    near_grads = swapped(to_slots(out_grad.reshape(tokens, width)))
    grad_rows = jnp.stack(
        [near_grads] + [along_planes(near_grads, -2 * hop) for hop in range(1, hops)]
    )
    rows = dispatch(to_slots(routed), False, 4, "send_rows")
    chosen = (
        jnp.arange(experts, dtype=jnp.int32) == lax.axis_index("exp")
    ).astype(jnp.float32)[None, :]
    expert_out, grad_row_in, grad_up, grad_down, far_up, far_down, grad_router = expert_apply(
        rows.reshape(hops * senders * capacity, width),
        grad_rows.reshape(hops * senders * capacity, width),
        weights,
        router_weight.T,
        chosen,
    )
    slotted = (hops, senders, capacity, width)
    back_rows = dispatch(grad_row_in.reshape(slotted), True, 5, "return_rows")
    grad_routed = rows_dot(
        jnp.concatenate([picks] * hops, axis=0), back_rows.reshape(hops * senders * capacity, width)
    )
    grad_top = out_grad.reshape(tokens, width).astype(jnp.float32)
    grad_resid_norm, grad_expert_norm = norm_backward(resid, scaling_two, expert_norm, grad_routed)
    grad_resid = grad_top + grad_resid_norm
    grad_mixer = grad_resid.astype(jnp.bfloat16)
    grad_out_proj = rows_dot(mixed, grad_mixer)
    grad_mixed = cols_dot(grad_mixer, out_proj)
    grad_scan = grad_mixed * gate_act
    grad_gate_half = grad_mixed * mixer_pre * silu_slope(gate_half)
    grad_gate_half = grad_gate_half.astype(jnp.bfloat16)
    grad_in_gate = rows_dot(normed_half, grad_gate_half)
    grad_normed_gate = cols_dot(grad_gate_half, in_proj[:, inner_width:])
    grad_skip_gain = jnp.sum(grad_scan * conv_flat, axis=0)
    (gradient_first,) = scan_call(
        back_summary_kernel,
        "back_summary",
        sequences,
        states,
        [("wide", delta), ("wide", grad_scan), ("spread", out_spread), ("rates", decay_log)],
        ["state"],
        [],
    )
    carried_back = exchange(gradient_first, delta_sum, decay_log, True)
    full_steps = pltpu.VMEM((piece_len, states, GROUP), jnp.float32)
    side = math.isqrt(senders // 2)
    big = (2, side, side, planes, inner_width // (senders * planes), width)

    def as_rows(values):
        blocks = values.shape[1] // width
        return jnp.concatenate(
            [values[:, at * width : (at + 1) * width] for at in range(blocks)], axis=0
        ).astype(jnp.bfloat16)

    def as_columns(values):
        return jnp.concatenate(
            [values[at : at + width] for at in range(0, values.shape[0], width)], axis=1
        ).astype(jnp.float32)

    early = [
        grad_out_proj.astype(jnp.bfloat16).reshape(big),
        as_rows(grad_in_gate).reshape(big),
    ]
    *block_grads, own_out, own_gate, near_up = scan_call(
        backward_sum_kernel,
        "backward_scan",
        sequences,
        states,
        [
            ("wide", delta),
            ("wide", conv_flat),
            ("wide", grad_scan),
            ("spread", in_spread),
            ("spread", out_spread),
            ("narrow", in_diag),
            ("rates", decay_log),
            ("state", carried),
            ("state", carried_back),
        ],
        ["wide", "wide", "narrow", "narrow", "state"],
        [float_steps, full_steps, full_steps, stack_of, stack_of],
        [planes, side] + early + [far_up],
    )
    grad_delta, grad_conv_scan, grad_in_wide, grad_out_wide, grad_log_parts = block_grads
    heights = [low_rank + 2 * states, low_rank, states, taps, 1, 1, 1, 1, experts // 2]
    in_grad, sum_out, sum_gate, sum_left, sum_right, sum_small, back_out, near_down = finish(
        [
            grad_delta,
            grad_conv_scan,
            grad_in_wide,
            grad_out_wide,
            grad_log_parts,
            grad_scan,
            delta_pre,
            delta_low,
            conv_flat,
            conv_pre.reshape(tokens, inner_width),
            extended,
            normed_half,
            grad_normed_gate,
            layer_in.reshape(tokens, width),
            grad_resid,
            delta_proj,
            state_proj.T,
            in_proj[:, :inner_width],
            conv_weight,
            skip_gain[None],
            mixer_gain[None],
            grad_skip_gain[None],
            grad_expert_norm[None],
            grad_router,
            own_out,
            own_gate,
            expert_out.reshape(slotted),
            far_down,
        ],
        sum(heights),
        side,
    )
    grad_up_own = grad_up + near_up.astype(jnp.float32)
    grad_down_own = grad_down + near_down.astype(jnp.float32)
    token_out = rows_dot(
        jnp.concatenate([picks] * hops, axis=0), back_out.reshape(hops * senders * capacity, width)
    )
    layer_out = (resid + token_out).astype(jnp.bfloat16).reshape(sequences, piece_len, width)
    sum_inner = jnp.concatenate([sum_left, sum_right], axis=4)
    in_grad = in_grad.reshape(sequences, piece_len, width)
    rows_of = (inner_width, width)
    grad_in_proj = jnp.concatenate(
        [as_columns(sum_inner.reshape(rows_of)), as_columns(sum_gate.reshape(rows_of))], axis=1
    )
    small_halves = sum_small.reshape(2, -1, width)
    small_wide = jnp.concatenate([small_halves[0], small_halves[1]], axis=1).astype(jnp.float32)
    offsets = [sum(heights[:at]) for at in range(len(heights) + 1)]
    pieces = [small_wide[offsets[at] : offsets[at + 1]] for at in range(len(heights))]
    summed = (
        pieces[7][0, :width],
        grad_in_proj,
        pieces[3],
        pieces[4][0],
        pieces[0].T,
        pieces[1],
        pieces[5][0],
        pieces[2],
        pieces[6][0],
        sum_out.reshape(rows_of).astype(jnp.float32),
        pieces[7][0, width:],
        pieces[8].reshape(experts, width).T,
    )
    return (
        layer_out,
        in_grad,
        summed[0],
        summed[1],
        summed[2],
        summed[3],
        summed[4],
        summed[5],
        summed[6],
        summed[7],
        summed[8],
        summed[9],
        summed[10],
        summed[11],
        grad_up_own,
        grad_down_own,
    )


def solution(mesh):
    placed = (
        P(None, ("seq", "exp"), None),
        P(),
        P(),
        P(),
        P(),
        P(),
        P(),
        P(),
        P(),
        P(),
        P(),
        P(),
        P(),
        P("exp", None, "seq"),
        P("exp", "seq", None),
        P(None, ("seq", "exp")),
        P(None, ("seq", "exp")),
        P(None, ("seq", "exp"), None),
    )
    return jax.shard_map(
        on_device,
        mesh=mesh,
        in_specs=placed,
        out_specs=(
            P(None, ("seq", "exp"), None),
            P(None, ("seq", "exp"), None),
            P(),
            P(),
            P(),
            P(),
            P(),
            P(),
            P(),
            P(),
            P(),
            P(),
            P(),
            P(),
            P("exp", None, "seq"),
            P("exp", "seq", None),
        ),
        check_vma=False,
    )
```

```python
import functools
import math

import jax
import jax.numpy as jnp
from jax import lax
from jax.experimental import pallas as pl
from jax.experimental.pallas import tpu as pltpu
from jax.sharding import PartitionSpec as P

BLK = 16
LANES = 128
GROUP = 512
LOG2E = 1.4426950408889634
LN2 = 0.6931471805599453
VMEM_BYTES = 50 * 1024 * 1024


EPSILON = 1e-05


def half_dot(left, right):
    return jnp.dot(left, right, preferred_element_type=jnp.float32)


def rows_dot(left, right, precision=None):
    return lax.dot_general(
        left,
        right,
        (((0,), (0,)), ((), ())),
        precision=precision,
        preferred_element_type=jnp.float32,
    )


def cols_dot(left, right, precision=None):
    return lax.dot_general(
        left,
        right,
        (((1,), (1,)), ((), ())),
        precision=precision,
        preferred_element_type=jnp.float32,
    )


def norm_backward(values, scaling, gain_vec, incoming):
    normal = values * scaling
    weighted = incoming * gain_vec
    grad_gain = jnp.sum(incoming * normal, axis=0, keepdims=True)
    grad_values = scaling * (
        weighted - normal * jnp.mean(weighted * normal, axis=-1, keepdims=True)
    )
    return (grad_values, grad_gain)


def silu_slope(values):
    sigma = jax.nn.sigmoid(values)
    return sigma * (1.0 + values * (1.0 - sigma))


def lane_parts(ref, k, states):
    width = ref.shape[-1]
    return [
        jnp.broadcast_to(ref[k : k + 1, at : at + LANES], (states, LANES))
        for at in range(0, width, LANES)
    ]


def block_of(ref, i):
    return ref.at[pl.ds(pl.multiple_of(i * BLK, BLK), BLK), :]


def rates_of(log_ref):
    rates = -jnp.exp(log_ref[...]) * LOG2E
    return [rates[:, at : at + LANES] for at in range(0, rates.shape[1], LANES)]


def first_pass_kernel(delta_ref, conv_ref, in_ref, log_ref, end_ref, drive):
    steps, width = delta_ref.shape
    states = log_ref.shape[0]
    rates = rates_of(log_ref)
    drive[...] = delta_ref[...] * conv_ref[...]

    def block(i, state):
        state = list(state)
        inwards = in_ref[i]
        for k in range(BLK):
            inward = jnp.broadcast_to(inwards[:, k : k + 1], (states, LANES))
            deltas = lane_parts(block_of(delta_ref, i), k, states)
            drives = lane_parts(block_of(drive, i), k, states)
            for j in range(width // LANES):
                state[j] = jnp.exp2(deltas[j] * rates[j]) * state[j] + inward * drives[j]
        return tuple(state)

    zero = tuple(jnp.zeros((states, LANES), jnp.float32) for _ in range(width // LANES))
    last = lax.fori_loop(0, steps // BLK, block, zero)
    for j in range(width // LANES):
        end_ref[0, :, j * LANES : (j + 1) * LANES] = last[j]


def second_pass_kernel(
    delta_ref, conv_ref, in_ref, log_ref, start_ref, out_ref, rest_ref, scanned_ref, drive, stack
):
    steps, width = delta_ref.shape
    states = log_ref.shape[0]
    rates = rates_of(log_ref)
    drive[...] = delta_ref[...] * conv_ref[...]

    def block(i, state):
        state = list(state)
        inwards = in_ref[i]
        for k in range(BLK):
            inward = jnp.broadcast_to(inwards[:, k : k + 1], (states, LANES))
            deltas = lane_parts(block_of(delta_ref, i), k, states)
            drives = lane_parts(block_of(drive, i), k, states)
            for j in range(width // LANES):
                state[j] = jnp.exp2(deltas[j] * rates[j]) * state[j] + inward * drives[j]
                stack[k * states : (k + 1) * states, j * LANES : (j + 1) * LANES] = state[j].astype(
                    jnp.bfloat16
                )
        rows = pl.ds(pl.multiple_of(i * BLK, BLK), BLK)
        both = jnp.concatenate([out_ref[rows, :], rest_ref[rows, :]], axis=0)
        product = jnp.dot(both, stack[...], preferred_element_type=jnp.float32)
        scanned_ref[rows, :] = product[:BLK] + product[BLK:]
        return tuple(state)

    begin = tuple(start_ref[0, :, j * LANES : (j + 1) * LANES] for j in range(width // LANES))
    lax.fori_loop(0, steps // BLK, block, begin)


def back_summary_kernel(delta_ref, grad_ref, out_ref, log_ref, end_ref):
    steps, width = delta_ref.shape
    states = log_ref.shape[0]
    rates = rates_of(log_ref)
    blocks = steps // BLK

    def block(i, state):
        state = list(state)
        outwards = out_ref[blocks - 1 - i]
        for k in reversed(range(BLK)):
            outward = jnp.broadcast_to(outwards[:, k : k + 1], (states, LANES))
            deltas = lane_parts(block_of(delta_ref, blocks - 1 - i), k, states)
            grads = lane_parts(block_of(grad_ref, blocks - 1 - i), k, states)
            for j in range(width // LANES):
                state[j] = jnp.exp2(deltas[j] * rates[j]) * (state[j] + outward * grads[j])
        return tuple(state)

    zero = tuple(jnp.zeros((states, LANES), jnp.float32) for _ in range(width // LANES))
    last = lax.fori_loop(0, blocks, block, zero)
    for j in range(width // LANES):
        end_ref[0, :, j * LANES : (j + 1) * LANES] = last[j]


def backward_body(
    middle,
    first,
    delta_ref,
    conv_ref,
    grad_ref,
    in_ref,
    out_ref,
    in_diag_ref,
    log_ref,
    start_ref,
    finish_ref,
    grad_delta_ref,
    grad_conv_ref,
    grad_in_ref,
    grad_out_ref,
    grad_log_ref,
    drive,
    carried,
    stack,
    slope,
):
    steps, width = delta_ref.shape
    states = log_ref.shape[0]
    parts = width // LANES
    rates = rates_of(log_ref)
    blocks = steps // BLK
    drive[...] = delta_ref[...] * conv_ref[...]

    def forward(i, state):
        state = list(state)
        inwards = in_ref[i]
        for k in range(BLK):
            t = i * BLK + k
            inward = jnp.broadcast_to(inwards[:, k : k + 1], (states, LANES))
            deltas = lane_parts(block_of(delta_ref, i), k, states)
            drives = lane_parts(block_of(drive, i), k, states)
            for j in range(parts):
                at = slice(j * LANES, (j + 1) * LANES)
                decay = jnp.exp2(deltas[j] * rates[j])
                kept = decay * state[j]
                carried[t, :, at] = kept
                state[j] = kept + inward * drives[j]
                stack[k * states : (k + 1) * states, at] = state[j].astype(jnp.bfloat16)
        rows = pl.ds(pl.multiple_of(i * BLK, BLK), BLK)
        partial = cols_dot(grad_ref[rows, :].astype(jnp.bfloat16), stack[...])

        @pl.when(first)
        def _():
            grad_out_ref[rows, :] = partial

        @pl.when(jnp.logical_not(first))
        def _():
            grad_out_ref[rows, :] += partial

        return tuple(state)

    begin = tuple(start_ref[0, :, j * LANES : (j + 1) * LANES] for j in range(parts))
    lax.fori_loop(0, blocks, forward, begin)
    middle()
    column = lax.broadcasted_iota(jnp.int32, (BLK, BLK * states), 1) // states
    row = lax.broadcasted_iota(jnp.int32, (BLK, BLK * states), 0)
    ones = jnp.where(column == row, 1.0, 0.0).astype(jnp.bfloat16)

    def backward(i, state):
        adjoint, gathered = list(state[:parts]), list(state[parts:])
        outwards = out_ref[blocks - 1 - i]
        for k in reversed(range(BLK)):
            t = (blocks - 1 - i) * BLK + k
            outward = jnp.broadcast_to(outwards[:, k : k + 1], (states, LANES))
            deltas = lane_parts(block_of(delta_ref, blocks - 1 - i), k, states)
            grads = lane_parts(block_of(grad_ref, blocks - 1 - i), k, states)
            for j in range(parts):
                at = slice(j * LANES, (j + 1) * LANES)
                whole = adjoint[j] + outward * grads[j]
                exponent = whole * carried[t, :, at]
                gathered[j] = gathered[j] + exponent * deltas[j]
                slope[k * states : (k + 1) * states, at] = (exponent * rates[j]).astype(
                    jnp.bfloat16
                )
                stack[k * states : (k + 1) * states, at] = whole.astype(jnp.bfloat16)
                adjoint[j] = jnp.exp2(deltas[j] * rates[j]) * whole
        rows = pl.ds(pl.multiple_of((blocks - 1 - i) * BLK, BLK), BLK)
        driven = jnp.dot(in_diag_ref[rows, :], stack[...], preferred_element_type=jnp.float32)
        summed = jnp.dot(ones, slope[...], preferred_element_type=jnp.float32) * LN2
        grad_delta_ref[rows, :] = summed + driven * conv_ref[rows, :]
        grad_conv_ref[rows, :] = driven * delta_ref[rows, :]
        partial = cols_dot(drive[rows, :].astype(jnp.bfloat16), stack[...])

        @pl.when(first)
        def _():
            grad_in_ref[rows, :] = partial

        @pl.when(jnp.logical_not(first))
        def _():
            grad_in_ref[rows, :] += partial

        return tuple(adjoint + gathered)

    ends = tuple(finish_ref[0, :, j * LANES : (j + 1) * LANES] for j in range(parts))
    zero = tuple(jnp.zeros((states, LANES), jnp.float32) for _ in range(parts))
    last = lax.fori_loop(0, blocks, backward, ends + zero)
    for j in range(parts):
        grad_log_ref[0, :, j * LANES : (j + 1) * LANES] = last[parts + j] * rates[j] * LN2


def scan_call(kernel, name, sequences, states, operands, results, scratch):
    tokens, width = next(value.shape for kind, value in operands if kind == "wide")
    steps = tokens // sequences
    specs = {
        "wide": pl.BlockSpec((steps, GROUP), lambda q, j: (q, j)),
        "cols": pl.BlockSpec((steps // BLK, states, BLK), lambda q, j: (q, 0, 0)),
        "narrow": pl.BlockSpec((steps, BLK * states), lambda q, j: (q, 0)),
        "rates": pl.BlockSpec((states, GROUP), lambda q, j: (0, j)),
        "state": pl.BlockSpec((1, states, GROUP), lambda q, j: (q, 0, j)),
    }
    shapes = {
        "wide": (tokens, width),
        "narrow": (tokens, BLK * states),
        "state": (sequences, states, width),
    }
    in_specs = [specs[kind] for kind, _ in operands]
    out_specs = [specs[kind] for kind in results]
    out_shape = [jax.ShapeDtypeStruct(shapes[kind], jnp.float32) for kind in results]
    return pl.pallas_call(
        kernel,
        name=name,
        grid=(sequences, width // GROUP),
        in_specs=in_specs,
        out_specs=out_specs,
        out_shape=out_shape,
        scratch_shapes=scratch,
        compiler_params=pltpu.CompilerParams(
            dimension_semantics=("arbitrary", "arbitrary"),
            vmem_limit_bytes=VMEM_BYTES,
        ),
        cost_estimate=pl.CostEstimate(
            flops=20 * tokens * states * width,
            transcendentals=tokens * states * width,
            bytes_accessed=16 * tokens * width,
        ),
    )(*(value for _, value in operands))


MESH = pl.DeviceIdType.MESH


def remote(src, dst, send, arrive, axis, peer):
    return pltpu.make_async_remote_copy(
        src_ref=src,
        dst_ref=dst,
        send_sem=send,
        recv_sem=arrive,
        device_id={axis: peer},
        device_id_type=MESH,
    )


def greet(axes):
    barrier = pltpu.get_barrier_semaphore()
    total = 0
    for axis, size in axes:
        mine = lax.axis_index(axis)
        for k in range(1, size):
            pl.semaphore_signal(
                barrier, inc=1, device_id={axis: lax.rem(mine + k, size)}, device_id_type=MESH
            )
        total += size - 1
    pl.semaphore_wait(barrier, total)


def exchange_body(
    reverse,
    planes,
    members,
    end_ref,
    sum_ref,
    rates_ref,
    carry_ref,
    packed,
    landed,
    summary,
    totals,
    starts,
    carries,
    send_one,
    recv_one,
    send_two,
    recv_two,
    send_three,
    recv_three,
):
    sequences, states, width = end_ref.shape
    rows = sequences * states // members
    plane, member = lax.axis_index("seq"), lax.axis_index("exp")
    rates = -jnp.exp(rates_ref[...])
    for i in range(members):
        q, n = (i * rows) // states, (i * rows) % states
        packed[i, :rows] = end_ref[q, n : n + rows]
        packed[i, rows:] = sum_ref[q : q + 1]
    for k in range(1, members):
        other = lax.rem(member + k, members)
        remote(
            packed.at[other],
            landed.at[member],
            send_one.at[k],
            recv_one.at[member],
            "exp",
            other,
        ).start()
    landed[member] = packed[member]
    for k in range(1, members):
        other = lax.rem(member + k, members)
        remote(
            packed.at[other], landed.at[other], send_one.at[k], recv_one.at[other], "exp", other
        ).wait()
    order = range(members)[::-1] if reverse else range(members)
    plane_order = range(planes)[::-1] if reverse else range(planes)

    def through(piece, before):
        return jnp.exp(piece[rows:] * rates) * before + piece[:rows]

    state = jnp.zeros((rows, width), jnp.float32)
    total = jnp.zeros((1, width), jnp.float32)
    for i in order:
        piece = landed[i]
        state = through(piece, state)
        total = total + piece[rows:]
    summary[:rows] = state
    summary[rows:] = total
    for k in range(1, planes):
        other = lax.rem(plane + k, planes)
        remote(
            summary, totals.at[plane], send_two.at[k], recv_two.at[plane], "seq", other
        ).start()
    totals[plane] = summary[...]
    for k in range(1, planes):
        other = lax.rem(plane + k, planes)
        remote(summary, totals.at[other], send_two.at[k], recv_two.at[other], "seq", other).wait()
    state = jnp.zeros((rows, width), jnp.float32)
    for s in plane_order:
        reached = plane < s if reverse else plane > s
        state = jnp.where(reached, through(totals[s], state), state)
    for i in order:
        starts[i] = state
        state = through(landed[i], state)
    for k in range(1, members):
        other = lax.rem(member + k, members)
        remote(
            starts.at[other],
            carries.at[member],
            send_three.at[k],
            recv_three.at[member],
            "exp",
            other,
        ).start()
    carries[member] = starts[member]
    for k in range(1, members):
        other = lax.rem(member + k, members)
        remote(
            starts.at[other],
            carries.at[other],
            send_three.at[k],
            recv_three.at[other],
            "exp",
            other,
        ).wait()
    for i in range(members):
        q, n = (i * rows) // states, (i * rows) % states
        carry_ref[q, n : n + rows] = carries[i]


def exchange_kernel(reverse, planes, members, *refs):
    greet((("seq", planes), ("exp", members)))
    exchange_body(reverse, planes, members, *refs)


def exchange_scratch(planes, members, rows, width):
    piece = (rows + 1, width)
    return [
        pltpu.VMEM((members,) + piece, jnp.float32),
        pltpu.VMEM((members,) + piece, jnp.float32),
        pltpu.VMEM(piece, jnp.float32),
        pltpu.VMEM((planes,) + piece, jnp.float32),
        pltpu.VMEM((members, rows, width), jnp.float32),
        pltpu.VMEM((members, rows, width), jnp.float32),
        pltpu.SemaphoreType.DMA((members,)),
        pltpu.SemaphoreType.DMA((members,)),
        pltpu.SemaphoreType.DMA((planes,)),
        pltpu.SemaphoreType.DMA((planes,)),
        pltpu.SemaphoreType.DMA((members,)),
        pltpu.SemaphoreType.DMA((members,)),
    ]


def exchange(local_end, delta_sum, own_log):
    planes, members = lax.axis_size("seq"), lax.axis_size("exp")
    rows, width = own_log.shape
    vmem = pl.BlockSpec(memory_space=pltpu.VMEM)
    return pl.pallas_call(
        functools.partial(exchange_kernel, True, planes, members),
        name="state_exchange_back",
        in_specs=[vmem] * 3,
        out_specs=vmem,
        out_shape=jax.ShapeDtypeStruct(local_end.shape, jnp.float32),
        scratch_shapes=exchange_scratch(planes, members, rows, width),
        compiler_params=pltpu.CompilerParams(
            collective_id=2, has_side_effects=True, vmem_limit_bytes=VMEM_BYTES
        ),
        cost_estimate=pl.CostEstimate(flops=10**6, transcendentals=10**5, bytes_accessed=2 * 10**7),
    )(local_end, delta_sum, own_log)


class Sums:
    def __init__(self, planes, side, sends, arrivals):
        self.planes, self.side = planes, side
        self.plane, self.member = lax.axis_index("seq"), lax.axis_index("exp")
        chip, self.core = self.member // 2, lax.rem(self.member, 2)
        high, low = chip // side, lax.rem(chip, side)
        self.first = low + (high - low) * self.core
        self.second = high + (low - high) * self.core
        self.partner = self.member + 1 - 2 * self.core
        self.sends, self.arrivals = sends, arrivals

    def chip_at(self, first, second):
        low = first + (second - first) * self.core
        high = second + (first - second) * self.core
        return (high * self.side + low) * 2 + self.core

    def first_peer(self, k):
        other = lax.rem(self.first + k, self.side)
        return other, self.chip_at(other, self.second)

    def second_peer(self, k):
        other = lax.rem(self.second + k, self.side)
        return other, self.chip_at(self.first, other)

    def plane_peer(self, k):
        return lax.rem(self.plane + k, self.planes)

    def signal_peers(self, barrier):
        peers = [{"exp": self.partner}]
        peers += [{"exp": self.first_peer(k)[1]} for k in range(1, self.side)]
        peers += [{"exp": self.second_peer(k)[1]} for k in range(1, self.side)]
        peers += [{"seq": self.plane_peer(k)} for k in range(1, self.planes)]
        for peer in peers:
            pl.semaphore_signal(barrier, inc=1, device_id=peer, device_id_type=MESH)
        return len(peers)

    def move(self, stage, at, slot, src, dst, axis, peer):
        return remote(
            src, dst, self.sends[stage].at[at], self.arrivals[stage].at[slot], axis, peer
        )

    def pair_half(self, i, given, half):
        return self.move(0, i, i, given.at[1 - self.core], half, "exp", self.partner)

    def scatter_first(self, i, k, half, slots, arriving):
        other, device = self.first_peer(k)
        slot = other if arriving else self.first
        return self.move(1, (i, k), (i, slot), half.at[other], slots.at[slot], "exp", device)

    def scatter_second(self, i, k, quarter, slots, arriving):
        other, device = self.second_peer(k)
        slot = other if arriving else self.second
        return self.move(2, (i, k), (i, slot), quarter.at[other], slots.at[slot], "exp", device)

    def scatter_plane(self, i, k, eighth, slots, arriving):
        other = self.plane_peer(k)
        slot = other if arriving else self.plane
        return self.move(3, (i, k), (i, slot), eighth.at[other], slots.at[slot], "seq", other)

    def gather_plane(self, i, k, block, arriving):
        other = self.plane_peer(k)
        slot = other if arriving else self.plane
        return self.move(
            4, (i, k), (i, slot), block.at[self.plane], block.at[slot], "seq", other
        )

    def gather_second(self, i, k, result, arriving):
        other, device = self.second_peer(k)
        slot = other if arriving else self.second
        row = result.at[self.core, self.first]
        return self.move(5, (i, k), (i, slot), row.at[self.second], row.at[slot], "exp", device)

    def gather_first(self, i, k, result, arriving):
        other, device = self.first_peer(k)
        slot = other if arriving else self.first
        own = result.at[self.core]
        return self.move(6, (i, k), (i, slot), own.at[self.first], own.at[slot], "exp", device)

    def pair_gather(self, i, k, result, arriving):
        other = lax.rem(self.first + k, self.side)
        low = lax.rem(self.partner // 2, self.side)
        theirs = low + (self.partner // (2 * self.side) - low) * (1 - self.core)
        other = lax.rem(theirs + k, self.side) if arriving else other
        half = 1 - self.core if arriving else self.core
        mine = result.at[self.core, lax.rem(self.first + k, self.side)]
        return self.move(7, (i, k), (i, k), mine, result.at[half, other], "exp", self.partner)

    def after_pair(self, i, given, half, slots):
        self.pair_half(i, given, half).wait()
        own = self.core
        for at in range(self.side):
            for to in range(self.side):
                both = given[own, at, to].astype(jnp.float32) + half[at, to].astype(jnp.float32)
                half[at, to] = both.astype(jnp.bfloat16)
        for k in range(1, self.side):
            self.scatter_first(i, k, half, slots, False).start()
        slots[self.first] = half[self.first]

    def after_first(self, i, half, slots, quarter, slots_two):
        for k in range(1, self.side):
            self.scatter_first(i, k, half, slots, True).wait_recv()
        for at in range(self.side):
            added = slots[0, at].astype(jnp.float32)
            for k in range(1, self.side):
                added = added + slots[k, at].astype(jnp.float32)
            quarter[at] = added.astype(jnp.bfloat16)
        for k in range(1, self.side):
            self.scatter_second(i, k, quarter, slots_two, False).start()
        slots_two[self.second] = quarter[self.second]

    def after_second(self, i, quarter, slots_two, eighth, slots_three):
        for k in range(1, self.side):
            self.scatter_second(i, k, quarter, slots_two, True).wait_recv()
        added = slots_two[0].astype(jnp.float32)
        for k in range(1, self.side):
            added = added + slots_two[k].astype(jnp.float32)
        eighth[...] = added.astype(jnp.bfloat16)
        for k in range(1, self.planes):
            self.scatter_plane(i, k, eighth, slots_three, False).start()
        slots_three[self.plane] = eighth[self.plane]

    def after_planes(self, i, eighth, slots_three, block):
        for k in range(1, self.planes):
            self.scatter_plane(i, k, eighth, slots_three, True).wait_recv()
        added = slots_three[0].astype(jnp.float32)
        for k in range(1, self.planes):
            added = added + slots_three[k].astype(jnp.float32)
        block[self.plane] = added.astype(jnp.bfloat16)
        for k in range(1, self.planes):
            self.gather_plane(i, k, block, False).start()

    def planes_gathered(self, i, block):
        for k in range(1, self.planes):
            self.gather_plane(i, k, block, True).wait_recv()

    def scatter_sent(self, i, half, slots, quarter, slots_two, eighth, slots_three, block):
        for k in range(1, self.side):
            self.scatter_first(i, k, half, slots, False).wait_send()
            self.scatter_second(i, k, quarter, slots_two, False).wait_send()
        for k in range(1, self.planes):
            self.scatter_plane(i, k, eighth, slots_three, False).wait_send()
            self.gather_plane(i, k, block, False).wait_send()

    def gather_second_start(self, i, result):
        for k in range(1, self.side):
            self.gather_second(i, k, result, False).start()

    def gather_across(self, i, result):
        for k in range(1, self.side):
            self.gather_second(i, k, result, True).wait_recv()
        for k in range(1, self.side):
            self.gather_first(i, k, result, False).start()
        self.pair_gather(i, 0, result, False).start()

    def gather_pass(self, i, result):
        for k in range(1, self.side):
            self.gather_first(i, k, result, True).wait_recv()
            self.pair_gather(i, k, result, False).start()

    def gather_end(self, i, result):
        for k in range(self.side):
            self.pair_gather(i, k, result, True).wait_recv()
            self.pair_gather(i, k, result, False).wait_send()
        for k in range(1, self.side):
            self.gather_first(i, k, result, False).wait_send()
            self.gather_second(i, k, result, False).wait_send()


def stage_semaphores(count, planes, side):
    each = [(count,)] + [(count, size) for size in (side, side, planes, planes, side, side, side)]
    return [pltpu.SemaphoreType.DMA(shape) for shape in each]


def scatter_buffers(tails, planes, side):
    leads = [(side, side, planes), (side, side, planes), (side, planes), (side, planes)]
    leads += [(planes,), (planes,)]
    return [pltpu.VMEM(lead + tail, jnp.bfloat16) for lead in leads for tail in tails]


def neighbour_plane():
    plane = lax.axis_index("seq")
    return {"seq": plane + 1 - 2 * lax.rem(plane, 2)}


def swapped(src, dst, send, arrive):
    return pltpu.make_async_remote_copy(
        src_ref=src,
        dst_ref=dst,
        send_sem=send,
        recv_sem=arrive,
        device_id=neighbour_plane(),
        device_id_type=MESH,
    )


class Routes:
    def __init__(self, planes, members, sends, arrivals, local):
        self.planes, self.members = planes, members
        self.plane, self.member = lax.axis_index("seq"), lax.axis_index("exp")
        self.hops = planes // 2
        self.sends, self.arrivals, self.local = sends, arrivals, local
        self.pairs = [
            (hop, k) for hop in reversed(range(self.hops)) for k in range(members) if hop or k
        ]

    def device(self, hop, k):
        return {
            "seq": lax.rem(self.plane + 2 * hop, self.planes),
            "exp": lax.rem(self.member + k, self.members),
        }

    def signal_peers(self, barrier):
        for hop, k in self.pairs:
            pl.semaphore_signal(
                barrier, inc=1, device_id=self.device(hop, k), device_id_type=MESH
            )
        return len(self.pairs)

    def moved(self, given, landed, returning, hop, k, arriving):
        device = self.device(hop, k)
        other = device["exp"]
        slot = hop if arriving else (-hop) % self.hops
        sender = other if arriving else self.member
        return pltpu.make_async_remote_copy(
            src_ref=given.at[hop, other] if returning else given.at[other],
            dst_ref=landed.at[slot, sender],
            send_sem=self.sends.at[hop, k],
            recv_sem=self.arrivals.at[slot, sender],
            device_id=device,
            device_id_type=MESH,
        )

    def own(self, given, landed, returning):
        src = given.at[0, self.member] if returning else given.at[self.member]
        return pltpu.make_async_copy(src, landed.at[0, self.member], self.local)

    def start(self, given, landed, returning):
        for hop, k in self.pairs:
            self.moved(given, landed, returning, hop, k, False).start()
        self.own(given, landed, returning).start()

    def wait_group(self, given, landed, hop):
        for at, k in self.pairs:
            if at == hop:
                self.moved(given, landed, False, hop, k, True).wait_recv()
        if hop == 0:
            self.own(given, landed, False).wait()

    def wait_sent(self, given, landed):
        for hop, k in self.pairs:
            self.moved(given, landed, False, hop, k, False).wait_send()

    def wait(self, given, landed, returning):
        for hop, k in self.pairs:
            self.moved(given, landed, returning, hop, k, True).wait_recv()
        self.own(given, landed, returning).wait()
        for hop, k in self.pairs:
            self.moved(given, landed, returning, hop, k, False).wait_send()


def route_semaphores(planes, members):
    shape = (planes // 2, members)
    return [
        pltpu.SemaphoreType.DMA(shape),
        pltpu.SemaphoreType.DMA(shape),
        pltpu.SemaphoreType.DMA,
    ]


def two_part(left, right, dims):
    high = left.astype(jnp.bfloat16)
    rest = (left - high.astype(jnp.float32)).astype(jnp.bfloat16)
    numbers = (dims, ((), ()))
    wide = jnp.float32
    return lax.dot_general(high, right, numbers, preferred_element_type=wide) + lax.dot_general(
        rest, right, numbers, preferred_element_type=wide
    )


LANE_UNIT = 256


def lane_unit(j):
    return pl.ds(pl.multiple_of(j * LANE_UNIT, LANE_UNIT), LANE_UNIT)


def normalized(values, gain):
    return values * lax.rsqrt(jnp.mean(values * values, axis=-1, keepdims=True) + EPSILON) * gain


def chain_device(at, members):
    return {"seq": at // members, "exp": lax.rem(at, members)}


def forward_kernel(
    planes,
    members,
    capacity,
    layer_ref,
    out_grad_ref,
    target_ref,
    vectors_ref,
    in_proj_ref,
    conv_weight_ref,
    state_proj_ref,
    delta_proj_ref,
    decay_log_ref,
    own_log_ref,
    out_proj_ref,
    up_ref,
    down_ref,
    normed_ref,
    extended_ref,
    gate_ref,
    conv_pre_ref,
    conv_ref,
    delta_pre_ref,
    delta_ref,
    delta_low_ref,
    in_cols_ref,
    out_cols_ref,
    in_diag_ref,
    delta_sum_ref,
    carried_ref,
    mixer_pre_ref,
    mixed_ref,
    resid_ref,
    row_slots_ref,
    grad_rows_ref,
    near_up_ref,
    near_half_ref,
    rim_in_ref,
    grad_slots_ref,
    drive_ref,
    stack_ref,
    low_sum_ref,
    wide_sum_ref,
    out_diag_ref,
    out_rest_ref,
    local_end_ref,
    rim_out_ref,
    rim_sent_ref,
    rim_landed_ref,
    up_sent_ref,
    up_landed_ref,
    down_sent_ref,
    down_landed_ref,
    *rest,
):
    exchange_refs, grad_semaphores = rest[:12], rest[12:15]
    wide, half = jnp.float32, jnp.bfloat16
    tokens, width = layer_ref.shape
    own_tokens = slice(0, tokens)
    inner_width = conv_ref.shape[1]
    sequences = extended_ref.shape[0]
    piece = tokens // sequences
    states, taps = decay_log_ref.shape[0], conv_weight_ref.shape[0]
    low_rank = delta_low_ref.shape[1]
    experts = row_slots_ref.shape[0]
    conv_bias_ref, delta_bias_ref, skip_ref = (vectors_ref.at[i : i + 1] for i in range(3))
    mixer_gain_ref, expert_norm_ref = vectors_ref.at[3:4, :width], vectors_ref.at[3:4, width:]
    devices = planes * members
    place = lax.axis_index("seq") * members + lax.axis_index("exp")
    before, after = lax.rem(place + devices - 1, devices), lax.rem(place + 1, devices)
    grad_routes = Routes(planes, members, *grad_semaphores)
    barrier = pltpu.get_barrier_semaphore()
    for peer in (before, after):
        device = chain_device(peer, members)
        pl.semaphore_signal(barrier, inc=1, device_id=device, device_id_type=MESH)
    greeted = 2 + grad_routes.signal_peers(barrier)
    for axis, size in (("seq", planes), ("exp", members)):
        mine = lax.axis_index(axis)
        for k in range(1, size):
            other = {axis: lax.rem(mine + k, size)}
            pl.semaphore_signal(barrier, inc=1, device_id=other, device_id_type=MESH)
        greeted += size - 1
    for q in range(sequences):
        rim_out_ref[q] = layer_ref[(q + 1) * piece - 8 : (q + 1) * piece]
    pl.semaphore_wait(barrier, greeted)
    rim_copy = pltpu.make_async_remote_copy(
        src_ref=rim_out_ref,
        dst_ref=rim_in_ref,
        send_sem=rim_sent_ref,
        recv_sem=rim_landed_ref,
        device_id=chain_device(after, members),
        device_id_type=MESH,
    )
    rim_copy.start()
    up_swap = swapped(up_ref, near_up_ref, up_sent_ref, up_landed_ref)
    up_swap.start()
    cut = down_ref.shape[1] // 2
    down_swap = swapped(down_ref.at[:, pl.ds(0, cut)], near_half_ref, down_sent_ref, down_landed_ref)

    count = inner_width // LANE_UNIT
    normed_ref[own_tokens, :] = normalized(layer_ref[...].astype(wide), mixer_gain_ref[...]).astype(half)

    def project(j, carry):
        at = lane_unit(j)
        product = half_dot(normed_ref[own_tokens, :], in_proj_ref[:, at])
        for q in range(sequences):
            extended_ref[q, 8:, at] = product[q * piece : (q + 1) * piece]
        gate_at = pl.ds(pl.multiple_of(inner_width + j * LANE_UNIT, LANE_UNIT), LANE_UNIT)
        gate_ref[:, at] = half_dot(normed_ref[own_tokens, :], in_proj_ref[:, gate_at])
        return carry

    lax.fori_loop(0, count, project, 0)
    rim_copy.wait()
    keep = jnp.where(place > 0, 1.0, 0.0)
    rims = [normalized(rim_in_ref[q].astype(wide), mixer_gain_ref[...]) for q in range(sequences)]
    rim_normed = jnp.concatenate(rims, axis=0).astype(half)
    normed_ref[tokens:, :] = rim_normed
    low_sum_ref[...] = jnp.zeros(low_sum_ref.shape, wide)
    wide_sum_ref[...] = jnp.zeros(wide_sum_ref.shape, wide)

    def convolve(j, carry):
        at = lane_unit(j)
        rim = half_dot(rim_normed, in_proj_ref[:, at]) * keep
        for q in range(sequences):
            extended_ref[q, :8, at] = rim[q * 8 : (q + 1) * 8]
            start = 8 - (taps - 1)
            pre = conv_bias_ref[:, at] + conv_weight_ref[:1, at] * extended_ref[q, start : start + piece, at]
            for tap in range(1, taps):
                moved = extended_ref[q, start + tap : start + tap + piece, at]
                pre = pre + conv_weight_ref[tap : tap + 1, at] * moved
            conv_pre_ref[q * piece : (q + 1) * piece, at] = pre
            conv_ref[q * piece : (q + 1) * piece, at] = pre * jax.nn.sigmoid(pre)
        act = conv_ref[:, at]
        high = act.astype(half)
        low = (act - high.astype(wide)).astype(half)
        weight = state_proj_ref[:, at]
        low_sum_ref[...] += cols_dot(high, weight) + cols_dot(low, weight)
        tail = weight[low_rank:]
        wide_sum_ref[...] += cols_dot(tail, high) + cols_dot(tail, low)
        return carry

    lax.fori_loop(0, count, convolve, 0)
    delta_low_ref[...] = low_sum_ref[:, :low_rank]
    for i in range(tokens // BLK):
        block = wide_sum_ref[:, i * BLK : (i + 1) * BLK]
        in_cols_ref[i] = block[:states]
        out_cols_ref[i] = block[states:]
    shape = (tokens, BLK * states)
    column = lax.broadcasted_iota(jnp.int32, shape, 1)
    row = lax.rem(lax.broadcasted_iota(jnp.int32, shape, 0), BLK)
    own = column // states == row
    tile = jnp.where(
        lax.rem(lax.broadcasted_iota(jnp.int32, (states, BLK * states), 1), states)
        == lax.broadcasted_iota(jnp.int32, (states, BLK * states), 0),
        1.0,
        0.0,
    ).astype(half)

    def spread_out(values):
        return jnp.where(own, half_dot(values, tile), 0.0).astype(half)

    outward = low_sum_ref[:, low_rank + states :]
    out_high = outward.astype(half)
    in_diag_ref[...] = spread_out(low_sum_ref[:, low_rank : low_rank + states].astype(half))
    out_diag_ref[...] = spread_out(out_high)
    out_rest_ref[...] = spread_out((outward - out_high.astype(wide)).astype(half))

    def time_steps(j, carry):
        at = lane_unit(j)
        pre = two_part(delta_low_ref[...], delta_proj_ref[:, at], ((1,), (0,))) + delta_bias_ref[:, at]
        delta = jnp.maximum(pre, 0.0) + jnp.log1p(jnp.exp(-jnp.abs(pre)))
        delta_pre_ref[:, at] = pre
        delta_ref[:, at] = delta
        for q in range(sequences):
            part = delta[q * piece : (q + 1) * piece]
            delta_sum_ref[q : q + 1, at] = jnp.sum(part, axis=0, keepdims=True)
        return carry

    lax.fori_loop(0, count, time_steps, 0)
    groups = inner_width // GROUP
    blocks = piece // BLK

    def views(i):
        q, j = i // groups, lax.rem(i, groups)
        rows = pl.ds(pl.multiple_of(q * piece, piece), piece)
        lanes = pl.ds(pl.multiple_of(j * GROUP, GROUP), GROUP)
        cols = pl.ds(q * blocks, blocks)
        return q, rows, lanes, cols

    def first(i, carry):
        q, rows, lanes, cols = views(i)
        first_pass_kernel(
            delta_ref.at[rows, lanes],
            conv_ref.at[rows, lanes],
            in_cols_ref.at[cols],
            decay_log_ref.at[:, lanes],
            local_end_ref.at[pl.ds(q, 1), :, lanes],
            drive_ref,
        )
        return carry

    lax.fori_loop(0, sequences * groups, first, 0)
    exchange_body(
        False, planes, members, local_end_ref, delta_sum_ref, own_log_ref, carried_ref, *exchange_refs
    )
    up_swap.wait()
    slot = lax.broadcasted_iota(jnp.int32, (experts * capacity, tokens), 0)
    picks = jnp.where(slot == target_ref[...], 1.0, 0.0).astype(half)

    def fill(slots, values):
        product = half_dot(picks, values).astype(half)
        for e in range(experts):
            slots[e] = product[e * capacity : (e + 1) * capacity]

    fill(grad_slots_ref, out_grad_ref[...])
    grad_routes.start(grad_slots_ref, grad_rows_ref, False)
    down_swap.start()

    def second(i, carry):
        q, rows, lanes, cols = views(i)
        second_pass_kernel(
            delta_ref.at[rows, lanes],
            conv_ref.at[rows, lanes],
            in_cols_ref.at[cols],
            decay_log_ref.at[:, lanes],
            carried_ref.at[pl.ds(q, 1), :, lanes],
            out_diag_ref.at[rows],
            out_rest_ref.at[rows],
            mixer_pre_ref.at[rows, lanes],
            drive_ref,
            stack_ref,
        )
        return carry

    lax.fori_loop(0, sequences * groups, second, 0)

    def mix(j, carry):
        at = lane_unit(j)
        pre = mixer_pre_ref[:, at] + skip_ref[:, at] * conv_ref[:, at]
        gate = gate_ref[:, at]
        mixer_pre_ref[:, at] = pre
        mixed_ref[:, at] = (pre * (gate * jax.nn.sigmoid(gate))).astype(half)
        return carry

    lax.fori_loop(0, count, mix, 0)
    resid_ref[...] = layer_ref[...].astype(wide) + half_dot(mixed_ref[...], out_proj_ref[...])
    fill(row_slots_ref, normalized(resid_ref[...], expert_norm_ref[...]).astype(half))
    grad_routes.wait(grad_slots_ref, grad_rows_ref, False)
    down_swap.wait()


def forward(operands, capacity, states, sequences, low_rank, experts):
    planes, members = lax.axis_size("seq"), lax.axis_size("exp")
    tokens, width = operands[0].shape
    inner_width = operands[3].shape[1]
    up, down = operands[11:13]
    half, wide = jnp.bfloat16, jnp.float32
    piece = tokens // sequences
    token_wide = jax.ShapeDtypeStruct((tokens, inner_width), wide)
    cols = jax.ShapeDtypeStruct((tokens // BLK, states, BLK), wide)
    diag = (tokens, BLK * states)
    routed = jax.ShapeDtypeStruct((planes // 2, members, capacity, width), half)
    state = (sequences, states, inner_width)
    vmem, anywhere = (pl.BlockSpec(memory_space=space) for space in (pltpu.VMEM, pl.ANY))
    scratch = [
        pltpu.VMEM((experts, capacity, width), half),
        pltpu.VMEM((piece, GROUP), wide),
        pltpu.VMEM((BLK * states, GROUP), half),
        pltpu.VMEM((tokens, low_rank + 2 * states), wide),
        pltpu.VMEM((2 * states, tokens), wide),
        pltpu.VMEM(diag, half),
        pltpu.VMEM(diag, half),
        pltpu.VMEM(state, wide),
        pltpu.VMEM((sequences, 8, width), half),
    ]
    scratch += [pltpu.SemaphoreType.DMA] * 6
    scratch += exchange_scratch(planes, members, sequences * states // members, inner_width)
    scratch += route_semaphores(planes, members)
    return pl.pallas_call(
        functools.partial(forward_kernel, planes, members, capacity),
        name="forward_to_experts",
        in_specs=[vmem] * 11 + [anywhere] * 2,
        out_specs=[vmem] * 17 + [anywhere] * 3 + [vmem],
        out_shape=[
            jax.ShapeDtypeStruct((tokens + 8 * sequences, width), half),
            jax.ShapeDtypeStruct((sequences, piece + 8, inner_width), wide),
            token_wide,
            token_wide,
            token_wide,
            token_wide,
            token_wide,
            jax.ShapeDtypeStruct((tokens, low_rank), wide),
            cols,
            cols,
            jax.ShapeDtypeStruct(diag, half),
            jax.ShapeDtypeStruct((sequences, inner_width), wide),
            jax.ShapeDtypeStruct(state, wide),
            token_wide,
            jax.ShapeDtypeStruct((tokens, inner_width), half),
            jax.ShapeDtypeStruct((tokens, width), wide),
            jax.ShapeDtypeStruct((experts, capacity, width), half),
            routed,
            jax.ShapeDtypeStruct(up.shape, half),
            jax.ShapeDtypeStruct((1, down.shape[1] // 2, width), half),
            jax.ShapeDtypeStruct((sequences, 8, width), half),
        ],
        scratch_shapes=scratch,
        compiler_params=pltpu.CompilerParams(
            collective_id=1, has_side_effects=True, vmem_limit_bytes=60 * 1024 * 1024
        ),
        cost_estimate=pl.CostEstimate(flops=10**8, transcendentals=0, bytes_accessed=2 * 10**8),
    )(*operands)


def expert_kernel(
    planes,
    members,
    row_slots_ref,
    grad_rows_ref,
    up_ref,
    down_ref,
    near_up_ref,
    near_half_ref,
    router_ref,
    chosen_ref,
    outs_ref,
    back_ref,
    grad_up_ref,
    grad_down_ref,
    far_up_ref,
    far_down_ref,
    grad_router_ref,
    landed_ref,
    rows_ref,
    grads_ref,
    sent_ref,
    near_down_ref,
    out_sum_ref,
    row_sum_ref,
    hidden_own_ref,
    hidden_near_ref,
    pre_own_ref,
    pre_near_ref,
    shares_ref,
    far_up_sum_ref,
    far_down_sum_ref,
    returns_ref,
    down_sent_ref,
    down_landed_ref,
    back_sent_ref,
    back_landed_ref,
    *rest,
):
    routes = Routes(planes, members, *rest)
    wide, half = jnp.float32, jnp.bfloat16
    plane, member, hops = routes.plane, routes.member, routes.hops
    capacity, width = row_slots_ref.shape[1:]
    batch = members // 2
    chunk = batch * capacity
    group = members * capacity
    units = up_ref.shape[2]
    cut = units // 2
    barrier = pltpu.get_barrier_semaphore()
    pl.semaphore_signal(barrier, inc=1, device_id=neighbour_plane(), device_id_type=MESH)
    pl.semaphore_wait(barrier, routes.signal_peers(barrier) + 1)
    routes.start(row_slots_ref, landed_ref, False)
    down_swap = swapped(
        down_ref.at[0, pl.ds(cut, cut)], near_down_ref.at[pl.ds(cut, cut)], down_sent_ref, down_landed_ref
    )
    down_swap.start()
    near_down_ref[:cut] = near_half_ref[0]
    grad_router_ref[...] = jnp.zeros(grad_router_ref.shape, wide)
    for hop in range(hops):
        for e in range(members):
            grads_ref[hop * group + e * capacity : hop * group + (e + 1) * capacity] = grad_rows_ref[
                hop, e
            ]

    def gather(hop):
        routes.wait_group(row_slots_ref, landed_ref, hop)
        for e in range(members):
            rows_ref[hop * group + e * capacity : hop * group + (e + 1) * capacity] = landed_ref[hop, e]

    def through(at, up, down, hidden, back, where):
        pre = half_dot(rows_ref[at, :], up)
        phi = 0.5 * (1.0 + lax.erf(pre * 0.7071067811865476))
        slope = phi + pre * (jnp.exp(-0.5 * pre * pre) * 0.3989422804014327)
        active = (pre * phi).astype(half)
        hidden[at, where] = active
        arrived = (slope * cols_dot(sent_ref[at, :], down)).astype(half)
        back[at, where] = arrived
        return half_dot(active, down), cols_dot(arrived, up)

    def place(hop, c):
        return pl.ds(pl.multiple_of(hop * group + c * chunk, chunk), chunk)

    def own_part(hop, c):
        at = place(hop, c)
        logits = cols_dot(rows_ref[at, :].astype(wide), router_ref[...], lax.Precision.HIGHEST)
        raised = jnp.exp(logits - jnp.max(logits, axis=-1, keepdims=True))
        shares = raised / jnp.sum(raised, axis=-1, keepdims=True)
        gate = jnp.sum(shares * chosen_ref[...], axis=-1, keepdims=True)
        shares_ref[at, :] = shares
        sent_ref[at, :] = (gate * grads_ref[at, :].astype(wide)).astype(half)
        every = slice(0, units)
        out, row = through(at, up_ref[0], down_ref[0], hidden_own_ref, pre_own_ref, every)
        early = slice(0, cut)
        near_out, near_row = through(
            at, near_up_ref[0, :, :cut], near_down_ref[:cut], hidden_near_ref, pre_near_ref, early
        )
        out_sum_ref[at, :] = out + near_out
        row_sum_ref[at, :] = row + near_row

    def late_part(hop, c):
        at = place(hop, c)
        near_out, near_row = through(
            at,
            near_up_ref[0, :, cut:],
            near_down_ref[cut:],
            hidden_near_ref,
            pre_near_ref,
            slice(cut, units),
        )
        out = out_sum_ref[at, :] + near_out
        shares, chosen = shares_ref[at, :], chosen_ref[...]
        gate = jnp.sum(shares * chosen, axis=-1, keepdims=True)
        grad_gate = jnp.sum(grads_ref[at, :].astype(wide) * out, axis=-1, keepdims=True)
        grad_logits = grad_gate * gate * (chosen - shares)
        outs = (gate * out).astype(half)
        row = row_sum_ref[at, :] + near_row
        row = row + jnp.dot(
            grad_logits,
            router_ref[...],
            precision=lax.Precision.HIGHEST,
            preferred_element_type=wide,
        )
        row = row.astype(half)
        grad_router_ref[...] += rows_dot(
            grad_logits, rows_ref[at, :].astype(wide), lax.Precision.HIGHEST
        )
        for k in range(batch):
            part = slice(k * capacity, (k + 1) * capacity)
            outs_ref[hop, c * batch + k] = outs[part]
            returns_ref[hop, c * batch + k] = row[part]

    def returned(hop, e, arriving):
        slot = hop if arriving else (-hop) % hops
        sender = e if arriving else member
        return pltpu.make_async_remote_copy(
            src_ref=returns_ref.at[hop, e],
            dst_ref=back_ref.at[slot, sender],
            send_sem=back_sent_ref.at[hop, e],
            recv_sem=back_landed_ref.at[slot, sender],
            device_id={"seq": lax.rem(plane + 2 * hop, planes), "exp": e},
            device_id_type=MESH,
        )

    def give_back(hop, c):
        for k in range(batch):
            e = c * batch + k
            if hop:
                returned(hop, e, False).start()
            else:

                @pl.when(e != member)
                def _():
                    returned(0, e, False).start()

    def loop(body):
        def run(c, carry):
            body(c)
            return carry

        lax.fori_loop(0, 2, run, 0)

    def weight_grads(hop):
        at = slice(hop * group, (hop + 1) * group)
        rows, sent = rows_ref[at, :], sent_ref[at, :]
        products = [
            (grad_up_ref.at[0], rows, pre_own_ref[at, :]),
            (grad_down_ref.at[0], hidden_own_ref[at, :], sent),
            (far_up_sum_ref, rows, pre_near_ref[at, :]),
            (far_down_sum_ref, hidden_near_ref[at, :], sent),
        ]
        for total, left, right in products:
            if hop:
                total[...] += rows_dot(left, right)
            else:
                total[...] = rows_dot(left, right)

    gather(0)
    loop(functools.partial(own_part, 0))
    down_swap.wait()

    def near_end(c):
        late_part(0, c)
        give_back(0, c)

    loop(near_end)
    weight_grads(0)
    for hop in range(1, hops):
        gather(hop)

        def far_end(c):
            own_part(hop, c)
            late_part(hop, c)
            give_back(hop, c)

        loop(far_end)
        weight_grads(hop)
    far_up_ref[0] = far_up_sum_ref[...].astype(half)
    far_down_ref[0] = far_down_sum_ref[...].astype(half)
    back_ref[0, member] = returns_ref[0, member]
    for hop in range(hops):
        for k in range(members):
            if hop or k:
                e = lax.rem(member + k, members)
                returned(hop, e, True).wait_recv()
                returned(hop, e, False).wait_send()
    routes.wait_sent(row_slots_ref, landed_ref)


def expert_apply(row_slots, grad_rows, weights, router, chosen):
    planes, members = lax.axis_size("seq"), lax.axis_size("exp")
    experts, capacity, width = row_slots.shape
    up, down, near_up, near_half = weights
    units = up.shape[2]
    hops = planes // 2
    count = hops * members * capacity
    half, wide = jnp.bfloat16, jnp.float32
    vmem = pl.BlockSpec(memory_space=pltpu.VMEM)
    slotted = (hops, members, capacity, width)
    every = (hops, members)
    return pl.pallas_call(
        functools.partial(expert_kernel, planes, members),
        name="expert_apply",
        in_specs=[vmem] * 8,
        out_specs=[vmem] * 7,
        out_shape=[
            jax.ShapeDtypeStruct(slotted, half),
            jax.ShapeDtypeStruct(slotted, half),
            jax.ShapeDtypeStruct(up.shape, wide),
            jax.ShapeDtypeStruct(down.shape, wide),
            jax.ShapeDtypeStruct(up.shape, half),
            jax.ShapeDtypeStruct(down.shape, half),
            jax.ShapeDtypeStruct(router.shape, wide),
        ],
        scratch_shapes=[
            pltpu.VMEM(slotted, half),
            pltpu.VMEM((count, width), half),
            pltpu.VMEM((count, width), half),
            pltpu.VMEM((count, width), half),
            pltpu.VMEM(down.shape[1:], half),
            pltpu.VMEM((count, width), wide),
            pltpu.VMEM((count, width), wide),
            pltpu.VMEM((count, units), half),
            pltpu.VMEM((count, units), half),
            pltpu.VMEM((count, units), half),
            pltpu.VMEM((count, units), half),
            pltpu.VMEM((count, experts), wide),
            pltpu.VMEM(up.shape[1:], wide),
            pltpu.VMEM(down.shape[1:], wide),
            pltpu.VMEM(slotted, half),
            pltpu.SemaphoreType.DMA,
            pltpu.SemaphoreType.DMA,
            pltpu.SemaphoreType.DMA(every),
            pltpu.SemaphoreType.DMA(every),
        ]
        + route_semaphores(planes, members),
        compiler_params=pltpu.CompilerParams(
            collective_id=4, has_side_effects=True, vmem_limit_bytes=60 * 1024 * 1024
        ),
        cost_estimate=pl.CostEstimate(
            flops=24 * count * width * units,
            transcendentals=4 * count * units,
            bytes_accessed=3 * 10**7,
        ),
    )(row_slots, grad_rows, *weights, router, chosen)


def gradient_kernel(
    planes,
    side,
    delta_ref,
    conv_ref,
    grad_scan_ref,
    in_cols_ref,
    out_cols_ref,
    in_diag_ref,
    decay_log_ref,
    carried_ref,
    carried_back_ref,
    delta_pre_ref,
    delta_low_ref,
    conv_pre_ref,
    extended_ref,
    normed_ref,
    normed_gate_ref,
    layer_ref,
    rim_layer_ref,
    grad_resid_ref,
    delta_proj_ref,
    state_proj_ref,
    in_proj_ref,
    conv_weight_ref,
    vectors_ref,
    skip_grad_ref,
    norm_grad_ref,
    router_grad_ref,
    early_out_ref,
    early_gate_ref,
    returned_ref,
    far_up_ref,
    far_down_ref,
    in_grad_ref,
    total_out_ref,
    total_gate_ref,
    total_inner_ref,
    total_small_ref,
    landed_ref,
    near_up_ref,
    near_down_ref,
    grad_delta,
    grad_conv,
    grad_in,
    grad_out,
    grad_log,
    drive,
    kept,
    stack,
    slope_stack,
    low_grads,
    padded,
    slopes,
    small,
    rim_out,
    rim_in,
    rim_sent,
    rim_landed,
    in_part,
    part_loaded,
    given_inner,
    given_small,
    *rest,
):
    early_buffers, tail_buffers, small_buffers = rest[:12], rest[12:18], rest[18:24]
    swap_sent, swap_landed, rest = rest[24], rest[25], rest[26:]
    sums = Sums(planes, side, rest[:8], rest[8:16])
    routes = Routes(planes, 2 * side * side, *rest[16:19])
    tokens, inner_width = conv_ref.shape
    width = layer_ref.shape[1]
    low_rank = delta_low_ref.shape[1]
    states, taps = decay_log_ref.shape[0], conv_weight_ref.shape[0]
    sequences = extended_ref.shape[0]
    piece = tokens // sequences
    chips = side * side
    wide, half = jnp.float32, jnp.bfloat16
    skip_ref, mixer_gain_ref = vectors_ref.at[2:3], vectors_ref.at[3:4, :width]
    devices = 2 * chips * planes
    place = sums.plane * (2 * chips) + sums.member
    before, after = lax.rem(place + devices - 1, devices), lax.rem(place + 1, devices)
    barrier = pltpu.get_barrier_semaphore()
    for peer in (before, after):
        device = chain_device(peer, 2 * chips)
        pl.semaphore_signal(barrier, inc=1, device_id=device, device_id_type=MESH)
    pl.semaphore_signal(barrier, inc=1, device_id=neighbour_plane(), device_id_type=MESH)
    greeted = 3 + sums.signal_peers(barrier) + routes.signal_peers(barrier)
    pl.semaphore_wait(barrier, greeted)

    in_load = pltpu.make_async_copy(in_proj_ref.at[:, pl.ds(0, inner_width)], in_part, part_loaded)
    in_load.start()
    pair = range(2)
    given = (early_out_ref, early_gate_ref)
    results = (total_out_ref, total_gate_ref)
    stages = [tuple(early_buffers[2 * stage + i] for stage in range(6)) for i in pair]
    blocks = [result.at[sums.core, sums.first, sums.second] for result in results]
    swaps = [
        swapped(src, dst, swap_sent.at[i], swap_landed.at[i])
        for i, (src, dst) in enumerate([(far_up_ref, near_up_ref), (far_down_ref, near_down_ref)])
    ]
    for i in pair:
        sums.pair_half(i, given[i], stages[i][0]).start()
    routes.start(returned_ref, landed_ref, True)
    swaps[0].start()
    groups = inner_width // GROUP
    count = sequences * groups
    cols_each = piece // BLK

    def scan_group(g, carry):
        q, j = g // groups, lax.rem(g, groups)
        rows = pl.ds(pl.multiple_of(q * piece, piece), piece)
        lanes = pl.ds(pl.multiple_of(j * GROUP, GROUP), GROUP)
        cols = pl.ds(q * cols_each, cols_each)

        def middle():
            @pl.when(g == 0)
            def _():
                for i in pair:
                    sums.after_pair(i, given[i], *stages[i][:2])

            @pl.when(g == count // 2)
            def _():
                for i in pair:
                    sums.after_first(i, *stages[i][:4])

            @pl.when(g == count - 2)
            def _():
                for i in pair:
                    sums.after_second(i, *stages[i][2:6])

            @pl.when(g == count - 1)
            def _():
                for i in pair:
                    sums.after_planes(i, *stages[i][4:6], blocks[i])
                swaps[1].start()

        one = pl.ds(q, 1)
        backward_body(
            middle,
            j == 0,
            delta_ref.at[rows, lanes],
            conv_ref.at[rows, lanes],
            grad_scan_ref.at[rows, lanes],
            in_cols_ref.at[cols],
            out_cols_ref.at[cols],
            in_diag_ref.at[rows],
            decay_log_ref.at[:, lanes],
            carried_ref.at[one, :, lanes],
            carried_back_ref.at[one, :, lanes],
            grad_delta.at[rows, lanes],
            grad_conv.at[rows, lanes],
            grad_in.at[rows],
            grad_out.at[rows],
            grad_log.at[one, :, lanes],
            drive,
            kept,
            stack,
            slope_stack,
        )
        return carry

    lax.fori_loop(0, count, scan_group, 0)
    unit = LANE_UNIT
    low_grads[...] = jnp.zeros(low_grads.shape, wide)
    small[...] = jnp.zeros(small.shape, wide)
    at_delta = low_rank + 2 * states
    at_log = at_delta + low_rank
    at_conv = at_log + states
    at_end = at_conv + taps + 2

    def first(j, carry):
        at = lane_unit(j)
        slope = grad_delta[:, at] * jax.nn.sigmoid(delta_pre_ref[:, at])
        small[at_conv + taps + 1 : at_conv + taps + 2, at] = jnp.sum(slope, axis=0, keepdims=True)
        small[at_delta:at_log, at] = rows_dot(delta_low_ref[...], slope, lax.Precision.HIGHEST)
        low_grads[...] += two_part(slope, delta_proj_ref[:, at], ((1,), (1,)))
        return carry

    lax.fori_loop(0, inner_width // unit, first, 0)
    for i in pair:
        sums.planes_gathered(i, blocks[i])
        sums.gather_second_start(i, results[i])
    column = lax.broadcasted_iota(jnp.int32, grad_in.shape, 1) // states
    row = lax.rem(lax.broadcasted_iota(jnp.int32, grad_in.shape, 0), BLK)
    fold = jnp.where(
        lax.rem(lax.broadcasted_iota(jnp.int32, (grad_in.shape[1], states), 0), states)
        == lax.broadcasted_iota(jnp.int32, (grad_in.shape[1], states), 1),
        1.0,
        0.0,
    ).astype(half)

    def folded(ref):
        return two_part(jnp.where(column == row, ref[...], 0.0), fold, ((1,), (0,)))

    coefs = jnp.concatenate([low_grads[...], folded(grad_in), folded(grad_out)], axis=1)
    keep = jnp.where(place > 0, 1.0, 0.0)
    rim_out[...] = jnp.zeros(rim_out.shape, half)

    def dense(at):
        small[:at_delta, at] = rows_dot(coefs, conv_ref[:, at], lax.Precision.HIGHEST)
        through = two_part(coefs, state_proj_ref[:, at], ((1,), (0,)))
        through = through + grad_scan_ref[:, at] * skip_ref[:, at] + grad_conv[:, at]
        pre = conv_pre_ref[:, at]
        sigma = jax.nn.sigmoid(pre)
        through = through * (sigma * (1.0 + pre * (1.0 - sigma)))
        small[at_conv + taps : at_conv + taps + 1, at] = jnp.sum(through, axis=0, keepdims=True)
        for q in range(sequences):
            padded[q, :8] = jnp.zeros((8, unit), wide)
            padded[q, 8 + piece :] = jnp.zeros((8, unit), wide)
            padded[q, 8 : 8 + piece] = through[q * piece : (q + 1) * piece]
            result = jnp.zeros((piece, unit), wide)
            rim = jnp.zeros((8, unit), wide)
            for tap in range(taps):
                weight = conv_weight_ref[tap : tap + 1, at]
                shift = taps - 1 - tap
                result = result + weight * padded[q, 8 + shift : 8 + shift + piece]
                rim = rim + weight * padded[q, 8 - tap : 16 - tap]
            slopes[q * piece : (q + 1) * piece, at] = result.astype(half)
            rim_out[q, 8 - (taps - 1) :, at] = (rim[: taps - 1] * keep).astype(half)
            slopes[tokens + q * 8 : tokens + (q + 1) * 8, at] = rim_out[q, :, at]
        for tap in range(taps):
            start = 8 - (taps - 1) + tap
            product = jnp.zeros((1, unit), wide)
            for q in range(sequences):
                product = product + jnp.sum(
                    padded[q, 8 : 8 + piece] * extended_ref[q, start : start + piece, at],
                    axis=0,
                    keepdims=True,
                )
            small[at_conv + tap : at_conv + tap + 1, at] = product

    slabs = given_inner.shape[0]
    tall = width // chips
    size = tall // planes

    def tail_of(s):
        return [buffer.at[s] for buffer in tail_buffers]

    def after_tail_pair(s):
        sums.after_pair(2 + s, given_inner.at[s], *tail_of(s)[:2])

    def slab(s, carry):
        for c in range(2):
            at = lane_unit(c * slabs + s)
            dense(at)
            for m in range(chips):
                product = rows_dot(
                    normed_ref[:, m * tall : (m + 1) * tall], slopes[:, at]
                ).astype(half)
                for z in range(planes):
                    part = product[z * size : (z + 1) * size]
                    given_inner[s, c, m // side, m % side, z] = part
        sums.pair_half(2 + s, given_inner.at[s], tail_buffers[0].at[s]).start()

        @pl.when(s > 0)
        def _():
            after_tail_pair(s - 1)

        return carry

    lax.fori_loop(0, slabs, slab, 0)
    after_tail_pair(slabs - 1)
    rim_copy = pltpu.make_async_remote_copy(
        src_ref=rim_out,
        dst_ref=rim_in,
        send_sem=rim_sent,
        recv_sem=rim_landed,
        device_id=chain_device(before, 2 * chips),
        device_id_type=MESH,
    )
    rim_copy.start()
    sums.gather_across(0, results[0])
    in_load.wait()
    projected = cols_dot(slopes[...], in_part[...])
    normed_grad = normed_gate_ref[...] + projected[:tokens]

    def normal_of(values):
        scaling = lax.rsqrt(jnp.mean(values * values, axis=-1, keepdims=True) + EPSILON)
        return values * scaling, scaling

    normal, scaling = normal_of(layer_ref[...].astype(wide))
    gain_grad = jnp.sum(normed_grad * normal, axis=0, keepdims=True)
    for q in range(sequences):
        rim_normal, _ = normal_of(rim_layer_ref[q].astype(wide))
        rim_grad = projected[tokens + q * 8 : tokens + (q + 1) * 8]
        gain_grad = gain_grad + jnp.sum(rim_grad * rim_normal, axis=0, keepdims=True)
    log_total = grad_log[0]
    for q in range(1, sequences):
        log_total = log_total + grad_log[q]
    small[at_log:at_conv] = log_total
    small[at_end : at_end + 1] = skip_grad_ref[...]
    small[at_end + 1 : at_end + 2, :width] = gain_grad
    small[at_end + 1 : at_end + 2, width:] = norm_grad_ref[...]
    for k in range(router_grad_ref.shape[0]):
        line = at_end + 2 + k // 2
        small[line : line + 1, (k % 2) * width : (k % 2 + 1) * width] = router_grad_ref[k : k + 1]
    low = given_small.shape[4]
    for c in range(2):
        for m in range(chips):
            for z in range(planes):
                line = (m * planes + z) * low
                given_small[c, m // side, m % side, z] = small[
                    line : line + low, c * width : (c + 1) * width
                ].astype(half)
    last = 2 + slabs
    every = range(slabs)
    sums.pair_half(last, given_small, small_buffers[0]).start()
    for s in every:
        sums.after_first(2 + s, *tail_of(s)[:4])
    sums.after_pair(last, given_small, *small_buffers[:2])
    sums.gather_across(1, results[1])
    weighted = normed_grad * mixer_gain_ref[...]
    in_grad_ref[...] = grad_resid_ref[...] + scaling * (
        weighted - normal * jnp.mean(weighted * normal, axis=-1, keepdims=True)
    )
    for s in every:
        sums.after_second(2 + s, *tail_of(s)[2:6])
    sums.after_first(last, *small_buffers[:4])
    tails = [total_inner_ref.at[s] for s in every] + [total_small_ref]
    tail_blocks = [total.at[sums.core, sums.first, sums.second] for total in tails]
    for s in every:
        sums.after_planes(2 + s, *tail_of(s)[4:6], tail_blocks[s])
    sums.after_second(last, *small_buffers[2:6])
    sums.gather_pass(0, results[0])
    for s in every:
        sums.planes_gathered(2 + s, tail_blocks[s])
        sums.gather_second_start(2 + s, tails[s])
    sums.after_planes(last, *small_buffers[4:6], tail_blocks[slabs])
    for s in every:
        sums.gather_across(2 + s, tails[s])
    sums.planes_gathered(last, tail_blocks[slabs])
    sums.gather_second_start(last, total_small_ref)
    sums.gather_pass(1, results[1])
    rim_copy.wait()
    keep_last = jnp.where(place < devices - 1, 1.0, 0.0)
    for q in range(sequences):
        rows = slice((q + 1) * piece - 8, (q + 1) * piece)
        added = cols_dot(rim_in[q], in_part[...]) * keep_last
        fixed = (normed_grad[rows] + added) * mixer_gain_ref[...]
        mean = jnp.mean(fixed * normal[rows], axis=-1, keepdims=True)
        in_grad_ref[rows, :] = grad_resid_ref[rows, :] + scaling[rows] * (
            fixed - normal[rows] * mean
        )
    sums.gather_across(last, total_small_ref)
    for s in every:
        sums.gather_pass(2 + s, tails[s])
    sums.gather_pass(last, total_small_ref)
    routes.wait(returned_ref, landed_ref, True)
    for swap in swaps:
        swap.wait()
    ends = [(i, stages[i], blocks[i], results[i]) for i in pair]
    ends += [(2 + s, tail_of(s), tail_blocks[s], tails[s]) for s in every]
    ends += [(last, small_buffers, tail_blocks[slabs], total_small_ref)]
    for i, buffers, block, result in ends:
        sums.scatter_sent(i, *buffers, block)
        sums.gather_end(i, result)


def all_gradients(operands, small_height, side):
    planes = lax.axis_size("seq")
    tokens, inner_width = operands[1].shape
    width = operands[15].shape[1]
    states, low_rank = operands[6].shape[0], operands[10].shape[1]
    sequences = operands[7].shape[0]
    piece = tokens // sequences
    low = -(-small_height // (side * side * planes))
    lead = (2, side, side, planes)
    big = operands[26].shape
    slabs = width // LANE_UNIT
    inner = (slabs,) + lead + (big[4], LANE_UNIT)
    little = lead + (low, width)
    vmem, anywhere = (pl.BlockSpec(memory_space=space) for space in (pltpu.VMEM, pl.ANY))
    half, wide = jnp.bfloat16, jnp.float32
    token_wide = pltpu.VMEM((tokens, inner_width), wide)
    narrow = pltpu.VMEM((tokens, BLK * states), wide)
    steps = pltpu.VMEM((piece, states, GROUP), wide)
    stack = pltpu.VMEM((BLK * states, GROUP), half)
    rim = pltpu.VMEM((sequences, 8, inner_width), half)
    tail_shapes = [value.shape for value in scatter_buffers([inner[5:]], planes, side)]
    moved = [jax.ShapeDtypeStruct(value.shape, half) for value in operands[28:]]
    semaphores = stage_semaphores(3 + slabs, planes, side)
    return pl.pallas_call(
        functools.partial(gradient_kernel, planes, side),
        name="backward_gradients",
        in_specs=[vmem] * 20 + [anywhere] + [vmem] * 7 + [anywhere] * 3,
        out_specs=[vmem] * 5 + [anywhere] * 3,
        out_shape=[jax.ShapeDtypeStruct((tokens, width), wide)]
        + [jax.ShapeDtypeStruct(shape, half) for shape in (big, big, inner, little)]
        + moved,
        scratch_shapes=[
            token_wide,
            token_wide,
            narrow,
            narrow,
            pltpu.VMEM((sequences, states, inner_width), wide),
            pltpu.VMEM((piece, GROUP), wide),
            steps,
            stack,
            stack,
            pltpu.VMEM((tokens, low_rank), wide),
            pltpu.VMEM((sequences, piece + 16, LANE_UNIT), wide),
            pltpu.VMEM((tokens + 8 * sequences, inner_width), half),
            pltpu.VMEM((low * side * side * planes, inner_width), wide),
            rim,
            rim,
            pltpu.SemaphoreType.DMA,
            pltpu.SemaphoreType.DMA,
            pltpu.VMEM((width, inner_width), half),
            pltpu.SemaphoreType.DMA,
            pltpu.VMEM(inner, half),
            pltpu.VMEM(little, half),
        ]
        + scatter_buffers([big[4:], big[4:]], planes, side)
        + [pltpu.VMEM((slabs,) + shape, half) for shape in tail_shapes]
        + scatter_buffers([little[4:]], planes, side)
        + [pltpu.SemaphoreType.DMA((2,)), pltpu.SemaphoreType.DMA((2,))]
        + semaphores
        + semaphores
        + route_semaphores(planes, 2 * side * side),
        compiler_params=pltpu.CompilerParams(
            collective_id=3, has_side_effects=True, vmem_limit_bytes=63 * 1024 * 1024
        ),
        cost_estimate=pl.CostEstimate(flops=10**8, transcendentals=0, bytes_accessed=2 * 10**8),
    )(*operands)


def on_device(
    layer_in,
    mixer_gain,
    in_proj,
    conv_weight,
    conv_bias,
    state_proj,
    delta_proj,
    delta_bias,
    decay_log,
    skip_gain,
    out_proj,
    expert_norm,
    router_weight,
    expert_up,
    expert_down,
    expert_ids,
    capacity_slot,
    out_grad,
):
    sequences, piece_len, width = layer_in.shape
    tokens = sequences * piece_len
    taps, inner_width = conv_weight.shape
    low_rank = delta_proj.shape[0]
    states = decay_log.shape[0]
    experts = router_weight.shape[1]
    senders = lax.axis_size("exp")
    capacity = (5 * tokens + 4 * experts - 1) // (4 * experts)
    planes = lax.axis_size("seq")
    hops = planes // 2
    flat_ids = expert_ids.reshape(1, tokens)
    flat_slot = capacity_slot.reshape(1, tokens)
    target = jnp.where(flat_slot < capacity, flat_ids * capacity + flat_slot, experts * capacity)
    slot_rows = jnp.arange(experts * capacity, dtype=jnp.int32)
    picks = (slot_rows[:, None] == target).astype(jnp.bfloat16)
    state_rows = sequences * states // senders
    first_row = lax.rem(lax.axis_index("exp") * state_rows, states)
    own_log = lax.dynamic_slice(decay_log, (first_row, 0), (state_rows, inner_width))
    norms = jnp.concatenate([mixer_gain, expert_norm])
    vectors = jnp.stack([conv_bias, delta_bias, skip_gain, norms])
    (
        normed_half,
        extended,
        gate_half,
        conv_pre,
        conv_flat,
        delta_pre,
        delta,
        delta_low,
        in_cols,
        out_cols,
        in_diag,
        delta_sum,
        carried,
        mixer_pre,
        mixed,
        resid,
        row_slots,
        grad_rows,
        near_up,
        near_half,
        rim_layer,
    ) = forward(
        [
            layer_in.reshape(tokens, width),
            out_grad.reshape(tokens, width),
            target,
            vectors,
            in_proj,
            conv_weight,
            state_proj.T,
            delta_proj,
            decay_log,
            own_log,
            out_proj,
            expert_up,
            expert_down,
        ],
        capacity,
        states,
        sequences,
        low_rank,
        experts,
    )
    gate_act = jax.nn.silu(gate_half)
    scaling_two = lax.rsqrt(jnp.mean(resid * resid, axis=-1, keepdims=True) + EPSILON)
    weights = [expert_up, expert_down, near_up, near_half]
    chosen = (
        jnp.arange(experts, dtype=jnp.int32) == lax.axis_index("exp")
    ).astype(jnp.float32)[None, :]
    expert_out, back_rows, grad_up, grad_down, far_up, far_down, grad_router = expert_apply(
        row_slots, grad_rows, weights, router_weight.T, chosen
    )
    grad_routed = rows_dot(
        jnp.concatenate([picks] * hops, axis=0), back_rows.reshape(hops * senders * capacity, width)
    )
    grad_top = out_grad.reshape(tokens, width).astype(jnp.float32)
    grad_resid_norm, grad_expert_norm = norm_backward(resid, scaling_two, expert_norm, grad_routed)
    grad_resid = grad_top + grad_resid_norm
    grad_mixer = grad_resid.astype(jnp.bfloat16)
    grad_out_proj = rows_dot(mixed, grad_mixer)
    grad_mixed = cols_dot(grad_mixer, out_proj)
    grad_scan = grad_mixed * gate_act
    grad_gate_half = grad_mixed * mixer_pre * silu_slope(gate_half)
    grad_gate_half = grad_gate_half.astype(jnp.bfloat16)
    grad_in_gate = rows_dot(normed_half[:tokens], grad_gate_half)
    grad_normed_gate = cols_dot(grad_gate_half, in_proj[:, inner_width:])
    grad_skip_gain = jnp.sum(grad_scan * conv_flat, axis=0, keepdims=True)
    (gradient_first,) = scan_call(
        back_summary_kernel,
        "back_summary",
        sequences,
        states,
        [("wide", delta), ("wide", grad_scan), ("cols", out_cols), ("rates", decay_log)],
        ["state"],
        [],
    )
    carried_back = exchange(gradient_first, delta_sum, own_log)
    side = math.isqrt(senders // 2)
    big = (2, side, side, planes, inner_width // (senders * planes), width)

    def as_rows(values):
        blocks = values.shape[1] // width
        return jnp.concatenate(
            [values[:, at * width : (at + 1) * width] for at in range(blocks)], axis=0
        ).astype(jnp.bfloat16)

    early = [
        grad_out_proj.astype(jnp.bfloat16).reshape(big),
        as_rows(grad_in_gate).reshape(big),
    ]
    heights = [low_rank + 2 * states, low_rank, states, taps, 1, 1, 1, 1, experts // 2]
    in_grad, sum_out, sum_gate, sum_inner, sum_small, back_out, near_up, near_down = all_gradients(
        [
            delta,
            conv_flat,
            grad_scan,
            in_cols,
            out_cols,
            in_diag,
            decay_log,
            carried,
            carried_back,
            delta_pre,
            delta_low,
            conv_pre,
            extended,
            normed_half,
            grad_normed_gate,
            layer_in.reshape(tokens, width),
            rim_layer,
            grad_resid,
            delta_proj,
            state_proj.T,
            in_proj,
            conv_weight,
            vectors,
            grad_skip_gain,
            grad_expert_norm,
            grad_router,
        ]
        + early
        + [expert_out, far_up, far_down],
        sum(heights),
        side,
    )
    grad_up_own = grad_up + near_up.astype(jnp.float32)
    grad_down_own = grad_down + near_down.astype(jnp.float32)
    token_out = rows_dot(
        jnp.concatenate([picks] * hops, axis=0), back_out.reshape(hops * senders * capacity, width)
    )
    layer_out = (resid + token_out).astype(jnp.bfloat16).reshape(sequences, piece_len, width)
    in_grad = in_grad.reshape(sequences, piece_len, width)
    rows_of = (inner_width, width)
    slabs = width // LANE_UNIT
    by_slab = sum_inner.reshape(slabs, 2, width, LANE_UNIT)
    inner_parts = [by_slab[s, c] for c in range(2) for s in range(slabs)]
    grad_in_proj = jnp.concatenate(
        inner_parts + [sum_gate[c].reshape(width, width) for c in range(2)], axis=1
    ).astype(jnp.float32)
    small_halves = sum_small.reshape(2, -1, width)
    small_wide = jnp.concatenate([small_halves[0], small_halves[1]], axis=1).astype(jnp.float32)
    offsets = [sum(heights[:at]) for at in range(len(heights) + 1)]
    pieces = [small_wide[offsets[at] : offsets[at + 1]] for at in range(len(heights))]
    summed = (
        pieces[7][0, :width],
        grad_in_proj,
        pieces[3],
        pieces[4][0],
        pieces[0].T,
        pieces[1],
        pieces[5][0],
        pieces[2],
        pieces[6][0],
        sum_out.reshape(rows_of).astype(jnp.float32),
        pieces[7][0, width:],
        pieces[8].reshape(experts, width).T,
    )
    return (
        layer_out,
        in_grad,
        summed[0],
        summed[1],
        summed[2],
        summed[3],
        summed[4],
        summed[5],
        summed[6],
        summed[7],
        summed[8],
        summed[9],
        summed[10],
        summed[11],
        grad_up_own,
        grad_down_own,
    )


def solution(mesh):
    placed = (
        P(None, ("seq", "exp"), None),
        P(),
        P(),
        P(),
        P(),
        P(),
        P(),
        P(),
        P(),
        P(),
        P(),
        P(),
        P(),
        P("exp", None, "seq"),
        P("exp", "seq", None),
        P(None, ("seq", "exp")),
        P(None, ("seq", "exp")),
        P(None, ("seq", "exp"), None),
    )
    return jax.shard_map(
        on_device,
        mesh=mesh,
        in_specs=placed,
        out_specs=(
            P(None, ("seq", "exp"), None),
            P(None, ("seq", "exp"), None),
            P(),
            P(),
            P(),
            P(),
            P(),
            P(),
            P(),
            P(),
            P(),
            P(),
            P(),
            P(),
            P("exp", None, "seq"),
            P("exp", "seq", None),
        ),
        check_vma=False,
    )
```

```python
import functools
import math

import jax
import jax.numpy as jnp
from jax import lax
from jax.experimental import pallas as pl
from jax.experimental.pallas import tpu as pltpu
from jax.sharding import PartitionSpec as P

BLK = 16
LANES = 128
GROUP = 512
LOG2E = 1.4426950408889634
LN2 = 0.6931471805599453
VMEM_BYTES = 50 * 1024 * 1024


EPSILON = 1e-05


def half_dot(left, right):
    return jnp.dot(left, right, preferred_element_type=jnp.float32)


def rows_dot(left, right, precision=None):
    return lax.dot_general(
        left,
        right,
        (((0,), (0,)), ((), ())),
        precision=precision,
        preferred_element_type=jnp.float32,
    )


def cols_dot(left, right, precision=None):
    return lax.dot_general(
        left,
        right,
        (((1,), (1,)), ((), ())),
        precision=precision,
        preferred_element_type=jnp.float32,
    )


def norm_backward(values, scaling, gain_vec, incoming):
    normal = values * scaling
    weighted = incoming * gain_vec
    grad_gain = jnp.sum(incoming * normal, axis=0, keepdims=True)
    grad_values = scaling * (
        weighted - normal * jnp.mean(weighted * normal, axis=-1, keepdims=True)
    )
    return (grad_values, grad_gain)


def silu_slope(values):
    sigma = jax.nn.sigmoid(values)
    return sigma * (1.0 + values * (1.0 - sigma))


def lane_parts(ref, k, states):
    width = ref.shape[-1]
    return [
        jnp.broadcast_to(ref[k : k + 1, at : at + LANES], (states, LANES))
        for at in range(0, width, LANES)
    ]


def block_of(ref, i):
    return ref.at[pl.ds(pl.multiple_of(i * BLK, BLK), BLK), :]


def rows_of_block(ref, i, states):
    size = BLK * states
    return ref.at[pl.ds(pl.multiple_of(i * size, size), size), :]


def rates_of(log_ref):
    rates = -jnp.exp(log_ref[...]) * LOG2E
    return [rates[:, at : at + LANES] for at in range(0, rates.shape[1], LANES)]


def first_pass_kernel(delta_ref, conv_ref, in_ref, log_ref, end_ref, drive):
    steps, width = delta_ref.shape
    states = log_ref.shape[0]
    rates = rates_of(log_ref)
    drive[...] = delta_ref[...] * conv_ref[...]

    def block(i, state):
        state = list(state)
        inwards = in_ref[i]
        for k in range(BLK):
            inward = jnp.broadcast_to(inwards[:, k : k + 1], (states, LANES))
            deltas = lane_parts(block_of(delta_ref, i), k, states)
            drives = lane_parts(block_of(drive, i), k, states)
            for j in range(width // LANES):
                state[j] = jnp.exp2(deltas[j] * rates[j]) * state[j] + inward * drives[j]
        return tuple(state)

    zero = tuple(jnp.zeros((states, LANES), jnp.float32) for _ in range(width // LANES))
    last = lax.fori_loop(0, steps // BLK, block, zero)
    for j in range(width // LANES):
        end_ref[0, :, j * LANES : (j + 1) * LANES] = last[j]


def second_pass_kernel(
    delta_ref, conv_ref, in_ref, log_ref, start_ref, out_ref, rest_ref, scanned_ref, drive, stack
):
    steps, width = delta_ref.shape
    states = log_ref.shape[0]
    rates = rates_of(log_ref)
    drive[...] = delta_ref[...] * conv_ref[...]

    def block(i, state):
        state = list(state)
        inwards = in_ref[i]
        kept = rows_of_block(stack, i, states)
        for k in range(BLK):
            inward = jnp.broadcast_to(inwards[:, k : k + 1], (states, LANES))
            deltas = lane_parts(block_of(delta_ref, i), k, states)
            drives = lane_parts(block_of(drive, i), k, states)
            for j in range(width // LANES):
                state[j] = jnp.exp2(deltas[j] * rates[j]) * state[j] + inward * drives[j]
                at = slice(j * LANES, (j + 1) * LANES)
                kept[k * states : (k + 1) * states, at] = state[j].astype(jnp.bfloat16)
        return tuple(state)

    begin = tuple(start_ref[0, :, j * LANES : (j + 1) * LANES] for j in range(width // LANES))
    lax.fori_loop(0, steps // BLK, block, begin)
    for i in range(steps // BLK):
        rows = slice(i * BLK, (i + 1) * BLK)
        both = jnp.concatenate([out_ref[rows, :], rest_ref[rows, :]], axis=0)
        product = half_dot(both, stack[i * BLK * states : (i + 1) * BLK * states, :])
        scanned_ref[rows, :] = product[:BLK] + product[BLK:]


def back_summary_kernel(delta_ref, grad_ref, out_ref, log_ref, end_ref):
    steps, width = delta_ref.shape
    states = log_ref.shape[0]
    rates = rates_of(log_ref)
    blocks = steps // BLK

    def block(i, state):
        state = list(state)
        outwards = out_ref[blocks - 1 - i]
        for k in reversed(range(BLK)):
            outward = jnp.broadcast_to(outwards[:, k : k + 1], (states, LANES))
            deltas = lane_parts(block_of(delta_ref, blocks - 1 - i), k, states)
            grads = lane_parts(block_of(grad_ref, blocks - 1 - i), k, states)
            for j in range(width // LANES):
                state[j] = jnp.exp2(deltas[j] * rates[j]) * (state[j] + outward * grads[j])
        return tuple(state)

    zero = tuple(jnp.zeros((states, LANES), jnp.float32) for _ in range(width // LANES))
    last = lax.fori_loop(0, blocks, block, zero)
    for j in range(width // LANES):
        end_ref[0, :, j * LANES : (j + 1) * LANES] = last[j]


def backward_body(
    middle,
    first,
    delta_ref,
    conv_ref,
    grad_ref,
    in_ref,
    out_ref,
    in_diag_ref,
    log_ref,
    start_ref,
    finish_ref,
    grad_delta_ref,
    grad_conv_ref,
    grad_in_ref,
    grad_out_ref,
    grad_log_ref,
    drive,
    carried,
    stack,
    slope,
):
    steps, width = delta_ref.shape
    states = log_ref.shape[0]
    parts = width // LANES
    rates = rates_of(log_ref)
    blocks = steps // BLK
    drive[...] = delta_ref[...] * conv_ref[...]

    def forward(i, state):
        state = list(state)
        inwards = in_ref[i]
        for k in range(BLK):
            t = i * BLK + k
            inward = jnp.broadcast_to(inwards[:, k : k + 1], (states, LANES))
            deltas = lane_parts(block_of(delta_ref, i), k, states)
            drives = lane_parts(block_of(drive, i), k, states)
            for j in range(parts):
                at = slice(j * LANES, (j + 1) * LANES)
                decay = jnp.exp2(deltas[j] * rates[j])
                kept = decay * state[j]
                carried[t, :, at] = kept
                state[j] = kept + inward * drives[j]
                stack[k * states : (k + 1) * states, at] = state[j].astype(jnp.bfloat16)
        rows = pl.ds(pl.multiple_of(i * BLK, BLK), BLK)
        partial = cols_dot(grad_ref[rows, :].astype(jnp.bfloat16), stack[...])

        @pl.when(first)
        def _():
            grad_out_ref[rows, :] = partial

        @pl.when(jnp.logical_not(first))
        def _():
            grad_out_ref[rows, :] += partial

        return tuple(state)

    begin = tuple(start_ref[0, :, j * LANES : (j + 1) * LANES] for j in range(parts))
    lax.fori_loop(0, blocks, forward, begin)
    middle()
    column = lax.broadcasted_iota(jnp.int32, (BLK, BLK * states), 1) // states
    row = lax.broadcasted_iota(jnp.int32, (BLK, BLK * states), 0)
    ones = jnp.where(column == row, 1.0, 0.0).astype(jnp.bfloat16)

    def backward(i, state):
        adjoint, gathered = list(state[:parts]), list(state[parts:])
        outwards = out_ref[blocks - 1 - i]
        for k in reversed(range(BLK)):
            t = (blocks - 1 - i) * BLK + k
            outward = jnp.broadcast_to(outwards[:, k : k + 1], (states, LANES))
            deltas = lane_parts(block_of(delta_ref, blocks - 1 - i), k, states)
            grads = lane_parts(block_of(grad_ref, blocks - 1 - i), k, states)
            for j in range(parts):
                at = slice(j * LANES, (j + 1) * LANES)
                whole = adjoint[j] + outward * grads[j]
                exponent = whole * carried[t, :, at]
                gathered[j] = gathered[j] + exponent * deltas[j]
                slope[k * states : (k + 1) * states, at] = (exponent * rates[j]).astype(
                    jnp.bfloat16
                )
                stack[k * states : (k + 1) * states, at] = whole.astype(jnp.bfloat16)
                adjoint[j] = jnp.exp2(deltas[j] * rates[j]) * whole
        rows = pl.ds(pl.multiple_of((blocks - 1 - i) * BLK, BLK), BLK)
        driven = jnp.dot(in_diag_ref[rows, :], stack[...], preferred_element_type=jnp.float32)
        summed = jnp.dot(ones, slope[...], preferred_element_type=jnp.float32) * LN2
        grad_delta_ref[rows, :] = summed + driven * conv_ref[rows, :]
        grad_conv_ref[rows, :] = driven * delta_ref[rows, :]
        partial = cols_dot(drive[rows, :].astype(jnp.bfloat16), stack[...])

        @pl.when(first)
        def _():
            grad_in_ref[rows, :] = partial

        @pl.when(jnp.logical_not(first))
        def _():
            grad_in_ref[rows, :] += partial

        return tuple(adjoint + gathered)

    ends = tuple(finish_ref[0, :, j * LANES : (j + 1) * LANES] for j in range(parts))
    zero = tuple(jnp.zeros((states, LANES), jnp.float32) for _ in range(parts))
    last = lax.fori_loop(0, blocks, backward, ends + zero)
    for j in range(parts):
        grad_log_ref[0, :, j * LANES : (j + 1) * LANES] = last[parts + j] * rates[j] * LN2


def scan_call(kernel, name, sequences, states, operands, results, scratch):
    tokens, width = next(value.shape for kind, value in operands if kind == "wide")
    steps = tokens // sequences
    specs = {
        "wide": pl.BlockSpec((steps, GROUP), lambda q, j: (q, j)),
        "cols": pl.BlockSpec((steps // BLK, states, BLK), lambda q, j: (q, 0, 0)),
        "narrow": pl.BlockSpec((steps, BLK * states), lambda q, j: (q, 0)),
        "rates": pl.BlockSpec((states, GROUP), lambda q, j: (0, j)),
        "state": pl.BlockSpec((1, states, GROUP), lambda q, j: (q, 0, j)),
    }
    shapes = {
        "wide": (tokens, width),
        "narrow": (tokens, BLK * states),
        "state": (sequences, states, width),
    }
    in_specs = [specs[kind] for kind, _ in operands]
    out_specs = [specs[kind] for kind in results]
    out_shape = [jax.ShapeDtypeStruct(shapes[kind], jnp.float32) for kind in results]
    return pl.pallas_call(
        kernel,
        name=name,
        grid=(sequences, width // GROUP),
        in_specs=in_specs,
        out_specs=out_specs,
        out_shape=out_shape,
        scratch_shapes=scratch,
        compiler_params=pltpu.CompilerParams(
            dimension_semantics=("arbitrary", "arbitrary"),
            vmem_limit_bytes=VMEM_BYTES,
        ),
        cost_estimate=pl.CostEstimate(
            flops=20 * tokens * states * width,
            transcendentals=tokens * states * width,
            bytes_accessed=16 * tokens * width,
        ),
    )(*(value for _, value in operands))


MESH = pl.DeviceIdType.MESH


def remote(src, dst, send, arrive, axis, peer):
    return pltpu.make_async_remote_copy(
        src_ref=src,
        dst_ref=dst,
        send_sem=send,
        recv_sem=arrive,
        device_id={axis: peer},
        device_id_type=MESH,
    )


def greet(axes):
    barrier = pltpu.get_barrier_semaphore()
    total = 0
    for axis, size in axes:
        mine = lax.axis_index(axis)
        for k in range(1, size):
            pl.semaphore_signal(
                barrier, inc=1, device_id={axis: lax.rem(mine + k, size)}, device_id_type=MESH
            )
        total += size - 1
    pl.semaphore_wait(barrier, total)


def exchange_body(
    after_first,
    after_second,
    reverse,
    planes,
    members,
    end_ref,
    sum_ref,
    rates_ref,
    carry_ref,
    packed,
    landed,
    summary,
    totals,
    starts,
    carries,
    send_one,
    recv_one,
    send_two,
    recv_two,
    send_three,
    recv_three,
):
    sequences, states, width = end_ref.shape
    rows = sequences * states // members
    plane, member = lax.axis_index("seq"), lax.axis_index("exp")
    rates = -jnp.exp(rates_ref[...])
    for i in range(members):
        q, n = (i * rows) // states, (i * rows) % states
        packed[i, :rows] = end_ref[q, n : n + rows]
        packed[i, rows:] = sum_ref[q : q + 1]
    for k in range(1, members):
        other = lax.rem(member + k, members)
        remote(
            packed.at[other],
            landed.at[member],
            send_one.at[k],
            recv_one.at[member],
            "exp",
            other,
        ).start()
    after_first()
    landed[member] = packed[member]
    for k in range(1, members):
        other = lax.rem(member + k, members)
        remote(
            packed.at[other], landed.at[other], send_one.at[k], recv_one.at[other], "exp", other
        ).wait()
    order = range(members)[::-1] if reverse else range(members)
    plane_order = range(planes)[::-1] if reverse else range(planes)

    def through(piece, before):
        return jnp.exp(piece[rows:] * rates) * before + piece[:rows]

    state = jnp.zeros((rows, width), jnp.float32)
    total = jnp.zeros((1, width), jnp.float32)
    for i in order:
        piece = landed[i]
        state = through(piece, state)
        total = total + piece[rows:]
    summary[:rows] = state
    summary[rows:] = total
    for k in range(1, planes):
        other = lax.rem(plane + k, planes)
        remote(
            summary, totals.at[plane], send_two.at[k], recv_two.at[plane], "seq", other
        ).start()
    totals[plane] = summary[...]
    for k in range(1, planes):
        other = lax.rem(plane + k, planes)
        remote(summary, totals.at[other], send_two.at[k], recv_two.at[other], "seq", other).wait()
    after_second()
    state = jnp.zeros((rows, width), jnp.float32)
    for s in plane_order:
        reached = plane < s if reverse else plane > s
        state = jnp.where(reached, through(totals[s], state), state)
    for i in order:
        starts[i] = state
        state = through(landed[i], state)
    for k in range(1, members):
        other = lax.rem(member + k, members)
        remote(
            starts.at[other],
            carries.at[member],
            send_three.at[k],
            recv_three.at[member],
            "exp",
            other,
        ).start()
    carries[member] = starts[member]
    for k in range(1, members):
        other = lax.rem(member + k, members)
        remote(
            starts.at[other],
            carries.at[other],
            send_three.at[k],
            recv_three.at[other],
            "exp",
            other,
        ).wait()
    for i in range(members):
        q, n = (i * rows) // states, (i * rows) % states
        carry_ref[q, n : n + rows] = carries[i]


def exchange_kernel(reverse, planes, members, *refs):
    greet((("seq", planes), ("exp", members)))
    exchange_body(lambda: None, lambda: None, reverse, planes, members, *refs)


def exchange_scratch(planes, members, rows, width):
    piece = (rows + 1, width)
    return [
        pltpu.VMEM((members,) + piece, jnp.float32),
        pltpu.VMEM((members,) + piece, jnp.float32),
        pltpu.VMEM(piece, jnp.float32),
        pltpu.VMEM((planes,) + piece, jnp.float32),
        pltpu.VMEM((members, rows, width), jnp.float32),
        pltpu.VMEM((members, rows, width), jnp.float32),
        pltpu.SemaphoreType.DMA((members,)),
        pltpu.SemaphoreType.DMA((members,)),
        pltpu.SemaphoreType.DMA((planes,)),
        pltpu.SemaphoreType.DMA((planes,)),
        pltpu.SemaphoreType.DMA((members,)),
        pltpu.SemaphoreType.DMA((members,)),
    ]


def exchange(local_end, delta_sum, own_log):
    planes, members = lax.axis_size("seq"), lax.axis_size("exp")
    rows, width = own_log.shape
    vmem = pl.BlockSpec(memory_space=pltpu.VMEM)
    return pl.pallas_call(
        functools.partial(exchange_kernel, True, planes, members),
        name="state_exchange_back",
        in_specs=[vmem] * 3,
        out_specs=vmem,
        out_shape=jax.ShapeDtypeStruct(local_end.shape, jnp.float32),
        scratch_shapes=exchange_scratch(planes, members, rows, width),
        compiler_params=pltpu.CompilerParams(
            collective_id=2, has_side_effects=True, vmem_limit_bytes=VMEM_BYTES
        ),
        cost_estimate=pl.CostEstimate(flops=10**6, transcendentals=10**5, bytes_accessed=2 * 10**7),
    )(local_end, delta_sum, own_log)


class Sums:
    def __init__(self, planes, side, sends, arrivals):
        self.planes, self.side = planes, side
        self.plane, self.member = lax.axis_index("seq"), lax.axis_index("exp")
        chip, self.core = self.member // 2, lax.rem(self.member, 2)
        high, low = chip // side, lax.rem(chip, side)
        self.first = low + (high - low) * self.core
        self.second = high + (low - high) * self.core
        self.partner = self.member + 1 - 2 * self.core
        self.sends, self.arrivals = sends, arrivals

    def chip_at(self, first, second):
        low = first + (second - first) * self.core
        high = second + (first - second) * self.core
        return (high * self.side + low) * 2 + self.core

    def first_peer(self, k):
        other = lax.rem(self.first + k, self.side)
        return other, self.chip_at(other, self.second)

    def second_peer(self, k):
        other = lax.rem(self.second + k, self.side)
        return other, self.chip_at(self.first, other)

    def plane_peer(self, k):
        return lax.rem(self.plane + k, self.planes)

    def signal_peers(self, barrier):
        peers = [{"exp": self.partner}]
        peers += [{"exp": self.first_peer(k)[1]} for k in range(1, self.side)]
        peers += [{"exp": self.second_peer(k)[1]} for k in range(1, self.side)]
        peers += [{"seq": self.plane_peer(k)} for k in range(1, self.planes)]
        for peer in peers:
            pl.semaphore_signal(barrier, inc=1, device_id=peer, device_id_type=MESH)
        return len(peers)

    def move(self, stage, at, slot, src, dst, axis, peer):
        return remote(
            src, dst, self.sends[stage].at[at], self.arrivals[stage].at[slot], axis, peer
        )

    def pair_half(self, i, given, half):
        return self.move(0, i, i, given.at[1 - self.core], half, "exp", self.partner)

    def scatter_first(self, i, k, half, slots, arriving):
        other, device = self.first_peer(k)
        slot = other if arriving else self.first
        return self.move(1, (i, k), (i, slot), half.at[other], slots.at[slot], "exp", device)

    def scatter_second(self, i, k, quarter, slots, arriving):
        other, device = self.second_peer(k)
        slot = other if arriving else self.second
        return self.move(2, (i, k), (i, slot), quarter.at[other], slots.at[slot], "exp", device)

    def scatter_plane(self, i, k, eighth, slots, arriving):
        other = self.plane_peer(k)
        slot = other if arriving else self.plane
        return self.move(3, (i, k), (i, slot), eighth.at[other], slots.at[slot], "seq", other)

    def gather_plane(self, i, k, block, arriving):
        other = self.plane_peer(k)
        slot = other if arriving else self.plane
        return self.move(
            4, (i, k), (i, slot), block.at[self.plane], block.at[slot], "seq", other
        )

    def gather_second(self, i, k, result, arriving):
        other, device = self.second_peer(k)
        slot = other if arriving else self.second
        row = result.at[self.core, self.first]
        return self.move(5, (i, k), (i, slot), row.at[self.second], row.at[slot], "exp", device)

    def gather_first(self, i, k, result, arriving):
        other, device = self.first_peer(k)
        slot = other if arriving else self.first
        own = result.at[self.core]
        return self.move(6, (i, k), (i, slot), own.at[self.first], own.at[slot], "exp", device)

    def pair_gather(self, i, k, result, arriving):
        other = lax.rem(self.first + k, self.side)
        low = lax.rem(self.partner // 2, self.side)
        theirs = low + (self.partner // (2 * self.side) - low) * (1 - self.core)
        other = lax.rem(theirs + k, self.side) if arriving else other
        half = 1 - self.core if arriving else self.core
        mine = result.at[self.core, lax.rem(self.first + k, self.side)]
        return self.move(7, (i, k), (i, k), mine, result.at[half, other], "exp", self.partner)

    def after_pair(self, i, given, half, slots):
        self.pair_half(i, given, half).wait()
        own = self.core
        for at in range(self.side):
            for to in range(self.side):
                both = given[own, at, to].astype(jnp.float32) + half[at, to].astype(jnp.float32)
                half[at, to] = both.astype(jnp.bfloat16)
        for k in range(1, self.side):
            self.scatter_first(i, k, half, slots, False).start()
        slots[self.first] = half[self.first]

    def after_first(self, i, half, slots, quarter, slots_two):
        for k in range(1, self.side):
            self.scatter_first(i, k, half, slots, True).wait_recv()
        for at in range(self.side):
            added = slots[0, at].astype(jnp.float32)
            for k in range(1, self.side):
                added = added + slots[k, at].astype(jnp.float32)
            quarter[at] = added.astype(jnp.bfloat16)
        for k in range(1, self.side):
            self.scatter_second(i, k, quarter, slots_two, False).start()
        slots_two[self.second] = quarter[self.second]

    def after_second(self, i, quarter, slots_two, eighth, slots_three):
        for k in range(1, self.side):
            self.scatter_second(i, k, quarter, slots_two, True).wait_recv()
        added = slots_two[0].astype(jnp.float32)
        for k in range(1, self.side):
            added = added + slots_two[k].astype(jnp.float32)
        eighth[...] = added.astype(jnp.bfloat16)
        for k in range(1, self.planes):
            self.scatter_plane(i, k, eighth, slots_three, False).start()
        slots_three[self.plane] = eighth[self.plane]

    def after_planes(self, i, eighth, slots_three, block):
        for k in range(1, self.planes):
            self.scatter_plane(i, k, eighth, slots_three, True).wait_recv()
        added = slots_three[0].astype(jnp.float32)
        for k in range(1, self.planes):
            added = added + slots_three[k].astype(jnp.float32)
        block[self.plane] = added.astype(jnp.bfloat16)
        for k in range(1, self.planes):
            self.gather_plane(i, k, block, False).start()

    def planes_gathered(self, i, block):
        for k in range(1, self.planes):
            self.gather_plane(i, k, block, True).wait_recv()

    def scatter_sent(self, i, half, slots, quarter, slots_two, eighth, slots_three, block):
        for k in range(1, self.side):
            self.scatter_first(i, k, half, slots, False).wait_send()
            self.scatter_second(i, k, quarter, slots_two, False).wait_send()
        for k in range(1, self.planes):
            self.scatter_plane(i, k, eighth, slots_three, False).wait_send()
            self.gather_plane(i, k, block, False).wait_send()

    def gather_second_start(self, i, result):
        for k in range(1, self.side):
            self.gather_second(i, k, result, False).start()

    def gather_across(self, i, result):
        for k in range(1, self.side):
            self.gather_second(i, k, result, True).wait_recv()
        for k in range(1, self.side):
            self.gather_first(i, k, result, False).start()
        self.pair_gather(i, 0, result, False).start()

    def gather_pass(self, i, result):
        for k in range(1, self.side):
            self.gather_first(i, k, result, True).wait_recv()
            self.pair_gather(i, k, result, False).start()

    def gather_end(self, i, result):
        for k in range(self.side):
            self.pair_gather(i, k, result, True).wait_recv()
            self.pair_gather(i, k, result, False).wait_send()
        for k in range(1, self.side):
            self.gather_first(i, k, result, False).wait_send()
            self.gather_second(i, k, result, False).wait_send()


def stage_semaphores(count, planes, side):
    each = [(count,)] + [(count, size) for size in (side, side, planes, planes, side, side, side)]
    return [pltpu.SemaphoreType.DMA(shape) for shape in each]


def scatter_buffers(tails, planes, side):
    leads = [(side, side, planes), (side, side, planes), (side, planes), (side, planes)]
    leads += [(planes,), (planes,)]
    return [pltpu.VMEM(lead + tail, jnp.bfloat16) for lead in leads for tail in tails]


def neighbour_plane():
    plane = lax.axis_index("seq")
    return {"seq": plane + 1 - 2 * lax.rem(plane, 2)}


def swapped(src, dst, send, arrive):
    return pltpu.make_async_remote_copy(
        src_ref=src,
        dst_ref=dst,
        send_sem=send,
        recv_sem=arrive,
        device_id=neighbour_plane(),
        device_id_type=MESH,
    )


class Routes:
    def __init__(self, planes, members, sends, arrivals, local):
        self.planes, self.members = planes, members
        self.plane, self.member = lax.axis_index("seq"), lax.axis_index("exp")
        self.hops = planes // 2
        self.sends, self.arrivals, self.local = sends, arrivals, local
        self.pairs = [
            (hop, k) for hop in range(self.hops) for k in range(members) if hop or k
        ]

    def device(self, hop, k):
        return {
            "seq": lax.rem(self.plane + 2 * hop, self.planes),
            "exp": lax.rem(self.member + k, self.members),
        }

    def signal_peers(self, barrier):
        for hop, k in self.pairs:
            pl.semaphore_signal(
                barrier, inc=1, device_id=self.device(hop, k), device_id_type=MESH
            )
        return len(self.pairs)

    def moved(self, given, landed, returning, hop, k, arriving):
        device = self.device(hop, k)
        other = device["exp"]
        slot = hop if arriving else (-hop) % self.hops
        if returning:
            index = other if arriving else self.member
            src = given.at[hop, (self.members - k) % self.members]
        else:
            index, src = k, given.at[other]
        return pltpu.make_async_remote_copy(
            src_ref=src,
            dst_ref=landed.at[slot, index],
            send_sem=self.sends.at[hop, k],
            recv_sem=self.arrivals.at[slot, index],
            device_id=device,
            device_id_type=MESH,
        )

    def own(self, given, landed, returning):
        src = given.at[0, 0] if returning else given.at[self.member]
        index = self.member if returning else 0
        return pltpu.make_async_copy(src, landed.at[0, index], self.local)

    def start(self, given, landed, returning):
        for hop, k in self.pairs:
            self.moved(given, landed, returning, hop, k, False).start()
        self.own(given, landed, returning).start()

    def wait_sent(self, given, landed):
        for hop, k in self.pairs:
            self.moved(given, landed, False, hop, k, False).wait_send()

    def wait(self, given, landed, returning):
        for hop, k in self.pairs:
            self.moved(given, landed, returning, hop, k, True).wait_recv()
        self.own(given, landed, returning).wait()
        for hop, k in self.pairs:
            self.moved(given, landed, returning, hop, k, False).wait_send()


def route_semaphores(planes, members):
    shape = (planes // 2, members)
    return [
        pltpu.SemaphoreType.DMA(shape),
        pltpu.SemaphoreType.DMA(shape),
        pltpu.SemaphoreType.DMA,
    ]


def two_part(left, right, dims):
    high = left.astype(jnp.bfloat16)
    rest = (left - high.astype(jnp.float32)).astype(jnp.bfloat16)
    numbers = (dims, ((), ()))
    wide = jnp.float32
    return lax.dot_general(high, right, numbers, preferred_element_type=wide) + lax.dot_general(
        rest, right, numbers, preferred_element_type=wide
    )


LANE_UNIT = 256


def lane_unit(j):
    return pl.ds(pl.multiple_of(j * LANE_UNIT, LANE_UNIT), LANE_UNIT)


def normalized(values, gain):
    return values * lax.rsqrt(jnp.mean(values * values, axis=-1, keepdims=True) + EPSILON) * gain


def chain_device(at, members):
    return {"seq": at // members, "exp": lax.rem(at, members)}


def forward_kernel(
    planes,
    members,
    capacity,
    layer_ref,
    out_grad_ref,
    target_ref,
    vectors_ref,
    in_proj_ref,
    conv_weight_ref,
    state_proj_ref,
    delta_proj_ref,
    decay_log_ref,
    own_log_ref,
    out_proj_ref,
    up_ref,
    down_ref,
    normed_ref,
    extended_ref,
    gate_ref,
    conv_pre_ref,
    conv_ref,
    delta_pre_ref,
    delta_ref,
    delta_low_ref,
    in_cols_ref,
    out_cols_ref,
    in_diag_ref,
    delta_sum_ref,
    carried_ref,
    mixer_pre_ref,
    mixed_ref,
    resid_ref,
    row_slots_ref,
    grad_rows_ref,
    near_up_ref,
    near_half_ref,
    rim_in_ref,
    grad_slots_ref,
    drive_ref,
    stack_ref,
    low_sum_ref,
    wide_sum_ref,
    out_diag_ref,
    out_rest_ref,
    local_end_ref,
    rim_out_ref,
    rim_sent_ref,
    rim_landed_ref,
    up_sent_ref,
    up_landed_ref,
    down_sent_ref,
    down_landed_ref,
    *rest,
):
    exchange_refs, grad_semaphores = rest[:12], rest[12:15]
    wide, half = jnp.float32, jnp.bfloat16
    tokens, width = layer_ref.shape
    own_tokens = slice(0, tokens)
    inner_width = conv_ref.shape[1]
    sequences = extended_ref.shape[0]
    piece = tokens // sequences
    states, taps = decay_log_ref.shape[0], conv_weight_ref.shape[0]
    low_rank = delta_low_ref.shape[1]
    experts = row_slots_ref.shape[0]
    conv_bias_ref, delta_bias_ref, skip_ref = (vectors_ref.at[i : i + 1] for i in range(3))
    mixer_gain_ref, expert_norm_ref = vectors_ref.at[3:4, :width], vectors_ref.at[3:4, width:]
    devices = planes * members
    place = lax.axis_index("seq") * members + lax.axis_index("exp")
    before, after = lax.rem(place + devices - 1, devices), lax.rem(place + 1, devices)
    grad_routes = Routes(planes, members, *grad_semaphores)
    barrier = pltpu.get_barrier_semaphore()
    for peer in (before, after):
        device = chain_device(peer, members)
        pl.semaphore_signal(barrier, inc=1, device_id=device, device_id_type=MESH)
    greeted = 2 + grad_routes.signal_peers(barrier)
    for axis, size in (("seq", planes), ("exp", members)):
        mine = lax.axis_index(axis)
        for k in range(1, size):
            other = {axis: lax.rem(mine + k, size)}
            pl.semaphore_signal(barrier, inc=1, device_id=other, device_id_type=MESH)
        greeted += size - 1
    for q in range(sequences):
        rim_out_ref[q] = layer_ref[(q + 1) * piece - 8 : (q + 1) * piece]
    pl.semaphore_wait(barrier, greeted)
    rim_copy = pltpu.make_async_remote_copy(
        src_ref=rim_out_ref,
        dst_ref=rim_in_ref,
        send_sem=rim_sent_ref,
        recv_sem=rim_landed_ref,
        device_id=chain_device(after, members),
        device_id_type=MESH,
    )
    rim_copy.start()
    up_rows = up_ref.shape[1]
    marks = (0, up_rows // 2, up_rows * 11 // 16, up_rows)
    up_swaps = []
    for i, (low, high) in enumerate(zip(marks, marks[1:])):
        at = pl.ds(low, high - low)
        ends = (up_ref.at[:, at], near_up_ref.at[:, at])
        up_swaps.append(swapped(*ends, up_sent_ref.at[i], up_landed_ref.at[i]))
    slot = lax.broadcasted_iota(jnp.int32, (experts * capacity, tokens), 0)
    picks = jnp.where(slot == target_ref[...], 1.0, 0.0).astype(half)

    def fill(slots, values):
        product = half_dot(picks, values).astype(half)
        for e in range(experts):
            slots[e] = product[e * capacity : (e + 1) * capacity]

    fill(grad_slots_ref, out_grad_ref[...])
    grad_routes.start(grad_slots_ref, grad_rows_ref, False)
    up_swaps[0].start()
    cut = down_ref.shape[1] // 2
    down_swap = swapped(down_ref.at[:, pl.ds(0, cut)], near_half_ref, down_sent_ref, down_landed_ref)

    count = inner_width // LANE_UNIT
    normed_ref[own_tokens, :] = normalized(layer_ref[...].astype(wide), mixer_gain_ref[...]).astype(half)

    def project(j, carry):
        at = lane_unit(j)
        product = half_dot(normed_ref[own_tokens, :], in_proj_ref[:, at])
        for q in range(sequences):
            extended_ref[q, 8:, at] = product[q * piece : (q + 1) * piece]
        gate_at = pl.ds(pl.multiple_of(inner_width + j * LANE_UNIT, LANE_UNIT), LANE_UNIT)
        gate_ref[:, at] = half_dot(normed_ref[own_tokens, :], in_proj_ref[:, gate_at])
        return carry

    lax.fori_loop(0, count, project, 0)
    rim_copy.wait()
    keep = jnp.where(place > 0, 1.0, 0.0)
    rims = [normalized(rim_in_ref[q].astype(wide), mixer_gain_ref[...]) for q in range(sequences)]
    rim_normed = jnp.concatenate(rims, axis=0).astype(half)
    normed_ref[tokens:, :] = rim_normed
    low_sum_ref[...] = jnp.zeros(low_sum_ref.shape, wide)
    wide_sum_ref[...] = jnp.zeros(wide_sum_ref.shape, wide)

    def convolve(j, carry):
        at = lane_unit(j)
        rim = half_dot(rim_normed, in_proj_ref[:, at]) * keep
        for q in range(sequences):
            extended_ref[q, :8, at] = rim[q * 8 : (q + 1) * 8]
            start = 8 - (taps - 1)
            pre = conv_bias_ref[:, at] + conv_weight_ref[:1, at] * extended_ref[q, start : start + piece, at]
            for tap in range(1, taps):
                moved = extended_ref[q, start + tap : start + tap + piece, at]
                pre = pre + conv_weight_ref[tap : tap + 1, at] * moved
            conv_pre_ref[q * piece : (q + 1) * piece, at] = pre
            conv_ref[q * piece : (q + 1) * piece, at] = pre * jax.nn.sigmoid(pre)
        act = conv_ref[:, at]
        high = act.astype(half)
        low = (act - high.astype(wide)).astype(half)
        weight = state_proj_ref[:, at]
        low_sum_ref[...] += cols_dot(high, weight) + cols_dot(low, weight)
        tail = weight[low_rank:]
        wide_sum_ref[...] += cols_dot(tail, high) + cols_dot(tail, low)
        return carry

    lax.fori_loop(0, count, convolve, 0)
    delta_low_ref[...] = low_sum_ref[:, :low_rank]
    for i in range(tokens // BLK):
        block = wide_sum_ref[:, i * BLK : (i + 1) * BLK]
        in_cols_ref[i] = block[:states]
        out_cols_ref[i] = block[states:]
    shape = (tokens, BLK * states)
    column = lax.broadcasted_iota(jnp.int32, shape, 1)
    row = lax.rem(lax.broadcasted_iota(jnp.int32, shape, 0), BLK)
    own = column // states == row
    tile = jnp.where(
        lax.rem(lax.broadcasted_iota(jnp.int32, (states, BLK * states), 1), states)
        == lax.broadcasted_iota(jnp.int32, (states, BLK * states), 0),
        1.0,
        0.0,
    ).astype(half)

    def spread_out(values):
        return jnp.where(own, half_dot(values, tile), 0.0).astype(half)

    outward = low_sum_ref[:, low_rank + states :]
    out_high = outward.astype(half)
    in_diag_ref[...] = spread_out(low_sum_ref[:, low_rank : low_rank + states].astype(half))
    out_diag_ref[...] = spread_out(out_high)
    out_rest_ref[...] = spread_out((outward - out_high.astype(wide)).astype(half))

    def time_steps(j, carry):
        at = lane_unit(j)
        pre = two_part(delta_low_ref[...], delta_proj_ref[:, at], ((1,), (0,))) + delta_bias_ref[:, at]
        delta = jnp.maximum(pre, 0.0) + jnp.log1p(jnp.exp(-jnp.abs(pre)))
        delta_pre_ref[:, at] = pre
        delta_ref[:, at] = delta
        for q in range(sequences):
            part = delta[q * piece : (q + 1) * piece]
            delta_sum_ref[q : q + 1, at] = jnp.sum(part, axis=0, keepdims=True)
        return carry

    lax.fori_loop(0, count, time_steps, 0)
    groups = inner_width // GROUP
    blocks = piece // BLK

    def views(i):
        q, j = i // groups, lax.rem(i, groups)
        rows = pl.ds(pl.multiple_of(q * piece, piece), piece)
        lanes = pl.ds(pl.multiple_of(j * GROUP, GROUP), GROUP)
        cols = pl.ds(q * blocks, blocks)
        return q, rows, lanes, cols

    def first(i, carry):
        q, rows, lanes, cols = views(i)
        first_pass_kernel(
            delta_ref.at[rows, lanes],
            conv_ref.at[rows, lanes],
            in_cols_ref.at[cols],
            decay_log_ref.at[:, lanes],
            local_end_ref.at[pl.ds(q, 1), :, lanes],
            drive_ref,
        )
        return carry

    lax.fori_loop(0, sequences * groups, first, 0)

    def between_planes():
        up_swaps[2].start()
        down_swap.start()

    exchange_body(
        up_swaps[1].start,
        between_planes,
        False,
        planes,
        members,
        local_end_ref,
        delta_sum_ref,
        own_log_ref,
        carried_ref,
        *exchange_refs,
    )

    def second(i, carry):
        q, rows, lanes, cols = views(i)
        second_pass_kernel(
            delta_ref.at[rows, lanes],
            conv_ref.at[rows, lanes],
            in_cols_ref.at[cols],
            decay_log_ref.at[:, lanes],
            carried_ref.at[pl.ds(q, 1), :, lanes],
            out_diag_ref.at[rows],
            out_rest_ref.at[rows],
            mixer_pre_ref.at[rows, lanes],
            drive_ref,
            stack_ref,
        )
        return carry

    lax.fori_loop(0, sequences * groups, second, 0)

    def mix(j, carry):
        at = lane_unit(j)
        pre = mixer_pre_ref[:, at] + skip_ref[:, at] * conv_ref[:, at]
        gate = gate_ref[:, at]
        mixer_pre_ref[:, at] = pre
        mixed_ref[:, at] = (pre * (gate * jax.nn.sigmoid(gate))).astype(half)
        return carry

    lax.fori_loop(0, count, mix, 0)
    resid_ref[...] = layer_ref[...].astype(wide) + half_dot(mixed_ref[...], out_proj_ref[...])
    fill(row_slots_ref, normalized(resid_ref[...], expert_norm_ref[...]).astype(half))
    grad_routes.wait(grad_slots_ref, grad_rows_ref, False)
    down_swap.wait()
    for swap in up_swaps:
        swap.wait()


def forward(operands, capacity, states, sequences, low_rank, experts):
    planes, members = lax.axis_size("seq"), lax.axis_size("exp")
    tokens, width = operands[0].shape
    inner_width = operands[3].shape[1]
    up, down = operands[11:13]
    half, wide = jnp.bfloat16, jnp.float32
    piece = tokens // sequences
    token_wide = jax.ShapeDtypeStruct((tokens, inner_width), wide)
    cols = jax.ShapeDtypeStruct((tokens // BLK, states, BLK), wide)
    diag = (tokens, BLK * states)
    routed = jax.ShapeDtypeStruct((planes // 2, members, capacity, width), half)
    state = (sequences, states, inner_width)
    vmem, anywhere = (pl.BlockSpec(memory_space=space) for space in (pltpu.VMEM, pl.ANY))
    scratch = [
        pltpu.VMEM((experts, capacity, width), half),
        pltpu.VMEM((piece, GROUP), wide),
        pltpu.VMEM((piece * states, GROUP), half),
        pltpu.VMEM((tokens, low_rank + 2 * states), wide),
        pltpu.VMEM((2 * states, tokens), wide),
        pltpu.VMEM(diag, half),
        pltpu.VMEM(diag, half),
        pltpu.VMEM(state, wide),
        pltpu.VMEM((sequences, 8, width), half),
    ]
    scratch += [pltpu.SemaphoreType.DMA] * 2 + [pltpu.SemaphoreType.DMA((3,))] * 2
    scratch += [pltpu.SemaphoreType.DMA] * 2
    scratch += exchange_scratch(planes, members, sequences * states // members, inner_width)
    scratch += route_semaphores(planes, members)
    return pl.pallas_call(
        functools.partial(forward_kernel, planes, members, capacity),
        name="forward_to_experts",
        in_specs=[vmem] * 11 + [anywhere] * 2,
        out_specs=[vmem] * 17 + [anywhere] * 3 + [vmem],
        out_shape=[
            jax.ShapeDtypeStruct((tokens + 8 * sequences, width), half),
            jax.ShapeDtypeStruct((sequences, piece + 8, inner_width), wide),
            token_wide,
            token_wide,
            token_wide,
            token_wide,
            token_wide,
            jax.ShapeDtypeStruct((tokens, low_rank), wide),
            cols,
            cols,
            jax.ShapeDtypeStruct(diag, half),
            jax.ShapeDtypeStruct((sequences, inner_width), wide),
            jax.ShapeDtypeStruct(state, wide),
            token_wide,
            jax.ShapeDtypeStruct((tokens, inner_width), half),
            jax.ShapeDtypeStruct((tokens, width), wide),
            jax.ShapeDtypeStruct((experts, capacity, width), half),
            routed,
            jax.ShapeDtypeStruct(up.shape, half),
            jax.ShapeDtypeStruct((1, down.shape[1] // 2, width), half),
            jax.ShapeDtypeStruct((sequences, 8, width), half),
        ],
        scratch_shapes=scratch,
        compiler_params=pltpu.CompilerParams(
            collective_id=1, has_side_effects=True, vmem_limit_bytes=60 * 1024 * 1024
        ),
        cost_estimate=pl.CostEstimate(flops=10**8, transcendentals=0, bytes_accessed=2 * 10**8),
    )(*operands)


def expert_kernel(
    planes,
    members,
    row_slots_ref,
    grad_rows_ref,
    up_ref,
    down_ref,
    near_up_ref,
    near_half_ref,
    router_ref,
    chosen_ref,
    outs_ref,
    back_ref,
    grad_up_ref,
    grad_down_ref,
    far_up_ref,
    far_down_ref,
    grad_router_ref,
    landed_ref,
    rows_ref,
    grads_ref,
    sent_ref,
    near_down_ref,
    out_sum_ref,
    row_sum_ref,
    hidden_own_ref,
    hidden_near_ref,
    pre_own_ref,
    pre_near_ref,
    shares_ref,
    far_up_sum_ref,
    far_down_sum_ref,
    returns_ref,
    down_sent_ref,
    down_landed_ref,
    back_sent_ref,
    back_landed_ref,
    *rest,
):
    routes = Routes(planes, members, *rest)
    wide, half = jnp.float32, jnp.bfloat16
    plane, member, hops = routes.plane, routes.member, routes.hops
    capacity, width = row_slots_ref.shape[1:]
    batch = members // 2
    chunk = batch * capacity
    group = members * capacity
    units = up_ref.shape[2]
    cut = units // 2
    barrier = pltpu.get_barrier_semaphore()
    pl.semaphore_signal(barrier, inc=1, device_id=neighbour_plane(), device_id_type=MESH)
    pl.semaphore_wait(barrier, routes.signal_peers(barrier) + 1)
    routes.start(row_slots_ref, landed_ref, False)
    down_swap = swapped(
        down_ref.at[0, pl.ds(cut, cut)], near_down_ref.at[pl.ds(cut, cut)], down_sent_ref, down_landed_ref
    )
    down_swap.start()
    near_down_ref[:cut] = near_half_ref[0]
    grad_router_ref[...] = jnp.zeros(grad_router_ref.shape, wide)
    for hop in range(hops):
        for e in range(members):
            grads_ref[hop * group + e * capacity : hop * group + (e + 1) * capacity] = grad_rows_ref[
                hop, e
            ]

    def gather(hop, c):
        rows = rows_ref.at[place(hop, c), :]
        for k in range(batch):
            r = c * batch + k
            if hop:
                routes.moved(row_slots_ref, landed_ref, False, hop, r, True).wait_recv()
            else:

                @pl.when(r > 0)
                def _():
                    routes.moved(row_slots_ref, landed_ref, False, 0, r, True).wait_recv()

            rows[k * capacity : (k + 1) * capacity, :] = landed_ref[hop, r]

    def through(at, up, down, hidden, back, where):
        pre = half_dot(rows_ref[at, :], up)
        phi = 0.5 * (1.0 + lax.erf(pre * 0.7071067811865476))
        slope = phi + pre * (jnp.exp(-0.5 * pre * pre) * 0.3989422804014327)
        active = (pre * phi).astype(half)
        hidden[at, where] = active
        arrived = (slope * cols_dot(sent_ref[at, :], down)).astype(half)
        back[at, where] = arrived
        return half_dot(active, down), cols_dot(arrived, up)

    def place(hop, c):
        return pl.ds(pl.multiple_of(hop * group + c * chunk, chunk), chunk)

    def own_part(hop, c):
        at = place(hop, c)
        logits = cols_dot(rows_ref[at, :].astype(wide), router_ref[...], lax.Precision.HIGHEST)
        raised = jnp.exp(logits - jnp.max(logits, axis=-1, keepdims=True))
        shares = raised / jnp.sum(raised, axis=-1, keepdims=True)
        gate = jnp.sum(shares * chosen_ref[...], axis=-1, keepdims=True)
        shares_ref[at, :] = shares
        sent_ref[at, :] = (gate * grads_ref[at, :].astype(wide)).astype(half)
        every = slice(0, units)
        out, row = through(at, up_ref[0], down_ref[0], hidden_own_ref, pre_own_ref, every)
        early = slice(0, cut)
        near_out, near_row = through(
            at, near_up_ref[0, :, :cut], near_down_ref[:cut], hidden_near_ref, pre_near_ref, early
        )
        out_sum_ref[at, :] = out + near_out
        row_sum_ref[at, :] = row + near_row

    def late_part(hop, c):
        at = place(hop, c)
        near_out, near_row = through(
            at,
            near_up_ref[0, :, cut:],
            near_down_ref[cut:],
            hidden_near_ref,
            pre_near_ref,
            slice(cut, units),
        )
        out = out_sum_ref[at, :] + near_out
        shares, chosen = shares_ref[at, :], chosen_ref[...]
        gate = jnp.sum(shares * chosen, axis=-1, keepdims=True)
        grad_gate = jnp.sum(grads_ref[at, :].astype(wide) * out, axis=-1, keepdims=True)
        grad_logits = grad_gate * gate * (chosen - shares)
        outs = (gate * out).astype(half)
        row = row_sum_ref[at, :] + near_row
        row = row + jnp.dot(
            grad_logits,
            router_ref[...],
            precision=lax.Precision.HIGHEST,
            preferred_element_type=wide,
        )
        row = row.astype(half)
        grad_router_ref[...] += rows_dot(
            grad_logits, rows_ref[at, :].astype(wide), lax.Precision.HIGHEST
        )
        for k in range(batch):
            part = slice(k * capacity, (k + 1) * capacity)
            outs_ref[hop, c * batch + k] = outs[part]
            returns_ref[hop, c * batch + k] = row[part]

    def returned(hop, r, arriving):
        other = lax.rem(member + members - r, members)
        slot = hop if arriving else (-hop) % hops
        sender = other if arriving else member
        return pltpu.make_async_remote_copy(
            src_ref=returns_ref.at[hop, r],
            dst_ref=back_ref.at[slot, sender],
            send_sem=back_sent_ref.at[hop, r],
            recv_sem=back_landed_ref.at[slot, sender],
            device_id={"seq": lax.rem(plane + 2 * hop, planes), "exp": other},
            device_id_type=MESH,
        )

    def give_back(hop, c):
        for k in range(batch):
            r = c * batch + k
            if hop:
                returned(hop, r, False).start()
            else:

                @pl.when(r > 0)
                def _():
                    returned(0, r, False).start()

    def loop(body):
        def run(c, carry):
            body(c)
            return carry

        lax.fori_loop(0, 2, run, 0)

    def weight_grads(hop):
        at = slice(hop * group, (hop + 1) * group)
        rows, sent = rows_ref[at, :], sent_ref[at, :]
        products = [
            (grad_up_ref.at[0], rows, pre_own_ref[at, :]),
            (grad_down_ref.at[0], hidden_own_ref[at, :], sent),
            (far_up_sum_ref, rows, pre_near_ref[at, :]),
            (far_down_sum_ref, hidden_near_ref[at, :], sent),
        ]
        for total, left, right in products:
            if hop:
                total[...] += rows_dot(left, right)
            else:
                total[...] = rows_dot(left, right)

    routes.own(row_slots_ref, landed_ref, False).wait()

    def near_start(c):
        gather(0, c)
        own_part(0, c)

    loop(near_start)
    for hop in range(1, hops):

        def far_end(c):
            gather(hop, c)
            own_part(hop, c)
            if hop == 1:

                @pl.when(c == 0)
                def _():
                    down_swap.wait()

            late_part(hop, c)
            give_back(hop, c)

        loop(far_end)

    def near_end(c):
        late_part(0, c)
        give_back(0, c)

    loop(near_end)
    for hop in range(hops):
        weight_grads(hop)
    far_up_ref[0] = far_up_sum_ref[...].astype(half)
    far_down_ref[0] = far_down_sum_ref[...].astype(half)
    back_ref[0, member] = returns_ref[0, 0]
    for hop in range(hops):
        for r in range(members):
            if hop or r:
                returned(hop, r, True).wait_recv()
                returned(hop, r, False).wait_send()
    routes.wait_sent(row_slots_ref, landed_ref)


def expert_apply(row_slots, grad_rows, weights, router, chosen):
    planes, members = lax.axis_size("seq"), lax.axis_size("exp")
    experts, capacity, width = row_slots.shape
    up, down, near_up, near_half = weights
    units = up.shape[2]
    hops = planes // 2
    count = hops * members * capacity
    half, wide = jnp.bfloat16, jnp.float32
    vmem = pl.BlockSpec(memory_space=pltpu.VMEM)
    slotted = (hops, members, capacity, width)
    every = (hops, members)
    return pl.pallas_call(
        functools.partial(expert_kernel, planes, members),
        name="expert_apply",
        in_specs=[vmem] * 8,
        out_specs=[vmem] * 7,
        out_shape=[
            jax.ShapeDtypeStruct(slotted, half),
            jax.ShapeDtypeStruct(slotted, half),
            jax.ShapeDtypeStruct(up.shape, wide),
            jax.ShapeDtypeStruct(down.shape, wide),
            jax.ShapeDtypeStruct(up.shape, half),
            jax.ShapeDtypeStruct(down.shape, half),
            jax.ShapeDtypeStruct(router.shape, wide),
        ],
        scratch_shapes=[
            pltpu.VMEM(slotted, half),
            pltpu.VMEM((count, width), half),
            pltpu.VMEM((count, width), half),
            pltpu.VMEM((count, width), half),
            pltpu.VMEM(down.shape[1:], half),
            pltpu.VMEM((count, width), wide),
            pltpu.VMEM((count, width), wide),
            pltpu.VMEM((count, units), half),
            pltpu.VMEM((count, units), half),
            pltpu.VMEM((count, units), half),
            pltpu.VMEM((count, units), half),
            pltpu.VMEM((count, experts), wide),
            pltpu.VMEM(up.shape[1:], wide),
            pltpu.VMEM(down.shape[1:], wide),
            pltpu.VMEM(slotted, half),
            pltpu.SemaphoreType.DMA,
            pltpu.SemaphoreType.DMA,
            pltpu.SemaphoreType.DMA(every),
            pltpu.SemaphoreType.DMA(every),
        ]
        + route_semaphores(planes, members),
        compiler_params=pltpu.CompilerParams(
            collective_id=4, has_side_effects=True, vmem_limit_bytes=60 * 1024 * 1024
        ),
        cost_estimate=pl.CostEstimate(
            flops=24 * count * width * units,
            transcendentals=4 * count * units,
            bytes_accessed=3 * 10**7,
        ),
    )(row_slots, grad_rows, *weights, router, chosen)


def gradient_kernel(
    planes,
    side,
    delta_ref,
    conv_ref,
    grad_scan_ref,
    in_cols_ref,
    out_cols_ref,
    in_diag_ref,
    decay_log_ref,
    carried_ref,
    carried_back_ref,
    delta_pre_ref,
    delta_low_ref,
    conv_pre_ref,
    extended_ref,
    normed_ref,
    normed_gate_ref,
    layer_ref,
    rim_layer_ref,
    grad_resid_ref,
    delta_proj_ref,
    state_proj_ref,
    in_proj_ref,
    conv_weight_ref,
    vectors_ref,
    skip_grad_ref,
    norm_grad_ref,
    router_grad_ref,
    early_out_ref,
    early_gate_ref,
    returned_ref,
    far_up_ref,
    far_down_ref,
    in_grad_ref,
    total_out_ref,
    total_gate_ref,
    total_inner_ref,
    total_small_ref,
    landed_ref,
    near_up_ref,
    near_down_ref,
    grad_delta,
    grad_conv,
    grad_in,
    grad_out,
    grad_log,
    drive,
    kept,
    stack,
    slope_stack,
    low_grads,
    padded,
    slopes,
    small,
    rim_out,
    rim_in,
    rim_sent,
    rim_landed,
    in_part,
    part_loaded,
    given_inner,
    given_small,
    *rest,
):
    early_buffers, tail_buffers, small_buffers = rest[:12], rest[12:18], rest[18:24]
    swap_sent, swap_landed, rest = rest[24], rest[25], rest[26:]
    sums = Sums(planes, side, rest[:8], rest[8:16])
    routes = Routes(planes, 2 * side * side, *rest[16:19])
    tokens, inner_width = conv_ref.shape
    width = layer_ref.shape[1]
    low_rank = delta_low_ref.shape[1]
    states, taps = decay_log_ref.shape[0], conv_weight_ref.shape[0]
    sequences = extended_ref.shape[0]
    piece = tokens // sequences
    chips = side * side
    wide, half = jnp.float32, jnp.bfloat16
    skip_ref, mixer_gain_ref = vectors_ref.at[2:3], vectors_ref.at[3:4, :width]
    devices = 2 * chips * planes
    place = sums.plane * (2 * chips) + sums.member
    before, after = lax.rem(place + devices - 1, devices), lax.rem(place + 1, devices)
    barrier = pltpu.get_barrier_semaphore()
    for peer in (before, after):
        device = chain_device(peer, 2 * chips)
        pl.semaphore_signal(barrier, inc=1, device_id=device, device_id_type=MESH)
    pl.semaphore_signal(barrier, inc=1, device_id=neighbour_plane(), device_id_type=MESH)
    greeted = 3 + sums.signal_peers(barrier) + routes.signal_peers(barrier)
    pl.semaphore_wait(barrier, greeted)

    in_load = pltpu.make_async_copy(in_proj_ref.at[:, pl.ds(0, inner_width)], in_part, part_loaded)
    in_load.start()
    pair = range(2)
    given = (early_out_ref, early_gate_ref)
    results = (total_out_ref, total_gate_ref)
    stages = [tuple(early_buffers[2 * stage + i] for stage in range(6)) for i in pair]
    blocks = [result.at[sums.core, sums.first, sums.second] for result in results]
    swaps = [
        swapped(src, dst, swap_sent.at[i], swap_landed.at[i])
        for i, (src, dst) in enumerate([(far_up_ref, near_up_ref), (far_down_ref, near_down_ref)])
    ]
    for i in pair:
        sums.pair_half(i, given[i], stages[i][0]).start()
    routes.start(returned_ref, landed_ref, True)
    swaps[0].start()
    groups = inner_width // GROUP
    count = sequences * groups
    cols_each = piece // BLK

    def scan_group(g, carry):
        q, j = g // groups, lax.rem(g, groups)
        rows = pl.ds(pl.multiple_of(q * piece, piece), piece)
        lanes = pl.ds(pl.multiple_of(j * GROUP, GROUP), GROUP)
        cols = pl.ds(q * cols_each, cols_each)

        def middle():
            @pl.when(g == 0)
            def _():
                for i in pair:
                    sums.after_pair(i, given[i], *stages[i][:2])

            @pl.when(g == count // 2)
            def _():
                for i in pair:
                    sums.after_first(i, *stages[i][:4])

            @pl.when(g == count - 2)
            def _():
                for i in pair:
                    sums.after_second(i, *stages[i][2:6])

            @pl.when(g == count - 1)
            def _():
                for i in pair:
                    sums.after_planes(i, *stages[i][4:6], blocks[i])
                swaps[1].start()

        one = pl.ds(q, 1)
        backward_body(
            middle,
            j == 0,
            delta_ref.at[rows, lanes],
            conv_ref.at[rows, lanes],
            grad_scan_ref.at[rows, lanes],
            in_cols_ref.at[cols],
            out_cols_ref.at[cols],
            in_diag_ref.at[rows],
            decay_log_ref.at[:, lanes],
            carried_ref.at[one, :, lanes],
            carried_back_ref.at[one, :, lanes],
            grad_delta.at[rows, lanes],
            grad_conv.at[rows, lanes],
            grad_in.at[rows],
            grad_out.at[rows],
            grad_log.at[one, :, lanes],
            drive,
            kept,
            stack,
            slope_stack,
        )
        return carry

    lax.fori_loop(0, count, scan_group, 0)
    unit = LANE_UNIT
    low_grads[...] = jnp.zeros(low_grads.shape, wide)
    small[...] = jnp.zeros(small.shape, wide)
    at_delta = low_rank + 2 * states
    at_log = at_delta + low_rank
    at_conv = at_log + states
    at_end = at_conv + taps + 2

    def first(j, carry):
        at = lane_unit(j)
        slope = grad_delta[:, at] * jax.nn.sigmoid(delta_pre_ref[:, at])
        small[at_conv + taps + 1 : at_conv + taps + 2, at] = jnp.sum(slope, axis=0, keepdims=True)
        small[at_delta:at_log, at] = rows_dot(delta_low_ref[...], slope, lax.Precision.HIGHEST)
        low_grads[...] += two_part(slope, delta_proj_ref[:, at], ((1,), (1,)))
        return carry

    lax.fori_loop(0, inner_width // unit, first, 0)
    for i in pair:
        sums.planes_gathered(i, blocks[i])
        sums.gather_second_start(i, results[i])
    column = lax.broadcasted_iota(jnp.int32, grad_in.shape, 1) // states
    row = lax.rem(lax.broadcasted_iota(jnp.int32, grad_in.shape, 0), BLK)
    fold = jnp.where(
        lax.rem(lax.broadcasted_iota(jnp.int32, (grad_in.shape[1], states), 0), states)
        == lax.broadcasted_iota(jnp.int32, (grad_in.shape[1], states), 1),
        1.0,
        0.0,
    ).astype(half)

    def folded(ref):
        return two_part(jnp.where(column == row, ref[...], 0.0), fold, ((1,), (0,)))

    coefs = jnp.concatenate([low_grads[...], folded(grad_in), folded(grad_out)], axis=1)
    keep = jnp.where(place > 0, 1.0, 0.0)
    rim_out[...] = jnp.zeros(rim_out.shape, half)

    def dense(at):
        small[:at_delta, at] = rows_dot(coefs, conv_ref[:, at], lax.Precision.HIGHEST)
        through = two_part(coefs, state_proj_ref[:, at], ((1,), (0,)))
        through = through + grad_scan_ref[:, at] * skip_ref[:, at] + grad_conv[:, at]
        pre = conv_pre_ref[:, at]
        sigma = jax.nn.sigmoid(pre)
        through = through * (sigma * (1.0 + pre * (1.0 - sigma)))
        small[at_conv + taps : at_conv + taps + 1, at] = jnp.sum(through, axis=0, keepdims=True)
        for q in range(sequences):
            padded[q, :8] = jnp.zeros((8, unit), wide)
            padded[q, 8 + piece :] = jnp.zeros((8, unit), wide)
            padded[q, 8 : 8 + piece] = through[q * piece : (q + 1) * piece]
            result = jnp.zeros((piece, unit), wide)
            rim = jnp.zeros((8, unit), wide)
            for tap in range(taps):
                weight = conv_weight_ref[tap : tap + 1, at]
                shift = taps - 1 - tap
                result = result + weight * padded[q, 8 + shift : 8 + shift + piece]
                rim = rim + weight * padded[q, 8 - tap : 16 - tap]
            slopes[q * piece : (q + 1) * piece, at] = result.astype(half)
            rim_out[q, 8 - (taps - 1) :, at] = (rim[: taps - 1] * keep).astype(half)
            slopes[tokens + q * 8 : tokens + (q + 1) * 8, at] = rim_out[q, :, at]
        for tap in range(taps):
            start = 8 - (taps - 1) + tap
            product = jnp.zeros((1, unit), wide)
            for q in range(sequences):
                product = product + jnp.sum(
                    padded[q, 8 : 8 + piece] * extended_ref[q, start : start + piece, at],
                    axis=0,
                    keepdims=True,
                )
            small[at_conv + tap : at_conv + tap + 1, at] = product

    slabs = given_inner.shape[0]
    tall = width // chips
    size = tall // planes

    def tail_of(s):
        return [buffer.at[s] for buffer in tail_buffers]

    def after_tail_pair(s):
        sums.after_pair(2 + s, given_inner.at[s], *tail_of(s)[:2])

    def slab(s, carry):
        for c in range(2):
            at = lane_unit(c * slabs + s)
            dense(at)
            for m in range(chips):
                product = rows_dot(
                    normed_ref[:, m * tall : (m + 1) * tall], slopes[:, at]
                ).astype(half)
                for z in range(planes):
                    part = product[z * size : (z + 1) * size]
                    given_inner[s, c, m // side, m % side, z] = part
        sums.pair_half(2 + s, given_inner.at[s], tail_buffers[0].at[s]).start()

        @pl.when(s > 0)
        def _():
            after_tail_pair(s - 1)

        return carry

    lax.fori_loop(0, slabs, slab, 0)
    after_tail_pair(slabs - 1)
    rim_copy = pltpu.make_async_remote_copy(
        src_ref=rim_out,
        dst_ref=rim_in,
        send_sem=rim_sent,
        recv_sem=rim_landed,
        device_id=chain_device(before, 2 * chips),
        device_id_type=MESH,
    )
    rim_copy.start()
    sums.gather_across(0, results[0])
    in_load.wait()
    projected = cols_dot(slopes[...], in_part[...])
    normed_grad = normed_gate_ref[...] + projected[:tokens]

    def normal_of(values):
        scaling = lax.rsqrt(jnp.mean(values * values, axis=-1, keepdims=True) + EPSILON)
        return values * scaling, scaling

    normal, scaling = normal_of(layer_ref[...].astype(wide))
    gain_grad = jnp.sum(normed_grad * normal, axis=0, keepdims=True)
    for q in range(sequences):
        rim_normal, _ = normal_of(rim_layer_ref[q].astype(wide))
        rim_grad = projected[tokens + q * 8 : tokens + (q + 1) * 8]
        gain_grad = gain_grad + jnp.sum(rim_grad * rim_normal, axis=0, keepdims=True)
    log_total = grad_log[0]
    for q in range(1, sequences):
        log_total = log_total + grad_log[q]
    small[at_log:at_conv] = log_total
    small[at_end : at_end + 1] = skip_grad_ref[...]
    small[at_end + 1 : at_end + 2, :width] = gain_grad
    small[at_end + 1 : at_end + 2, width:] = norm_grad_ref[...]
    for k in range(router_grad_ref.shape[0]):
        line = at_end + 2 + k // 2
        small[line : line + 1, (k % 2) * width : (k % 2 + 1) * width] = router_grad_ref[k : k + 1]
    low = given_small.shape[4]
    for c in range(2):
        for m in range(chips):
            for z in range(planes):
                line = (m * planes + z) * low
                given_small[c, m // side, m % side, z] = small[
                    line : line + low, c * width : (c + 1) * width
                ].astype(half)
    last = 2 + slabs
    every = range(slabs)
    sums.pair_half(last, given_small, small_buffers[0]).start()
    for s in every:
        sums.after_first(2 + s, *tail_of(s)[:4])
    sums.after_pair(last, given_small, *small_buffers[:2])
    sums.gather_across(1, results[1])
    weighted = normed_grad * mixer_gain_ref[...]
    in_grad_ref[...] = grad_resid_ref[...] + scaling * (
        weighted - normal * jnp.mean(weighted * normal, axis=-1, keepdims=True)
    )
    for s in every:
        sums.after_second(2 + s, *tail_of(s)[2:6])
    sums.after_first(last, *small_buffers[:4])
    tails = [total_inner_ref.at[s] for s in every] + [total_small_ref]
    tail_blocks = [total.at[sums.core, sums.first, sums.second] for total in tails]
    for s in every:
        sums.after_planes(2 + s, *tail_of(s)[4:6], tail_blocks[s])
    sums.after_second(last, *small_buffers[2:6])
    sums.gather_pass(0, results[0])
    for s in every:
        sums.planes_gathered(2 + s, tail_blocks[s])
        sums.gather_second_start(2 + s, tails[s])
    sums.after_planes(last, *small_buffers[4:6], tail_blocks[slabs])
    for s in every:
        sums.gather_across(2 + s, tails[s])
    sums.planes_gathered(last, tail_blocks[slabs])
    sums.gather_second_start(last, total_small_ref)
    sums.gather_pass(1, results[1])
    rim_copy.wait()
    keep_last = jnp.where(place < devices - 1, 1.0, 0.0)
    for q in range(sequences):
        rows = slice((q + 1) * piece - 8, (q + 1) * piece)
        added = cols_dot(rim_in[q], in_part[...]) * keep_last
        fixed = (normed_grad[rows] + added) * mixer_gain_ref[...]
        mean = jnp.mean(fixed * normal[rows], axis=-1, keepdims=True)
        in_grad_ref[rows, :] = grad_resid_ref[rows, :] + scaling[rows] * (
            fixed - normal[rows] * mean
        )
    sums.gather_across(last, total_small_ref)
    for s in every:
        sums.gather_pass(2 + s, tails[s])
    sums.gather_pass(last, total_small_ref)
    routes.wait(returned_ref, landed_ref, True)
    for swap in swaps:
        swap.wait()
    ends = [(i, stages[i], blocks[i], results[i]) for i in pair]
    ends += [(2 + s, tail_of(s), tail_blocks[s], tails[s]) for s in every]
    ends += [(last, small_buffers, tail_blocks[slabs], total_small_ref)]
    for i, buffers, block, result in ends:
        sums.scatter_sent(i, *buffers, block)
        sums.gather_end(i, result)


def all_gradients(operands, small_height, side):
    planes = lax.axis_size("seq")
    tokens, inner_width = operands[1].shape
    width = operands[15].shape[1]
    states, low_rank = operands[6].shape[0], operands[10].shape[1]
    sequences = operands[7].shape[0]
    piece = tokens // sequences
    low = -(-small_height // (side * side * planes))
    lead = (2, side, side, planes)
    big = operands[26].shape
    slabs = width // LANE_UNIT
    inner = (slabs,) + lead + (big[4], LANE_UNIT)
    little = lead + (low, width)
    vmem, anywhere = (pl.BlockSpec(memory_space=space) for space in (pltpu.VMEM, pl.ANY))
    half, wide = jnp.bfloat16, jnp.float32
    token_wide = pltpu.VMEM((tokens, inner_width), wide)
    narrow = pltpu.VMEM((tokens, BLK * states), wide)
    steps = pltpu.VMEM((piece, states, GROUP), wide)
    stack = pltpu.VMEM((BLK * states, GROUP), half)
    rim = pltpu.VMEM((sequences, 8, inner_width), half)
    tail_shapes = [value.shape for value in scatter_buffers([inner[5:]], planes, side)]
    moved = [jax.ShapeDtypeStruct(value.shape, half) for value in operands[28:]]
    semaphores = stage_semaphores(3 + slabs, planes, side)
    return pl.pallas_call(
        functools.partial(gradient_kernel, planes, side),
        name="backward_gradients",
        in_specs=[vmem] * 20 + [anywhere] + [vmem] * 7 + [anywhere] * 3,
        out_specs=[vmem] * 5 + [anywhere] * 3,
        out_shape=[jax.ShapeDtypeStruct((tokens, width), wide)]
        + [jax.ShapeDtypeStruct(shape, half) for shape in (big, big, inner, little)]
        + moved,
        scratch_shapes=[
            token_wide,
            token_wide,
            narrow,
            narrow,
            pltpu.VMEM((sequences, states, inner_width), wide),
            pltpu.VMEM((piece, GROUP), wide),
            steps,
            stack,
            stack,
            pltpu.VMEM((tokens, low_rank), wide),
            pltpu.VMEM((sequences, piece + 16, LANE_UNIT), wide),
            pltpu.VMEM((tokens + 8 * sequences, inner_width), half),
            pltpu.VMEM((low * side * side * planes, inner_width), wide),
            rim,
            rim,
            pltpu.SemaphoreType.DMA,
            pltpu.SemaphoreType.DMA,
            pltpu.VMEM((width, inner_width), half),
            pltpu.SemaphoreType.DMA,
            pltpu.VMEM(inner, half),
            pltpu.VMEM(little, half),
        ]
        + scatter_buffers([big[4:], big[4:]], planes, side)
        + [pltpu.VMEM((slabs,) + shape, half) for shape in tail_shapes]
        + scatter_buffers([little[4:]], planes, side)
        + [pltpu.SemaphoreType.DMA((2,)), pltpu.SemaphoreType.DMA((2,))]
        + semaphores
        + semaphores
        + route_semaphores(planes, 2 * side * side),
        compiler_params=pltpu.CompilerParams(
            collective_id=3, has_side_effects=True, vmem_limit_bytes=63 * 1024 * 1024
        ),
        cost_estimate=pl.CostEstimate(flops=10**8, transcendentals=0, bytes_accessed=2 * 10**8),
    )(*operands)


def on_device(
    layer_in,
    mixer_gain,
    in_proj,
    conv_weight,
    conv_bias,
    state_proj,
    delta_proj,
    delta_bias,
    decay_log,
    skip_gain,
    out_proj,
    expert_norm,
    router_weight,
    expert_up,
    expert_down,
    expert_ids,
    capacity_slot,
    out_grad,
):
    sequences, piece_len, width = layer_in.shape
    tokens = sequences * piece_len
    taps, inner_width = conv_weight.shape
    low_rank = delta_proj.shape[0]
    states = decay_log.shape[0]
    experts = router_weight.shape[1]
    senders = lax.axis_size("exp")
    capacity = (5 * tokens + 4 * experts - 1) // (4 * experts)
    planes = lax.axis_size("seq")
    hops = planes // 2
    flat_ids = expert_ids.reshape(1, tokens)
    flat_slot = capacity_slot.reshape(1, tokens)
    target = jnp.where(flat_slot < capacity, flat_ids * capacity + flat_slot, experts * capacity)
    slot_rows = jnp.arange(experts * capacity, dtype=jnp.int32)
    picks = (slot_rows[:, None] == target).astype(jnp.bfloat16)
    state_rows = sequences * states // senders
    first_row = lax.rem(lax.axis_index("exp") * state_rows, states)
    own_log = lax.dynamic_slice(decay_log, (first_row, 0), (state_rows, inner_width))
    norms = jnp.concatenate([mixer_gain, expert_norm])
    vectors = jnp.stack([conv_bias, delta_bias, skip_gain, norms])
    (
        normed_half,
        extended,
        gate_half,
        conv_pre,
        conv_flat,
        delta_pre,
        delta,
        delta_low,
        in_cols,
        out_cols,
        in_diag,
        delta_sum,
        carried,
        mixer_pre,
        mixed,
        resid,
        row_slots,
        grad_rows,
        near_up,
        near_half,
        rim_layer,
    ) = forward(
        [
            layer_in.reshape(tokens, width),
            out_grad.reshape(tokens, width),
            target,
            vectors,
            in_proj,
            conv_weight,
            state_proj.T,
            delta_proj,
            decay_log,
            own_log,
            out_proj,
            expert_up,
            expert_down,
        ],
        capacity,
        states,
        sequences,
        low_rank,
        experts,
    )
    gate_act = jax.nn.silu(gate_half)
    scaling_two = lax.rsqrt(jnp.mean(resid * resid, axis=-1, keepdims=True) + EPSILON)
    weights = [expert_up, expert_down, near_up, near_half]
    chosen = (
        jnp.arange(experts, dtype=jnp.int32) == lax.axis_index("exp")
    ).astype(jnp.float32)[None, :]
    expert_out, back_rows, grad_up, grad_down, far_up, far_down, grad_router = expert_apply(
        row_slots, grad_rows, weights, router_weight.T, chosen
    )
    grad_routed = rows_dot(
        jnp.concatenate([picks] * hops, axis=0), back_rows.reshape(hops * senders * capacity, width)
    )
    grad_top = out_grad.reshape(tokens, width).astype(jnp.float32)
    grad_resid_norm, grad_expert_norm = norm_backward(resid, scaling_two, expert_norm, grad_routed)
    grad_resid = grad_top + grad_resid_norm
    grad_mixer = grad_resid.astype(jnp.bfloat16)
    grad_out_proj = rows_dot(mixed, grad_mixer)
    grad_mixed = cols_dot(grad_mixer, out_proj)
    grad_scan = grad_mixed * gate_act
    grad_gate_half = grad_mixed * mixer_pre * silu_slope(gate_half)
    grad_gate_half = grad_gate_half.astype(jnp.bfloat16)
    grad_in_gate = rows_dot(normed_half[:tokens], grad_gate_half)
    grad_normed_gate = cols_dot(grad_gate_half, in_proj[:, inner_width:])
    grad_skip_gain = jnp.sum(grad_scan * conv_flat, axis=0, keepdims=True)
    (gradient_first,) = scan_call(
        back_summary_kernel,
        "back_summary",
        sequences,
        states,
        [("wide", delta), ("wide", grad_scan), ("cols", out_cols), ("rates", decay_log)],
        ["state"],
        [],
    )
    carried_back = exchange(gradient_first, delta_sum, own_log)
    side = math.isqrt(senders // 2)
    big = (2, side, side, planes, inner_width // (senders * planes), width)

    def as_rows(values):
        blocks = values.shape[1] // width
        return jnp.concatenate(
            [values[:, at * width : (at + 1) * width] for at in range(blocks)], axis=0
        ).astype(jnp.bfloat16)

    early = [
        grad_out_proj.astype(jnp.bfloat16).reshape(big),
        as_rows(grad_in_gate).reshape(big),
    ]
    heights = [low_rank + 2 * states, low_rank, states, taps, 1, 1, 1, 1, experts // 2]
    in_grad, sum_out, sum_gate, sum_inner, sum_small, back_out, near_up, near_down = all_gradients(
        [
            delta,
            conv_flat,
            grad_scan,
            in_cols,
            out_cols,
            in_diag,
            decay_log,
            carried,
            carried_back,
            delta_pre,
            delta_low,
            conv_pre,
            extended,
            normed_half,
            grad_normed_gate,
            layer_in.reshape(tokens, width),
            rim_layer,
            grad_resid,
            delta_proj,
            state_proj.T,
            in_proj,
            conv_weight,
            vectors,
            grad_skip_gain,
            grad_expert_norm,
            grad_router,
        ]
        + early
        + [expert_out, far_up, far_down],
        sum(heights),
        side,
    )
    grad_up_own = grad_up + near_up.astype(jnp.float32)
    grad_down_own = grad_down + near_down.astype(jnp.float32)
    token_out = rows_dot(
        jnp.concatenate([picks] * hops, axis=0), back_out.reshape(hops * senders * capacity, width)
    )
    layer_out = (resid + token_out).astype(jnp.bfloat16).reshape(sequences, piece_len, width)
    in_grad = in_grad.reshape(sequences, piece_len, width)
    rows_of = (inner_width, width)
    slabs = width // LANE_UNIT
    by_slab = sum_inner.reshape(slabs, 2, width, LANE_UNIT)
    inner_parts = [by_slab[s, c] for c in range(2) for s in range(slabs)]
    grad_in_proj = jnp.concatenate(
        inner_parts + [sum_gate[c].reshape(width, width) for c in range(2)], axis=1
    ).astype(jnp.float32)
    small_halves = sum_small.reshape(2, -1, width)
    small_wide = jnp.concatenate([small_halves[0], small_halves[1]], axis=1).astype(jnp.float32)
    offsets = [sum(heights[:at]) for at in range(len(heights) + 1)]
    pieces = [small_wide[offsets[at] : offsets[at + 1]] for at in range(len(heights))]
    summed = (
        pieces[7][0, :width],
        grad_in_proj,
        pieces[3],
        pieces[4][0],
        pieces[0].T,
        pieces[1],
        pieces[5][0],
        pieces[2],
        pieces[6][0],
        sum_out.reshape(rows_of).astype(jnp.float32),
        pieces[7][0, width:],
        pieces[8].reshape(experts, width).T,
    )
    return (
        layer_out,
        in_grad,
        summed[0],
        summed[1],
        summed[2],
        summed[3],
        summed[4],
        summed[5],
        summed[6],
        summed[7],
        summed[8],
        summed[9],
        summed[10],
        summed[11],
        grad_up_own,
        grad_down_own,
    )


def solution(mesh):
    placed = (
        P(None, ("seq", "exp"), None),
        P(),
        P(),
        P(),
        P(),
        P(),
        P(),
        P(),
        P(),
        P(),
        P(),
        P(),
        P(),
        P("exp", None, "seq"),
        P("exp", "seq", None),
        P(None, ("seq", "exp")),
        P(None, ("seq", "exp")),
        P(None, ("seq", "exp"), None),
    )
    return jax.shard_map(
        on_device,
        mesh=mesh,
        in_specs=placed,
        out_specs=(
            P(None, ("seq", "exp"), None),
            P(None, ("seq", "exp"), None),
            P(),
            P(),
            P(),
            P(),
            P(),
            P(),
            P(),
            P(),
            P(),
            P(),
            P(),
            P(),
            P("exp", None, "seq"),
            P("exp", "seq", None),
        ),
        check_vma=False,
    )
```

```python
import functools
import math

import jax
import jax.numpy as jnp
from jax import lax
from jax.experimental import pallas as pl
from jax.experimental.pallas import tpu as pltpu
from jax.sharding import PartitionSpec as P

BLK = 16
LANES = 128
GROUP = 512
LOG2E = 1.4426950408889634
LN2 = 0.6931471805599453
VMEM_BYTES = 50 * 1024 * 1024


EPSILON = 1e-05


def half_dot(left, right):
    return jnp.dot(left, right, preferred_element_type=jnp.float32)


def rows_dot(left, right, precision=None):
    return lax.dot_general(
        left,
        right,
        (((0,), (0,)), ((), ())),
        precision=precision,
        preferred_element_type=jnp.float32,
    )


def cols_dot(left, right, precision=None):
    return lax.dot_general(
        left,
        right,
        (((1,), (1,)), ((), ())),
        precision=precision,
        preferred_element_type=jnp.float32,
    )


def norm_backward(values, scaling, gain_vec, incoming):
    normal = values * scaling
    weighted = incoming * gain_vec
    grad_gain = jnp.sum(incoming * normal, axis=0, keepdims=True)
    grad_values = scaling * (
        weighted - normal * jnp.mean(weighted * normal, axis=-1, keepdims=True)
    )
    return (grad_values, grad_gain)


def silu_slope(values):
    sigma = jax.nn.sigmoid(values)
    return sigma * (1.0 + values * (1.0 - sigma))


def lane_parts(ref, k, states):
    width = ref.shape[-1]
    return [
        jnp.broadcast_to(ref[k : k + 1, at : at + LANES], (states, LANES))
        for at in range(0, width, LANES)
    ]


def block_of(ref, i):
    return ref.at[pl.ds(pl.multiple_of(i * BLK, BLK), BLK), :]


def rows_of_block(ref, i, states):
    size = BLK * states
    return ref.at[pl.ds(pl.multiple_of(i * size, size), size), :]


def rates_of(log_ref):
    rates = -jnp.exp(log_ref[...]) * LOG2E
    return [rates[:, at : at + LANES] for at in range(0, rates.shape[1], LANES)]


def first_pass_kernel(delta_ref, conv_ref, in_ref, log_ref, end_ref, drive):
    steps, width = delta_ref.shape
    states = log_ref.shape[0]
    rates = rates_of(log_ref)
    drive[...] = delta_ref[...] * conv_ref[...]

    def block(i, state):
        state = list(state)
        inwards = in_ref[i]
        for k in range(BLK):
            inward = jnp.broadcast_to(inwards[:, k : k + 1], (states, LANES))
            deltas = lane_parts(block_of(delta_ref, i), k, states)
            drives = lane_parts(block_of(drive, i), k, states)
            for j in range(width // LANES):
                state[j] = jnp.exp2(deltas[j] * rates[j]) * state[j] + inward * drives[j]
        return tuple(state)

    zero = tuple(jnp.zeros((states, LANES), jnp.float32) for _ in range(width // LANES))
    last = lax.fori_loop(0, steps // BLK, block, zero)
    for j in range(width // LANES):
        end_ref[0, :, j * LANES : (j + 1) * LANES] = last[j]


def second_pass_kernel(
    delta_ref, conv_ref, in_ref, log_ref, start_ref, out_ref, rest_ref, scanned_ref, drive, stack
):
    steps, width = delta_ref.shape
    states = log_ref.shape[0]
    rates = rates_of(log_ref)
    drive[...] = delta_ref[...] * conv_ref[...]

    def block(i, state):
        state = list(state)
        inwards = in_ref[i]
        kept = rows_of_block(stack, i, states)
        for k in range(BLK):
            inward = jnp.broadcast_to(inwards[:, k : k + 1], (states, LANES))
            deltas = lane_parts(block_of(delta_ref, i), k, states)
            drives = lane_parts(block_of(drive, i), k, states)
            for j in range(width // LANES):
                state[j] = jnp.exp2(deltas[j] * rates[j]) * state[j] + inward * drives[j]
                at = slice(j * LANES, (j + 1) * LANES)
                kept[k * states : (k + 1) * states, at] = state[j].astype(jnp.bfloat16)
        return tuple(state)

    begin = tuple(start_ref[0, :, j * LANES : (j + 1) * LANES] for j in range(width // LANES))
    lax.fori_loop(0, steps // BLK, block, begin)
    for i in range(steps // BLK):
        rows = slice(i * BLK, (i + 1) * BLK)
        both = jnp.concatenate([out_ref[rows, :], rest_ref[rows, :]], axis=0)
        product = half_dot(both, stack[i * BLK * states : (i + 1) * BLK * states, :])
        scanned_ref[rows, :] = product[:BLK] + product[BLK:]


def back_summary_kernel(delta_ref, grad_ref, out_ref, log_ref, end_ref):
    steps, width = delta_ref.shape
    states = log_ref.shape[0]
    rates = rates_of(log_ref)
    blocks = steps // BLK

    def block(i, state):
        state = list(state)
        outwards = out_ref[blocks - 1 - i]
        for k in reversed(range(BLK)):
            outward = jnp.broadcast_to(outwards[:, k : k + 1], (states, LANES))
            deltas = lane_parts(block_of(delta_ref, blocks - 1 - i), k, states)
            grads = lane_parts(block_of(grad_ref, blocks - 1 - i), k, states)
            for j in range(width // LANES):
                state[j] = jnp.exp2(deltas[j] * rates[j]) * (state[j] + outward * grads[j])
        return tuple(state)

    zero = tuple(jnp.zeros((states, LANES), jnp.float32) for _ in range(width // LANES))
    last = lax.fori_loop(0, blocks, block, zero)
    for j in range(width // LANES):
        end_ref[0, :, j * LANES : (j + 1) * LANES] = last[j]


def backward_body(
    middle,
    first,
    delta_ref,
    conv_ref,
    grad_ref,
    in_ref,
    out_ref,
    in_diag_ref,
    log_ref,
    start_ref,
    finish_ref,
    grad_delta_ref,
    grad_conv_ref,
    grad_in_ref,
    grad_out_ref,
    grad_log_ref,
    drive,
    carried,
    stack,
    slope,
):
    steps, width = delta_ref.shape
    states = log_ref.shape[0]
    parts = width // LANES
    rates = rates_of(log_ref)
    blocks = steps // BLK
    drive[...] = delta_ref[...] * conv_ref[...]

    def forward(i, state):
        state = list(state)
        inwards = in_ref[i]
        for k in range(BLK):
            t = i * BLK + k
            inward = jnp.broadcast_to(inwards[:, k : k + 1], (states, LANES))
            deltas = lane_parts(block_of(delta_ref, i), k, states)
            drives = lane_parts(block_of(drive, i), k, states)
            for j in range(parts):
                at = slice(j * LANES, (j + 1) * LANES)
                decay = jnp.exp2(deltas[j] * rates[j])
                kept = decay * state[j]
                carried[t, :, at] = kept
                state[j] = kept + inward * drives[j]
                stack[k * states : (k + 1) * states, at] = state[j].astype(jnp.bfloat16)
        rows = pl.ds(pl.multiple_of(i * BLK, BLK), BLK)
        partial = cols_dot(grad_ref[rows, :].astype(jnp.bfloat16), stack[...])

        @pl.when(first)
        def _():
            grad_out_ref[rows, :] = partial

        @pl.when(jnp.logical_not(first))
        def _():
            grad_out_ref[rows, :] += partial

        return tuple(state)

    begin = tuple(start_ref[0, :, j * LANES : (j + 1) * LANES] for j in range(parts))
    lax.fori_loop(0, blocks, forward, begin)
    middle()
    column = lax.broadcasted_iota(jnp.int32, (BLK, BLK * states), 1) // states
    row = lax.broadcasted_iota(jnp.int32, (BLK, BLK * states), 0)
    ones = jnp.where(column == row, 1.0, 0.0).astype(jnp.bfloat16)

    def backward(i, state):
        adjoint, gathered = list(state[:parts]), list(state[parts:])
        outwards = out_ref[blocks - 1 - i]
        for k in reversed(range(BLK)):
            t = (blocks - 1 - i) * BLK + k
            outward = jnp.broadcast_to(outwards[:, k : k + 1], (states, LANES))
            deltas = lane_parts(block_of(delta_ref, blocks - 1 - i), k, states)
            grads = lane_parts(block_of(grad_ref, blocks - 1 - i), k, states)
            for j in range(parts):
                at = slice(j * LANES, (j + 1) * LANES)
                whole = adjoint[j] + outward * grads[j]
                exponent = whole * carried[t, :, at]
                gathered[j] = gathered[j] + exponent * deltas[j]
                slope[k * states : (k + 1) * states, at] = (exponent * rates[j]).astype(
                    jnp.bfloat16
                )
                stack[k * states : (k + 1) * states, at] = whole.astype(jnp.bfloat16)
                adjoint[j] = jnp.exp2(deltas[j] * rates[j]) * whole
        rows = pl.ds(pl.multiple_of((blocks - 1 - i) * BLK, BLK), BLK)
        driven = jnp.dot(in_diag_ref[rows, :], stack[...], preferred_element_type=jnp.float32)
        summed = jnp.dot(ones, slope[...], preferred_element_type=jnp.float32) * LN2
        grad_delta_ref[rows, :] = summed + driven * conv_ref[rows, :]
        grad_conv_ref[rows, :] = driven * delta_ref[rows, :]
        partial = cols_dot(drive[rows, :].astype(jnp.bfloat16), stack[...])

        @pl.when(first)
        def _():
            grad_in_ref[rows, :] = partial

        @pl.when(jnp.logical_not(first))
        def _():
            grad_in_ref[rows, :] += partial

        return tuple(adjoint + gathered)

    ends = tuple(finish_ref[0, :, j * LANES : (j + 1) * LANES] for j in range(parts))
    zero = tuple(jnp.zeros((states, LANES), jnp.float32) for _ in range(parts))
    last = lax.fori_loop(0, blocks, backward, ends + zero)
    for j in range(parts):
        grad_log_ref[0, :, j * LANES : (j + 1) * LANES] = last[parts + j] * rates[j] * LN2


def scan_call(kernel, name, sequences, states, operands, results, scratch):
    tokens, width = next(value.shape for kind, value in operands if kind == "wide")
    steps = tokens // sequences
    specs = {
        "wide": pl.BlockSpec((steps, GROUP), lambda q, j: (q, j)),
        "cols": pl.BlockSpec((steps // BLK, states, BLK), lambda q, j: (q, 0, 0)),
        "narrow": pl.BlockSpec((steps, BLK * states), lambda q, j: (q, 0)),
        "rates": pl.BlockSpec((states, GROUP), lambda q, j: (0, j)),
        "state": pl.BlockSpec((1, states, GROUP), lambda q, j: (q, 0, j)),
    }
    shapes = {
        "wide": (tokens, width),
        "narrow": (tokens, BLK * states),
        "state": (sequences, states, width),
    }
    in_specs = [specs[kind] for kind, _ in operands]
    out_specs = [specs[kind] for kind in results]
    out_shape = [jax.ShapeDtypeStruct(shapes[kind], jnp.float32) for kind in results]
    return pl.pallas_call(
        kernel,
        name=name,
        grid=(sequences, width // GROUP),
        in_specs=in_specs,
        out_specs=out_specs,
        out_shape=out_shape,
        scratch_shapes=scratch,
        compiler_params=pltpu.CompilerParams(
            dimension_semantics=("arbitrary", "arbitrary"),
            vmem_limit_bytes=VMEM_BYTES,
        ),
        cost_estimate=pl.CostEstimate(
            flops=20 * tokens * states * width,
            transcendentals=tokens * states * width,
            bytes_accessed=16 * tokens * width,
        ),
    )(*(value for _, value in operands))


MESH = pl.DeviceIdType.MESH


def remote(src, dst, send, arrive, axis, peer):
    return pltpu.make_async_remote_copy(
        src_ref=src,
        dst_ref=dst,
        send_sem=send,
        recv_sem=arrive,
        device_id={axis: peer},
        device_id_type=MESH,
    )


def greet(axes):
    barrier = pltpu.get_barrier_semaphore()
    total = 0
    for axis, size in axes:
        mine = lax.axis_index(axis)
        for k in range(1, size):
            pl.semaphore_signal(
                barrier, inc=1, device_id={axis: lax.rem(mine + k, size)}, device_id_type=MESH
            )
        total += size - 1
    pl.semaphore_wait(barrier, total)


def exchange_body(
    after_first,
    after_second,
    reverse,
    planes,
    members,
    end_ref,
    sum_ref,
    log_ref,
    carry_ref,
    packed,
    landed,
    summary,
    totals,
    starts,
    carries,
    send_one,
    recv_one,
    send_two,
    recv_two,
    send_three,
    recv_three,
):
    sequences, states, width = end_ref.shape
    rows = sequences * states // members
    plane, member = lax.axis_index("seq"), lax.axis_index("exp")
    own = lax.rem(member, states // rows)
    logs = jnp.zeros((rows, width), jnp.float32)
    for i in range(states // rows):
        logs = jnp.where(own == i, log_ref[i * rows : (i + 1) * rows], logs)
    rates = -jnp.exp(logs)
    for i in range(members):
        q, n = (i * rows) // states, (i * rows) % states
        packed[i, :rows] = end_ref[q, n : n + rows]
        packed[i, rows:] = sum_ref[q : q + 1]
    for k in range(1, members):
        other = lax.rem(member + k, members)
        remote(
            packed.at[other],
            landed.at[member],
            send_one.at[k],
            recv_one.at[member],
            "exp",
            other,
        ).start()
    after_first()
    landed[member] = packed[member]
    for k in range(1, members):
        other = lax.rem(member + k, members)
        remote(
            packed.at[other], landed.at[other], send_one.at[k], recv_one.at[other], "exp", other
        ).wait()
    order = range(members)[::-1] if reverse else range(members)
    plane_order = range(planes)[::-1] if reverse else range(planes)

    def through(piece, before):
        return jnp.exp(piece[rows:] * rates) * before + piece[:rows]

    state = jnp.zeros((rows, width), jnp.float32)
    total = jnp.zeros((1, width), jnp.float32)
    for i in order:
        piece = landed[i]
        state = through(piece, state)
        total = total + piece[rows:]
    summary[:rows] = state
    summary[rows:] = total
    for k in range(1, planes):
        other = lax.rem(plane + k, planes)
        remote(
            summary, totals.at[plane], send_two.at[k], recv_two.at[plane], "seq", other
        ).start()
    totals[plane] = summary[...]
    for k in range(1, planes):
        other = lax.rem(plane + k, planes)
        remote(summary, totals.at[other], send_two.at[k], recv_two.at[other], "seq", other).wait()
    after_second()
    state = jnp.zeros((rows, width), jnp.float32)
    for s in plane_order:
        reached = plane < s if reverse else plane > s
        state = jnp.where(reached, through(totals[s], state), state)
    for i in order:
        starts[i] = state
        state = through(landed[i], state)
    for k in range(1, members):
        other = lax.rem(member + k, members)
        remote(
            starts.at[other],
            carries.at[member],
            send_three.at[k],
            recv_three.at[member],
            "exp",
            other,
        ).start()
    carries[member] = starts[member]
    for k in range(1, members):
        other = lax.rem(member + k, members)
        remote(
            starts.at[other],
            carries.at[other],
            send_three.at[k],
            recv_three.at[other],
            "exp",
            other,
        ).wait()
    for i in range(members):
        q, n = (i * rows) // states, (i * rows) % states
        carry_ref[q, n : n + rows] = carries[i]


def exchange_kernel(reverse, planes, members, *refs):
    greet((("seq", planes), ("exp", members)))
    exchange_body(lambda: None, lambda: None, reverse, planes, members, *refs)


def exchange_scratch(planes, members, rows, width):
    piece = (rows + 1, width)
    return [
        pltpu.VMEM((members,) + piece, jnp.float32),
        pltpu.VMEM((members,) + piece, jnp.float32),
        pltpu.VMEM(piece, jnp.float32),
        pltpu.VMEM((planes,) + piece, jnp.float32),
        pltpu.VMEM((members, rows, width), jnp.float32),
        pltpu.VMEM((members, rows, width), jnp.float32),
        pltpu.SemaphoreType.DMA((members,)),
        pltpu.SemaphoreType.DMA((members,)),
        pltpu.SemaphoreType.DMA((planes,)),
        pltpu.SemaphoreType.DMA((planes,)),
        pltpu.SemaphoreType.DMA((members,)),
        pltpu.SemaphoreType.DMA((members,)),
    ]


def exchange(local_end, delta_sum, decay_log):
    planes, members = lax.axis_size("seq"), lax.axis_size("exp")
    sequences, states, width = local_end.shape
    rows = sequences * states // members
    vmem = pl.BlockSpec(memory_space=pltpu.VMEM)
    return pl.pallas_call(
        functools.partial(exchange_kernel, True, planes, members),
        name="state_exchange_back",
        in_specs=[vmem] * 3,
        out_specs=vmem,
        out_shape=jax.ShapeDtypeStruct(local_end.shape, jnp.float32),
        scratch_shapes=exchange_scratch(planes, members, rows, width),
        compiler_params=pltpu.CompilerParams(
            collective_id=2, has_side_effects=True, vmem_limit_bytes=VMEM_BYTES
        ),
        cost_estimate=pl.CostEstimate(flops=10**6, transcendentals=10**5, bytes_accessed=2 * 10**7),
    )(local_end, delta_sum, decay_log)


class Sums:
    def __init__(self, planes, side, sends, arrivals):
        self.planes, self.side = planes, side
        self.plane, self.member = lax.axis_index("seq"), lax.axis_index("exp")
        chip, self.core = self.member // 2, lax.rem(self.member, 2)
        high, low = chip // side, lax.rem(chip, side)
        self.first = low + (high - low) * self.core
        self.second = high + (low - high) * self.core
        self.partner = self.member + 1 - 2 * self.core
        self.sends, self.arrivals = sends, arrivals

    def chip_at(self, first, second):
        low = first + (second - first) * self.core
        high = second + (first - second) * self.core
        return (high * self.side + low) * 2 + self.core

    def first_peer(self, k):
        other = lax.rem(self.first + k, self.side)
        return other, self.chip_at(other, self.second)

    def second_peer(self, k):
        other = lax.rem(self.second + k, self.side)
        return other, self.chip_at(self.first, other)

    def plane_peer(self, k):
        return lax.rem(self.plane + k, self.planes)

    def signal_peers(self, barrier):
        peers = [{"exp": self.partner}]
        peers += [{"exp": self.first_peer(k)[1]} for k in range(1, self.side)]
        peers += [{"exp": self.second_peer(k)[1]} for k in range(1, self.side)]
        peers += [{"seq": self.plane_peer(k)} for k in range(1, self.planes)]
        for peer in peers:
            pl.semaphore_signal(barrier, inc=1, device_id=peer, device_id_type=MESH)
        return len(peers)

    def move(self, stage, at, slot, src, dst, axis, peer):
        return remote(
            src, dst, self.sends[stage].at[at], self.arrivals[stage].at[slot], axis, peer
        )

    def pair_half(self, i, given, half):
        return self.move(0, i, i, given.at[1 - self.core], half, "exp", self.partner)

    def scatter_first(self, i, k, half, slots, arriving):
        other, device = self.first_peer(k)
        slot = other if arriving else self.first
        return self.move(1, (i, k), (i, slot), half.at[other], slots.at[slot], "exp", device)

    def scatter_second(self, i, k, quarter, slots, arriving):
        other, device = self.second_peer(k)
        slot = other if arriving else self.second
        return self.move(2, (i, k), (i, slot), quarter.at[other], slots.at[slot], "exp", device)

    def scatter_plane(self, i, k, eighth, slots, arriving):
        other = self.plane_peer(k)
        slot = other if arriving else self.plane
        return self.move(3, (i, k), (i, slot), eighth.at[other], slots.at[slot], "seq", other)

    def gather_plane(self, i, k, block, arriving):
        other = self.plane_peer(k)
        slot = other if arriving else self.plane
        return self.move(
            4, (i, k), (i, slot), block.at[self.plane], block.at[slot], "seq", other
        )

    def gather_second(self, i, k, result, arriving):
        other, device = self.second_peer(k)
        slot = other if arriving else self.second
        row = result.at[self.core, self.first]
        return self.move(5, (i, k), (i, slot), row.at[self.second], row.at[slot], "exp", device)

    def gather_first(self, i, k, result, arriving):
        other, device = self.first_peer(k)
        slot = other if arriving else self.first
        own = result.at[self.core]
        return self.move(6, (i, k), (i, slot), own.at[self.first], own.at[slot], "exp", device)

    def pair_gather(self, i, k, result, arriving):
        other = lax.rem(self.first + k, self.side)
        low = lax.rem(self.partner // 2, self.side)
        theirs = low + (self.partner // (2 * self.side) - low) * (1 - self.core)
        other = lax.rem(theirs + k, self.side) if arriving else other
        half = 1 - self.core if arriving else self.core
        mine = result.at[self.core, lax.rem(self.first + k, self.side)]
        return self.move(7, (i, k), (i, k), mine, result.at[half, other], "exp", self.partner)

    def after_pair(self, i, given, half, slots):
        self.pair_half(i, given, half).wait()
        own = self.core
        for at in range(self.side):
            for to in range(self.side):
                both = given[own, at, to].astype(jnp.float32) + half[at, to].astype(jnp.float32)
                half[at, to] = both.astype(jnp.bfloat16)
        for k in range(1, self.side):
            self.scatter_first(i, k, half, slots, False).start()
        slots[self.first] = half[self.first]

    def after_first(self, i, half, slots, quarter, slots_two):
        for k in range(1, self.side):
            self.scatter_first(i, k, half, slots, True).wait_recv()
        for at in range(self.side):
            added = slots[0, at].astype(jnp.float32)
            for k in range(1, self.side):
                added = added + slots[k, at].astype(jnp.float32)
            quarter[at] = added.astype(jnp.bfloat16)
        for k in range(1, self.side):
            self.scatter_second(i, k, quarter, slots_two, False).start()
        slots_two[self.second] = quarter[self.second]

    def after_second(self, i, quarter, slots_two, eighth, slots_three):
        for k in range(1, self.side):
            self.scatter_second(i, k, quarter, slots_two, True).wait_recv()
        added = slots_two[0].astype(jnp.float32)
        for k in range(1, self.side):
            added = added + slots_two[k].astype(jnp.float32)
        eighth[...] = added.astype(jnp.bfloat16)
        for k in range(1, self.planes):
            self.scatter_plane(i, k, eighth, slots_three, False).start()
        slots_three[self.plane] = eighth[self.plane]

    def after_planes(self, i, eighth, slots_three, block):
        for k in range(1, self.planes):
            self.scatter_plane(i, k, eighth, slots_three, True).wait_recv()
        added = slots_three[0].astype(jnp.float32)
        for k in range(1, self.planes):
            added = added + slots_three[k].astype(jnp.float32)
        block[self.plane] = added.astype(jnp.bfloat16)
        for k in range(1, self.planes):
            self.gather_plane(i, k, block, False).start()

    def planes_gathered(self, i, block):
        for k in range(1, self.planes):
            self.gather_plane(i, k, block, True).wait_recv()

    def scatter_sent(self, i, half, slots, quarter, slots_two, eighth, slots_three, block):
        for k in range(1, self.side):
            self.scatter_first(i, k, half, slots, False).wait_send()
            self.scatter_second(i, k, quarter, slots_two, False).wait_send()
        for k in range(1, self.planes):
            self.scatter_plane(i, k, eighth, slots_three, False).wait_send()
            self.gather_plane(i, k, block, False).wait_send()

    def gather_second_start(self, i, result):
        for k in range(1, self.side):
            self.gather_second(i, k, result, False).start()

    def gather_across(self, i, result):
        for k in range(1, self.side):
            self.gather_second(i, k, result, True).wait_recv()
        for k in range(1, self.side):
            self.gather_first(i, k, result, False).start()
        self.pair_gather(i, 0, result, False).start()

    def gather_pass(self, i, result):
        for k in range(1, self.side):
            self.gather_first(i, k, result, True).wait_recv()
            self.pair_gather(i, k, result, False).start()

    def gather_end(self, i, result):
        for k in range(self.side):
            self.pair_gather(i, k, result, True).wait_recv()
            self.pair_gather(i, k, result, False).wait_send()
        for k in range(1, self.side):
            self.gather_first(i, k, result, False).wait_send()
            self.gather_second(i, k, result, False).wait_send()


def stage_semaphores(count, planes, side):
    each = [(count,)] + [(count, size) for size in (side, side, planes, planes, side, side, side)]
    return [pltpu.SemaphoreType.DMA(shape) for shape in each]


def scatter_buffers(tails, planes, side):
    leads = [(side, side, planes), (side, side, planes), (side, planes), (side, planes)]
    leads += [(planes,), (planes,)]
    return [pltpu.VMEM(lead + tail, jnp.bfloat16) for lead in leads for tail in tails]


def neighbour_plane():
    plane = lax.axis_index("seq")
    return {"seq": plane + 1 - 2 * lax.rem(plane, 2)}


def swapped(src, dst, send, arrive):
    return pltpu.make_async_remote_copy(
        src_ref=src,
        dst_ref=dst,
        send_sem=send,
        recv_sem=arrive,
        device_id=neighbour_plane(),
        device_id_type=MESH,
    )


class Routes:
    def __init__(self, planes, members, sends, arrivals, local):
        self.planes, self.members = planes, members
        self.plane, self.member = lax.axis_index("seq"), lax.axis_index("exp")
        self.hops = planes // 2
        self.sends, self.arrivals, self.local = sends, arrivals, local
        self.pairs = [
            (hop, k) for hop in range(self.hops) for k in range(members) if hop or k
        ]

    def device(self, hop, k):
        return {
            "seq": lax.rem(self.plane + 2 * hop, self.planes),
            "exp": lax.rem(self.member + k, self.members),
        }

    def signal_peers(self, barrier):
        for hop, k in self.pairs:
            pl.semaphore_signal(
                barrier, inc=1, device_id=self.device(hop, k), device_id_type=MESH
            )
        return len(self.pairs)

    def moved(self, given, landed, returning, hop, k, arriving):
        device = self.device(hop, k)
        other = device["exp"]
        slot = hop if arriving else (-hop) % self.hops
        if returning:
            index = other if arriving else self.member
            src = given.at[hop, (self.members - k) % self.members]
        else:
            index, src = k, given.at[other]
        return pltpu.make_async_remote_copy(
            src_ref=src,
            dst_ref=landed.at[slot, index],
            send_sem=self.sends.at[hop, k],
            recv_sem=self.arrivals.at[slot, index],
            device_id=device,
            device_id_type=MESH,
        )

    def own(self, given, landed, returning):
        src = given.at[0, 0] if returning else given.at[self.member]
        index = self.member if returning else 0
        return pltpu.make_async_copy(src, landed.at[0, index], self.local)

    def start(self, given, landed, returning):
        for hop, k in self.pairs:
            self.moved(given, landed, returning, hop, k, False).start()
        self.own(given, landed, returning).start()

    def wait_sent(self, given, landed):
        for hop, k in self.pairs:
            self.moved(given, landed, False, hop, k, False).wait_send()

    def wait(self, given, landed, returning):
        for hop, k in self.pairs:
            self.moved(given, landed, returning, hop, k, True).wait_recv()
        self.own(given, landed, returning).wait()
        for hop, k in self.pairs:
            self.moved(given, landed, returning, hop, k, False).wait_send()


def route_semaphores(planes, members):
    shape = (planes // 2, members)
    return [
        pltpu.SemaphoreType.DMA(shape),
        pltpu.SemaphoreType.DMA(shape),
        pltpu.SemaphoreType.DMA,
    ]


def two_part(left, right, dims):
    high = left.astype(jnp.bfloat16)
    rest = (left - high.astype(jnp.float32)).astype(jnp.bfloat16)
    numbers = (dims, ((), ()))
    wide = jnp.float32
    return lax.dot_general(high, right, numbers, preferred_element_type=wide) + lax.dot_general(
        rest, right, numbers, preferred_element_type=wide
    )


LANE_UNIT = 256


def lane_unit(j):
    return pl.ds(pl.multiple_of(j * LANE_UNIT, LANE_UNIT), LANE_UNIT)


def normalized(values, gain):
    return values * lax.rsqrt(jnp.mean(values * values, axis=-1, keepdims=True) + EPSILON) * gain


def chain_device(at, members):
    return {"seq": at // members, "exp": lax.rem(at, members)}


def forward_kernel(
    planes,
    members,
    capacity,
    layer_ref,
    out_grad_ref,
    target_ref,
    mixer_gain_all_ref,
    conv_bias_all_ref,
    delta_bias_all_ref,
    skip_all_ref,
    expert_norm_all_ref,
    in_proj_ref,
    conv_weight_ref,
    state_proj_ref,
    delta_proj_ref,
    decay_log_ref,
    out_proj_ref,
    up_ref,
    down_ref,
    normed_ref,
    extended_ref,
    gate_ref,
    conv_pre_ref,
    conv_ref,
    delta_pre_ref,
    delta_ref,
    delta_low_ref,
    in_cols_ref,
    out_cols_ref,
    in_diag_ref,
    delta_sum_ref,
    carried_ref,
    mixer_pre_ref,
    mixed_ref,
    resid_ref,
    row_slots_ref,
    grad_rows_ref,
    near_up_ref,
    near_half_ref,
    rim_in_ref,
    vectors_ref,
    grad_slots_ref,
    drive_ref,
    stack_ref,
    low_sum_ref,
    wide_sum_ref,
    out_diag_ref,
    out_rest_ref,
    local_end_ref,
    rim_out_ref,
    rim_sent_ref,
    rim_landed_ref,
    up_sent_ref,
    up_landed_ref,
    down_sent_ref,
    down_landed_ref,
    *rest,
):
    exchange_refs, grad_semaphores = rest[:12], rest[12:15]
    wide, half = jnp.float32, jnp.bfloat16
    tokens, width = layer_ref.shape
    own_tokens = slice(0, tokens)
    inner_width = conv_ref.shape[1]
    sequences = extended_ref.shape[0]
    piece = tokens // sequences
    states, taps = decay_log_ref.shape[0], conv_weight_ref.shape[0]
    low_rank = delta_low_ref.shape[1]
    experts = row_slots_ref.shape[0]
    for i, source in enumerate((conv_bias_all_ref, delta_bias_all_ref, skip_all_ref)):
        vectors_ref[i : i + 1, :] = source[...].reshape(1, inner_width)
    vectors_ref[3:4, :width] = mixer_gain_all_ref[...].reshape(1, width)
    vectors_ref[3:4, width:] = expert_norm_all_ref[...].reshape(1, width)
    conv_bias_ref, delta_bias_ref, skip_ref = (vectors_ref.at[i : i + 1] for i in range(3))
    mixer_gain_ref, expert_norm_ref = vectors_ref.at[3:4, :width], vectors_ref.at[3:4, width:]
    devices = planes * members
    place = lax.axis_index("seq") * members + lax.axis_index("exp")
    before, after = lax.rem(place + devices - 1, devices), lax.rem(place + 1, devices)
    grad_routes = Routes(planes, members, *grad_semaphores)
    barrier = pltpu.get_barrier_semaphore()
    for peer in (before, after):
        device = chain_device(peer, members)
        pl.semaphore_signal(barrier, inc=1, device_id=device, device_id_type=MESH)
    greeted = 2 + grad_routes.signal_peers(barrier)
    for axis, size in (("seq", planes), ("exp", members)):
        mine = lax.axis_index(axis)
        for k in range(1, size):
            other = {axis: lax.rem(mine + k, size)}
            pl.semaphore_signal(barrier, inc=1, device_id=other, device_id_type=MESH)
        greeted += size - 1
    for q in range(sequences):
        rim_out_ref[q] = layer_ref[(q + 1) * piece - 8 : (q + 1) * piece]
    pl.semaphore_wait(barrier, greeted)
    rim_copy = pltpu.make_async_remote_copy(
        src_ref=rim_out_ref,
        dst_ref=rim_in_ref,
        send_sem=rim_sent_ref,
        recv_sem=rim_landed_ref,
        device_id=chain_device(after, members),
        device_id_type=MESH,
    )
    rim_copy.start()
    up_rows = up_ref.shape[1]
    marks = (0, up_rows // 2, up_rows * 11 // 16, up_rows)
    up_swaps = []
    for i, (low, high) in enumerate(zip(marks, marks[1:])):
        at = pl.ds(low, high - low)
        ends = (up_ref.at[:, at], near_up_ref.at[:, at])
        up_swaps.append(swapped(*ends, up_sent_ref.at[i], up_landed_ref.at[i]))
    slot = lax.broadcasted_iota(jnp.int32, (experts * capacity, tokens), 0)
    picks = jnp.where(slot == target_ref[...], 1.0, 0.0).astype(half)

    def fill(slots, values):
        product = half_dot(picks, values).astype(half)
        for e in range(experts):
            slots[e] = product[e * capacity : (e + 1) * capacity]

    fill(grad_slots_ref, out_grad_ref[...])
    grad_routes.start(grad_slots_ref, grad_rows_ref, False)
    up_swaps[0].start()
    cut = down_ref.shape[1] // 2
    down_swap = swapped(down_ref.at[:, pl.ds(0, cut)], near_half_ref, down_sent_ref, down_landed_ref)

    count = inner_width // LANE_UNIT
    normed_ref[own_tokens, :] = normalized(layer_ref[...].astype(wide), mixer_gain_ref[...]).astype(half)

    def project(j, carry):
        at = lane_unit(j)
        product = half_dot(normed_ref[own_tokens, :], in_proj_ref[:, at])
        for q in range(sequences):
            extended_ref[q, 8:, at] = product[q * piece : (q + 1) * piece]
        gate_at = pl.ds(pl.multiple_of(inner_width + j * LANE_UNIT, LANE_UNIT), LANE_UNIT)
        gate_ref[:, at] = half_dot(normed_ref[own_tokens, :], in_proj_ref[:, gate_at])
        return carry

    lax.fori_loop(0, count, project, 0)
    rim_copy.wait()
    keep = jnp.where(place > 0, 1.0, 0.0)
    rims = [normalized(rim_in_ref[q].astype(wide), mixer_gain_ref[...]) for q in range(sequences)]
    rim_normed = jnp.concatenate(rims, axis=0).astype(half)
    normed_ref[tokens:, :] = rim_normed
    low_sum_ref[...] = jnp.zeros(low_sum_ref.shape, wide)
    wide_sum_ref[...] = jnp.zeros(wide_sum_ref.shape, wide)

    def convolve(j, carry):
        at = lane_unit(j)
        rim = half_dot(rim_normed, in_proj_ref[:, at]) * keep
        for q in range(sequences):
            extended_ref[q, :8, at] = rim[q * 8 : (q + 1) * 8]
            start = 8 - (taps - 1)
            pre = conv_bias_ref[:, at] + conv_weight_ref[:1, at] * extended_ref[q, start : start + piece, at]
            for tap in range(1, taps):
                moved = extended_ref[q, start + tap : start + tap + piece, at]
                pre = pre + conv_weight_ref[tap : tap + 1, at] * moved
            conv_pre_ref[q * piece : (q + 1) * piece, at] = pre
            conv_ref[q * piece : (q + 1) * piece, at] = pre * jax.nn.sigmoid(pre)
        act = conv_ref[:, at]
        high = act.astype(half)
        low = (act - high.astype(wide)).astype(half)
        weight = state_proj_ref[:, at]
        low_sum_ref[...] += cols_dot(high, weight) + cols_dot(low, weight)
        tail = weight[low_rank:]
        wide_sum_ref[...] += cols_dot(tail, high) + cols_dot(tail, low)
        return carry

    lax.fori_loop(0, count, convolve, 0)
    delta_low_ref[...] = low_sum_ref[:, :low_rank]
    for i in range(tokens // BLK):
        block = wide_sum_ref[:, i * BLK : (i + 1) * BLK]
        in_cols_ref[i] = block[:states]
        out_cols_ref[i] = block[states:]
    shape = (tokens, BLK * states)
    column = lax.broadcasted_iota(jnp.int32, shape, 1)
    row = lax.rem(lax.broadcasted_iota(jnp.int32, shape, 0), BLK)
    own = column // states == row
    tile = jnp.where(
        lax.rem(lax.broadcasted_iota(jnp.int32, (states, BLK * states), 1), states)
        == lax.broadcasted_iota(jnp.int32, (states, BLK * states), 0),
        1.0,
        0.0,
    ).astype(half)

    def spread_out(values):
        return jnp.where(own, half_dot(values, tile), 0.0).astype(half)

    outward = low_sum_ref[:, low_rank + states :]
    out_high = outward.astype(half)
    in_diag_ref[...] = spread_out(low_sum_ref[:, low_rank : low_rank + states].astype(half))
    out_diag_ref[...] = spread_out(out_high)
    out_rest_ref[...] = spread_out((outward - out_high.astype(wide)).astype(half))

    def time_steps(j, carry):
        at = lane_unit(j)
        pre = two_part(delta_low_ref[...], delta_proj_ref[:, at], ((1,), (0,))) + delta_bias_ref[:, at]
        delta = jnp.maximum(pre, 0.0) + jnp.log1p(jnp.exp(-jnp.abs(pre)))
        delta_pre_ref[:, at] = pre
        delta_ref[:, at] = delta
        for q in range(sequences):
            part = delta[q * piece : (q + 1) * piece]
            delta_sum_ref[q : q + 1, at] = jnp.sum(part, axis=0, keepdims=True)
        return carry

    lax.fori_loop(0, count, time_steps, 0)
    groups = inner_width // GROUP
    blocks = piece // BLK

    def views(i):
        q, j = i // groups, lax.rem(i, groups)
        rows = pl.ds(pl.multiple_of(q * piece, piece), piece)
        lanes = pl.ds(pl.multiple_of(j * GROUP, GROUP), GROUP)
        cols = pl.ds(q * blocks, blocks)
        return q, rows, lanes, cols

    def first(i, carry):
        q, rows, lanes, cols = views(i)
        first_pass_kernel(
            delta_ref.at[rows, lanes],
            conv_ref.at[rows, lanes],
            in_cols_ref.at[cols],
            decay_log_ref.at[:, lanes],
            local_end_ref.at[pl.ds(q, 1), :, lanes],
            drive_ref,
        )
        return carry

    lax.fori_loop(0, sequences * groups, first, 0)

    def between_planes():
        up_swaps[2].start()
        down_swap.start()

    exchange_body(
        up_swaps[1].start,
        between_planes,
        False,
        planes,
        members,
        local_end_ref,
        delta_sum_ref,
        decay_log_ref,
        carried_ref,
        *exchange_refs,
    )

    def second(i, carry):
        q, rows, lanes, cols = views(i)
        second_pass_kernel(
            delta_ref.at[rows, lanes],
            conv_ref.at[rows, lanes],
            in_cols_ref.at[cols],
            decay_log_ref.at[:, lanes],
            carried_ref.at[pl.ds(q, 1), :, lanes],
            out_diag_ref.at[rows],
            out_rest_ref.at[rows],
            mixer_pre_ref.at[rows, lanes],
            drive_ref,
            stack_ref,
        )
        return carry

    lax.fori_loop(0, sequences * groups, second, 0)

    def mix(j, carry):
        at = lane_unit(j)
        pre = mixer_pre_ref[:, at] + skip_ref[:, at] * conv_ref[:, at]
        gate = gate_ref[:, at]
        mixer_pre_ref[:, at] = pre
        mixed_ref[:, at] = (pre * (gate * jax.nn.sigmoid(gate))).astype(half)
        return carry

    lax.fori_loop(0, count, mix, 0)
    resid_ref[...] = layer_ref[...].astype(wide) + half_dot(mixed_ref[...], out_proj_ref[...])
    fill(row_slots_ref, normalized(resid_ref[...], expert_norm_ref[...]).astype(half))
    grad_routes.wait(grad_slots_ref, grad_rows_ref, False)
    down_swap.wait()
    for swap in up_swaps:
        swap.wait()


def forward(operands, capacity, states, sequences, low_rank, experts):
    planes, members = lax.axis_size("seq"), lax.axis_size("exp")
    tokens, width = operands[0].shape
    inner_width = operands[9].shape[1]
    up, down = operands[14:16]
    half, wide = jnp.bfloat16, jnp.float32
    piece = tokens // sequences
    token_wide = jax.ShapeDtypeStruct((tokens, inner_width), wide)
    cols = jax.ShapeDtypeStruct((tokens // BLK, states, BLK), wide)
    diag = (tokens, BLK * states)
    routed = jax.ShapeDtypeStruct((planes // 2, members, capacity, width), half)
    state = (sequences, states, inner_width)
    vmem, anywhere = (pl.BlockSpec(memory_space=space) for space in (pltpu.VMEM, pl.ANY))
    scratch = [
        pltpu.VMEM((experts, capacity, width), half),
        pltpu.VMEM((piece, GROUP), wide),
        pltpu.VMEM((piece * states, GROUP), half),
        pltpu.VMEM((tokens, low_rank + 2 * states), wide),
        pltpu.VMEM((2 * states, tokens), wide),
        pltpu.VMEM(diag, half),
        pltpu.VMEM(diag, half),
        pltpu.VMEM(state, wide),
        pltpu.VMEM((sequences, 8, width), half),
    ]
    scratch += [pltpu.SemaphoreType.DMA] * 2 + [pltpu.SemaphoreType.DMA((3,))] * 2
    scratch += [pltpu.SemaphoreType.DMA] * 2
    scratch += exchange_scratch(planes, members, sequences * states // members, inner_width)
    scratch += route_semaphores(planes, members)
    return pl.pallas_call(
        functools.partial(forward_kernel, planes, members, capacity),
        name="forward_to_experts",
        in_specs=[vmem] * 14 + [anywhere] * 2,
        out_specs=[vmem] * 17 + [anywhere] * 3 + [vmem] * 2,
        out_shape=[
            jax.ShapeDtypeStruct((tokens + 8 * sequences, width), half),
            jax.ShapeDtypeStruct((sequences, piece + 8, inner_width), wide),
            token_wide,
            token_wide,
            token_wide,
            token_wide,
            token_wide,
            jax.ShapeDtypeStruct((tokens, low_rank), wide),
            cols,
            cols,
            jax.ShapeDtypeStruct(diag, half),
            jax.ShapeDtypeStruct((sequences, inner_width), wide),
            jax.ShapeDtypeStruct(state, wide),
            token_wide,
            jax.ShapeDtypeStruct((tokens, inner_width), half),
            jax.ShapeDtypeStruct((tokens, width), wide),
            jax.ShapeDtypeStruct((experts, capacity, width), half),
            routed,
            jax.ShapeDtypeStruct(up.shape, half),
            jax.ShapeDtypeStruct((1, down.shape[1] // 2, width), half),
            jax.ShapeDtypeStruct((sequences, 8, width), half),
            jax.ShapeDtypeStruct((4, inner_width), wide),
        ],
        scratch_shapes=scratch,
        compiler_params=pltpu.CompilerParams(
            collective_id=1, has_side_effects=True, vmem_limit_bytes=60 * 1024 * 1024
        ),
        cost_estimate=pl.CostEstimate(flops=10**8, transcendentals=0, bytes_accessed=2 * 10**8),
    )(*operands)


def expert_kernel(
    planes,
    members,
    row_slots_ref,
    grad_rows_ref,
    up_ref,
    down_ref,
    near_up_ref,
    near_half_ref,
    router_ref,
    outs_ref,
    back_ref,
    grad_up_ref,
    grad_down_ref,
    far_up_ref,
    far_down_ref,
    grad_router_ref,
    landed_ref,
    rows_ref,
    grads_ref,
    sent_ref,
    near_down_ref,
    out_sum_ref,
    row_sum_ref,
    hidden_own_ref,
    hidden_near_ref,
    pre_own_ref,
    pre_near_ref,
    shares_ref,
    far_up_sum_ref,
    far_down_sum_ref,
    returns_ref,
    down_sent_ref,
    down_landed_ref,
    back_sent_ref,
    back_landed_ref,
    *rest,
):
    routes = Routes(planes, members, *rest)
    wide, half = jnp.float32, jnp.bfloat16
    plane, member, hops = routes.plane, routes.member, routes.hops
    capacity, width = row_slots_ref.shape[1:]
    batch = members // 2
    chunk = batch * capacity
    group = members * capacity
    units = up_ref.shape[2]
    cut = units // 2
    experts = router_ref.shape[0]
    chosen_row = jnp.where(
        lax.broadcasted_iota(jnp.int32, (1, experts), 1) == member, 1.0, 0.0
    )
    barrier = pltpu.get_barrier_semaphore()
    pl.semaphore_signal(barrier, inc=1, device_id=neighbour_plane(), device_id_type=MESH)
    pl.semaphore_wait(barrier, routes.signal_peers(barrier) + 1)
    routes.start(row_slots_ref, landed_ref, False)
    down_swap = swapped(
        down_ref.at[0, pl.ds(cut, cut)], near_down_ref.at[pl.ds(cut, cut)], down_sent_ref, down_landed_ref
    )
    down_swap.start()
    near_down_ref[:cut] = near_half_ref[0]
    grad_router_ref[...] = jnp.zeros(grad_router_ref.shape, wide)
    for hop in range(hops):
        for e in range(members):
            grads_ref[hop * group + e * capacity : hop * group + (e + 1) * capacity] = grad_rows_ref[
                hop, e
            ]

    def gather(hop, c):
        rows = rows_ref.at[place(hop, c), :]
        for k in range(batch):
            r = c * batch + k
            if hop:
                routes.moved(row_slots_ref, landed_ref, False, hop, r, True).wait_recv()
            else:

                @pl.when(r > 0)
                def _():
                    routes.moved(row_slots_ref, landed_ref, False, 0, r, True).wait_recv()

            rows[k * capacity : (k + 1) * capacity, :] = landed_ref[hop, r]

    def through(at, up, down, hidden, back, where):
        pre = half_dot(rows_ref[at, :], up)
        phi = 0.5 * (1.0 + lax.erf(pre * 0.7071067811865476))
        slope = phi + pre * (jnp.exp(-0.5 * pre * pre) * 0.3989422804014327)
        active = (pre * phi).astype(half)
        hidden[at, where] = active
        arrived = (slope * cols_dot(sent_ref[at, :], down)).astype(half)
        back[at, where] = arrived
        return half_dot(active, down), cols_dot(arrived, up)

    def place(hop, c):
        return pl.ds(pl.multiple_of(hop * group + c * chunk, chunk), chunk)

    def own_part(hop, c):
        at = place(hop, c)
        logits = cols_dot(rows_ref[at, :].astype(wide), router_ref[...], lax.Precision.HIGHEST)
        raised = jnp.exp(logits - jnp.max(logits, axis=-1, keepdims=True))
        shares = raised / jnp.sum(raised, axis=-1, keepdims=True)
        gate = jnp.sum(shares * chosen_row, axis=-1, keepdims=True)
        shares_ref[at, :] = shares
        sent_ref[at, :] = (gate * grads_ref[at, :].astype(wide)).astype(half)
        every = slice(0, units)
        out, row = through(at, up_ref[0], down_ref[0], hidden_own_ref, pre_own_ref, every)
        early = slice(0, cut)
        near_out, near_row = through(
            at, near_up_ref[0, :, :cut], near_down_ref[:cut], hidden_near_ref, pre_near_ref, early
        )
        out_sum_ref[at, :] = out + near_out
        row_sum_ref[at, :] = row + near_row

    def late_part(hop, c):
        at = place(hop, c)
        near_out, near_row = through(
            at,
            near_up_ref[0, :, cut:],
            near_down_ref[cut:],
            hidden_near_ref,
            pre_near_ref,
            slice(cut, units),
        )
        out = out_sum_ref[at, :] + near_out
        shares, chosen = shares_ref[at, :], chosen_row
        gate = jnp.sum(shares * chosen, axis=-1, keepdims=True)
        grad_gate = jnp.sum(grads_ref[at, :].astype(wide) * out, axis=-1, keepdims=True)
        grad_logits = grad_gate * gate * (chosen - shares)
        outs = (gate * out).astype(half)
        row = row_sum_ref[at, :] + near_row
        row = row + jnp.dot(
            grad_logits,
            router_ref[...],
            precision=lax.Precision.HIGHEST,
            preferred_element_type=wide,
        )
        row = row.astype(half)
        grad_router_ref[...] += rows_dot(
            grad_logits, rows_ref[at, :].astype(wide), lax.Precision.HIGHEST
        )
        for k in range(batch):
            part = slice(k * capacity, (k + 1) * capacity)
            outs_ref[hop, c * batch + k] = outs[part]
            returns_ref[hop, c * batch + k] = row[part]

    def returned(hop, r, arriving):
        other = lax.rem(member + members - r, members)
        slot = hop if arriving else (-hop) % hops
        sender = other if arriving else member
        return pltpu.make_async_remote_copy(
            src_ref=returns_ref.at[hop, r],
            dst_ref=back_ref.at[slot, sender],
            send_sem=back_sent_ref.at[hop, r],
            recv_sem=back_landed_ref.at[slot, sender],
            device_id={"seq": lax.rem(plane + 2 * hop, planes), "exp": other},
            device_id_type=MESH,
        )

    def give_back(hop, c):
        for k in range(batch):
            r = c * batch + k
            if hop:
                returned(hop, r, False).start()
            else:

                @pl.when(r > 0)
                def _():
                    returned(0, r, False).start()

    def loop(body):
        def run(c, carry):
            body(c)
            return carry

        lax.fori_loop(0, 2, run, 0)

    def weight_grads(hop):
        at = slice(hop * group, (hop + 1) * group)
        rows, sent = rows_ref[at, :], sent_ref[at, :]
        products = [
            (grad_up_ref.at[0], rows, pre_own_ref[at, :]),
            (grad_down_ref.at[0], hidden_own_ref[at, :], sent),
            (far_up_sum_ref, rows, pre_near_ref[at, :]),
            (far_down_sum_ref, hidden_near_ref[at, :], sent),
        ]
        for total, left, right in products:
            if hop:
                total[...] += rows_dot(left, right)
            else:
                total[...] = rows_dot(left, right)

    routes.own(row_slots_ref, landed_ref, False).wait()

    def near_start(c):
        gather(0, c)
        own_part(0, c)

    loop(near_start)
    for hop in range(1, hops):

        def far_end(c):
            gather(hop, c)
            own_part(hop, c)
            if hop == 1:

                @pl.when(c == 0)
                def _():
                    down_swap.wait()

            late_part(hop, c)
            give_back(hop, c)

        loop(far_end)

    def near_end(c):
        late_part(0, c)
        give_back(0, c)

    loop(near_end)
    for hop in range(hops):
        weight_grads(hop)
    far_up_ref[0] = far_up_sum_ref[...].astype(half)
    far_down_ref[0] = far_down_sum_ref[...].astype(half)
    back_ref[0, member] = returns_ref[0, 0]
    for hop in range(hops):
        for r in range(members):
            if hop or r:
                returned(hop, r, True).wait_recv()
                returned(hop, r, False).wait_send()
    routes.wait_sent(row_slots_ref, landed_ref)


def expert_apply(row_slots, grad_rows, weights, router):
    planes, members = lax.axis_size("seq"), lax.axis_size("exp")
    experts, capacity, width = row_slots.shape
    up, down, near_up, near_half = weights
    units = up.shape[2]
    hops = planes // 2
    count = hops * members * capacity
    half, wide = jnp.bfloat16, jnp.float32
    vmem = pl.BlockSpec(memory_space=pltpu.VMEM)
    slotted = (hops, members, capacity, width)
    every = (hops, members)
    return pl.pallas_call(
        functools.partial(expert_kernel, planes, members),
        name="expert_apply",
        in_specs=[vmem] * 7,
        out_specs=[vmem] * 7,
        out_shape=[
            jax.ShapeDtypeStruct(slotted, half),
            jax.ShapeDtypeStruct(slotted, half),
            jax.ShapeDtypeStruct(up.shape, wide),
            jax.ShapeDtypeStruct(down.shape, wide),
            jax.ShapeDtypeStruct(up.shape, half),
            jax.ShapeDtypeStruct(down.shape, half),
            jax.ShapeDtypeStruct(router.shape, wide),
        ],
        scratch_shapes=[
            pltpu.VMEM(slotted, half),
            pltpu.VMEM((count, width), half),
            pltpu.VMEM((count, width), half),
            pltpu.VMEM((count, width), half),
            pltpu.VMEM(down.shape[1:], half),
            pltpu.VMEM((count, width), wide),
            pltpu.VMEM((count, width), wide),
            pltpu.VMEM((count, units), half),
            pltpu.VMEM((count, units), half),
            pltpu.VMEM((count, units), half),
            pltpu.VMEM((count, units), half),
            pltpu.VMEM((count, experts), wide),
            pltpu.VMEM(up.shape[1:], wide),
            pltpu.VMEM(down.shape[1:], wide),
            pltpu.VMEM(slotted, half),
            pltpu.SemaphoreType.DMA,
            pltpu.SemaphoreType.DMA,
            pltpu.SemaphoreType.DMA(every),
            pltpu.SemaphoreType.DMA(every),
        ]
        + route_semaphores(planes, members),
        compiler_params=pltpu.CompilerParams(
            collective_id=4, has_side_effects=True, vmem_limit_bytes=60 * 1024 * 1024
        ),
        cost_estimate=pl.CostEstimate(
            flops=24 * count * width * units,
            transcendentals=4 * count * units,
            bytes_accessed=3 * 10**7,
        ),
    )(row_slots, grad_rows, *weights, router)


def gradient_kernel(
    planes,
    side,
    delta_ref,
    conv_ref,
    grad_scan_ref,
    in_cols_ref,
    out_cols_ref,
    in_diag_ref,
    decay_log_ref,
    carried_ref,
    carried_back_ref,
    delta_pre_ref,
    delta_low_ref,
    conv_pre_ref,
    extended_ref,
    normed_ref,
    normed_gate_ref,
    layer_ref,
    rim_layer_ref,
    grad_resid_ref,
    delta_proj_ref,
    state_proj_ref,
    in_proj_ref,
    conv_weight_ref,
    vectors_ref,
    skip_grad_ref,
    norm_grad_ref,
    router_grad_ref,
    early_out_ref,
    early_gate_ref,
    returned_ref,
    far_up_ref,
    far_down_ref,
    in_grad_ref,
    total_out_ref,
    total_gate_ref,
    total_inner_ref,
    total_small_ref,
    landed_ref,
    near_up_ref,
    near_down_ref,
    grad_delta,
    grad_conv,
    grad_in,
    grad_out,
    grad_log,
    drive,
    kept,
    stack,
    slope_stack,
    low_grads,
    padded,
    slopes,
    small,
    rim_out,
    rim_in,
    rim_sent,
    rim_landed,
    in_part,
    part_loaded,
    given_inner,
    given_small,
    *rest,
):
    early_buffers, tail_buffers, small_buffers = rest[:12], rest[12:18], rest[18:24]
    swap_sent, swap_landed, rest = rest[24], rest[25], rest[26:]
    sums = Sums(planes, side, rest[:8], rest[8:16])
    routes = Routes(planes, 2 * side * side, *rest[16:19])
    tokens, inner_width = conv_ref.shape
    width = layer_ref.shape[1]
    low_rank = delta_low_ref.shape[1]
    states, taps = decay_log_ref.shape[0], conv_weight_ref.shape[0]
    sequences = extended_ref.shape[0]
    piece = tokens // sequences
    chips = side * side
    wide, half = jnp.float32, jnp.bfloat16
    skip_ref, mixer_gain_ref = vectors_ref.at[2:3], vectors_ref.at[3:4, :width]
    devices = 2 * chips * planes
    place = sums.plane * (2 * chips) + sums.member
    before, after = lax.rem(place + devices - 1, devices), lax.rem(place + 1, devices)
    barrier = pltpu.get_barrier_semaphore()
    for peer in (before, after):
        device = chain_device(peer, 2 * chips)
        pl.semaphore_signal(barrier, inc=1, device_id=device, device_id_type=MESH)
    pl.semaphore_signal(barrier, inc=1, device_id=neighbour_plane(), device_id_type=MESH)
    greeted = 3 + sums.signal_peers(barrier) + routes.signal_peers(barrier)
    pl.semaphore_wait(barrier, greeted)

    in_load = pltpu.make_async_copy(in_proj_ref.at[:, pl.ds(0, inner_width)], in_part, part_loaded)
    in_load.start()
    pair = range(2)
    given = (early_out_ref, early_gate_ref)
    results = (total_out_ref, total_gate_ref)
    stages = [tuple(early_buffers[2 * stage + i] for stage in range(6)) for i in pair]
    blocks = [result.at[sums.core, sums.first, sums.second] for result in results]
    swaps = [
        swapped(src, dst, swap_sent.at[i], swap_landed.at[i])
        for i, (src, dst) in enumerate([(far_up_ref, near_up_ref), (far_down_ref, near_down_ref)])
    ]
    for i in pair:
        sums.pair_half(i, given[i], stages[i][0]).start()
    routes.start(returned_ref, landed_ref, True)
    swaps[0].start()
    groups = inner_width // GROUP
    count = sequences * groups
    cols_each = piece // BLK

    def scan_group(g, carry):
        q, j = g // groups, lax.rem(g, groups)
        rows = pl.ds(pl.multiple_of(q * piece, piece), piece)
        lanes = pl.ds(pl.multiple_of(j * GROUP, GROUP), GROUP)
        cols = pl.ds(q * cols_each, cols_each)

        def middle():
            @pl.when(g == 0)
            def _():
                for i in pair:
                    sums.after_pair(i, given[i], *stages[i][:2])

            @pl.when(g == count // 2)
            def _():
                for i in pair:
                    sums.after_first(i, *stages[i][:4])

            @pl.when(g == count - 2)
            def _():
                for i in pair:
                    sums.after_second(i, *stages[i][2:6])

            @pl.when(g == count - 1)
            def _():
                for i in pair:
                    sums.after_planes(i, *stages[i][4:6], blocks[i])
                swaps[1].start()

        one = pl.ds(q, 1)
        backward_body(
            middle,
            j == 0,
            delta_ref.at[rows, lanes],
            conv_ref.at[rows, lanes],
            grad_scan_ref.at[rows, lanes],
            in_cols_ref.at[cols],
            out_cols_ref.at[cols],
            in_diag_ref.at[rows],
            decay_log_ref.at[:, lanes],
            carried_ref.at[one, :, lanes],
            carried_back_ref.at[one, :, lanes],
            grad_delta.at[rows, lanes],
            grad_conv.at[rows, lanes],
            grad_in.at[rows],
            grad_out.at[rows],
            grad_log.at[one, :, lanes],
            drive,
            kept,
            stack,
            slope_stack,
        )
        return carry

    lax.fori_loop(0, count, scan_group, 0)
    unit = LANE_UNIT
    low_grads[...] = jnp.zeros(low_grads.shape, wide)
    small[...] = jnp.zeros(small.shape, wide)
    at_delta = low_rank + 2 * states
    at_log = at_delta + low_rank
    at_conv = at_log + states
    at_end = at_conv + taps + 2

    def first(j, carry):
        at = lane_unit(j)
        slope = grad_delta[:, at] * jax.nn.sigmoid(delta_pre_ref[:, at])
        small[at_conv + taps + 1 : at_conv + taps + 2, at] = jnp.sum(slope, axis=0, keepdims=True)
        small[at_delta:at_log, at] = rows_dot(delta_low_ref[...], slope, lax.Precision.HIGHEST)
        low_grads[...] += two_part(slope, delta_proj_ref[:, at], ((1,), (1,)))
        return carry

    lax.fori_loop(0, inner_width // unit, first, 0)
    for i in pair:
        sums.planes_gathered(i, blocks[i])
        sums.gather_second_start(i, results[i])
    column = lax.broadcasted_iota(jnp.int32, grad_in.shape, 1) // states
    row = lax.rem(lax.broadcasted_iota(jnp.int32, grad_in.shape, 0), BLK)
    fold = jnp.where(
        lax.rem(lax.broadcasted_iota(jnp.int32, (grad_in.shape[1], states), 0), states)
        == lax.broadcasted_iota(jnp.int32, (grad_in.shape[1], states), 1),
        1.0,
        0.0,
    ).astype(half)

    def folded(ref):
        return two_part(jnp.where(column == row, ref[...], 0.0), fold, ((1,), (0,)))

    coefs = jnp.concatenate([low_grads[...], folded(grad_in), folded(grad_out)], axis=1)
    keep = jnp.where(place > 0, 1.0, 0.0)
    rim_out[...] = jnp.zeros(rim_out.shape, half)

    def dense(at):
        small[:at_delta, at] = rows_dot(coefs, conv_ref[:, at], lax.Precision.HIGHEST)
        through = two_part(coefs, state_proj_ref[:, at], ((1,), (0,)))
        through = through + grad_scan_ref[:, at] * skip_ref[:, at] + grad_conv[:, at]
        pre = conv_pre_ref[:, at]
        sigma = jax.nn.sigmoid(pre)
        through = through * (sigma * (1.0 + pre * (1.0 - sigma)))
        small[at_conv + taps : at_conv + taps + 1, at] = jnp.sum(through, axis=0, keepdims=True)
        for q in range(sequences):
            padded[q, :8] = jnp.zeros((8, unit), wide)
            padded[q, 8 + piece :] = jnp.zeros((8, unit), wide)
            padded[q, 8 : 8 + piece] = through[q * piece : (q + 1) * piece]
            result = jnp.zeros((piece, unit), wide)
            rim = jnp.zeros((8, unit), wide)
            for tap in range(taps):
                weight = conv_weight_ref[tap : tap + 1, at]
                shift = taps - 1 - tap
                result = result + weight * padded[q, 8 + shift : 8 + shift + piece]
                rim = rim + weight * padded[q, 8 - tap : 16 - tap]
            slopes[q * piece : (q + 1) * piece, at] = result.astype(half)
            rim_out[q, 8 - (taps - 1) :, at] = (rim[: taps - 1] * keep).astype(half)
            slopes[tokens + q * 8 : tokens + (q + 1) * 8, at] = rim_out[q, :, at]
        for tap in range(taps):
            start = 8 - (taps - 1) + tap
            product = jnp.zeros((1, unit), wide)
            for q in range(sequences):
                product = product + jnp.sum(
                    padded[q, 8 : 8 + piece] * extended_ref[q, start : start + piece, at],
                    axis=0,
                    keepdims=True,
                )
            small[at_conv + tap : at_conv + tap + 1, at] = product

    slabs = given_inner.shape[0]
    tall = width // chips
    size = tall // planes

    def tail_of(s):
        return [buffer.at[s] for buffer in tail_buffers]

    def after_tail_pair(s):
        sums.after_pair(2 + s, given_inner.at[s], *tail_of(s)[:2])

    def slab(s, carry):
        for c in range(2):
            at = lane_unit(c * slabs + s)
            dense(at)
            for m in range(chips):
                product = rows_dot(
                    normed_ref[:, m * tall : (m + 1) * tall], slopes[:, at]
                ).astype(half)
                for z in range(planes):
                    part = product[z * size : (z + 1) * size]
                    given_inner[s, c, m // side, m % side, z] = part
        sums.pair_half(2 + s, given_inner.at[s], tail_buffers[0].at[s]).start()

        @pl.when(s > 0)
        def _():
            after_tail_pair(s - 1)

        return carry

    lax.fori_loop(0, slabs, slab, 0)
    after_tail_pair(slabs - 1)
    rim_copy = pltpu.make_async_remote_copy(
        src_ref=rim_out,
        dst_ref=rim_in,
        send_sem=rim_sent,
        recv_sem=rim_landed,
        device_id=chain_device(before, 2 * chips),
        device_id_type=MESH,
    )
    rim_copy.start()
    in_load.wait()
    projected = cols_dot(slopes[...], in_part[...])
    normed_grad = normed_gate_ref[...] + projected[:tokens]

    def normal_of(values):
        scaling = lax.rsqrt(jnp.mean(values * values, axis=-1, keepdims=True) + EPSILON)
        return values * scaling, scaling

    normal, scaling = normal_of(layer_ref[...].astype(wide))
    gain_grad = jnp.sum(normed_grad * normal, axis=0, keepdims=True)
    for q in range(sequences):
        rim_normal, _ = normal_of(rim_layer_ref[q].astype(wide))
        rim_grad = projected[tokens + q * 8 : tokens + (q + 1) * 8]
        gain_grad = gain_grad + jnp.sum(rim_grad * rim_normal, axis=0, keepdims=True)
    log_total = grad_log[0]
    for q in range(1, sequences):
        log_total = log_total + grad_log[q]
    small[at_log:at_conv] = log_total
    small[at_end : at_end + 1] = skip_grad_ref[...]
    small[at_end + 1 : at_end + 2, :width] = gain_grad
    small[at_end + 1 : at_end + 2, width:] = norm_grad_ref[...]
    for k in range(router_grad_ref.shape[0]):
        line = at_end + 2 + k // 2
        small[line : line + 1, (k % 2) * width : (k % 2 + 1) * width] = router_grad_ref[k : k + 1]
    low = given_small.shape[4]
    for c in range(2):
        for m in range(chips):
            for z in range(planes):
                line = (m * planes + z) * low
                given_small[c, m // side, m % side, z] = small[
                    line : line + low, c * width : (c + 1) * width
                ].astype(half)
    last = 2 + slabs
    every = range(slabs)
    sums.pair_half(last, given_small, small_buffers[0]).start()
    for s in every:
        sums.after_first(2 + s, *tail_of(s)[:4])
    sums.after_pair(last, given_small, *small_buffers[:2])
    for s in every:
        sums.after_second(2 + s, *tail_of(s)[2:6])
    for i in pair:
        sums.gather_across(i, results[i])
    weighted = normed_grad * mixer_gain_ref[...]
    in_grad_ref[...] = grad_resid_ref[...] + scaling * (
        weighted - normal * jnp.mean(weighted * normal, axis=-1, keepdims=True)
    )
    sums.after_first(last, *small_buffers[:4])
    tails = [total_inner_ref.at[s] for s in every] + [total_small_ref]
    tail_blocks = [total.at[sums.core, sums.first, sums.second] for total in tails]
    for s in every:
        sums.after_planes(2 + s, *tail_of(s)[4:6], tail_blocks[s])
    sums.after_second(last, *small_buffers[2:6])
    for s in every:
        sums.planes_gathered(2 + s, tail_blocks[s])
        sums.gather_second_start(2 + s, tails[s])
    sums.after_planes(last, *small_buffers[4:6], tail_blocks[slabs])
    for s in every:
        sums.gather_across(2 + s, tails[s])
    sums.planes_gathered(last, tail_blocks[slabs])
    sums.gather_second_start(last, total_small_ref)
    for i in pair:
        sums.gather_pass(i, results[i])
    rim_copy.wait()
    keep_last = jnp.where(place < devices - 1, 1.0, 0.0)
    for q in range(sequences):
        rows = slice((q + 1) * piece - 8, (q + 1) * piece)
        added = cols_dot(rim_in[q], in_part[...]) * keep_last
        fixed = (normed_grad[rows] + added) * mixer_gain_ref[...]
        mean = jnp.mean(fixed * normal[rows], axis=-1, keepdims=True)
        in_grad_ref[rows, :] = grad_resid_ref[rows, :] + scaling[rows] * (
            fixed - normal[rows] * mean
        )
    sums.gather_across(last, total_small_ref)
    for s in every:
        sums.gather_pass(2 + s, tails[s])
    sums.gather_pass(last, total_small_ref)
    routes.wait(returned_ref, landed_ref, True)
    for swap in swaps:
        swap.wait()
    ends = [(i, stages[i], blocks[i], results[i]) for i in pair]
    ends += [(2 + s, tail_of(s), tail_blocks[s], tails[s]) for s in every]
    ends += [(last, small_buffers, tail_blocks[slabs], total_small_ref)]
    for i, buffers, block, result in ends:
        sums.scatter_sent(i, *buffers, block)
        sums.gather_end(i, result)


def all_gradients(operands, small_height, side):
    planes = lax.axis_size("seq")
    tokens, inner_width = operands[1].shape
    width = operands[15].shape[1]
    states, low_rank = operands[6].shape[0], operands[10].shape[1]
    sequences = operands[7].shape[0]
    piece = tokens // sequences
    low = -(-small_height // (side * side * planes))
    lead = (2, side, side, planes)
    big = operands[26].shape
    slabs = width // LANE_UNIT
    inner = (slabs,) + lead + (big[4], LANE_UNIT)
    little = lead + (low, width)
    vmem, anywhere = (pl.BlockSpec(memory_space=space) for space in (pltpu.VMEM, pl.ANY))
    half, wide = jnp.bfloat16, jnp.float32
    token_wide = pltpu.VMEM((tokens, inner_width), wide)
    narrow = pltpu.VMEM((tokens, BLK * states), wide)
    steps = pltpu.VMEM((piece, states, GROUP), wide)
    stack = pltpu.VMEM((BLK * states, GROUP), half)
    rim = pltpu.VMEM((sequences, 8, inner_width), half)
    tail_shapes = [value.shape for value in scatter_buffers([inner[5:]], planes, side)]
    moved = [jax.ShapeDtypeStruct(value.shape, half) for value in operands[28:]]
    semaphores = stage_semaphores(3 + slabs, planes, side)
    return pl.pallas_call(
        functools.partial(gradient_kernel, planes, side),
        name="backward_gradients",
        in_specs=[vmem] * 20 + [anywhere] + [vmem] * 7 + [anywhere] * 3,
        out_specs=[vmem] * 5 + [anywhere] * 3,
        out_shape=[jax.ShapeDtypeStruct((tokens, width), wide)]
        + [jax.ShapeDtypeStruct(shape, half) for shape in (big, big, inner, little)]
        + moved,
        scratch_shapes=[
            token_wide,
            token_wide,
            narrow,
            narrow,
            pltpu.VMEM((sequences, states, inner_width), wide),
            pltpu.VMEM((piece, GROUP), wide),
            steps,
            stack,
            stack,
            pltpu.VMEM((tokens, low_rank), wide),
            pltpu.VMEM((sequences, piece + 16, LANE_UNIT), wide),
            pltpu.VMEM((tokens + 8 * sequences, inner_width), half),
            pltpu.VMEM((low * side * side * planes, inner_width), wide),
            rim,
            rim,
            pltpu.SemaphoreType.DMA,
            pltpu.SemaphoreType.DMA,
            pltpu.VMEM((width, inner_width), half),
            pltpu.SemaphoreType.DMA,
            pltpu.VMEM(inner, half),
            pltpu.VMEM(little, half),
        ]
        + scatter_buffers([big[4:], big[4:]], planes, side)
        + [pltpu.VMEM((slabs,) + shape, half) for shape in tail_shapes]
        + scatter_buffers([little[4:]], planes, side)
        + [pltpu.SemaphoreType.DMA((2,)), pltpu.SemaphoreType.DMA((2,))]
        + semaphores
        + semaphores
        + route_semaphores(planes, 2 * side * side),
        compiler_params=pltpu.CompilerParams(
            collective_id=3, has_side_effects=True, vmem_limit_bytes=63 * 1024 * 1024
        ),
        cost_estimate=pl.CostEstimate(flops=10**8, transcendentals=0, bytes_accessed=2 * 10**8),
    )(*operands)


def on_device(
    layer_in,
    mixer_gain,
    in_proj,
    conv_weight,
    conv_bias,
    state_proj,
    delta_proj,
    delta_bias,
    decay_log,
    skip_gain,
    out_proj,
    expert_norm,
    router_weight,
    expert_up,
    expert_down,
    expert_ids,
    capacity_slot,
    out_grad,
):
    sequences, piece_len, width = layer_in.shape
    tokens = sequences * piece_len
    taps, inner_width = conv_weight.shape
    low_rank = delta_proj.shape[0]
    states = decay_log.shape[0]
    experts = router_weight.shape[1]
    senders = lax.axis_size("exp")
    capacity = (5 * tokens + 4 * experts - 1) // (4 * experts)
    planes = lax.axis_size("seq")
    hops = planes // 2
    flat_ids = expert_ids.reshape(1, tokens)
    flat_slot = capacity_slot.reshape(1, tokens)
    target = jnp.where(flat_slot < capacity, flat_ids * capacity + flat_slot, experts * capacity)
    slot_rows = jnp.arange(experts * capacity, dtype=jnp.int32)
    picks = (slot_rows[:, None] == target).astype(jnp.bfloat16)
    (
        normed_half,
        extended,
        gate_half,
        conv_pre,
        conv_flat,
        delta_pre,
        delta,
        delta_low,
        in_cols,
        out_cols,
        in_diag,
        delta_sum,
        carried,
        mixer_pre,
        mixed,
        resid,
        row_slots,
        grad_rows,
        near_up,
        near_half,
        rim_layer,
        vectors,
    ) = forward(
        [
            layer_in.reshape(tokens, width),
            out_grad.reshape(tokens, width),
            target,
            mixer_gain,
            conv_bias,
            delta_bias,
            skip_gain,
            expert_norm,
            in_proj,
            conv_weight,
            state_proj.T,
            delta_proj,
            decay_log,
            out_proj,
            expert_up,
            expert_down,
        ],
        capacity,
        states,
        sequences,
        low_rank,
        experts,
    )
    gate_act = jax.nn.silu(gate_half)
    scaling_two = lax.rsqrt(jnp.mean(resid * resid, axis=-1, keepdims=True) + EPSILON)
    weights = [expert_up, expert_down, near_up, near_half]
    expert_out, back_rows, grad_up, grad_down, far_up, far_down, grad_router = expert_apply(
        row_slots, grad_rows, weights, router_weight.T
    )
    grad_routed = rows_dot(
        jnp.concatenate([picks] * hops, axis=0), back_rows.reshape(hops * senders * capacity, width)
    )
    grad_top = out_grad.reshape(tokens, width).astype(jnp.float32)
    grad_resid_norm, grad_expert_norm = norm_backward(resid, scaling_two, expert_norm, grad_routed)
    grad_resid = grad_top + grad_resid_norm
    grad_mixer = grad_resid.astype(jnp.bfloat16)
    grad_out_proj = rows_dot(mixed, grad_mixer)
    grad_mixed = cols_dot(grad_mixer, out_proj)
    grad_scan = grad_mixed * gate_act
    grad_gate_half = grad_mixed * mixer_pre * silu_slope(gate_half)
    grad_gate_half = grad_gate_half.astype(jnp.bfloat16)
    grad_in_gate = rows_dot(normed_half[:tokens], grad_gate_half)
    grad_normed_gate = cols_dot(grad_gate_half, in_proj[:, inner_width:])
    grad_skip_gain = jnp.sum(grad_scan * conv_flat, axis=0, keepdims=True)
    (gradient_first,) = scan_call(
        back_summary_kernel,
        "back_summary",
        sequences,
        states,
        [("wide", delta), ("wide", grad_scan), ("cols", out_cols), ("rates", decay_log)],
        ["state"],
        [],
    )
    carried_back = exchange(gradient_first, delta_sum, decay_log)
    side = math.isqrt(senders // 2)
    big = (2, side, side, planes, inner_width // (senders * planes), width)

    def as_rows(values):
        blocks = values.shape[1] // width
        return jnp.concatenate(
            [values[:, at * width : (at + 1) * width] for at in range(blocks)], axis=0
        ).astype(jnp.bfloat16)

    early = [
        grad_out_proj.astype(jnp.bfloat16).reshape(big),
        as_rows(grad_in_gate).reshape(big),
    ]
    heights = [low_rank + 2 * states, low_rank, states, taps, 1, 1, 1, 1, experts // 2]
    in_grad, sum_out, sum_gate, sum_inner, sum_small, back_out, near_up, near_down = all_gradients(
        [
            delta,
            conv_flat,
            grad_scan,
            in_cols,
            out_cols,
            in_diag,
            decay_log,
            carried,
            carried_back,
            delta_pre,
            delta_low,
            conv_pre,
            extended,
            normed_half,
            grad_normed_gate,
            layer_in.reshape(tokens, width),
            rim_layer,
            grad_resid,
            delta_proj,
            state_proj.T,
            in_proj,
            conv_weight,
            vectors,
            grad_skip_gain,
            grad_expert_norm,
            grad_router,
        ]
        + early
        + [expert_out, far_up, far_down],
        sum(heights),
        side,
    )
    grad_up_own = grad_up + near_up.astype(jnp.float32)
    grad_down_own = grad_down + near_down.astype(jnp.float32)
    token_out = rows_dot(
        jnp.concatenate([picks] * hops, axis=0), back_out.reshape(hops * senders * capacity, width)
    )
    layer_out = (resid + token_out).astype(jnp.bfloat16).reshape(sequences, piece_len, width)
    in_grad = in_grad.reshape(sequences, piece_len, width)
    rows_of = (inner_width, width)
    slabs = width // LANE_UNIT
    by_slab = sum_inner.reshape(slabs, 2, width, LANE_UNIT)
    inner_parts = [by_slab[s, c] for c in range(2) for s in range(slabs)]
    grad_in_proj = jnp.concatenate(
        inner_parts + [sum_gate[c].reshape(width, width) for c in range(2)], axis=1
    ).astype(jnp.float32)
    small_halves = sum_small.reshape(2, -1, width)
    small_wide = jnp.concatenate([small_halves[0], small_halves[1]], axis=1).astype(jnp.float32)
    offsets = [sum(heights[:at]) for at in range(len(heights) + 1)]
    pieces = [small_wide[offsets[at] : offsets[at + 1]] for at in range(len(heights))]
    summed = (
        pieces[7][0, :width],
        grad_in_proj,
        pieces[3],
        pieces[4][0],
        pieces[0].T,
        pieces[1],
        pieces[5][0],
        pieces[2],
        pieces[6][0],
        sum_out.reshape(rows_of).astype(jnp.float32),
        pieces[7][0, width:],
        pieces[8].reshape(experts, width).T,
    )
    return (
        layer_out,
        in_grad,
        summed[0],
        summed[1],
        summed[2],
        summed[3],
        summed[4],
        summed[5],
        summed[6],
        summed[7],
        summed[8],
        summed[9],
        summed[10],
        summed[11],
        grad_up_own,
        grad_down_own,
    )


def solution(mesh):
    placed = (
        P(None, ("seq", "exp"), None),
        P(),
        P(),
        P(),
        P(),
        P(),
        P(),
        P(),
        P(),
        P(),
        P(),
        P(),
        P(),
        P("exp", None, "seq"),
        P("exp", "seq", None),
        P(None, ("seq", "exp")),
        P(None, ("seq", "exp")),
        P(None, ("seq", "exp"), None),
    )
    return jax.shard_map(
        on_device,
        mesh=mesh,
        in_specs=placed,
        out_specs=(
            P(None, ("seq", "exp"), None),
            P(None, ("seq", "exp"), None),
            P(),
            P(),
            P(),
            P(),
            P(),
            P(),
            P(),
            P(),
            P(),
            P(),
            P(),
            P(),
            P("exp", None, "seq"),
            P("exp", "seq", None),
        ),
        check_vma=False,
    )
```

```python
import functools
import math

import jax
import jax.numpy as jnp
from jax import lax
from jax.experimental import pallas as pl
from jax.experimental.pallas import tpu as pltpu
from jax.sharding import PartitionSpec as P

BLK = 16
LANES = 128
GROUP = 512
LOG2E = 1.4426950408889634
LN2 = 0.6931471805599453
VMEM_BYTES = 50 * 1024 * 1024


EPSILON = 1e-05


def half_dot(left, right):
    return jnp.dot(left, right, preferred_element_type=jnp.float32)


def rows_dot(left, right, precision=None):
    return lax.dot_general(
        left,
        right,
        (((0,), (0,)), ((), ())),
        precision=precision,
        preferred_element_type=jnp.float32,
    )


def cols_dot(left, right, precision=None):
    return lax.dot_general(
        left,
        right,
        (((1,), (1,)), ((), ())),
        precision=precision,
        preferred_element_type=jnp.float32,
    )


def norm_backward(values, scaling, gain_vec, incoming):
    normal = values * scaling
    weighted = incoming * gain_vec
    grad_gain = jnp.sum(incoming * normal, axis=0, keepdims=True)
    grad_values = scaling * (
        weighted - normal * jnp.mean(weighted * normal, axis=-1, keepdims=True)
    )
    return (grad_values, grad_gain)


def silu_slope(values):
    sigma = jax.nn.sigmoid(values)
    return sigma * (1.0 + values * (1.0 - sigma))


def lane_parts(ref, k, states):
    width = ref.shape[-1]
    return [
        jnp.broadcast_to(ref[k : k + 1, at : at + LANES], (states, LANES))
        for at in range(0, width, LANES)
    ]


def block_of(ref, i):
    return ref.at[pl.ds(pl.multiple_of(i * BLK, BLK), BLK), :]


def rows_of_block(ref, i, states):
    size = BLK * states
    return ref.at[pl.ds(pl.multiple_of(i * size, size), size), :]


def rates_of(log_ref):
    rates = -jnp.exp(log_ref[...]) * LOG2E
    return [rates[:, at : at + LANES] for at in range(0, rates.shape[1], LANES)]


def first_pass_kernel(delta_ref, conv_ref, in_ref, log_ref, end_ref, drive):
    steps, width = delta_ref.shape
    states = log_ref.shape[0]
    rates = rates_of(log_ref)
    drive[...] = delta_ref[...] * conv_ref[...]

    def block(i, state):
        state = list(state)
        inwards = in_ref[i]
        for k in range(BLK):
            inward = jnp.broadcast_to(inwards[:, k : k + 1], (states, LANES))
            deltas = lane_parts(block_of(delta_ref, i), k, states)
            drives = lane_parts(block_of(drive, i), k, states)
            for j in range(width // LANES):
                state[j] = jnp.exp2(deltas[j] * rates[j]) * state[j] + inward * drives[j]
        return tuple(state)

    zero = tuple(jnp.zeros((states, LANES), jnp.float32) for _ in range(width // LANES))
    last = lax.fori_loop(0, steps // BLK, block, zero)
    for j in range(width // LANES):
        end_ref[0, :, j * LANES : (j + 1) * LANES] = last[j]


def second_pass_kernel(
    delta_ref, conv_ref, in_ref, log_ref, start_ref, out_ref, rest_ref, scanned_ref, drive, stack
):
    steps, width = delta_ref.shape
    states = log_ref.shape[0]
    rates = rates_of(log_ref)
    drive[...] = delta_ref[...] * conv_ref[...]

    def block(i, state):
        state = list(state)
        inwards = in_ref[i]
        kept = rows_of_block(stack, i, states)
        for k in range(BLK):
            inward = jnp.broadcast_to(inwards[:, k : k + 1], (states, LANES))
            deltas = lane_parts(block_of(delta_ref, i), k, states)
            drives = lane_parts(block_of(drive, i), k, states)
            for j in range(width // LANES):
                state[j] = jnp.exp2(deltas[j] * rates[j]) * state[j] + inward * drives[j]
                at = slice(j * LANES, (j + 1) * LANES)
                kept[k * states : (k + 1) * states, at] = state[j].astype(jnp.bfloat16)
        return tuple(state)

    begin = tuple(start_ref[0, :, j * LANES : (j + 1) * LANES] for j in range(width // LANES))
    lax.fori_loop(0, steps // BLK, block, begin)
    for i in range(steps // BLK):
        rows = slice(i * BLK, (i + 1) * BLK)
        both = jnp.concatenate([out_ref[rows, :], rest_ref[rows, :]], axis=0)
        product = half_dot(both, stack[i * BLK * states : (i + 1) * BLK * states, :])
        scanned_ref[rows, :] = product[:BLK] + product[BLK:]


def back_summary_kernel(delta_ref, grad_ref, out_ref, log_ref, end_ref):
    steps, width = delta_ref.shape
    states = log_ref.shape[0]
    rates = rates_of(log_ref)
    blocks = steps // BLK

    def block(i, state):
        state = list(state)
        outwards = out_ref[blocks - 1 - i]
        for k in reversed(range(BLK)):
            outward = jnp.broadcast_to(outwards[:, k : k + 1], (states, LANES))
            deltas = lane_parts(block_of(delta_ref, blocks - 1 - i), k, states)
            grads = lane_parts(block_of(grad_ref, blocks - 1 - i), k, states)
            for j in range(width // LANES):
                state[j] = jnp.exp2(deltas[j] * rates[j]) * (state[j] + outward * grads[j])
        return tuple(state)

    zero = tuple(jnp.zeros((states, LANES), jnp.float32) for _ in range(width // LANES))
    last = lax.fori_loop(0, blocks, block, zero)
    for j in range(width // LANES):
        end_ref[0, :, j * LANES : (j + 1) * LANES] = last[j]


def backward_body(
    middle,
    first,
    delta_ref,
    conv_ref,
    grad_ref,
    in_ref,
    out_ref,
    in_diag_ref,
    log_ref,
    start_ref,
    finish_ref,
    grad_delta_ref,
    grad_conv_ref,
    grad_in_ref,
    grad_out_ref,
    grad_log_ref,
    drive,
    carried,
    stack,
    slope,
):
    steps, width = delta_ref.shape
    states = log_ref.shape[0]
    parts = width // LANES
    rates = rates_of(log_ref)
    blocks = steps // BLK
    drive[...] = delta_ref[...] * conv_ref[...]

    def forward(i, state):
        state = list(state)
        inwards = in_ref[i]
        for k in range(BLK):
            t = i * BLK + k
            inward = jnp.broadcast_to(inwards[:, k : k + 1], (states, LANES))
            deltas = lane_parts(block_of(delta_ref, i), k, states)
            drives = lane_parts(block_of(drive, i), k, states)
            for j in range(parts):
                at = slice(j * LANES, (j + 1) * LANES)
                decay = jnp.exp2(deltas[j] * rates[j])
                kept = decay * state[j]
                carried[t, :, at] = kept
                state[j] = kept + inward * drives[j]
                stack[k * states : (k + 1) * states, at] = state[j].astype(jnp.bfloat16)
        rows = pl.ds(pl.multiple_of(i * BLK, BLK), BLK)
        partial = cols_dot(grad_ref[rows, :].astype(jnp.bfloat16), stack[...])

        @pl.when(first)
        def _():
            grad_out_ref[rows, :] = partial

        @pl.when(jnp.logical_not(first))
        def _():
            grad_out_ref[rows, :] += partial

        return tuple(state)

    begin = tuple(start_ref[0, :, j * LANES : (j + 1) * LANES] for j in range(parts))
    lax.fori_loop(0, blocks, forward, begin)
    middle()
    column = lax.broadcasted_iota(jnp.int32, (BLK, BLK * states), 1) // states
    row = lax.broadcasted_iota(jnp.int32, (BLK, BLK * states), 0)
    ones = jnp.where(column == row, 1.0, 0.0).astype(jnp.bfloat16)

    def backward(i, state):
        adjoint, gathered = list(state[:parts]), list(state[parts:])
        outwards = out_ref[blocks - 1 - i]
        for k in reversed(range(BLK)):
            t = (blocks - 1 - i) * BLK + k
            outward = jnp.broadcast_to(outwards[:, k : k + 1], (states, LANES))
            deltas = lane_parts(block_of(delta_ref, blocks - 1 - i), k, states)
            grads = lane_parts(block_of(grad_ref, blocks - 1 - i), k, states)
            for j in range(parts):
                at = slice(j * LANES, (j + 1) * LANES)
                whole = adjoint[j] + outward * grads[j]
                exponent = whole * carried[t, :, at]
                gathered[j] = gathered[j] + exponent * deltas[j]
                slope[k * states : (k + 1) * states, at] = (exponent * rates[j]).astype(
                    jnp.bfloat16
                )
                stack[k * states : (k + 1) * states, at] = whole.astype(jnp.bfloat16)
                adjoint[j] = jnp.exp2(deltas[j] * rates[j]) * whole
        rows = pl.ds(pl.multiple_of((blocks - 1 - i) * BLK, BLK), BLK)
        driven = jnp.dot(in_diag_ref[rows, :], stack[...], preferred_element_type=jnp.float32)
        summed = jnp.dot(ones, slope[...], preferred_element_type=jnp.float32) * LN2
        grad_delta_ref[rows, :] = summed + driven * conv_ref[rows, :]
        grad_conv_ref[rows, :] = driven * delta_ref[rows, :]
        partial = cols_dot(drive[rows, :].astype(jnp.bfloat16), stack[...])

        @pl.when(first)
        def _():
            grad_in_ref[rows, :] = partial

        @pl.when(jnp.logical_not(first))
        def _():
            grad_in_ref[rows, :] += partial

        return tuple(adjoint + gathered)

    ends = tuple(finish_ref[0, :, j * LANES : (j + 1) * LANES] for j in range(parts))
    zero = tuple(jnp.zeros((states, LANES), jnp.float32) for _ in range(parts))
    last = lax.fori_loop(0, blocks, backward, ends + zero)
    for j in range(parts):
        grad_log_ref[0, :, j * LANES : (j + 1) * LANES] = last[parts + j] * rates[j] * LN2


def scan_call(kernel, name, sequences, states, operands, results, scratch):
    tokens, width = next(value.shape for kind, value in operands if kind == "wide")
    steps = tokens // sequences
    specs = {
        "wide": pl.BlockSpec((steps, GROUP), lambda q, j: (q, j)),
        "cols": pl.BlockSpec((steps // BLK, states, BLK), lambda q, j: (q, 0, 0)),
        "narrow": pl.BlockSpec((steps, BLK * states), lambda q, j: (q, 0)),
        "rates": pl.BlockSpec((states, GROUP), lambda q, j: (0, j)),
        "state": pl.BlockSpec((1, states, GROUP), lambda q, j: (q, 0, j)),
    }
    shapes = {
        "wide": (tokens, width),
        "narrow": (tokens, BLK * states),
        "state": (sequences, states, width),
    }
    in_specs = [specs[kind] for kind, _ in operands]
    out_specs = [specs[kind] for kind in results]
    out_shape = [jax.ShapeDtypeStruct(shapes[kind], jnp.float32) for kind in results]
    return pl.pallas_call(
        kernel,
        name=name,
        grid=(sequences, width // GROUP),
        in_specs=in_specs,
        out_specs=out_specs,
        out_shape=out_shape,
        scratch_shapes=scratch,
        compiler_params=pltpu.CompilerParams(
            dimension_semantics=("arbitrary", "arbitrary"),
            vmem_limit_bytes=VMEM_BYTES,
        ),
        cost_estimate=pl.CostEstimate(
            flops=20 * tokens * states * width,
            transcendentals=tokens * states * width,
            bytes_accessed=16 * tokens * width,
        ),
    )(*(value for _, value in operands))


MESH = pl.DeviceIdType.MESH


def remote(src, dst, send, arrive, axis, peer):
    return pltpu.make_async_remote_copy(
        src_ref=src,
        dst_ref=dst,
        send_sem=send,
        recv_sem=arrive,
        device_id={axis: peer},
        device_id_type=MESH,
    )


def greet(axes):
    barrier = pltpu.get_barrier_semaphore()
    total = 0
    for axis, size in axes:
        mine = lax.axis_index(axis)
        for k in range(1, size):
            pl.semaphore_signal(
                barrier, inc=1, device_id={axis: lax.rem(mine + k, size)}, device_id_type=MESH
            )
        total += size - 1
    pl.semaphore_wait(barrier, total)


def exchange_body(
    after_first,
    after_second,
    reverse,
    planes,
    members,
    end_ref,
    sum_ref,
    log_ref,
    carry_ref,
    packed,
    landed,
    summary,
    totals,
    starts,
    carries,
    send_one,
    recv_one,
    send_two,
    recv_two,
    send_three,
    recv_three,
):
    sequences, states, width = end_ref.shape
    rows = sequences * states // members
    plane, member = lax.axis_index("seq"), lax.axis_index("exp")
    own = lax.rem(member, states // rows)
    logs = jnp.zeros((rows, width), jnp.float32)
    for i in range(states // rows):
        logs = jnp.where(own == i, log_ref[i * rows : (i + 1) * rows], logs)
    rates = -jnp.exp(logs)
    for i in range(members):
        q, n = (i * rows) // states, (i * rows) % states
        packed[i, :rows] = end_ref[q, n : n + rows]
        packed[i, rows:] = sum_ref[q : q + 1]
    for k in range(1, members):
        other = lax.rem(member + k, members)
        remote(
            packed.at[other],
            landed.at[member],
            send_one.at[k],
            recv_one.at[member],
            "exp",
            other,
        ).start()
    after_first()
    landed[member] = packed[member]
    for k in range(1, members):
        other = lax.rem(member + k, members)
        remote(
            packed.at[other], landed.at[other], send_one.at[k], recv_one.at[other], "exp", other
        ).wait()
    order = range(members)[::-1] if reverse else range(members)
    plane_order = range(planes)[::-1] if reverse else range(planes)

    def through(piece, before):
        return jnp.exp(piece[rows:] * rates) * before + piece[:rows]

    state = jnp.zeros((rows, width), jnp.float32)
    total = jnp.zeros((1, width), jnp.float32)
    for i in order:
        piece = landed[i]
        state = through(piece, state)
        total = total + piece[rows:]
    summary[:rows] = state
    summary[rows:] = total
    for k in range(1, planes):
        other = lax.rem(plane + k, planes)
        remote(
            summary, totals.at[plane], send_two.at[k], recv_two.at[plane], "seq", other
        ).start()
    totals[plane] = summary[...]
    for k in range(1, planes):
        other = lax.rem(plane + k, planes)
        remote(summary, totals.at[other], send_two.at[k], recv_two.at[other], "seq", other).wait()
    after_second()
    state = jnp.zeros((rows, width), jnp.float32)
    for s in plane_order:
        reached = plane < s if reverse else plane > s
        state = jnp.where(reached, through(totals[s], state), state)
    for i in order:
        starts[i] = state
        state = through(landed[i], state)
    for k in range(1, members):
        other = lax.rem(member + k, members)
        remote(
            starts.at[other],
            carries.at[member],
            send_three.at[k],
            recv_three.at[member],
            "exp",
            other,
        ).start()
    carries[member] = starts[member]
    for k in range(1, members):
        other = lax.rem(member + k, members)
        remote(
            starts.at[other],
            carries.at[other],
            send_three.at[k],
            recv_three.at[other],
            "exp",
            other,
        ).wait()
    for i in range(members):
        q, n = (i * rows) // states, (i * rows) % states
        carry_ref[q, n : n + rows] = carries[i]


def exchange_kernel(reverse, planes, members, *refs):
    greet((("seq", planes), ("exp", members)))
    exchange_body(lambda: None, lambda: None, reverse, planes, members, *refs)


def exchange_scratch(planes, members, rows, width):
    piece = (rows + 1, width)
    return [
        pltpu.VMEM((members,) + piece, jnp.float32),
        pltpu.VMEM((members,) + piece, jnp.float32),
        pltpu.VMEM(piece, jnp.float32),
        pltpu.VMEM((planes,) + piece, jnp.float32),
        pltpu.VMEM((members, rows, width), jnp.float32),
        pltpu.VMEM((members, rows, width), jnp.float32),
        pltpu.SemaphoreType.DMA((members,)),
        pltpu.SemaphoreType.DMA((members,)),
        pltpu.SemaphoreType.DMA((planes,)),
        pltpu.SemaphoreType.DMA((planes,)),
        pltpu.SemaphoreType.DMA((members,)),
        pltpu.SemaphoreType.DMA((members,)),
    ]


def exchange(local_end, delta_sum, decay_log):
    planes, members = lax.axis_size("seq"), lax.axis_size("exp")
    sequences, states, width = local_end.shape
    rows = sequences * states // members
    vmem = pl.BlockSpec(memory_space=pltpu.VMEM)
    return pl.pallas_call(
        functools.partial(exchange_kernel, True, planes, members),
        name="state_exchange_back",
        in_specs=[vmem] * 3,
        out_specs=vmem,
        out_shape=jax.ShapeDtypeStruct(local_end.shape, jnp.float32),
        scratch_shapes=exchange_scratch(planes, members, rows, width),
        compiler_params=pltpu.CompilerParams(
            collective_id=2, has_side_effects=True, vmem_limit_bytes=VMEM_BYTES
        ),
        cost_estimate=pl.CostEstimate(flops=10**6, transcendentals=10**5, bytes_accessed=2 * 10**7),
    )(local_end, delta_sum, decay_log)


class Sums:
    def __init__(self, planes, side, sends, arrivals):
        self.planes, self.side = planes, side
        self.plane, self.member = lax.axis_index("seq"), lax.axis_index("exp")
        chip, self.core = self.member // 2, lax.rem(self.member, 2)
        high, low = chip // side, lax.rem(chip, side)
        self.first = low + (high - low) * self.core
        self.second = high + (low - high) * self.core
        self.partner = self.member + 1 - 2 * self.core
        self.sends, self.arrivals = sends, arrivals

    def chip_at(self, first, second):
        low = first + (second - first) * self.core
        high = second + (first - second) * self.core
        return (high * self.side + low) * 2 + self.core

    def first_peer(self, k):
        other = lax.rem(self.first + k, self.side)
        return other, self.chip_at(other, self.second)

    def second_peer(self, k):
        other = lax.rem(self.second + k, self.side)
        return other, self.chip_at(self.first, other)

    def plane_peer(self, k):
        return lax.rem(self.plane + k, self.planes)

    def signal_peers(self, barrier):
        peers = [{"exp": self.partner}]
        peers += [{"exp": self.first_peer(k)[1]} for k in range(1, self.side)]
        peers += [{"exp": self.second_peer(k)[1]} for k in range(1, self.side)]
        peers += [{"seq": self.plane_peer(k)} for k in range(1, self.planes)]
        for peer in peers:
            pl.semaphore_signal(barrier, inc=1, device_id=peer, device_id_type=MESH)
        return len(peers)

    def move(self, stage, at, slot, src, dst, axis, peer):
        return remote(
            src, dst, self.sends[stage].at[at], self.arrivals[stage].at[slot], axis, peer
        )

    def pair_half(self, i, given, half):
        return self.move(0, i, i, given.at[1 - self.core], half, "exp", self.partner)

    def scatter_first(self, i, k, half, slots, arriving):
        other, device = self.first_peer(k)
        slot = other if arriving else self.first
        return self.move(1, (i, k), (i, slot), half.at[other], slots.at[slot], "exp", device)

    def scatter_second(self, i, k, quarter, slots, arriving):
        other, device = self.second_peer(k)
        slot = other if arriving else self.second
        return self.move(2, (i, k), (i, slot), quarter.at[other], slots.at[slot], "exp", device)

    def scatter_plane(self, i, k, eighth, slots, arriving):
        other = self.plane_peer(k)
        slot = other if arriving else self.plane
        return self.move(3, (i, k), (i, slot), eighth.at[other], slots.at[slot], "seq", other)

    def gather_plane(self, i, k, block, arriving):
        other = self.plane_peer(k)
        slot = other if arriving else self.plane
        return self.move(
            4, (i, k), (i, slot), block.at[self.plane], block.at[slot], "seq", other
        )

    def gather_second(self, i, k, result, arriving):
        other, device = self.second_peer(k)
        slot = other if arriving else self.second
        row = result.at[self.core, self.first]
        return self.move(5, (i, k), (i, slot), row.at[self.second], row.at[slot], "exp", device)

    def gather_first(self, i, k, result, arriving):
        other, device = self.first_peer(k)
        slot = other if arriving else self.first
        own = result.at[self.core]
        return self.move(6, (i, k), (i, slot), own.at[self.first], own.at[slot], "exp", device)

    def pair_gather(self, i, k, result, arriving):
        other = lax.rem(self.first + k, self.side)
        low = lax.rem(self.partner // 2, self.side)
        theirs = low + (self.partner // (2 * self.side) - low) * (1 - self.core)
        other = lax.rem(theirs + k, self.side) if arriving else other
        half = 1 - self.core if arriving else self.core
        mine = result.at[self.core, lax.rem(self.first + k, self.side)]
        return self.move(7, (i, k), (i, k), mine, result.at[half, other], "exp", self.partner)

    def after_pair(self, i, given, half, slots):
        self.pair_half(i, given, half).wait()
        own = self.core
        for at in range(self.side):
            for to in range(self.side):
                both = given[own, at, to].astype(jnp.float32) + half[at, to].astype(jnp.float32)
                half[at, to] = both.astype(jnp.bfloat16)
        for k in range(1, self.side):
            self.scatter_first(i, k, half, slots, False).start()
        slots[self.first] = half[self.first]

    def after_first(self, i, half, slots, quarter, slots_two):
        for k in range(1, self.side):
            self.scatter_first(i, k, half, slots, True).wait_recv()
        for at in range(self.side):
            added = slots[0, at].astype(jnp.float32)
            for k in range(1, self.side):
                added = added + slots[k, at].astype(jnp.float32)
            quarter[at] = added.astype(jnp.bfloat16)
        for k in range(1, self.side):
            self.scatter_second(i, k, quarter, slots_two, False).start()
        slots_two[self.second] = quarter[self.second]

    def after_second(self, i, quarter, slots_two, eighth, slots_three):
        for k in range(1, self.side):
            self.scatter_second(i, k, quarter, slots_two, True).wait_recv()
        added = slots_two[0].astype(jnp.float32)
        for k in range(1, self.side):
            added = added + slots_two[k].astype(jnp.float32)
        eighth[...] = added.astype(jnp.bfloat16)
        for k in range(1, self.planes):
            self.scatter_plane(i, k, eighth, slots_three, False).start()
        slots_three[self.plane] = eighth[self.plane]

    def after_planes(self, i, eighth, slots_three, block):
        for k in range(1, self.planes):
            self.scatter_plane(i, k, eighth, slots_three, True).wait_recv()
        added = slots_three[0].astype(jnp.float32)
        for k in range(1, self.planes):
            added = added + slots_three[k].astype(jnp.float32)
        block[self.plane] = added.astype(jnp.bfloat16)
        for k in range(1, self.planes):
            self.gather_plane(i, k, block, False).start()

    def planes_gathered(self, i, block):
        for k in range(1, self.planes):
            self.gather_plane(i, k, block, True).wait_recv()

    def scatter_sent(self, i, half, slots, quarter, slots_two, eighth, slots_three, block):
        for k in range(1, self.side):
            self.scatter_first(i, k, half, slots, False).wait_send()
            self.scatter_second(i, k, quarter, slots_two, False).wait_send()
        for k in range(1, self.planes):
            self.scatter_plane(i, k, eighth, slots_three, False).wait_send()
            self.gather_plane(i, k, block, False).wait_send()

    def gather_second_start(self, i, result):
        for k in range(1, self.side):
            self.gather_second(i, k, result, False).start()

    def gather_across(self, i, result):
        for k in range(1, self.side):
            self.gather_second(i, k, result, True).wait_recv()
        for k in range(1, self.side):
            self.gather_first(i, k, result, False).start()
        self.pair_gather(i, 0, result, False).start()

    def gather_pass(self, i, result):
        for k in range(1, self.side):
            self.gather_first(i, k, result, True).wait_recv()
            self.pair_gather(i, k, result, False).start()

    def gather_end(self, i, result):
        for k in range(self.side):
            self.pair_gather(i, k, result, True).wait_recv()
            self.pair_gather(i, k, result, False).wait_send()
        for k in range(1, self.side):
            self.gather_first(i, k, result, False).wait_send()
            self.gather_second(i, k, result, False).wait_send()


def stage_semaphores(count, planes, side):
    each = [(count,)] + [(count, size) for size in (side, side, planes, planes, side, side, side)]
    return [pltpu.SemaphoreType.DMA(shape) for shape in each]


def scatter_buffers(tails, planes, side):
    leads = [(side, side, planes), (side, side, planes), (side, planes), (side, planes)]
    leads += [(planes,), (planes,)]
    return [pltpu.VMEM(lead + tail, jnp.bfloat16) for lead in leads for tail in tails]


def neighbour_plane():
    plane = lax.axis_index("seq")
    return {"seq": plane + 1 - 2 * lax.rem(plane, 2)}


def swapped(src, dst, send, arrive):
    return pltpu.make_async_remote_copy(
        src_ref=src,
        dst_ref=dst,
        send_sem=send,
        recv_sem=arrive,
        device_id=neighbour_plane(),
        device_id_type=MESH,
    )


class Routes:
    def __init__(self, planes, members, sends, arrivals, local):
        self.planes, self.members = planes, members
        self.plane, self.member = lax.axis_index("seq"), lax.axis_index("exp")
        self.hops = planes // 2
        self.sends, self.arrivals, self.local = sends, arrivals, local
        self.pairs = [
            (hop, k) for hop in range(self.hops) for k in range(members) if hop or k
        ]

    def device(self, hop, k):
        return {
            "seq": lax.rem(self.plane + 2 * hop, self.planes),
            "exp": lax.rem(self.member + k, self.members),
        }

    def signal_peers(self, barrier):
        for hop, k in self.pairs:
            pl.semaphore_signal(
                barrier, inc=1, device_id=self.device(hop, k), device_id_type=MESH
            )
        return len(self.pairs)

    def moved(self, given, landed, returning, hop, k, arriving):
        device = self.device(hop, k)
        other = device["exp"]
        slot = hop if arriving else (-hop) % self.hops
        if returning:
            index = other if arriving else self.member
            src = given.at[hop, (self.members - k) % self.members]
        else:
            index, src = k, given.at[other]
        return pltpu.make_async_remote_copy(
            src_ref=src,
            dst_ref=landed.at[slot, index],
            send_sem=self.sends.at[hop, k],
            recv_sem=self.arrivals.at[slot, index],
            device_id=device,
            device_id_type=MESH,
        )

    def own(self, given, landed, returning):
        src = given.at[0, 0] if returning else given.at[self.member]
        index = self.member if returning else 0
        return pltpu.make_async_copy(src, landed.at[0, index], self.local)

    def start(self, given, landed, returning):
        for hop, k in self.pairs:
            self.moved(given, landed, returning, hop, k, False).start()
        self.own(given, landed, returning).start()

    def wait_sent(self, given, landed):
        for hop, k in self.pairs:
            self.moved(given, landed, False, hop, k, False).wait_send()

    def wait(self, given, landed, returning):
        for hop, k in self.pairs:
            self.moved(given, landed, returning, hop, k, True).wait_recv()
        self.own(given, landed, returning).wait()
        for hop, k in self.pairs:
            self.moved(given, landed, returning, hop, k, False).wait_send()


def route_semaphores(planes, members):
    shape = (planes // 2, members)
    return [
        pltpu.SemaphoreType.DMA(shape),
        pltpu.SemaphoreType.DMA(shape),
        pltpu.SemaphoreType.DMA,
    ]


def two_part(left, right, dims):
    high = left.astype(jnp.bfloat16)
    rest = (left - high.astype(jnp.float32)).astype(jnp.bfloat16)
    numbers = (dims, ((), ()))
    wide = jnp.float32
    return lax.dot_general(high, right, numbers, preferred_element_type=wide) + lax.dot_general(
        rest, right, numbers, preferred_element_type=wide
    )


LANE_UNIT = 256


def lane_unit(j):
    return pl.ds(pl.multiple_of(j * LANE_UNIT, LANE_UNIT), LANE_UNIT)


def normalized(values, gain):
    return values * lax.rsqrt(jnp.mean(values * values, axis=-1, keepdims=True) + EPSILON) * gain


def chain_device(at, members):
    return {"seq": at // members, "exp": lax.rem(at, members)}


def forward_kernel(
    planes,
    members,
    capacity,
    layer_ref,
    out_grad_ref,
    target_ref,
    mixer_gain_all_ref,
    conv_bias_all_ref,
    delta_bias_all_ref,
    skip_all_ref,
    expert_norm_all_ref,
    in_proj_ref,
    conv_weight_ref,
    state_proj_ref,
    delta_proj_ref,
    decay_log_ref,
    out_proj_ref,
    up_ref,
    down_ref,
    normed_ref,
    extended_ref,
    gate_ref,
    conv_pre_ref,
    conv_ref,
    delta_pre_ref,
    delta_ref,
    delta_low_ref,
    in_cols_ref,
    out_cols_ref,
    in_diag_ref,
    delta_sum_ref,
    carried_ref,
    mixer_pre_ref,
    mixed_ref,
    resid_ref,
    row_slots_ref,
    grad_rows_ref,
    near_up_ref,
    near_half_ref,
    rim_in_ref,
    vectors_ref,
    grad_slots_ref,
    drive_ref,
    stack_ref,
    low_sum_ref,
    wide_sum_ref,
    out_diag_ref,
    out_rest_ref,
    local_end_ref,
    rim_out_ref,
    rim_sent_ref,
    rim_landed_ref,
    up_sent_ref,
    up_landed_ref,
    down_sent_ref,
    down_landed_ref,
    *rest,
):
    exchange_refs, grad_semaphores = rest[:12], rest[12:15]
    wide, half = jnp.float32, jnp.bfloat16
    tokens, width = layer_ref.shape
    own_tokens = slice(0, tokens)
    inner_width = conv_ref.shape[1]
    sequences = extended_ref.shape[0]
    piece = tokens // sequences
    states, taps = decay_log_ref.shape[0], conv_weight_ref.shape[0]
    low_rank = delta_low_ref.shape[1]
    experts = row_slots_ref.shape[0]
    for i, source in enumerate((conv_bias_all_ref, delta_bias_all_ref, skip_all_ref)):
        vectors_ref[i : i + 1, :] = source[...].reshape(1, inner_width)
    vectors_ref[3:4, :width] = mixer_gain_all_ref[...].reshape(1, width)
    vectors_ref[3:4, width:] = expert_norm_all_ref[...].reshape(1, width)
    conv_bias_ref, delta_bias_ref, skip_ref = (vectors_ref.at[i : i + 1] for i in range(3))
    mixer_gain_ref, expert_norm_ref = vectors_ref.at[3:4, :width], vectors_ref.at[3:4, width:]
    devices = planes * members
    place = lax.axis_index("seq") * members + lax.axis_index("exp")
    before, after = lax.rem(place + devices - 1, devices), lax.rem(place + 1, devices)
    grad_routes = Routes(planes, members, *grad_semaphores)
    barrier = pltpu.get_barrier_semaphore()
    for peer in (before, after):
        device = chain_device(peer, members)
        pl.semaphore_signal(barrier, inc=1, device_id=device, device_id_type=MESH)
    greeted = 2 + grad_routes.signal_peers(barrier)
    for axis, size in (("seq", planes), ("exp", members)):
        mine = lax.axis_index(axis)
        for k in range(1, size):
            other = {axis: lax.rem(mine + k, size)}
            pl.semaphore_signal(barrier, inc=1, device_id=other, device_id_type=MESH)
        greeted += size - 1
    for q in range(sequences):
        rim_out_ref[q] = layer_ref[(q + 1) * piece - 8 : (q + 1) * piece]
    pl.semaphore_wait(barrier, greeted)
    rim_copy = pltpu.make_async_remote_copy(
        src_ref=rim_out_ref,
        dst_ref=rim_in_ref,
        send_sem=rim_sent_ref,
        recv_sem=rim_landed_ref,
        device_id=chain_device(after, members),
        device_id_type=MESH,
    )
    rim_copy.start()
    up_rows = up_ref.shape[1]
    marks = (0, up_rows // 2, up_rows * 11 // 16, up_rows)
    up_swaps = []
    for i, (low, high) in enumerate(zip(marks, marks[1:])):
        at = pl.ds(low, high - low)
        ends = (up_ref.at[:, at], near_up_ref.at[:, at])
        up_swaps.append(swapped(*ends, up_sent_ref.at[i], up_landed_ref.at[i]))
    slot = lax.broadcasted_iota(jnp.int32, (experts * capacity, tokens), 0)
    picks = jnp.where(slot == target_ref[...], 1.0, 0.0).astype(half)

    def fill(slots, values):
        product = half_dot(picks, values).astype(half)
        for e in range(experts):
            slots[e] = product[e * capacity : (e + 1) * capacity]

    fill(grad_slots_ref, out_grad_ref[...])
    grad_routes.start(grad_slots_ref, grad_rows_ref, False)
    up_swaps[0].start()
    cut = down_ref.shape[1] // 2
    down_swap = swapped(down_ref.at[:, pl.ds(0, cut)], near_half_ref, down_sent_ref, down_landed_ref)

    count = inner_width // LANE_UNIT
    normed_ref[own_tokens, :] = normalized(layer_ref[...].astype(wide), mixer_gain_ref[...]).astype(half)

    def project(j, carry):
        at = lane_unit(j)
        product = half_dot(normed_ref[own_tokens, :], in_proj_ref[:, at])
        for q in range(sequences):
            extended_ref[q, 8:, at] = product[q * piece : (q + 1) * piece]
        gate_at = pl.ds(pl.multiple_of(inner_width + j * LANE_UNIT, LANE_UNIT), LANE_UNIT)
        gate_ref[:, at] = half_dot(normed_ref[own_tokens, :], in_proj_ref[:, gate_at])
        return carry

    lax.fori_loop(0, count, project, 0)
    rim_copy.wait()
    keep = jnp.where(place > 0, 1.0, 0.0)
    rims = [normalized(rim_in_ref[q].astype(wide), mixer_gain_ref[...]) for q in range(sequences)]
    rim_normed = jnp.concatenate(rims, axis=0).astype(half)
    normed_ref[tokens:, :] = rim_normed
    low_sum_ref[...] = jnp.zeros(low_sum_ref.shape, wide)
    wide_sum_ref[...] = jnp.zeros(wide_sum_ref.shape, wide)

    def convolve(j, carry):
        at = lane_unit(j)
        rim = half_dot(rim_normed, in_proj_ref[:, at]) * keep
        for q in range(sequences):
            extended_ref[q, :8, at] = rim[q * 8 : (q + 1) * 8]
            start = 8 - (taps - 1)
            pre = conv_bias_ref[:, at] + conv_weight_ref[:1, at] * extended_ref[q, start : start + piece, at]
            for tap in range(1, taps):
                moved = extended_ref[q, start + tap : start + tap + piece, at]
                pre = pre + conv_weight_ref[tap : tap + 1, at] * moved
            conv_pre_ref[q * piece : (q + 1) * piece, at] = pre
            conv_ref[q * piece : (q + 1) * piece, at] = pre * jax.nn.sigmoid(pre)
        act = conv_ref[:, at]
        high = act.astype(half)
        low = (act - high.astype(wide)).astype(half)
        weight = state_proj_ref[:, at]
        low_sum_ref[...] += cols_dot(high, weight) + cols_dot(low, weight)
        tail = weight[low_rank:]
        wide_sum_ref[...] += cols_dot(tail, high) + cols_dot(tail, low)
        return carry

    lax.fori_loop(0, count, convolve, 0)
    delta_low_ref[...] = low_sum_ref[:, :low_rank]
    for i in range(tokens // BLK):
        block = wide_sum_ref[:, i * BLK : (i + 1) * BLK]
        in_cols_ref[i] = block[:states]
        out_cols_ref[i] = block[states:]
    shape = (tokens, BLK * states)
    column = lax.broadcasted_iota(jnp.int32, shape, 1)
    row = lax.rem(lax.broadcasted_iota(jnp.int32, shape, 0), BLK)
    own = column // states == row
    tile = jnp.where(
        lax.rem(lax.broadcasted_iota(jnp.int32, (states, BLK * states), 1), states)
        == lax.broadcasted_iota(jnp.int32, (states, BLK * states), 0),
        1.0,
        0.0,
    ).astype(half)

    def spread_out(values):
        return jnp.where(own, half_dot(values, tile), 0.0).astype(half)

    outward = low_sum_ref[:, low_rank + states :]
    out_high = outward.astype(half)
    in_diag_ref[...] = spread_out(low_sum_ref[:, low_rank : low_rank + states].astype(half))
    out_diag_ref[...] = spread_out(out_high)
    out_rest_ref[...] = spread_out((outward - out_high.astype(wide)).astype(half))

    def time_steps(j, carry):
        at = lane_unit(j)
        pre = two_part(delta_low_ref[...], delta_proj_ref[:, at], ((1,), (0,))) + delta_bias_ref[:, at]
        delta = jnp.maximum(pre, 0.0) + jnp.log1p(jnp.exp(-jnp.abs(pre)))
        delta_pre_ref[:, at] = pre
        delta_ref[:, at] = delta
        for q in range(sequences):
            part = delta[q * piece : (q + 1) * piece]
            delta_sum_ref[q : q + 1, at] = jnp.sum(part, axis=0, keepdims=True)
        return carry

    lax.fori_loop(0, count, time_steps, 0)
    groups = inner_width // GROUP
    blocks = piece // BLK

    def views(i):
        q, j = i // groups, lax.rem(i, groups)
        rows = pl.ds(pl.multiple_of(q * piece, piece), piece)
        lanes = pl.ds(pl.multiple_of(j * GROUP, GROUP), GROUP)
        cols = pl.ds(q * blocks, blocks)
        return q, rows, lanes, cols

    def first(i, carry):
        q, rows, lanes, cols = views(i)
        first_pass_kernel(
            delta_ref.at[rows, lanes],
            conv_ref.at[rows, lanes],
            in_cols_ref.at[cols],
            decay_log_ref.at[:, lanes],
            local_end_ref.at[pl.ds(q, 1), :, lanes],
            drive_ref,
        )
        return carry

    lax.fori_loop(0, sequences * groups, first, 0)

    def between_planes():
        up_swaps[2].start()
        down_swap.start()

    exchange_body(
        up_swaps[1].start,
        between_planes,
        False,
        planes,
        members,
        local_end_ref,
        delta_sum_ref,
        decay_log_ref,
        carried_ref,
        *exchange_refs,
    )

    def second(i, carry):
        q, rows, lanes, cols = views(i)
        second_pass_kernel(
            delta_ref.at[rows, lanes],
            conv_ref.at[rows, lanes],
            in_cols_ref.at[cols],
            decay_log_ref.at[:, lanes],
            carried_ref.at[pl.ds(q, 1), :, lanes],
            out_diag_ref.at[rows],
            out_rest_ref.at[rows],
            mixer_pre_ref.at[rows, lanes],
            drive_ref,
            stack_ref,
        )
        return carry

    lax.fori_loop(0, sequences * groups, second, 0)

    def mix(j, carry):
        at = lane_unit(j)
        pre = mixer_pre_ref[:, at] + skip_ref[:, at] * conv_ref[:, at]
        gate = gate_ref[:, at]
        mixer_pre_ref[:, at] = pre
        mixed_ref[:, at] = (pre * (gate * jax.nn.sigmoid(gate))).astype(half)
        return carry

    lax.fori_loop(0, count, mix, 0)
    resid_ref[...] = layer_ref[...].astype(wide) + half_dot(mixed_ref[...], out_proj_ref[...])
    fill(row_slots_ref, normalized(resid_ref[...], expert_norm_ref[...]).astype(half))
    grad_routes.wait(grad_slots_ref, grad_rows_ref, False)
    down_swap.wait()
    for swap in up_swaps:
        swap.wait()


def forward(operands, capacity, states, sequences, low_rank, experts):
    planes, members = lax.axis_size("seq"), lax.axis_size("exp")
    tokens, width = operands[0].shape
    inner_width = operands[9].shape[1]
    up, down = operands[14:16]
    half, wide = jnp.bfloat16, jnp.float32
    piece = tokens // sequences
    token_wide = jax.ShapeDtypeStruct((tokens, inner_width), wide)
    cols = jax.ShapeDtypeStruct((tokens // BLK, states, BLK), wide)
    diag = (tokens, BLK * states)
    routed = jax.ShapeDtypeStruct((planes // 2, members, capacity, width), half)
    state = (sequences, states, inner_width)
    vmem, anywhere = (pl.BlockSpec(memory_space=space) for space in (pltpu.VMEM, pl.ANY))
    scratch = [
        pltpu.VMEM((experts, capacity, width), half),
        pltpu.VMEM((piece, GROUP), wide),
        pltpu.VMEM((piece * states, GROUP), half),
        pltpu.VMEM((tokens, low_rank + 2 * states), wide),
        pltpu.VMEM((2 * states, tokens), wide),
        pltpu.VMEM(diag, half),
        pltpu.VMEM(diag, half),
        pltpu.VMEM(state, wide),
        pltpu.VMEM((sequences, 8, width), half),
    ]
    scratch += [pltpu.SemaphoreType.DMA] * 2 + [pltpu.SemaphoreType.DMA((3,))] * 2
    scratch += [pltpu.SemaphoreType.DMA] * 2
    scratch += exchange_scratch(planes, members, sequences * states // members, inner_width)
    scratch += route_semaphores(planes, members)
    return pl.pallas_call(
        functools.partial(forward_kernel, planes, members, capacity),
        name="forward_to_experts",
        in_specs=[vmem] * 14 + [anywhere] * 2,
        out_specs=[vmem] * 17 + [anywhere] * 3 + [vmem] * 2,
        out_shape=[
            jax.ShapeDtypeStruct((tokens + 8 * sequences, width), half),
            jax.ShapeDtypeStruct((sequences, piece + 8, inner_width), wide),
            token_wide,
            token_wide,
            token_wide,
            token_wide,
            token_wide,
            jax.ShapeDtypeStruct((tokens, low_rank), wide),
            cols,
            cols,
            jax.ShapeDtypeStruct(diag, half),
            jax.ShapeDtypeStruct((sequences, inner_width), wide),
            jax.ShapeDtypeStruct(state, wide),
            token_wide,
            jax.ShapeDtypeStruct((tokens, inner_width), half),
            jax.ShapeDtypeStruct((tokens, width), wide),
            jax.ShapeDtypeStruct((experts, capacity, width), half),
            routed,
            jax.ShapeDtypeStruct(up.shape, half),
            jax.ShapeDtypeStruct((1, down.shape[1] // 2, width), half),
            jax.ShapeDtypeStruct((sequences, 8, width), half),
            jax.ShapeDtypeStruct((4, inner_width), wide),
        ],
        scratch_shapes=scratch,
        compiler_params=pltpu.CompilerParams(
            collective_id=1, has_side_effects=True, vmem_limit_bytes=60 * 1024 * 1024
        ),
        cost_estimate=pl.CostEstimate(flops=10**8, transcendentals=0, bytes_accessed=2 * 10**8),
    )(*operands)


def expert_kernel(
    planes,
    members,
    row_slots_ref,
    grad_rows_ref,
    up_ref,
    down_ref,
    near_up_ref,
    near_half_ref,
    router_ref,
    outs_ref,
    back_ref,
    grad_up_ref,
    grad_down_ref,
    far_up_ref,
    far_down_ref,
    grad_router_ref,
    landed_ref,
    rows_ref,
    grads_ref,
    sent_ref,
    near_down_ref,
    out_sum_ref,
    row_sum_ref,
    hidden_own_ref,
    hidden_near_ref,
    pre_own_ref,
    pre_near_ref,
    shares_ref,
    far_up_sum_ref,
    far_down_sum_ref,
    returns_ref,
    down_sent_ref,
    down_landed_ref,
    back_sent_ref,
    back_landed_ref,
    *rest,
):
    routes = Routes(planes, members, *rest)
    wide, half = jnp.float32, jnp.bfloat16
    plane, member, hops = routes.plane, routes.member, routes.hops
    capacity, width = row_slots_ref.shape[1:]
    batch = members // 2
    chunk = batch * capacity
    group = members * capacity
    units = up_ref.shape[2]
    cut = units // 2
    experts = router_ref.shape[0]
    chosen_row = jnp.where(
        lax.broadcasted_iota(jnp.int32, (1, experts), 1) == member, 1.0, 0.0
    )
    barrier = pltpu.get_barrier_semaphore()
    pl.semaphore_signal(barrier, inc=1, device_id=neighbour_plane(), device_id_type=MESH)
    pl.semaphore_wait(barrier, routes.signal_peers(barrier) + 1)
    routes.start(row_slots_ref, landed_ref, False)
    down_swap = swapped(
        down_ref.at[0, pl.ds(cut, cut)], near_down_ref.at[pl.ds(cut, cut)], down_sent_ref, down_landed_ref
    )
    down_swap.start()
    near_down_ref[:cut] = near_half_ref[0]
    grad_router_ref[...] = jnp.zeros(grad_router_ref.shape, wide)
    for hop in range(hops):
        for e in range(members):
            grads_ref[hop * group + e * capacity : hop * group + (e + 1) * capacity] = grad_rows_ref[
                hop, e
            ]

    def gather(hop, c):
        rows = rows_ref.at[place(hop, c), :]
        for k in range(batch):
            r = c * batch + k
            if hop:
                routes.moved(row_slots_ref, landed_ref, False, hop, r, True).wait_recv()
            else:

                @pl.when(r > 0)
                def _():
                    routes.moved(row_slots_ref, landed_ref, False, 0, r, True).wait_recv()

            rows[k * capacity : (k + 1) * capacity, :] = landed_ref[hop, r]

    def through(at, up, down, hidden, back, where):
        pre = half_dot(rows_ref[at, :], up)
        phi = 0.5 * (1.0 + lax.erf(pre * 0.7071067811865476))
        slope = phi + pre * (jnp.exp(-0.5 * pre * pre) * 0.3989422804014327)
        active = (pre * phi).astype(half)
        hidden[at, where] = active
        arrived = (slope * cols_dot(sent_ref[at, :], down)).astype(half)
        back[at, where] = arrived
        return half_dot(active, down), cols_dot(arrived, up)

    def place(hop, c):
        return pl.ds(pl.multiple_of(hop * group + c * chunk, chunk), chunk)

    def own_part(hop, c):
        at = place(hop, c)
        logits = cols_dot(rows_ref[at, :].astype(wide), router_ref[...], lax.Precision.HIGHEST)
        raised = jnp.exp(logits - jnp.max(logits, axis=-1, keepdims=True))
        shares = raised / jnp.sum(raised, axis=-1, keepdims=True)
        gate = jnp.sum(shares * chosen_row, axis=-1, keepdims=True)
        shares_ref[at, :] = shares
        sent_ref[at, :] = (gate * grads_ref[at, :].astype(wide)).astype(half)
        every = slice(0, units)
        out, row = through(at, up_ref[0], down_ref[0], hidden_own_ref, pre_own_ref, every)
        early = slice(0, cut)
        near_out, near_row = through(
            at, near_up_ref[0, :, :cut], near_down_ref[:cut], hidden_near_ref, pre_near_ref, early
        )
        out_sum_ref[at, :] = out + near_out
        row_sum_ref[at, :] = row + near_row

    def late_part(hop, c):
        at = place(hop, c)
        near_out, near_row = through(
            at,
            near_up_ref[0, :, cut:],
            near_down_ref[cut:],
            hidden_near_ref,
            pre_near_ref,
            slice(cut, units),
        )
        out = out_sum_ref[at, :] + near_out
        shares, chosen = shares_ref[at, :], chosen_row
        gate = jnp.sum(shares * chosen, axis=-1, keepdims=True)
        grad_gate = jnp.sum(grads_ref[at, :].astype(wide) * out, axis=-1, keepdims=True)
        grad_logits = grad_gate * gate * (chosen - shares)
        outs = (gate * out).astype(half)
        row = row_sum_ref[at, :] + near_row
        row = row + jnp.dot(
            grad_logits,
            router_ref[...],
            precision=lax.Precision.HIGHEST,
            preferred_element_type=wide,
        )
        row = row.astype(half)
        grad_router_ref[...] += rows_dot(
            grad_logits, rows_ref[at, :].astype(wide), lax.Precision.HIGHEST
        )
        for k in range(batch):
            part = slice(k * capacity, (k + 1) * capacity)
            outs_ref[hop, c * batch + k] = outs[part]
            returns_ref[hop, c * batch + k] = row[part]

    def returned(hop, r, arriving):
        other = lax.rem(member + members - r, members)
        slot = hop if arriving else (-hop) % hops
        sender = other if arriving else member
        return pltpu.make_async_remote_copy(
            src_ref=returns_ref.at[hop, r],
            dst_ref=back_ref.at[slot, sender],
            send_sem=back_sent_ref.at[hop, r],
            recv_sem=back_landed_ref.at[slot, sender],
            device_id={"seq": lax.rem(plane + 2 * hop, planes), "exp": other},
            device_id_type=MESH,
        )

    def give_back(hop, c):
        for k in range(batch):
            r = c * batch + k
            if hop:
                returned(hop, r, False).start()
            else:

                @pl.when(r > 0)
                def _():
                    returned(0, r, False).start()

    def loop(body):
        def run(c, carry):
            body(c)
            return carry

        lax.fori_loop(0, 2, run, 0)

    def weight_grads(hop):
        at = slice(hop * group, (hop + 1) * group)
        rows, sent = rows_ref[at, :], sent_ref[at, :]
        products = [
            (grad_up_ref.at[0], rows, pre_own_ref[at, :]),
            (grad_down_ref.at[0], hidden_own_ref[at, :], sent),
            (far_up_sum_ref, rows, pre_near_ref[at, :]),
            (far_down_sum_ref, hidden_near_ref[at, :], sent),
        ]
        for total, left, right in products:
            if hop:
                total[...] += rows_dot(left, right)
            else:
                total[...] = rows_dot(left, right)

    routes.own(row_slots_ref, landed_ref, False).wait()

    def near_start(c):
        gather(0, c)
        own_part(0, c)

    loop(near_start)
    for hop in range(1, hops):

        def far_end(c):
            gather(hop, c)
            own_part(hop, c)
            if hop == 1:

                @pl.when(c == 0)
                def _():
                    down_swap.wait()

            late_part(hop, c)
            give_back(hop, c)

        loop(far_end)

    def near_end(c):
        late_part(0, c)
        give_back(0, c)

    loop(near_end)
    for hop in range(hops):
        weight_grads(hop)
    far_up_ref[0] = far_up_sum_ref[...].astype(half)
    far_down_ref[0] = far_down_sum_ref[...].astype(half)
    back_ref[0, member] = returns_ref[0, 0]
    for hop in range(hops):
        for r in range(members):
            if hop or r:
                returned(hop, r, True).wait_recv()
                returned(hop, r, False).wait_send()
    routes.wait_sent(row_slots_ref, landed_ref)


def expert_apply(row_slots, grad_rows, weights, router):
    planes, members = lax.axis_size("seq"), lax.axis_size("exp")
    experts, capacity, width = row_slots.shape
    up, down, near_up, near_half = weights
    units = up.shape[2]
    hops = planes // 2
    count = hops * members * capacity
    half, wide = jnp.bfloat16, jnp.float32
    vmem = pl.BlockSpec(memory_space=pltpu.VMEM)
    slotted = (hops, members, capacity, width)
    every = (hops, members)
    return pl.pallas_call(
        functools.partial(expert_kernel, planes, members),
        name="expert_apply",
        in_specs=[vmem] * 7,
        out_specs=[vmem] * 7,
        out_shape=[
            jax.ShapeDtypeStruct(slotted, half),
            jax.ShapeDtypeStruct(slotted, half),
            jax.ShapeDtypeStruct(up.shape, wide),
            jax.ShapeDtypeStruct(down.shape, wide),
            jax.ShapeDtypeStruct(up.shape, half),
            jax.ShapeDtypeStruct(down.shape, half),
            jax.ShapeDtypeStruct(router.shape, wide),
        ],
        scratch_shapes=[
            pltpu.VMEM(slotted, half),
            pltpu.VMEM((count, width), half),
            pltpu.VMEM((count, width), half),
            pltpu.VMEM((count, width), half),
            pltpu.VMEM(down.shape[1:], half),
            pltpu.VMEM((count, width), wide),
            pltpu.VMEM((count, width), wide),
            pltpu.VMEM((count, units), half),
            pltpu.VMEM((count, units), half),
            pltpu.VMEM((count, units), half),
            pltpu.VMEM((count, units), half),
            pltpu.VMEM((count, experts), wide),
            pltpu.VMEM(up.shape[1:], wide),
            pltpu.VMEM(down.shape[1:], wide),
            pltpu.VMEM(slotted, half),
            pltpu.SemaphoreType.DMA,
            pltpu.SemaphoreType.DMA,
            pltpu.SemaphoreType.DMA(every),
            pltpu.SemaphoreType.DMA(every),
        ]
        + route_semaphores(planes, members),
        compiler_params=pltpu.CompilerParams(
            collective_id=4, has_side_effects=True, vmem_limit_bytes=60 * 1024 * 1024
        ),
        cost_estimate=pl.CostEstimate(
            flops=24 * count * width * units,
            transcendentals=4 * count * units,
            bytes_accessed=3 * 10**7,
        ),
    )(row_slots, grad_rows, *weights, router)


def gradient_kernel(
    planes,
    side,
    delta_ref,
    conv_ref,
    grad_scan_ref,
    in_cols_ref,
    out_cols_ref,
    in_diag_ref,
    decay_log_ref,
    carried_ref,
    carried_back_ref,
    delta_pre_ref,
    delta_low_ref,
    conv_pre_ref,
    extended_ref,
    normed_ref,
    normed_gate_ref,
    layer_ref,
    rim_layer_ref,
    grad_resid_ref,
    delta_proj_ref,
    state_proj_ref,
    in_proj_ref,
    conv_weight_ref,
    vectors_ref,
    skip_grad_ref,
    norm_grad_ref,
    router_grad_ref,
    early_out_ref,
    gate_slope_ref,
    returned_ref,
    far_up_ref,
    far_down_ref,
    in_grad_ref,
    total_out_ref,
    total_gate_ref,
    total_inner_ref,
    total_small_ref,
    landed_ref,
    near_up_ref,
    near_down_ref,
    grad_delta,
    grad_conv,
    grad_in,
    grad_out,
    grad_log,
    drive,
    kept,
    stack,
    slope_stack,
    low_grads,
    padded,
    slopes,
    small,
    rim_out,
    rim_in,
    rim_sent,
    rim_landed,
    in_part,
    part_loaded,
    given_inner,
    given_small,
    early_gate_ref,
    *rest,
):
    early_buffers, tail_buffers, small_buffers = rest[:12], rest[12:18], rest[18:24]
    swap_sent, swap_landed, rest = rest[24], rest[25], rest[26:]
    sums = Sums(planes, side, rest[:8], rest[8:16])
    routes = Routes(planes, 2 * side * side, *rest[16:19])
    tokens, inner_width = conv_ref.shape
    width = layer_ref.shape[1]
    low_rank = delta_low_ref.shape[1]
    states, taps = decay_log_ref.shape[0], conv_weight_ref.shape[0]
    sequences = extended_ref.shape[0]
    piece = tokens // sequences
    chips = side * side
    wide, half = jnp.float32, jnp.bfloat16
    skip_ref, mixer_gain_ref = vectors_ref.at[2:3], vectors_ref.at[3:4, :width]
    devices = 2 * chips * planes
    place = sums.plane * (2 * chips) + sums.member
    before, after = lax.rem(place + devices - 1, devices), lax.rem(place + 1, devices)
    barrier = pltpu.get_barrier_semaphore()
    for peer in (before, after):
        device = chain_device(peer, 2 * chips)
        pl.semaphore_signal(barrier, inc=1, device_id=device, device_id_type=MESH)
    pl.semaphore_signal(barrier, inc=1, device_id=neighbour_plane(), device_id_type=MESH)
    greeted = 3 + sums.signal_peers(barrier) + routes.signal_peers(barrier)
    tall = width // chips
    size = tall // planes
    for c in range(2):
        gate_part = gate_slope_ref[:, c * width : (c + 1) * width]
        for m in range(chips):
            part = normed_ref[:tokens, m * tall : (m + 1) * tall]
            product = rows_dot(part, gate_part).astype(half)
            for z in range(planes):
                early_gate_ref[c, m // side, m % side, z] = product[z * size : (z + 1) * size]
    pl.semaphore_wait(barrier, greeted)

    in_load = pltpu.make_async_copy(in_proj_ref.at[:, pl.ds(0, inner_width)], in_part, part_loaded)
    in_load.start()
    pair = range(2)
    given = (early_out_ref, early_gate_ref)
    results = (total_out_ref, total_gate_ref)
    stages = [tuple(early_buffers[2 * stage + i] for stage in range(6)) for i in pair]
    blocks = [result.at[sums.core, sums.first, sums.second] for result in results]
    swaps = [
        swapped(src, dst, swap_sent.at[i], swap_landed.at[i])
        for i, (src, dst) in enumerate([(far_up_ref, near_up_ref), (far_down_ref, near_down_ref)])
    ]
    for i in pair:
        sums.pair_half(i, given[i], stages[i][0]).start()
    routes.start(returned_ref, landed_ref, True)
    swaps[0].start()
    groups = inner_width // GROUP
    count = sequences * groups
    cols_each = piece // BLK

    def scan_group(g, carry):
        q, j = g // groups, lax.rem(g, groups)
        rows = pl.ds(pl.multiple_of(q * piece, piece), piece)
        lanes = pl.ds(pl.multiple_of(j * GROUP, GROUP), GROUP)
        cols = pl.ds(q * cols_each, cols_each)

        def middle():
            @pl.when(g == 0)
            def _():
                for i in pair:
                    sums.after_pair(i, given[i], *stages[i][:2])

            @pl.when(g == count // 2)
            def _():
                for i in pair:
                    sums.after_first(i, *stages[i][:4])

            @pl.when(g == count - 2)
            def _():
                for i in pair:
                    sums.after_second(i, *stages[i][2:6])

            @pl.when(g == count - 1)
            def _():
                for i in pair:
                    sums.after_planes(i, *stages[i][4:6], blocks[i])
                swaps[1].start()

        one = pl.ds(q, 1)
        backward_body(
            middle,
            j == 0,
            delta_ref.at[rows, lanes],
            conv_ref.at[rows, lanes],
            grad_scan_ref.at[rows, lanes],
            in_cols_ref.at[cols],
            out_cols_ref.at[cols],
            in_diag_ref.at[rows],
            decay_log_ref.at[:, lanes],
            carried_ref.at[one, :, lanes],
            carried_back_ref.at[one, :, lanes],
            grad_delta.at[rows, lanes],
            grad_conv.at[rows, lanes],
            grad_in.at[rows],
            grad_out.at[rows],
            grad_log.at[one, :, lanes],
            drive,
            kept,
            stack,
            slope_stack,
        )
        return carry

    lax.fori_loop(0, count, scan_group, 0)
    unit = LANE_UNIT
    low_grads[...] = jnp.zeros(low_grads.shape, wide)
    small[...] = jnp.zeros(small.shape, wide)
    at_delta = low_rank + 2 * states
    at_log = at_delta + low_rank
    at_conv = at_log + states
    at_end = at_conv + taps + 2

    def first(j, carry):
        at = lane_unit(j)
        slope = grad_delta[:, at] * jax.nn.sigmoid(delta_pre_ref[:, at])
        small[at_conv + taps + 1 : at_conv + taps + 2, at] = jnp.sum(slope, axis=0, keepdims=True)
        small[at_delta:at_log, at] = rows_dot(delta_low_ref[...], slope, lax.Precision.HIGHEST)
        low_grads[...] += two_part(slope, delta_proj_ref[:, at], ((1,), (1,)))
        return carry

    lax.fori_loop(0, inner_width // unit, first, 0)
    for i in pair:
        sums.planes_gathered(i, blocks[i])
        sums.gather_second_start(i, results[i])
    column = lax.broadcasted_iota(jnp.int32, grad_in.shape, 1) // states
    row = lax.rem(lax.broadcasted_iota(jnp.int32, grad_in.shape, 0), BLK)
    fold = jnp.where(
        lax.rem(lax.broadcasted_iota(jnp.int32, (grad_in.shape[1], states), 0), states)
        == lax.broadcasted_iota(jnp.int32, (grad_in.shape[1], states), 1),
        1.0,
        0.0,
    ).astype(half)

    def folded(ref):
        return two_part(jnp.where(column == row, ref[...], 0.0), fold, ((1,), (0,)))

    coefs = jnp.concatenate([low_grads[...], folded(grad_in), folded(grad_out)], axis=1)
    keep = jnp.where(place > 0, 1.0, 0.0)
    rim_out[...] = jnp.zeros(rim_out.shape, half)

    def dense(at):
        small[:at_delta, at] = rows_dot(coefs, conv_ref[:, at], lax.Precision.HIGHEST)
        through = two_part(coefs, state_proj_ref[:, at], ((1,), (0,)))
        through = through + grad_scan_ref[:, at] * skip_ref[:, at] + grad_conv[:, at]
        pre = conv_pre_ref[:, at]
        sigma = jax.nn.sigmoid(pre)
        through = through * (sigma * (1.0 + pre * (1.0 - sigma)))
        small[at_conv + taps : at_conv + taps + 1, at] = jnp.sum(through, axis=0, keepdims=True)
        for q in range(sequences):
            padded[q, :8] = jnp.zeros((8, unit), wide)
            padded[q, 8 + piece :] = jnp.zeros((8, unit), wide)
            padded[q, 8 : 8 + piece] = through[q * piece : (q + 1) * piece]
            result = jnp.zeros((piece, unit), wide)
            rim = jnp.zeros((8, unit), wide)
            for tap in range(taps):
                weight = conv_weight_ref[tap : tap + 1, at]
                shift = taps - 1 - tap
                result = result + weight * padded[q, 8 + shift : 8 + shift + piece]
                rim = rim + weight * padded[q, 8 - tap : 16 - tap]
            slopes[q * piece : (q + 1) * piece, at] = result.astype(half)
            rim_out[q, 8 - (taps - 1) :, at] = (rim[: taps - 1] * keep).astype(half)
            slopes[tokens + q * 8 : tokens + (q + 1) * 8, at] = rim_out[q, :, at]
        for tap in range(taps):
            start = 8 - (taps - 1) + tap
            product = jnp.zeros((1, unit), wide)
            for q in range(sequences):
                product = product + jnp.sum(
                    padded[q, 8 : 8 + piece] * extended_ref[q, start : start + piece, at],
                    axis=0,
                    keepdims=True,
                )
            small[at_conv + tap : at_conv + tap + 1, at] = product

    slabs = given_inner.shape[0]

    def tail_of(s):
        return [buffer.at[s] for buffer in tail_buffers]

    def after_tail_pair(s):
        sums.after_pair(2 + s, given_inner.at[s], *tail_of(s)[:2])

    def slab(s, carry):
        for c in range(2):
            at = lane_unit(c * slabs + s)
            dense(at)
            for m in range(chips):
                product = rows_dot(
                    normed_ref[:, m * tall : (m + 1) * tall], slopes[:, at]
                ).astype(half)
                for z in range(planes):
                    part = product[z * size : (z + 1) * size]
                    given_inner[s, c, m // side, m % side, z] = part
        sums.pair_half(2 + s, given_inner.at[s], tail_buffers[0].at[s]).start()

        @pl.when(s > 0)
        def _():
            after_tail_pair(s - 1)

        return carry

    lax.fori_loop(0, slabs, slab, 0)
    after_tail_pair(slabs - 1)
    rim_copy = pltpu.make_async_remote_copy(
        src_ref=rim_out,
        dst_ref=rim_in,
        send_sem=rim_sent,
        recv_sem=rim_landed,
        device_id=chain_device(before, 2 * chips),
        device_id_type=MESH,
    )
    rim_copy.start()
    in_load.wait()
    projected = cols_dot(slopes[...], in_part[...])
    normed_grad = normed_gate_ref[...] + projected[:tokens]

    def normal_of(values):
        scaling = lax.rsqrt(jnp.mean(values * values, axis=-1, keepdims=True) + EPSILON)
        return values * scaling, scaling

    normal, scaling = normal_of(layer_ref[...].astype(wide))
    gain_grad = jnp.sum(normed_grad * normal, axis=0, keepdims=True)
    for q in range(sequences):
        rim_normal, _ = normal_of(rim_layer_ref[q].astype(wide))
        rim_grad = projected[tokens + q * 8 : tokens + (q + 1) * 8]
        gain_grad = gain_grad + jnp.sum(rim_grad * rim_normal, axis=0, keepdims=True)
    log_total = grad_log[0]
    for q in range(1, sequences):
        log_total = log_total + grad_log[q]
    small[at_log:at_conv] = log_total
    small[at_end : at_end + 1] = skip_grad_ref[...]
    small[at_end + 1 : at_end + 2, :width] = gain_grad
    small[at_end + 1 : at_end + 2, width:] = norm_grad_ref[...]
    for k in range(router_grad_ref.shape[0]):
        line = at_end + 2 + k // 2
        small[line : line + 1, (k % 2) * width : (k % 2 + 1) * width] = router_grad_ref[k : k + 1]
    low = given_small.shape[4]
    for c in range(2):
        for m in range(chips):
            for z in range(planes):
                line = (m * planes + z) * low
                given_small[c, m // side, m % side, z] = small[
                    line : line + low, c * width : (c + 1) * width
                ].astype(half)
    last = 2 + slabs
    every = range(slabs)
    sums.pair_half(last, given_small, small_buffers[0]).start()
    for s in every:
        sums.after_first(2 + s, *tail_of(s)[:4])
    sums.after_pair(last, given_small, *small_buffers[:2])
    for s in every:
        sums.after_second(2 + s, *tail_of(s)[2:6])
    for i in pair:
        sums.gather_across(i, results[i])
    weighted = normed_grad * mixer_gain_ref[...]
    in_grad_ref[...] = grad_resid_ref[...] + scaling * (
        weighted - normal * jnp.mean(weighted * normal, axis=-1, keepdims=True)
    )
    sums.after_first(last, *small_buffers[:4])
    tails = [total_inner_ref.at[s] for s in every] + [total_small_ref]
    tail_blocks = [total.at[sums.core, sums.first, sums.second] for total in tails]
    for s in every:
        sums.after_planes(2 + s, *tail_of(s)[4:6], tail_blocks[s])
    sums.after_second(last, *small_buffers[2:6])
    for s in every:
        sums.planes_gathered(2 + s, tail_blocks[s])
        sums.gather_second_start(2 + s, tails[s])
    sums.after_planes(last, *small_buffers[4:6], tail_blocks[slabs])
    for s in every:
        sums.gather_across(2 + s, tails[s])
    sums.planes_gathered(last, tail_blocks[slabs])
    sums.gather_second_start(last, total_small_ref)
    for i in pair:
        sums.gather_pass(i, results[i])
    rim_copy.wait()
    keep_last = jnp.where(place < devices - 1, 1.0, 0.0)
    for q in range(sequences):
        rows = slice((q + 1) * piece - 8, (q + 1) * piece)
        added = cols_dot(rim_in[q], in_part[...]) * keep_last
        fixed = (normed_grad[rows] + added) * mixer_gain_ref[...]
        mean = jnp.mean(fixed * normal[rows], axis=-1, keepdims=True)
        in_grad_ref[rows, :] = grad_resid_ref[rows, :] + scaling[rows] * (
            fixed - normal[rows] * mean
        )
    sums.gather_across(last, total_small_ref)
    for s in every:
        sums.gather_pass(2 + s, tails[s])
    sums.gather_pass(last, total_small_ref)
    routes.wait(returned_ref, landed_ref, True)
    for swap in swaps:
        swap.wait()
    ends = [(i, stages[i], blocks[i], results[i]) for i in pair]
    ends += [(2 + s, tail_of(s), tail_blocks[s], tails[s]) for s in every]
    ends += [(last, small_buffers, tail_blocks[slabs], total_small_ref)]
    for i, buffers, block, result in ends:
        sums.scatter_sent(i, *buffers, block)
        sums.gather_end(i, result)


def all_gradients(operands, small_height, side):
    planes = lax.axis_size("seq")
    tokens, inner_width = operands[1].shape
    width = operands[15].shape[1]
    states, low_rank = operands[6].shape[0], operands[10].shape[1]
    sequences = operands[7].shape[0]
    piece = tokens // sequences
    low = -(-small_height // (side * side * planes))
    lead = (2, side, side, planes)
    big = operands[26].shape
    slabs = width // LANE_UNIT
    inner = (slabs,) + lead + (big[4], LANE_UNIT)
    little = lead + (low, width)
    vmem, anywhere = (pl.BlockSpec(memory_space=space) for space in (pltpu.VMEM, pl.ANY))
    half, wide = jnp.bfloat16, jnp.float32
    token_wide = pltpu.VMEM((tokens, inner_width), wide)
    narrow = pltpu.VMEM((tokens, BLK * states), wide)
    steps = pltpu.VMEM((piece, states, GROUP), wide)
    stack = pltpu.VMEM((BLK * states, GROUP), half)
    rim = pltpu.VMEM((sequences, 8, inner_width), half)
    tail_shapes = [value.shape for value in scatter_buffers([inner[5:]], planes, side)]
    moved = [jax.ShapeDtypeStruct(value.shape, half) for value in operands[28:]]
    semaphores = stage_semaphores(3 + slabs, planes, side)
    return pl.pallas_call(
        functools.partial(gradient_kernel, planes, side),
        name="backward_gradients",
        in_specs=[vmem] * 20 + [anywhere] + [vmem] * 7 + [anywhere] * 3,
        out_specs=[vmem] * 5 + [anywhere] * 3,
        out_shape=[jax.ShapeDtypeStruct((tokens, width), wide)]
        + [jax.ShapeDtypeStruct(shape, half) for shape in (big, big, inner, little)]
        + moved,
        scratch_shapes=[
            token_wide,
            token_wide,
            narrow,
            narrow,
            pltpu.VMEM((sequences, states, inner_width), wide),
            pltpu.VMEM((piece, GROUP), wide),
            steps,
            stack,
            stack,
            pltpu.VMEM((tokens, low_rank), wide),
            pltpu.VMEM((sequences, piece + 16, LANE_UNIT), wide),
            pltpu.VMEM((tokens + 8 * sequences, inner_width), half),
            pltpu.VMEM((low * side * side * planes, inner_width), wide),
            rim,
            rim,
            pltpu.SemaphoreType.DMA,
            pltpu.SemaphoreType.DMA,
            pltpu.VMEM((width, inner_width), half),
            pltpu.SemaphoreType.DMA,
            pltpu.VMEM(inner, half),
            pltpu.VMEM(little, half),
            pltpu.VMEM(big, half),
        ]
        + scatter_buffers([big[4:], big[4:]], planes, side)
        + [pltpu.VMEM((slabs,) + shape, half) for shape in tail_shapes]
        + scatter_buffers([little[4:]], planes, side)
        + [pltpu.SemaphoreType.DMA((2,)), pltpu.SemaphoreType.DMA((2,))]
        + semaphores
        + semaphores
        + route_semaphores(planes, 2 * side * side),
        compiler_params=pltpu.CompilerParams(
            collective_id=3, has_side_effects=True, vmem_limit_bytes=63 * 1024 * 1024
        ),
        cost_estimate=pl.CostEstimate(flops=10**8, transcendentals=0, bytes_accessed=2 * 10**8),
    )(*operands)


def on_device(
    layer_in,
    mixer_gain,
    in_proj,
    conv_weight,
    conv_bias,
    state_proj,
    delta_proj,
    delta_bias,
    decay_log,
    skip_gain,
    out_proj,
    expert_norm,
    router_weight,
    expert_up,
    expert_down,
    expert_ids,
    capacity_slot,
    out_grad,
):
    sequences, piece_len, width = layer_in.shape
    tokens = sequences * piece_len
    taps, inner_width = conv_weight.shape
    low_rank = delta_proj.shape[0]
    states = decay_log.shape[0]
    experts = router_weight.shape[1]
    senders = lax.axis_size("exp")
    capacity = (5 * tokens + 4 * experts - 1) // (4 * experts)
    planes = lax.axis_size("seq")
    hops = planes // 2
    flat_ids = expert_ids.reshape(1, tokens)
    flat_slot = capacity_slot.reshape(1, tokens)
    target = jnp.where(flat_slot < capacity, flat_ids * capacity + flat_slot, experts * capacity)
    slot_rows = jnp.arange(experts * capacity, dtype=jnp.int32)
    picks = (slot_rows[:, None] == target).astype(jnp.bfloat16)
    (
        normed_half,
        extended,
        gate_half,
        conv_pre,
        conv_flat,
        delta_pre,
        delta,
        delta_low,
        in_cols,
        out_cols,
        in_diag,
        delta_sum,
        carried,
        mixer_pre,
        mixed,
        resid,
        row_slots,
        grad_rows,
        near_up,
        near_half,
        rim_layer,
        vectors,
    ) = forward(
        [
            layer_in.reshape(tokens, width),
            out_grad.reshape(tokens, width),
            target,
            mixer_gain,
            conv_bias,
            delta_bias,
            skip_gain,
            expert_norm,
            in_proj,
            conv_weight,
            state_proj.T,
            delta_proj,
            decay_log,
            out_proj,
            expert_up,
            expert_down,
        ],
        capacity,
        states,
        sequences,
        low_rank,
        experts,
    )
    gate_act = jax.nn.silu(gate_half)
    scaling_two = lax.rsqrt(jnp.mean(resid * resid, axis=-1, keepdims=True) + EPSILON)
    weights = [expert_up, expert_down, near_up, near_half]
    expert_out, back_rows, grad_up, grad_down, far_up, far_down, grad_router = expert_apply(
        row_slots, grad_rows, weights, router_weight.T
    )
    grad_routed = rows_dot(
        jnp.concatenate([picks] * hops, axis=0), back_rows.reshape(hops * senders * capacity, width)
    )
    grad_top = out_grad.reshape(tokens, width).astype(jnp.float32)
    grad_resid_norm, grad_expert_norm = norm_backward(resid, scaling_two, expert_norm, grad_routed)
    grad_resid = grad_top + grad_resid_norm
    grad_mixer = grad_resid.astype(jnp.bfloat16)
    grad_out_proj = rows_dot(mixed, grad_mixer)
    grad_mixed = cols_dot(grad_mixer, out_proj)
    grad_scan = grad_mixed * gate_act
    grad_gate_half = grad_mixed * mixer_pre * silu_slope(gate_half)
    grad_gate_half = grad_gate_half.astype(jnp.bfloat16)
    grad_normed_gate = cols_dot(grad_gate_half, in_proj[:, inner_width:])
    grad_skip_gain = jnp.sum(grad_scan * conv_flat, axis=0, keepdims=True)
    (gradient_first,) = scan_call(
        back_summary_kernel,
        "back_summary",
        sequences,
        states,
        [("wide", delta), ("wide", grad_scan), ("cols", out_cols), ("rates", decay_log)],
        ["state"],
        [],
    )
    carried_back = exchange(gradient_first, delta_sum, decay_log)
    side = math.isqrt(senders // 2)
    big = (2, side, side, planes, inner_width // (senders * planes), width)

    early = [
        grad_out_proj.astype(jnp.bfloat16).reshape(big),
        grad_gate_half,
    ]
    heights = [low_rank + 2 * states, low_rank, states, taps, 1, 1, 1, 1, experts // 2]
    in_grad, sum_out, sum_gate, sum_inner, sum_small, back_out, near_up, near_down = all_gradients(
        [
            delta,
            conv_flat,
            grad_scan,
            in_cols,
            out_cols,
            in_diag,
            decay_log,
            carried,
            carried_back,
            delta_pre,
            delta_low,
            conv_pre,
            extended,
            normed_half,
            grad_normed_gate,
            layer_in.reshape(tokens, width),
            rim_layer,
            grad_resid,
            delta_proj,
            state_proj.T,
            in_proj,
            conv_weight,
            vectors,
            grad_skip_gain,
            grad_expert_norm,
            grad_router,
        ]
        + early
        + [expert_out, far_up, far_down],
        sum(heights),
        side,
    )
    grad_up_own = grad_up + near_up.astype(jnp.float32)
    grad_down_own = grad_down + near_down.astype(jnp.float32)
    token_out = rows_dot(
        jnp.concatenate([picks] * hops, axis=0), back_out.reshape(hops * senders * capacity, width)
    )
    layer_out = (resid + token_out).astype(jnp.bfloat16).reshape(sequences, piece_len, width)
    in_grad = in_grad.reshape(sequences, piece_len, width)
    rows_of = (inner_width, width)
    slabs = width // LANE_UNIT
    by_slab = sum_inner.reshape(slabs, 2, width, LANE_UNIT)
    inner_parts = [by_slab[s, c] for c in range(2) for s in range(slabs)]
    grad_in_proj = jnp.concatenate(
        inner_parts + [sum_gate[c].reshape(width, width) for c in range(2)], axis=1
    ).astype(jnp.float32)
    small_halves = sum_small.reshape(2, -1, width)
    small_wide = jnp.concatenate([small_halves[0], small_halves[1]], axis=1).astype(jnp.float32)
    offsets = [sum(heights[:at]) for at in range(len(heights) + 1)]
    pieces = [small_wide[offsets[at] : offsets[at + 1]] for at in range(len(heights))]
    summed = (
        pieces[7][0, :width],
        grad_in_proj,
        pieces[3],
        pieces[4][0],
        pieces[0].T,
        pieces[1],
        pieces[5][0],
        pieces[2],
        pieces[6][0],
        sum_out.reshape(rows_of).astype(jnp.float32),
        pieces[7][0, width:],
        pieces[8].reshape(experts, width).T,
    )
    return (
        layer_out,
        in_grad,
        summed[0],
        summed[1],
        summed[2],
        summed[3],
        summed[4],
        summed[5],
        summed[6],
        summed[7],
        summed[8],
        summed[9],
        summed[10],
        summed[11],
        grad_up_own,
        grad_down_own,
    )


def solution(mesh):
    placed = (
        P(None, ("seq", "exp"), None),
        P(),
        P(),
        P(),
        P(),
        P(),
        P(),
        P(),
        P(),
        P(),
        P(),
        P(),
        P(),
        P("exp", None, "seq"),
        P("exp", "seq", None),
        P(None, ("seq", "exp")),
        P(None, ("seq", "exp")),
        P(None, ("seq", "exp"), None),
    )
    return jax.shard_map(
        on_device,
        mesh=mesh,
        in_specs=placed,
        out_specs=(
            P(None, ("seq", "exp"), None),
            P(None, ("seq", "exp"), None),
            P(),
            P(),
            P(),
            P(),
            P(),
            P(),
            P(),
            P(),
            P(),
            P(),
            P(),
            P(),
            P("exp", None, "seq"),
            P("exp", "seq", None),
        ),
        check_vma=False,
    )
```
